32 devices in a mesh: dp: 16 (over z, x, core), tensor: 2 (over y).
Axes of the slice: x: 2, y: 2, z: 4, core: 2. Of those that a mesh axis runs over, the one named last changes fastest.
Arguments:
- hidden_in: bfloat16 [16384, 768], P(('dp', 'tensor')), may hold values from -6 to 6
- segment_ids: int32 [16384], P('dp'), may hold values from 0 to 6, as said below
- norm_gain: bfloat16 [768], P('dp'), may hold values from 0.5 to 1.5
- proj_inner: bfloat16 [768, 2, 1536], P('dp', None, 'tensor'), may hold values from -0.21875 to 0.21875
- proj_shared: bfloat16 [768, 2, 128], P('dp'), may hold values from -0.21875 to 0.21875
- proj_step: bfloat16 [768, 24], P('dp', 'tensor'), may hold values from -0.21875 to 0.21875
- conv_inner: bfloat16 [4, 1536], P(None, 'tensor'), may hold values from -3 to 3
- conv_shared: bfloat16 [4, 2, 128], P(None, None, 'dp'), may hold values from -3 to 3
- step_bias: float32 [24], P('tensor'), may hold values from -6 to -3
- log_decay: float32 [24], P('tensor'), may hold values from 0 to 2
- skip_gain: float32 [24], P('tensor'), may hold values from 0.5 to 1.5
- gate_gain: bfloat16 [1536], P('tensor'), may hold values from 0.5 to 1.5
- proj_out: bfloat16 [1536, 768], P('tensor', 'dp'), may hold values from -0.15625 to 0.15625
- out_grad: bfloat16 [16384, 768], P(('dp', 'tensor')), may hold values from -6 to 6
Outputs:
- hidden_out: bfloat16 [16384, 768], P(('dp', 'tensor'))
- hidden_grad: float32 [16384, 768], P(('dp', 'tensor'))
- norm_grad: float32 [768], P('dp')
- inner_grad: float32 [768, 2, 1536], P('dp', None, 'tensor')
- shared_grad: float32 [768, 2, 128], P('dp')
- step_grad: float32 [768, 24], P('dp', 'tensor')
- conv_inner_grad: float32 [4, 1536], P(None, 'tensor')
- conv_shared_grad: float32 [4, 2, 128], P(None, None, 'dp')
- bias_grad: float32 [24], P('tensor')
- decay_grad: float32 [24], P('tensor')
- skip_grad: float32 [24], P('tensor')
- gate_grad: float32 [1536], P('tensor')
- out_proj_grad: float32 [1536, 768], P('tensor', 'dp')
The draws below stay inside these ranges and needn't reach their ends.
Inputs may be any that keep to these rules, and one draw needn't show every extreme that they name: `segment_ids`: in each sequence of 1024 tokens, 6 documents of one token or more carry ids 1 to 6 in rising order, followed by one run of padding with id 0 that ends the sequence.
All inputs are finite; a program needn't handle non-finite values.
Results may differ from the reference program's by a relative error of at most 0.019.
Values may be sent and summed in bfloat16 or wider, within the bound.
No kernel may reach another device: no remote copies, remote signals or barrier semaphores. Data moves between devices by JAX's collectives and lax.ppermute only.
A program may use at most 192 MiB of HBM per device.

```python
import jax
import jax.numpy as jnp
from jax import lax

D = 768
HEADS = 24
HEAD_DIM = 64
STATE = 128
CONV = 4
BLOCK = 256
DOCS = 6
INNER = 1536
SEQ_LEN = 1024
TOKENS = 16384


def one_packing(key):
    pad_key, weight_key = jax.random.split(key)
    padding = jax.random.randint(pad_key, (), max(1, SEQ_LEN // 32), max(2, SEQ_LEN // 8 + 1))
    filled = SEQ_LEN - padding
    powers = jax.random.randint(weight_key, (DOCS,), 0, 9)
    doc_weights = jnp.left_shift(jnp.ones((DOCS,), jnp.int32), powers)
    spare = filled - DOCS
    lengths = 1 + doc_weights * spare // jnp.sum(doc_weights)
    bounds = jnp.cumsum(lengths)[:DOCS - 1]
    positions = jnp.arange(SEQ_LEN, dtype=jnp.int32)
    doc_ids = 1 + jnp.sum((positions[:, None] >= bounds[None, :]).astype(jnp.int32), axis=1)
    return jnp.where(positions < filled, doc_ids, 0).astype(jnp.int32)


def draw_segment_ids(key, part):
    seq_keys = jax.random.split(jax.random.fold_in(key, 11), TOKENS // SEQ_LEN)
    return jax.vmap(one_packing)(seq_keys).reshape(TOKENS)


def level_of(key, extent, cuts, smallest, high):
    loudness, own = 1.0, jax.random.fold_in(key, 6)
    for dim, blocks in cuts:
        heights = jnp.exp(jax.random.uniform(jax.random.fold_in(own, dim), (blocks,), jnp.float32, smallest / len(cuts), high / len(cuts)))
        loudness = loudness * jnp.repeat(heights, extent[dim] // blocks).reshape([-1 if axis == dim else 1 for axis in range(len(extent))])
    return loudness


def normal_values(own_key, dims, scale, reach, shards=(), kind=jnp.bfloat16):
    result = scale * jax.random.normal(own_key, dims, jnp.float32)
    if shards:
        result = result * level_of(own_key, dims, shards, -0.22, 0.18)
    return jnp.clip(result, -reach, reach).astype(kind)


def setup_inputs(seed: int = 0) -> dict:
    key_list = jax.random.split(jax.random.key(seed), 15)
    hidden_in = normal_values(key_list[0], (TOKENS, D), 1.0, 6.0, ((0, 32),))
    segment_ids = draw_segment_ids(jax.random.fold_in(key_list[14], 71), 0)
    norm_gain = jnp.clip(1.0 + 0.1 * jax.random.normal(key_list[2], (D,), jnp.float32), 0.5, 1.5).astype(jnp.bfloat16)
    proj_inner = normal_values(key_list[3], (D, 2, INNER), D ** -0.5, 0.21875, ((0, 16), (2, 2)))
    proj_shared = normal_values(key_list[4], (D, 2, STATE), D ** -0.5, 0.21875, ((0, 16),))
    proj_step = normal_values(key_list[5], (D, HEADS), D ** -0.5, 0.21875, ((0, 16), (1, 2)))
    conv_inner = normal_values(key_list[6], (CONV, INNER), CONV ** -0.5, 3.0, ((1, 2),))
    conv_shared = normal_values(key_list[7], (CONV, 2, STATE), CONV ** -0.5, 3.0, ((2, 16),))
    step_bias = jnp.clip(-6.0 + 3.0 * jax.random.uniform(key_list[8], (HEADS,), jnp.float32) ** level_of(key_list[8], (HEADS,), ((0, 2),), -0.2, 0.2), -6.0, -3.0)
    log_decay = jnp.clip(2.0 * jax.random.uniform(key_list[9], (HEADS,), jnp.float32) ** level_of(key_list[9], (HEADS,), ((0, 2),), -0.2, 0.2), 0.0, 2.0)
    skip_gain = jnp.clip(0.5 + 1.0 * jax.random.uniform(key_list[10], (HEADS,), jnp.float32) ** level_of(key_list[10], (HEADS,), ((0, 2),), -0.2, 0.2), 0.5, 1.5)
    gate_gain = jnp.clip(1.0 + 0.1 * jax.random.normal(key_list[11], (INNER,), jnp.float32), 0.5, 1.5).astype(jnp.bfloat16)
    proj_out = normal_values(key_list[12], (INNER, D), INNER ** -0.5, 0.15625, ((0, 2), (1, 16)))
    out_grad = normal_values(key_list[13], (TOKENS, D), 1.0, 6.0, ((0, 32),))
    return dict(hidden_in=hidden_in, segment_ids=segment_ids, norm_gain=norm_gain, proj_inner=proj_inner, proj_shared=proj_shared, proj_step=proj_step, conv_inner=conv_inner, conv_shared=conv_shared, step_bias=step_bias, log_decay=log_decay, skip_gain=skip_gain, gate_gain=gate_gain, proj_out=proj_out, out_grad=out_grad)


epsilon = 1e-05
highest = lax.Precision.HIGHEST

@jax.custom_vjp
def low(v):
    return lax.optimization_barrier(v.astype(jnp.bfloat16)).astype(jnp.float32)

@jax.custom_vjp
def low_back(v):
    return v

def low_keep(v):
    return (low(v), None)

def low_pass(kept, grad):
    return (grad,)

def back_keep(v):
    return (v, None)

def back_low(kept, grad):
    return (low(grad),)
low.defvjp(low_keep, low_pass)
low_back.defvjp(back_keep, back_low)

def causal_conv(values, kernel, segment):
    kernel_len = kernel.shape[0]
    length = values.shape[0]
    summed = kernel[kernel_len - 1] * values
    for offset in range(1, kernel_len):
        shifted = jnp.concatenate([jnp.zeros((offset, values.shape[1]), values.dtype), values[:length - offset]], axis=0)
        earlier = jnp.concatenate([jnp.full((offset,), -1, jnp.int32), segment[:length - offset]])
        matching = (earlier == segment).astype(values.dtype)
        summed = summed + kernel[kernel_len - 1 - offset] * shifted * matching[:, None]
    return summed

def ssd_core(inputs, b_rows, c_rows, step_size, decay_rate, segment, block_len):
    length, head_count, head_size = inputs.shape
    block_count = length // block_len
    x_blocks = inputs.reshape(block_count, block_len, head_count, head_size)
    b_blocks = b_rows.reshape(block_count, block_len, b_rows.shape[1])
    c_blocks = c_rows.reshape(block_count, block_len, c_rows.shape[1])
    step_blocks = step_size.reshape(block_count, block_len, head_count)
    seg_blocks = segment.reshape(block_count, block_len)
    decay_sum = jnp.cumsum(step_blocks * decay_rate, axis=1)
    last_seg = seg_blocks[:, block_len - 1]
    prior_seg = jnp.concatenate([jnp.full((1,), -1, jnp.int32), last_seg[:block_count - 1]])
    causal = jnp.arange(block_len)[:, None] >= jnp.arange(block_len)[None, :]
    inside = ((seg_blocks[:, :, None] == seg_blocks[:, None, :]) & causal[None])[..., None]
    gap_decay = jnp.where(inside, decay_sum[:, :, None, :] - decay_sum[:, None, :, :], 0.0)
    within = jnp.where(inside, jnp.exp(gap_decay), 0.0)
    scores = jnp.einsum('ctn,csn->cts', c_blocks, b_blocks, precision=highest)
    mixing = scores[..., None] * within * step_blocks[:, None, :, :]
    in_block = jnp.einsum('ctsh,cshp->cthp', mixing, x_blocks, precision=highest)
    block_decay = decay_sum[:, block_len - 1, :]
    keeps_end = (seg_blocks == last_seg[:, None]).astype(inputs.dtype)
    to_end = jnp.exp(block_decay[:, None, :] - decay_sum) * keeps_end[..., None] * step_blocks
    block_state = jnp.einsum('cshp,csn->chpn', to_end[..., None] * x_blocks, b_blocks, precision=highest)
    block_index = jnp.arange(block_count)
    between = ((block_index[None, None, :] > block_index[None, :, None]) & (block_index[None, None, :] < block_index[:, None, None])).astype(inputs.dtype)
    span_decay = jnp.einsum('dek,kh->deh', between, block_decay, precision=highest)
    linked = ((block_index[None, :] < block_index[:, None]) & (prior_seg[:, None] == last_seg[None, :]))[..., None]
    carried = jnp.where(linked, jnp.exp(jnp.where(linked, span_decay, 0.0)), 0.0)
    entry_state = jnp.einsum('deh,ehpn->dhpn', carried, block_state, precision=highest)
    entry_gate = jnp.exp(decay_sum) * (seg_blocks == prior_seg[:, None]).astype(inputs.dtype)[..., None]
    from_past = jnp.einsum('ctn,chpn->cthp', c_blocks, entry_state, precision=highest) * entry_gate[..., None]
    return (in_block + from_past).reshape(length, head_count, head_size)

def mixer_local(gate_in, conv_in, shared_in, step_raw, taps_inner, taps_shared, step_bias, log_decay, skip_gain, segment, block_len, head_size):
    length = gate_in.shape[0]
    head_count = step_raw.shape[1]
    state_size = shared_in.shape[1] // 2
    live_mask = (segment != 0).astype(gate_in.dtype)
    conv_out = jax.nn.silu(causal_conv(conv_in, taps_inner, segment))
    shared_out = jax.nn.silu(causal_conv(shared_in, taps_shared, segment))
    step_size = jax.nn.softplus(step_raw + step_bias) * live_mask[:, None]
    decay_rate = -jnp.exp(log_decay)
    heads_view = conv_out.reshape(length, head_count, head_size)
    mixed = ssd_core(heads_view, shared_out[:, :state_size], shared_out[:, state_size:], step_size, decay_rate, segment, block_len)
    mixed = mixed + skip_gain[:, None] * heads_view
    mixed = mixed.reshape(length, head_count * head_size) * live_mask[:, None]
    return mixed * jax.nn.silu(gate_in)

def block_forward(hidden, segment, norm_gain, proj_inner, proj_shared, proj_step, conv_inner, conv_shared, step_bias, log_decay, skip_gain, gate_gain, proj_out):
    normed = low(hidden * lax.rsqrt(lax.optimization_barrier(jnp.mean(hidden * hidden, axis=-1, keepdims=True)) + epsilon) * norm_gain)
    gate_in = low_back(jnp.dot(normed, proj_inner[:, 0, :], precision=highest))
    conv_in = low_back(jnp.dot(normed, proj_inner[:, 1, :], precision=highest))
    shared_in = low_back(jnp.dot(normed, proj_shared.reshape(proj_shared.shape[0], -1), precision=highest))
    step_raw = low_back(jnp.dot(normed, proj_step, precision=highest))
    gated = mixer_local(gate_in, conv_in, shared_in, step_raw, conv_inner, conv_shared.reshape(conv_shared.shape[0], -1), step_bias, log_decay, skip_gain, segment, BLOCK, HEAD_DIM)
    normed_out = low(gated * lax.rsqrt(lax.optimization_barrier(jnp.mean(gated * gated, axis=-1, keepdims=True)) + epsilon) * gate_gain)
    return hidden + jnp.dot(normed_out, proj_out, precision=highest)

def reference(hidden_in, segment_ids, norm_gain, proj_inner, proj_shared, proj_step, conv_inner, conv_shared, step_bias, log_decay, skip_gain, gate_gain, proj_out, out_grad):
    weights = tuple((w.astype(jnp.float32) for w in (norm_gain, proj_inner, proj_shared, proj_step, conv_inner, conv_shared, step_bias, log_decay, skip_gain, gate_gain, proj_out)))
    seq_count = hidden_in.shape[0] // SEQ_LEN
    seq_hidden = hidden_in.astype(jnp.float32).reshape(seq_count, SEQ_LEN, D)
    seq_grad = out_grad.astype(jnp.float32).reshape(seq_count, SEQ_LEN, D)
    seq_segment = segment_ids.reshape(seq_count, SEQ_LEN)

    def one_sequence(totals, slices):
        hidden_now, segment_now, grad_now = slices

        def forward(hidden_value, *params):
            return block_forward(hidden_value, segment_now, *params)
        output, pullback = jax.vjp(forward, hidden_now, *weights)
        gradients = pullback(grad_now)
        return (tuple((a + b for a, b in zip(totals, gradients[1:]))), (output.astype(jnp.bfloat16), gradients[0]))
    totals, (seq_outputs, seq_input_grads) = lax.scan(one_sequence, tuple((jnp.zeros_like(w) for w in weights)), (seq_hidden, seq_segment, seq_grad))
    return (seq_outputs.reshape(-1, D), seq_input_grads.reshape(-1, D), totals[0], totals[1], totals[2], totals[3], totals[4], totals[5], totals[6], totals[7], totals[8], totals[9], totals[10])
```

```python
from functools import partial

import jax
import jax.numpy as jnp
from jax import lax
from jax.experimental import pallas as pl
from jax.experimental.pallas import tpu as pltpu
from jax.sharding import PartitionSpec as P

HEAD_DIM = 64
CHUNK = 128
LANES = 128
epsilon = 1e-05
f32 = jnp.float32
bf16 = jnp.bfloat16
highest = lax.Precision.HIGHEST


def dot_nn(a, b):
    return lax.dot_general(a, b, (((1,), (0,)), ((), ())), preferred_element_type=f32)


def dot_nt(a, b):
    return lax.dot_general(a, b, (((1,), (1,)), ((), ())), preferred_element_type=f32)


def dot_tn(a, b):
    return lax.dot_general(a, b, (((0,), (0,)), ((), ())), preferred_element_type=f32)


def dot_exact(a, b):
    return lax.dot_general(
        a, b, (((1,), (0,)), ((), ())), preferred_element_type=f32, precision=highest
    )


def dot_split(a, b):
    high = a.astype(bf16)
    rest = (a - high.astype(f32)).astype(bf16)
    return dot_nn(high, b) + dot_nn(rest, b)


def sigmoid(v):
    return 1.0 / (1.0 + jnp.exp(-v))


def softplus(v):
    return jnp.maximum(v, 0.0) + jnp.log1p(jnp.exp(-jnp.abs(v)))


def halves(lane_low, values, head):
    return jnp.where(lane_low, values[:, head : head + 1], values[:, head + 1 : head + 2])


def back_shift(window, offset):
    return pltpu.roll(window, offset, 0)[8:, :]


def ahead_shift(window, offset):
    rows = window.shape[0]
    return pltpu.roll(window, rows - offset, 0)[: rows - 8, :]


def conv_rows(window, taps, aux):
    total = taps[3:4, :] * window[8:, :]
    for offset in range(1, 4):
        total = total + taps[3 - offset : 4 - offset, :] * (
            back_shift(window, offset) * aux[:, offset : offset + 1]
        )
    return total


def forward_kernel(
    proj_ref,
    tapi_ref,
    taps_ref,
    bias_ref,
    rate_ref,
    skip_ref,
    aux_ref,
    segr_ref,
    mixed_ref,
    u_ref,
    su_ref,
    entry_ref,
    sums_ref,
    state_ref,
    carry_ref,
    scarry_ref,
    xw_ref,
):
    length, width = mixed_ref.shape
    chunks = length // CHUNK
    pairs = width // LANES
    shared_size = su_ref.shape[1]
    state_size = shared_size // 2
    shared_cols = slice(2 * width, 2 * width + shared_size)
    step_cols = slice(2 * width + shared_size, 2 * width + shared_size + LANES)
    state_ref[...] = jnp.zeros_like(state_ref)
    carry_ref[...] = jnp.zeros_like(carry_ref)
    scarry_ref[...] = jnp.zeros_like(scarry_ref)
    rows = lax.broadcasted_iota(jnp.int32, (CHUNK, CHUNK), 0)
    cols = lax.broadcasted_iota(jnp.int32, (CHUNK, CHUNK), 1)
    lower = rows >= cols
    summing = lower.astype(f32)
    lane_low = lax.broadcasted_iota(jnp.int32, (CHUNK, LANES), 1) < HEAD_DIM

    def chunk_step(chunk, _):
        start = pl.multiple_of(chunk * CHUNK, CHUNK)
        here = pl.ds(start, CHUNK)
        aux = aux_ref[here, :]
        live = aux[:, 7:8]
        same = lower & (aux[:, 0:1] == segr_ref[pl.ds(chunk, 1), :])
        shared_now = proj_ref[here, shared_cols]
        su = conv_rows(jnp.concatenate([scarry_ref[...], shared_now], axis=0), taps_ref[...], aux)
        scarry_ref[...] = shared_now[CHUNK - 8 :, :]
        su_ref[here, :] = su
        shared = (su * sigmoid(su)).astype(bf16)
        b_rows = shared[:, :state_size]
        c_rows = shared[:, state_size:]
        scores = jnp.where(same, dot_nt(c_rows, b_rows), 0.0)
        step = softplus(proj_ref[here, step_cols] + bias_ref[...]) * live
        decay = dot_exact(summing, step * rate_ref[...])
        decay_t = decay.T
        last = decay[CHUNK - 1 :, :]
        entry_scale = jnp.exp(decay) * aux[:, 8:9]
        end_scale = jnp.exp(last - decay) * aux[:, 9:10]
        keep = jnp.exp(last) * aux[:1, 10:11]
        state = state_ref[...]
        state_low = state.astype(bf16)
        entry_ref[pl.ds(chunk, 1)] = state_low[None]
        past = dot_nn(c_rows, state_low)
        square = jnp.zeros((CHUNK, LANES), f32)
        for pair in range(pairs):
            lanes = slice(pair * LANES, (pair + 1) * LANES)
            head = 2 * pair
            now = proj_ref[here, width + pair * LANES : width + (pair + 1) * LANES]
            window = jnp.concatenate([carry_ref[:, lanes], now], axis=0)
            carry_ref[:, lanes] = now[CHUNK - 8 :, :]
            u = conv_rows(window, tapi_ref[:, lanes], aux)
            u_ref[here, lanes] = u
            x = u * sigmoid(u)
            scaled = x * halves(lane_low, step, head)
            mixing = jnp.concatenate(
                [
                    (
                        scores
                        * jnp.exp(
                            jnp.minimum(decay[:, h : h + 1] - decay_t[h : h + 1, :], 0.0)
                        )
                    ).astype(bf16)
                    for h in (head, head + 1)
                ],
                axis=1,
            )
            stacked = jnp.concatenate(
                [jnp.where(lane_low, scaled, 0.0), jnp.where(lane_low, 0.0, scaled)], axis=0
            ).astype(bf16)
            inside = dot_nn(mixing, stacked)
            xw_ref[:, lanes] = (scaled * halves(lane_low, end_scale, head)).astype(bf16)
            mixed = (
                inside
                + past[:, lanes] * halves(lane_low, entry_scale, head)
                + skip_ref[:, lanes] * x
            ) * live
            mixed_ref[here, lanes] = mixed
            state_ref[:, lanes] = state[:, lanes] * halves(
                lane_low[:1], keep, head
            )
            gate = proj_ref[here, lanes]
            gated = mixed * gate * sigmoid(gate)
            square = square + gated * gated
        state_ref[...] += dot_tn(b_rows, xw_ref[...])
        sums_ref[here, :] = jnp.sum(square, axis=1, keepdims=True)
        return 0

    lax.fori_loop(0, chunks, chunk_step, 0)


def silu_slope(v, s):
    return s * (1.0 + v * (1.0 - s))


def backward_kernel(
    proj_ref,
    mixed_ref,
    u_ref,
    su_ref,
    entry_ref,
    nog_ref,
    sums_ref,
    tapi_ref,
    taps_ref,
    bias_ref,
    rate_ref,
    skip_ref,
    gain_ref,
    aux_ref,
    segr_ref,
    place_ref,
    dproj_ref,
    wide_ref,
    shared_ref,
    state_ref,
    ahead_ref,
    sahead_ref,
    xw_ref,
    ge_ref,
    row_ref,
    proda_ref,
    prodb_ref,
    *,
    full_inner,
):
    length, width = mixed_ref.shape
    chunks = length // CHUNK
    pairs = width // LANES
    shared_size = su_ref.shape[1]
    state_size = shared_size // 2
    shared_cols = slice(2 * width, 2 * width + shared_size)
    step_cols = slice(2 * width + shared_size, 2 * width + shared_size + LANES)
    for ref in (state_ref, ahead_ref, sahead_ref, row_ref, wide_ref, shared_ref):
        ref[...] = jnp.zeros_like(ref)
    rows = lax.broadcasted_iota(jnp.int32, (CHUNK, CHUNK), 0)
    cols = lax.broadcasted_iota(jnp.int32, (CHUNK, CHUNK), 1)
    upper = rows <= cols
    summing = (rows >= cols).astype(f32)
    unsumming = upper.astype(f32)
    last_row = (lax.broadcasted_iota(jnp.int32, (CHUNK, LANES), 0) == CHUNK - 1).astype(f32)
    lane_ids = lax.broadcasted_iota(jnp.int32, (CHUNK, LANES), 1)
    lane_low = lane_ids < HEAD_DIM

    def chunk_step(step_index, _):
        chunk = chunks - 1 - step_index
        start = pl.multiple_of(chunk * CHUNK, CHUNK)
        here = pl.ds(start, CHUNK)
        aux = aux_ref[here, :]
        live = aux[:, 7:8]
        same = upper & (aux[:, 0:1] == segr_ref[pl.ds(chunk, 1), :])
        sums = sums_ref[here, :]
        inv = lax.rsqrt(sums[:, 0:1] / full_inner + epsilon)
        mean = inv * sums[:, 1:2] / full_inner
        su = su_ref[here, :]
        su_sig = sigmoid(su)
        shared = (su * su_sig).astype(bf16)
        b_rows = shared[:, :state_size]
        c_rows = shared[:, state_size:]
        scores = jnp.where(same, dot_nt(b_rows, c_rows), 0.0)
        pre = proj_ref[here, step_cols] + bias_ref[...]
        step = softplus(pre) * live
        rate = rate_ref[...]
        decay = dot_exact(summing, step * rate)
        decay_t = decay.T
        last = decay[CHUNK - 1 :, :]
        entry_scale = jnp.exp(decay) * aux[:, 8:9]
        end_scale = jnp.exp(last - decay) * aux[:, 9:10]
        keep = jnp.exp(last) * aux[:1, 10:11]
        entry = entry_ref[pl.ds(chunk, 1)][0]
        dstate = state_ref[...]
        dstate_low = dstate.astype(bf16)
        past = dot_nn(c_rows, entry)
        bds = dot_nn(b_rows, dstate_low)
        score_grad = jnp.zeros((CHUNK, CHUNK), f32)
        col_part = jnp.zeros((CHUNK, LANES), f32)
        for pair in range(pairs):
            lanes = slice(pair * LANES, (pair + 1) * LANES)
            head = 2 * pair
            inner_lanes = slice(width + pair * LANES, width + (pair + 1) * LANES)
            gate = proj_ref[here, lanes]
            gate_sig = sigmoid(gate)
            gate_silu = gate * gate_sig
            mixed = mixed_ref[here, lanes]
            unit = mixed * gate_silu * inv
            nog = nog_ref[here, lanes]
            gg = inv * (nog * gain_ref[:, lanes] - unit * mean)
            dproj_ref[here, lanes] = (gg * mixed * silu_slope(gate, gate_sig)).astype(bf16)
            g = gg * gate_silu * live
            u = u_ref[here, lanes]
            u_sig = sigmoid(u)
            x = u * u_sig
            step_c = halves(lane_low, step, head)
            scaled = x * step_c
            stacked = jnp.concatenate(
                [jnp.where(lane_low, scaled, 0.0), jnp.where(lane_low, 0.0, scaled)], axis=0
            ).astype(bf16)
            g_low = g.astype(bf16)
            dmix = dot_nt(stacked, g_low)
            mixing = []
            for k, h in enumerate((head, head + 1)):
                decays = jnp.exp(jnp.minimum(decay_t[h : h + 1, :] - decay[:, h : h + 1], 0.0))
                dmix_h = dmix[k * CHUNK : (k + 1) * CHUNK, :]
                score_grad = score_grad + dmix_h * decays
                mixing_h = scores * decays
                mixing.append(mixing_h.astype(bf16))
                both = mixing_h * dmix_h
                col_part = jnp.where(lane_ids == h, jnp.sum(both, axis=1, keepdims=True), col_part)
                row_ref[h : h + 1, :] = jnp.sum(both, axis=0, keepdims=True)
            g_stacked = jnp.concatenate(
                [jnp.where(lane_low, g, 0.0), jnp.where(lane_low, 0.0, g)], axis=0
            ).astype(bf16)
            end_c = halves(lane_low, end_scale, head)
            entry_c = halves(lane_low, entry_scale, head)
            keep_c = halves(lane_low[:1], keep, head)
            from_state = end_c * bds[:, lanes]
            dscaled = dot_nn(jnp.concatenate(mixing, axis=1), g_stacked) + from_state
            xw_ref[:, lanes] = (scaled * end_c).astype(bf16)
            q = scaled * from_state
            ge = g * entry_c
            ge_ref[:, lanes] = ge.astype(bf16)
            dstate_p = dstate[:, lanes]
            tail = jnp.sum(q, axis=0, keepdims=True) + keep_c * jnp.sum(
                dstate_p * entry[:, lanes].astype(f32), axis=0, keepdims=True
            )
            proda_ref[:, lanes] = x * dscaled
            prodb_ref[:, lanes] = ge * past[:, lanes] - q + last_row * tail
            state_ref[:, lanes] = dstate_p * keep_c
            dx = step_c * dscaled + skip_ref[:, lanes] * g
            du = dx * silu_slope(u, u_sig)
            window = jnp.concatenate([du, ahead_ref[:, lanes]], axis=0)
            ahead_ref[:, lanes] = du[:8, :]
            cin = proj_ref[here, inner_lanes]
            taps = tapi_ref[:, lanes]
            dcin = taps[3:4, :] * du
            wide_ref[3:4, lanes] += jnp.sum(cin * du, axis=0, keepdims=True)
            for offset in range(1, 4):
                moved = ahead_shift(window, offset) * aux[:, 3 + offset : 4 + offset]
                dcin = dcin + taps[3 - offset : 4 - offset, :] * moved
                wide_ref[3 - offset : 4 - offset, lanes] += jnp.sum(
                    cin * moved, axis=0, keepdims=True
                )
            dproj_ref[here, inner_lanes] = dcin.astype(bf16)
            wide_ref[4:5, lanes] += jnp.sum(nog * unit, axis=0, keepdims=True)
            wide_ref[5:6, lanes] += jnp.sum(g * x, axis=0, keepdims=True)
        score_low = jnp.where(same, score_grad, 0.0).astype(bf16)
        ge_all = ge_ref[...]
        db = dot_nn(score_low, c_rows) + dot_nt(xw_ref[...], dstate_low)
        dc = dot_tn(score_low, b_rows) + dot_nt(ge_all, entry)
        state_ref[...] += dot_tn(c_rows, ge_all)
        ds = jnp.concatenate([db, dc], axis=1) * silu_slope(su, su_sig)
        window = jnp.concatenate([ds, sahead_ref[...]], axis=0)
        sahead_ref[...] = ds[:8, :]
        taps = taps_ref[...]
        sin = proj_ref[here, shared_cols]
        dsin = taps[3:4, :] * ds
        shared_ref[3:4, :] += jnp.sum(sin * ds, axis=0, keepdims=True)
        for offset in range(1, 4):
            moved = ahead_shift(window, offset) * aux[:, 3 + offset : 4 + offset]
            dsin = dsin + taps[3 - offset : 4 - offset, :] * moved
            shared_ref[3 - offset : 4 - offset, :] += jnp.sum(sin * moved, axis=0, keepdims=True)
        dproj_ref[here, shared_cols] = dsin.astype(bf16)
        place = place_ref[...]
        ddecay = row_ref[...].T - col_part + dot_split(prodb_ref[...], place)
        dlog = dot_exact(unsumming, ddecay)
        dstep = (dot_split(proda_ref[...], place) + rate * dlog) * live * sigmoid(pre)
        dproj_ref[here, step_cols] = dstep.astype(bf16)
        wide_ref[6:7, :LANES] += jnp.sum(dstep, axis=0, keepdims=True)
        wide_ref[6:7, LANES : 2 * LANES] += jnp.sum(step * dlog, axis=0, keepdims=True) * rate
        return 0

    lax.fori_loop(0, chunks, chunk_step, 0)


def token_facts(segments):
    length = segments.shape[0]
    chunks = length // CHUNK
    columns = [segments]
    for offset in range(1, 4):
        earlier = jnp.concatenate([jnp.full((offset,), -1, jnp.int32), segments[: length - offset]])
        columns.append(earlier == segments)
    for offset in range(1, 4):
        later = jnp.concatenate([segments[offset:], jnp.full((offset,), -1, jnp.int32)])
        columns.append(later == segments)
    columns.append(segments != 0)
    blocks = segments.reshape(chunks, CHUNK)
    last = blocks[:, CHUNK - 1 :]
    prior = jnp.concatenate([jnp.full((1, 1), -1, jnp.int32), last[: chunks - 1]], axis=0)
    columns.append((blocks == prior).reshape(length))
    columns.append((blocks == last).reshape(length))
    columns.append(jnp.broadcast_to(last == prior, blocks.shape).reshape(length))
    columns += [jnp.zeros_like(segments)] * 5
    aux = jnp.stack([c.astype(f32) for c in columns], axis=1)
    return aux, blocks.astype(f32)


def run_forward(proj, tapi, taps, bias, rate, skip, aux, segr):
    length = proj.shape[0]
    width = tapi.shape[1]
    shared_size = taps.shape[1]
    chunks = length // CHUNK
    sds = jax.ShapeDtypeStruct
    return pl.pallas_call(
        forward_kernel,
        out_shape=(
            sds((length, width), f32),
            sds((length, width), f32),
            sds((length, shared_size), f32),
            sds((chunks, shared_size // 2, width), bf16),
            sds((length, 1), f32),
        ),
        scratch_shapes=[
            pltpu.VMEM((shared_size // 2, width), f32),
            pltpu.VMEM((8, width), f32),
            pltpu.VMEM((8, shared_size), f32),
            pltpu.VMEM((CHUNK, width), bf16),
        ],
        name="scan_forward",
    )(proj, tapi, taps, bias, rate, skip, aux, segr)


def run_backward(
    proj, mixed, u, su, entry, nog, sums, tapi, taps, bias, rate, skip, gain, aux, segr, place, full_inner
):
    length, width = mixed.shape
    shared_size = su.shape[1]
    sds = jax.ShapeDtypeStruct
    return pl.pallas_call(
        partial(backward_kernel, full_inner=float(full_inner)),
        out_shape=(
            sds(proj.shape, bf16),
            sds((8, width), f32),
            sds((8, shared_size), f32),
        ),
        scratch_shapes=[
            pltpu.VMEM((shared_size // 2, width), f32),
            pltpu.VMEM((8, width), f32),
            pltpu.VMEM((8, shared_size), f32),
            pltpu.VMEM((CHUNK, width), bf16),
            pltpu.VMEM((CHUNK, width), bf16),
            pltpu.VMEM((LANES, CHUNK), f32),
            pltpu.VMEM((CHUNK, width), f32),
            pltpu.VMEM((CHUNK, width), f32),
        ],
        name="scan_backward",
    )(proj, mixed, u, su, entry, nog, sums, tapi, taps, bias, rate, skip, gain, aux, segr, place)


def gather_rows(shard):
    count = lax.axis_size("dp")
    index = lax.axis_index("dp")
    whole = shard[None]
    bit = count // 2
    while bit:
        other = lax.ppermute(whole, "dp", [(i, i ^ bit) for i in range(count)])
        mine = (index & bit) == 0
        first = jnp.where(mine, whole, other)
        second = jnp.where(mine, other, whole)
        whole = jnp.stack([first, second], axis=1)
        whole = whole.reshape((-1,) + shard.shape)
        bit //= 2
    return whole.reshape((-1,) + shard.shape[1:])


def scatter_rows(partial_sum):
    count = lax.axis_size("dp")
    index = lax.axis_index("dp")
    rows = partial_sum.shape[0] // count
    total = partial_sum.reshape((count, rows) + partial_sum.shape[1:])
    bit = 1
    while bit < count:
        total = total.reshape((-1, 2) + total.shape[1:])
        side = jnp.where((index & bit) == 0, 0, 1)
        keep = lax.dynamic_index_in_dim(total, side, 1, keepdims=False)
        send = lax.dynamic_index_in_dim(total, 1 - side, 1, keepdims=False)
        got = lax.ppermute(send.astype(bf16), "dp", [(i, i ^ bit) for i in range(count)])
        total = keep.astype(f32) + got.astype(f32)
        bit *= 2
    return total[0]


def total_over_dp(values):
    count = lax.axis_size("dp")
    bit = 1
    while bit < count:
        values = values + lax.ppermute(values, "dp", [(i, i ^ bit) for i in range(count)])
        bit *= 2
    return values


def swap(values):
    return lax.ppermute(values, "tensor", [(0, 1), (1, 0)])


def total_over_tensor(values):
    if lax.axis_size("tensor") == 2:
        return values + swap(values)
    return lax.psum(values, "tensor")


def gather_tokens(own):
    if lax.axis_size("tensor") == 2:
        other = swap(own)
        mine = lax.axis_index("tensor") == 0
        return jnp.concatenate([jnp.where(mine, own, other), jnp.where(mine, other, own)], axis=0)
    return lax.all_gather(own, "tensor", axis=0, tiled=True)


def scatter_tokens(whole):
    if lax.axis_size("tensor") == 2:
        half = whole.shape[0] // 2
        index = lax.axis_index("tensor")
        keep = lax.dynamic_slice_in_dim(whole, index * half, half)
        send = lax.dynamic_slice_in_dim(whole, (1 - index) * half, half)
        return keep.astype(f32) + swap(send).astype(f32)
    return lax.psum_scatter(whole, "tensor", scatter_dimension=0, tiled=True).astype(f32)


def pad_to(values, axis, size):
    pads = [(0, 0)] * values.ndim
    pads[axis] = (0, size - values.shape[axis])
    return jnp.pad(values, pads)


def body(
    hidden_in,
    segment_ids,
    norm_gain,
    proj_inner,
    proj_shared,
    proj_step,
    conv_inner,
    conv_shared,
    step_bias,
    log_decay,
    skip_gain,
    gate_gain,
    proj_out,
    out_grad,
):
    dp_count = lax.axis_size("dp")
    rows = proj_inner.shape[0]
    model_dim = hidden_in.shape[1]
    local_inner = proj_inner.shape[2]
    heads = proj_step.shape[1]
    state_size = proj_shared.shape[2]
    kernel_len = conv_inner.shape[0]
    shared_size = 2 * state_size
    full_inner = local_inner * lax.axis_size("tensor")
    width = -(-local_inner // (2 * LANES)) * 2 * LANES
    tap_block = conv_shared.shape[2]
    tap_count = kernel_len * 2 * tap_block
    tap_cols = -(-tap_count // rows)
    shared_at = 2 * width
    step_at = shared_at + shared_size

    hidden = gather_tokens(hidden_in).astype(f32)
    extra = pad_to(conv_shared.reshape(-1), 0, rows * tap_cols).reshape(rows, tap_cols)
    packed = jnp.concatenate(
        [
            pad_to(proj_inner[:, 0, :], 1, width),
            pad_to(proj_inner[:, 1, :], 1, width),
            proj_shared.reshape(rows, shared_size),
            pad_to(jnp.concatenate([proj_step, norm_gain[:, None], extra], axis=1), 1, LANES),
        ],
        axis=1,
    )
    weights = gather_rows(packed)
    gain_col = weights[:, step_at + heads]
    extra = weights[:, step_at + heads + 1 : step_at + heads + 1 + tap_cols]
    extra = extra.reshape(dp_count, rows * tap_cols)[:, :tap_count]
    taps = (
        extra.reshape(dp_count, kernel_len, 2, tap_block)
        .transpose(1, 2, 0, 3)
        .reshape(kernel_len, shared_size)
        .astype(f32)
    )
    out_rows = gather_rows(pad_to(proj_out.T, 1, width))
    grad_full = gather_tokens(out_grad)

    norm_scale = gain_col.astype(f32)
    inv_norm = lax.rsqrt(jnp.mean(hidden * hidden, axis=-1, keepdims=True) + epsilon)
    unit_in = hidden * inv_norm
    normed = (unit_in * norm_scale).astype(bf16)
    proj = dot_nn(normed, weights)

    aux, segr = token_facts(segment_ids)
    tapi = pad_to(pad_to(conv_inner.astype(f32), 1, width), 0, 8)
    taps = pad_to(taps, 0, 8)
    bias = pad_to(step_bias[None], 1, LANES)
    rate = pad_to(-jnp.exp(log_decay)[None], 1, LANES)
    skip = pad_to(jnp.repeat(skip_gain, HEAD_DIM)[None], 1, width)
    gain = pad_to(gate_gain.astype(f32)[None], 1, width)
    mixed, u, su, entry, squares = run_forward(proj, tapi, taps, bias, rate, skip, aux, segr)

    nog = dot_nn(grad_full, out_rows)
    gate = proj[:, :width]
    gated = mixed * gate * jax.nn.sigmoid(gate)
    products = jnp.sum(nog * gain * gated, axis=1, keepdims=True)
    sums = total_over_tensor(jnp.concatenate([squares, products], axis=1))
    inv_gate = lax.rsqrt(sums[:, :1] / full_inner + epsilon)
    normed_out = (gated * inv_gate * gain).astype(bf16)
    hidden_out = (
        hidden_in.astype(f32) + scatter_tokens(dot_nt(normed_out, out_rows).astype(bf16))
    ).astype(bf16)
    out_sum = scatter_rows(dot_tn(grad_full, normed_out)).T[:local_inner]

    lane = jnp.arange(width)[:, None] // HEAD_DIM
    place = (lane == jnp.arange(LANES)[None]).astype(bf16)
    dproj, wide, dtaps = run_backward(
        proj, mixed, u, su, entry, nog, sums, tapi, taps, bias, rate, skip, gain, aux, segr, place, full_inner
    )
    normed_grad = dot_nt(dproj, weights)
    norm_wgrad = jnp.sum(normed_grad * unit_in, axis=0)
    own_grad = scatter_tokens(normed_grad.astype(bf16))
    wgrad = dot_tn(normed, dproj)
    dtaps = (
        dtaps[:kernel_len]
        .reshape(kernel_len, 2, dp_count, tap_block)
        .transpose(2, 0, 1, 3)
        .reshape(dp_count, tap_count)
    )
    dtaps = pad_to(dtaps, 1, rows * tap_cols).reshape(model_dim, tap_cols)
    wgrad = jnp.concatenate(
        [
            wgrad[:, : step_at + heads],
            pad_to(jnp.concatenate([norm_wgrad[:, None], dtaps], axis=1), 1, LANES - heads),
        ],
        axis=1,
    )
    wsum = scatter_rows(wgrad)
    both = total_over_tensor(wsum[:, shared_at:])
    inner_sum = jnp.stack([wsum[:, :local_inner], wsum[:, width : width + local_inner]], axis=1)
    step_sum = wsum[:, step_at : step_at + heads]
    shared_total = both[:, :shared_size].reshape(rows, 2, state_size)
    norm_total = both[:, shared_size + heads]
    taps_total = both[:, shared_size + heads + 1 : shared_size + heads + 1 + tap_cols]
    taps_total = taps_total.reshape(-1)[:tap_count].reshape(kernel_len, 2, tap_block)
    wide = total_over_dp(wide)
    conv_total = wide[:kernel_len, :local_inner]
    gain_total = wide[4, :local_inner]
    skip_total = jnp.sum(wide[5].reshape(-1, HEAD_DIM), axis=1)[:heads]
    bias_total = wide[6, :heads]
    decay_total = wide[6, LANES : LANES + heads]

    own = hidden_in.astype(f32)
    own_inv = lax.rsqrt(jnp.mean(own * own, axis=-1, keepdims=True) + epsilon)
    own_unit = own * own_inv
    scaled_in = own_grad * norm_scale
    hidden_grad = own_inv * (
        scaled_in - own_unit * jnp.mean(scaled_in * own_unit, axis=-1, keepdims=True)
    ) + out_grad.astype(f32)
    return (
        hidden_out,
        hidden_grad,
        norm_total,
        inner_sum,
        shared_total,
        step_sum,
        conv_total,
        taps_total,
        bias_total,
        decay_total,
        skip_total,
        gain_total,
        out_sum,
    )


def solution(mesh):
    in_specs = (
        P(("dp", "tensor"), None),
        P("dp"),
        P("dp"),
        P("dp", None, "tensor"),
        P("dp", None, None),
        P("dp", "tensor"),
        P(None, "tensor"),
        P(None, None, "dp"),
        P("tensor"),
        P("tensor"),
        P("tensor"),
        P("tensor"),
        P("tensor", "dp"),
        P(("dp", "tensor"), None),
    )
    out_specs = (
        P(("dp", "tensor"), None),
        P(("dp", "tensor"), None),
        P("dp"),
        P("dp", None, "tensor"),
        P("dp", None, None),
        P("dp", "tensor"),
        P(None, "tensor"),
        P(None, None, "dp"),
        P("tensor"),
        P("tensor"),
        P("tensor"),
        P("tensor"),
        P("tensor", "dp"),
    )
    return jax.shard_map(body, mesh=mesh, in_specs=in_specs, out_specs=out_specs, check_vma=False)
```

```python
from functools import partial

import jax
import jax.numpy as jnp
import numpy as np
from jax import lax
from jax.experimental import pallas as pl
from jax.experimental.pallas import tpu as pltpu
from jax.sharding import PartitionSpec as P

HEAD_DIM = 64
CHUNK = 128
LANES = 128
TOKEN_BLOCK = 256
epsilon = 1e-05
f32 = jnp.float32
bf16 = jnp.bfloat16
highest = lax.Precision.HIGHEST


def dot_nn(a, b):
    return lax.dot_general(a, b, (((1,), (0,)), ((), ())), preferred_element_type=f32)


def dot_nt(a, b):
    return lax.dot_general(a, b, (((1,), (1,)), ((), ())), preferred_element_type=f32)


def dot_tn(a, b):
    return lax.dot_general(a, b, (((0,), (0,)), ((), ())), preferred_element_type=f32)


def dot_exact(a, b):
    return lax.dot_general(
        a, b, (((1,), (0,)), ((), ())), preferred_element_type=f32, precision=highest
    )


def dot_split(a, b):
    high = a.astype(bf16)
    rest = (a - high.astype(f32)).astype(bf16)
    return dot_nn(high, b) + dot_nn(rest, b)


def sigmoid(v):
    return 1.0 / (1.0 + jnp.exp(-v))


def softplus(v):
    return jnp.maximum(v, 0.0) + jnp.log1p(jnp.exp(-jnp.abs(v)))


def halves(lane_low, values, head):
    return jnp.where(lane_low, values[:, head : head + 1], values[:, head + 1 : head + 2])


def back_shift(window, offset):
    return pltpu.roll(window, offset, 0)[8:, :]


def ahead_shift(window, offset):
    rows = window.shape[0]
    return pltpu.roll(window, rows - offset, 0)[: rows - 8, :]


def conv_rows(window, taps, aux):
    total = taps[3:4, :] * window[8:, :]
    for offset in range(1, 4):
        total = total + taps[3 - offset : 4 - offset, :] * (
            back_shift(window, offset) * aux[:, offset : offset + 1]
        )
    return total


def forward_kernel(
    proj_ref,
    step_ref,
    tapi_ref,
    taps_ref,
    heads_ref,
    aux_ref,
    segr_ref,
    mixed_ref,
    u_ref,
    su_ref,
    entry_ref,
    state_ref,
    carry_ref,
    scarry_ref,
    xw_ref,
):
    width = mixed_ref.shape[1]
    pairs = width // LANES
    shared_size = su_ref.shape[1]
    state_size = shared_size // 2
    chunk = pl.program_id(0)

    @pl.when(chunk == 0)
    def _():
        for ref in (state_ref, carry_ref, scarry_ref):
            ref[...] = jnp.zeros_like(ref)

    rows = lax.broadcasted_iota(jnp.int32, (CHUNK, CHUNK), 0)
    cols = lax.broadcasted_iota(jnp.int32, (CHUNK, CHUNK), 1)
    lower = rows >= cols
    summing = lower.astype(f32)
    lane_low = lax.broadcasted_iota(jnp.int32, (CHUNK, LANES), 1) < HEAD_DIM
    bias = heads_ref[0:1, :]
    rate = -jnp.exp(heads_ref[1:2, :])
    skips = heads_ref[2:3, :]
    aux = aux_ref[...]
    live = aux[:, 7:8]
    same = lower & (aux[:, 0:1] == segr_ref[pl.ds(chunk, 1), :])
    shared_now = proj_ref[:, width:].astype(f32)
    su = conv_rows(jnp.concatenate([scarry_ref[...], shared_now], axis=0), taps_ref[...], aux)
    scarry_ref[...] = shared_now[CHUNK - 8 :, :]
    su_ref[...] = su
    shared = (su * sigmoid(su)).astype(bf16)
    b_rows = shared[:, :state_size]
    c_rows = shared[:, state_size:]
    scores = jnp.where(same, dot_nt(c_rows, b_rows), 0.0)
    step = softplus(step_ref[...] + bias) * live
    decay = dot_exact(summing, step * rate)
    decay_t = decay.T
    last = decay[CHUNK - 1 :, :]
    entry_scale = jnp.exp(decay) * aux[:, 8:9]
    end_scale = jnp.exp(last - decay) * aux[:, 9:10]
    keep = jnp.exp(last) * aux[:1, 10:11]
    state = state_ref[...]
    state_low = state.astype(bf16)
    entry_ref[...] = state_low[None]
    past = dot_nn(c_rows, state_low)
    for pair in range(pairs):
        lanes = slice(pair * LANES, (pair + 1) * LANES)
        head = 2 * pair
        now = proj_ref[:, lanes].astype(f32)
        window = jnp.concatenate([carry_ref[:, lanes], now], axis=0)
        carry_ref[:, lanes] = now[CHUNK - 8 :, :]
        u = conv_rows(window, tapi_ref[:, lanes].astype(f32), aux)
        u_ref[:, lanes] = u.astype(bf16)
        x = u * sigmoid(u)
        scaled = x * halves(lane_low, step, head)
        mixing = jnp.concatenate(
            [
                (
                    scores
                    * jnp.exp(jnp.minimum(decay[:, h : h + 1] - decay_t[h : h + 1, :], 0.0))
                ).astype(bf16)
                for h in (head, head + 1)
            ],
            axis=1,
        )
        stacked = jnp.concatenate(
            [jnp.where(lane_low, scaled, 0.0), jnp.where(lane_low, 0.0, scaled)], axis=0
        ).astype(bf16)
        inside = dot_nn(mixing, stacked)
        xw_ref[:, lanes] = (scaled * halves(lane_low, end_scale, head)).astype(bf16)
        mixed = (
            inside
            + past[:, lanes] * halves(lane_low, entry_scale, head)
            + halves(lane_low[:1], skips, head) * x
        ) * live
        mixed_ref[:, lanes] = mixed.astype(bf16)
        state_ref[:, lanes] = state[:, lanes] * halves(lane_low[:1], keep, head)
    state_ref[...] += dot_tn(b_rows, xw_ref[...])


def token_scales(sums, full_inner):
    columns = sums.T
    inv = lax.rsqrt(columns[:, 0:1] / full_inner + epsilon)
    return inv, inv * columns[:, 1:2] / full_inner


def silu_slope(v, s):
    return s * (1.0 + v * (1.0 - s))


def backward_kernel(
    proj_ref,
    praw_ref,
    u_ref,
    su_ref,
    entry_ref,
    grad_ref,
    tapi_ref,
    taps_ref,
    heads_ref,
    aux_ref,
    segr_ref,
    dproj_ref,
    wide_ref,
    shared_ref,
    state_ref,
    ahead_ref,
    sahead_ref,
    xw_ref,
    ge_ref,
    row_ref,
    proda_ref,
    prodb_ref,
):
    width = u_ref.shape[1]
    chunks = pl.num_programs(0)
    pairs = width // LANES
    shared_size = su_ref.shape[1]
    state_size = shared_size // 2
    shared_cols = slice(width, width + shared_size)
    step_cols = slice(width + shared_size, width + shared_size + LANES)
    chunk = chunks - 1 - pl.program_id(0)

    @pl.when(pl.program_id(0) == 0)
    def _():
        for ref in (state_ref, ahead_ref, sahead_ref, row_ref, wide_ref, shared_ref):
            ref[...] = jnp.zeros_like(ref)

    rows = lax.broadcasted_iota(jnp.int32, (CHUNK, CHUNK), 0)
    cols = lax.broadcasted_iota(jnp.int32, (CHUNK, CHUNK), 1)
    upper = rows <= cols
    summing = (rows >= cols).astype(f32)
    unsumming = upper.astype(f32)
    last_row = (lax.broadcasted_iota(jnp.int32, (CHUNK, LANES), 0) == CHUNK - 1).astype(f32)
    lane_ids = lax.broadcasted_iota(jnp.int32, (CHUNK, LANES), 1)
    lane_low = lane_ids < HEAD_DIM
    bias = heads_ref[0:1, :]
    rate = -jnp.exp(heads_ref[1:2, :])
    skips = heads_ref[2:3, :]
    place = (
        lax.broadcasted_iota(jnp.int32, (width, LANES), 0) // HEAD_DIM
        == lax.broadcasted_iota(jnp.int32, (width, LANES), 1)
    ).astype(bf16)

    aux = aux_ref[...]
    live = aux[:, 7:8]
    same = upper & (aux[:, 0:1] == segr_ref[pl.ds(chunk, 1), :])
    su = su_ref[...]
    su_sig = sigmoid(su)
    shared = (su * su_sig).astype(bf16)
    b_rows = shared[:, :state_size]
    c_rows = shared[:, state_size:]
    scores = jnp.where(same, dot_nt(b_rows, c_rows), 0.0)
    pre = praw_ref[...] + bias
    step = softplus(pre) * live
    decay = dot_exact(summing, step * rate)
    decay_t = decay.T
    last = decay[CHUNK - 1 :, :]
    entry_scale = jnp.exp(decay) * aux[:, 8:9]
    end_scale = jnp.exp(last - decay) * aux[:, 9:10]
    keep = jnp.exp(last) * aux[:1, 10:11]
    entry = entry_ref[0]
    dstate = state_ref[...]
    dstate_low = dstate.astype(bf16)
    past = dot_nn(c_rows, entry)
    bds = dot_nn(b_rows, dstate_low)
    score_grad = jnp.zeros((CHUNK, CHUNK), f32)
    col_part = jnp.zeros((CHUNK, LANES), f32)
    for pair in range(pairs):
        lanes = slice(pair * LANES, (pair + 1) * LANES)
        head = 2 * pair
        g_low = grad_ref[:, lanes]
        g = g_low.astype(f32)
        u = u_ref[:, lanes].astype(f32)
        u_sig = sigmoid(u)
        x = u * u_sig
        step_c = halves(lane_low, step, head)
        scaled = x * step_c
        stacked = jnp.concatenate(
            [jnp.where(lane_low, scaled, 0.0), jnp.where(lane_low, 0.0, scaled)], axis=0
        ).astype(bf16)
        dmix = dot_nt(stacked, g_low)
        mixing = []
        for k, h in enumerate((head, head + 1)):
            decays = jnp.exp(jnp.minimum(decay_t[h : h + 1, :] - decay[:, h : h + 1], 0.0))
            dmix_h = dmix[k * CHUNK : (k + 1) * CHUNK, :]
            score_grad = score_grad + dmix_h * decays
            mixing_h = scores * decays
            mixing.append(mixing_h.astype(bf16))
            both = mixing_h * dmix_h
            col_part = jnp.where(lane_ids == h, jnp.sum(both, axis=1, keepdims=True), col_part)
            row_ref[h : h + 1, :] = jnp.sum(both, axis=0, keepdims=True)
        g_stacked = jnp.concatenate(
            [jnp.where(lane_low, g, 0.0), jnp.where(lane_low, 0.0, g)], axis=0
        ).astype(bf16)
        end_c = halves(lane_low, end_scale, head)
        entry_c = halves(lane_low, entry_scale, head)
        keep_c = halves(lane_low[:1], keep, head)
        from_state = end_c * bds[:, lanes]
        dscaled = dot_nn(jnp.concatenate(mixing, axis=1), g_stacked) + from_state
        xw_ref[:, lanes] = (scaled * end_c).astype(bf16)
        q = scaled * from_state
        ge = g * entry_c
        ge_ref[:, lanes] = ge.astype(bf16)
        dstate_p = dstate[:, lanes]
        tail = jnp.sum(q, axis=0, keepdims=True) + keep_c * jnp.sum(
            dstate_p * entry[:, lanes].astype(f32), axis=0, keepdims=True
        )
        proda_ref[:, lanes] = x * dscaled
        prodb_ref[:, lanes] = ge * past[:, lanes] - q + last_row * tail
        state_ref[:, lanes] = dstate_p * keep_c
        dx = step_c * dscaled + halves(lane_low[:1], skips, head) * g
        du = dx * silu_slope(u, u_sig)
        window = jnp.concatenate([du, ahead_ref[:, lanes]], axis=0)
        ahead_ref[:, lanes] = du[:8, :]
        cin = proj_ref[:, lanes].astype(f32)
        taps = tapi_ref[:, lanes].astype(f32)
        dcin = taps[3:4, :] * du
        wide_ref[3:4, lanes] += jnp.sum(cin * du, axis=0, keepdims=True)
        for offset in range(1, 4):
            moved = ahead_shift(window, offset) * aux[:, 3 + offset : 4 + offset]
            dcin = dcin + taps[3 - offset : 4 - offset, :] * moved
            wide_ref[3 - offset : 4 - offset, lanes] += jnp.sum(
                cin * moved, axis=0, keepdims=True
            )
        dproj_ref[:, lanes] = dcin.astype(bf16)
        wide_ref[5:6, lanes] += jnp.sum(g * x, axis=0, keepdims=True)
    score_low = jnp.where(same, score_grad, 0.0).astype(bf16)
    ge_all = ge_ref[...]
    db = dot_nn(score_low, c_rows) + dot_nt(xw_ref[...], dstate_low)
    dc = dot_tn(score_low, b_rows) + dot_nt(ge_all, entry)
    state_ref[...] += dot_tn(c_rows, ge_all)
    ds = jnp.concatenate([db, dc], axis=1) * silu_slope(su, su_sig)
    window = jnp.concatenate([ds, sahead_ref[...]], axis=0)
    sahead_ref[...] = ds[:8, :]
    taps = taps_ref[...]
    sin = proj_ref[:, shared_cols].astype(f32)
    dsin = taps[3:4, :] * ds
    shared_ref[3:4, :] += jnp.sum(sin * ds, axis=0, keepdims=True)
    for offset in range(1, 4):
        moved = ahead_shift(window, offset) * aux[:, 3 + offset : 4 + offset]
        dsin = dsin + taps[3 - offset : 4 - offset, :] * moved
        shared_ref[3 - offset : 4 - offset, :] += jnp.sum(sin * moved, axis=0, keepdims=True)
    dproj_ref[:, shared_cols] = dsin.astype(bf16)
    ddecay = row_ref[...].T - col_part + dot_split(prodb_ref[...], place)
    dlog = dot_exact(unsumming, ddecay)
    dstep = (dot_split(proda_ref[...], place) + rate * dlog) * live * sigmoid(pre)
    dproj_ref[:, step_cols] = dstep.astype(bf16)
    wide_ref[6:7, :LANES] += jnp.sum(dstep, axis=0, keepdims=True)
    wide_ref[6:7, LANES : 2 * LANES] += jnp.sum(step * dlog, axis=0, keepdims=True) * rate


def token_facts(segments):
    length = segments.shape[0]
    chunks = length // CHUNK
    columns = [segments]
    for offset in range(1, 4):
        earlier = jnp.concatenate([jnp.full((offset,), -1, jnp.int32), segments[: length - offset]])
        columns.append(earlier == segments)
    for offset in range(1, 4):
        later = jnp.concatenate([segments[offset:], jnp.full((offset,), -1, jnp.int32)])
        columns.append(later == segments)
    columns.append(segments != 0)
    blocks = segments.reshape(chunks, CHUNK)
    last = blocks[:, CHUNK - 1 :]
    prior = jnp.concatenate([jnp.full((1, 1), -1, jnp.int32), last[: chunks - 1]], axis=0)
    columns.append((blocks == prior).reshape(length))
    columns.append((blocks == last).reshape(length))
    columns.append(jnp.broadcast_to(last == prior, blocks.shape).reshape(length))
    columns += [jnp.zeros_like(segments)] * 5
    aux = jnp.stack([c.astype(f32) for c in columns], axis=1)
    return aux, blocks.astype(f32)


def chunk_spec(columns, last):
    if last is None:
        return pl.BlockSpec((CHUNK, columns), lambda i: (i, 0))
    return pl.BlockSpec((CHUNK, columns), lambda i: (last - i, 0))


def fixed_spec(values):
    zeros = (0,) * values.ndim
    return pl.BlockSpec(values.shape, lambda i: zeros)


def run_forward(proj, praw, tapi, taps, heads, aux, segr):
    length = proj.shape[0]
    width = tapi.shape[1]
    shared_size = taps.shape[1]
    state_size = shared_size // 2
    chunks = length // CHUNK
    sds = jax.ShapeDtypeStruct
    return pl.pallas_call(
        forward_kernel,
        grid=(chunks,),
        in_specs=[
            chunk_spec(proj.shape[1], None),
            chunk_spec(LANES, None),
            fixed_spec(tapi),
            fixed_spec(taps),
            fixed_spec(heads),
            chunk_spec(aux.shape[1], None),
            fixed_spec(segr),
        ],
        out_specs=[
            chunk_spec(width, None),
            chunk_spec(width, None),
            chunk_spec(shared_size, None),
            pl.BlockSpec((1, state_size, width), lambda i: (i, 0, 0)),
        ],
        out_shape=(
            sds((length, width), bf16),
            sds((length, width), bf16),
            sds((length, shared_size), f32),
            sds((chunks, state_size, width), bf16),
        ),
        scratch_shapes=[
            pltpu.VMEM((state_size, width), f32),
            pltpu.VMEM((8, width), f32),
            pltpu.VMEM((8, shared_size), f32),
            pltpu.VMEM((CHUNK, width), bf16),
        ],
        name="scan_forward",
        cost_estimate=cost(18),
    )(proj, praw, tapi, taps, heads, aux, segr)


def run_backward(proj, praw, u, su, entry, grad, tapi, taps, heads, aux, segr):
    length, width = u.shape
    shared_size = su.shape[1]
    state_size = shared_size // 2
    chunks = length // CHUNK
    last = chunks - 1
    columns = width + shared_size + LANES
    sds = jax.ShapeDtypeStruct
    return pl.pallas_call(
        backward_kernel,
        grid=(chunks,),
        in_specs=[
            chunk_spec(proj.shape[1], last),
            chunk_spec(LANES, last),
            chunk_spec(width, last),
            chunk_spec(shared_size, last),
            pl.BlockSpec((1, state_size, width), lambda i: (last - i, 0, 0)),
            chunk_spec(width, last),
            fixed_spec(tapi),
            fixed_spec(taps),
            fixed_spec(heads),
            chunk_spec(aux.shape[1], last),
            fixed_spec(segr),
        ],
        out_specs=[
            chunk_spec(columns, last),
            pl.BlockSpec((8, width), lambda i: (0, 0)),
            pl.BlockSpec((8, shared_size), lambda i: (0, 0)),
        ],
        out_shape=(
            sds((length, columns), bf16),
            sds((8, width), f32),
            sds((8, shared_size), f32),
        ),
        scratch_shapes=[
            pltpu.VMEM((state_size, width), f32),
            pltpu.VMEM((8, width), f32),
            pltpu.VMEM((8, shared_size), f32),
            pltpu.VMEM((CHUNK, width), bf16),
            pltpu.VMEM((CHUNK, width), bf16),
            pltpu.VMEM((LANES, CHUNK), f32),
            pltpu.VMEM((CHUNK, width), f32),
            pltpu.VMEM((CHUNK, width), f32),
        ],
        name="scan_backward",
        cost_estimate=cost(32),
    )(proj, praw, u, su, entry, grad, tapi, taps, heads, aux, segr)


def block_plan():
    count = lax.axis_size("dp")
    bits = []
    bit = count // 2
    while bit > 1:
        bits.append(bit)
        bit //= 2
    mixed = bits[:-2] + bits[-2:][::-1]
    by_core = (bits, mixed)
    stages = []
    for stage in range(len(bits)):
        stages.append([(i, i ^ by_core[i % 2][stage]) for i in range(count)])
    core = [(i, i ^ 1) for i in range(count)]
    device = np.zeros((count, count), np.int32)
    for own in range(count):
        for spot in range(count):
            other = own ^ 1 if spot >= count // 2 else own
            for stage, bit in enumerate(by_core[other % 2]):
                if (spot >> stage) & 1:
                    other ^= bit
            device[own, spot] = other
    table = jnp.asarray(device)[lax.axis_index("dp")]
    return stages, core, table


def core_groups():
    count = lax.axis_size("dp")
    groups = [list(range(side, count, 2)) for side in range(2)]
    return groups, jnp.asarray(
        [groups[0] + groups[1], groups[1] + groups[0]], jnp.int32
    )[lax.axis_index("dp") % 2]


def exchange(blocks, groups):
    return lax.all_to_all(
        blocks, "dp", 0, 0, axis_index_groups=groups, tiled=True
    )


def sum_blocks(blocks, rows):
    return jnp.sum(blocks.reshape(-1, rows, blocks.shape[1]).astype(f32), axis=0)


def total_over_dp(values):
    count = lax.axis_size("dp")
    bit = 1
    while bit < count:
        values = values + lax.ppermute(values, "dp", [(i, i ^ bit) for i in range(count)])
        bit *= 2
    return values


def swap(values):
    return lax.ppermute(values, "tensor", [(0, 1), (1, 0)])


def total_over_tensor(values):
    if lax.axis_size("tensor") == 2:
        return values + swap(values)
    return lax.psum(values, "tensor")


def both_halves(own):
    if lax.axis_size("tensor") == 2:
        return own, swap(own)
    whole = lax.all_gather(own, "tensor", axis=0, tiled=True)
    return whole, whole


def token_starts(blocks):
    if lax.axis_size("tensor") == 2:
        index = lax.axis_index("tensor")
        return jnp.stack([index * (blocks // 2), (1 - index) * (blocks // 2)]).astype(jnp.int32)
    return jnp.zeros((2,), jnp.int32)


def add_halves(send, keep):
    if lax.axis_size("tensor") == 2:
        return keep.astype(f32) + swap(send).astype(f32)
    whole = jnp.concatenate([send.astype(bf16), keep.astype(bf16)], axis=0)
    return lax.psum_scatter(whole, "tensor", scatter_dimension=0, tiled=True).astype(f32)


def own_block(step, starts, own_blocks):
    return jnp.clip(step - starts[0], 0, own_blocks - 1)


def other_block(step, starts, own_blocks):
    return jnp.clip(step - starts[1], 0, own_blocks - 1)


def place_blocks(table_ref, low_ref, high_ref, whole_ref, sem_ref):
    count = table_ref.shape[0]
    rows = whole_ref.shape[0] // count
    copies = []
    for spot in range(count):
        source = low_ref if spot < count // 2 else high_ref
        where = pl.multiple_of(table_ref[spot] * rows, rows)
        copies.append(
            pltpu.make_async_copy(
                source.at[pl.ds((spot % (count // 2)) * rows, rows), :],
                whole_ref.at[pl.ds(where, rows), :],
                sem_ref.at[spot],
            )
        )
    for copy in copies:
        copy.start()
    for copy in copies:
        copy.wait()


def project_kernel(
    starts_ref,
    table_ref,
    own_ref,
    other_ref,
    spread_ref,
    low_ref,
    high_ref,
    proj_ref,
    step_ref,
    normed_ref,
    turned_ref,
    weights_ref,
    taps_ref,
    scale_ref,
    sem_ref,
    *,
    own_blocks,
    heads,
):
    step = pl.program_id(0)
    model_dim, columns = weights_ref.shape

    @pl.when(step == 0)
    def _():
        place_blocks(table_ref, low_ref, high_ref, weights_ref, sem_ref)
        extra = weights_ref[:, columns - LANES :].astype(f32).T
        scale_ref[...] = jnp.broadcast_to(extra[heads : heads + 1, :], scale_ref.shape)
        taps = extra[heads + 1 : heads + 5, :]
        taps = jnp.concatenate([taps, jnp.zeros_like(taps)], axis=0).astype(bf16)
        taps_ref[...] = dot_nn(taps, spread_ref[...])

    mine = (step >= starts_ref[0]) & (step < starts_ref[0] + own_blocks)
    tokens = jnp.where(mine, own_ref[...].astype(f32), other_ref[...].astype(f32))
    inv = lax.rsqrt(jnp.mean(tokens * tokens, axis=-1, keepdims=True) + epsilon)
    normed = (tokens * inv * scale_ref[:1, :]).astype(bf16)
    normed_ref[...] = normed
    turned_ref[...] = normed.T
    proj = dot_nn(normed, weights_ref[...])
    proj_ref[...] = proj[:, : columns - LANES].astype(bf16)
    step_ref[...] = proj[:, columns - LANES :]


def run_project(starts, table, own, other, spread, low, high, heads):
    own_rows, model_dim = own.shape
    columns = low.shape[1]
    own_blocks = own_rows // TOKEN_BLOCK
    blocks = own_blocks * (2 if other is not own else 1)
    length = blocks * TOKEN_BLOCK
    sds = jax.ShapeDtypeStruct
    return pl.pallas_call(
        partial(project_kernel, own_blocks=own_blocks, heads=heads),
        grid_spec=pltpu.PrefetchScalarGridSpec(
            num_scalar_prefetch=2,
            grid=(blocks,),
            in_specs=[
                pl.BlockSpec(
                    (TOKEN_BLOCK, model_dim), lambda i, s, t: (own_block(i, s, own_blocks), 0)
                ),
                pl.BlockSpec(
                    (TOKEN_BLOCK, model_dim), lambda i, s, t: (other_block(i, s, own_blocks), 0)
                ),
                pl.BlockSpec(spread.shape, lambda i, s, t: (0, 0)),
                pl.BlockSpec(memory_space=pl.ANY),
                pl.BlockSpec(memory_space=pl.ANY),
            ],
            out_specs=[
                pl.BlockSpec((TOKEN_BLOCK, columns - LANES), lambda i, s, t: (i, 0)),
                pl.BlockSpec((TOKEN_BLOCK, LANES), lambda i, s, t: (i, 0)),
                pl.BlockSpec((TOKEN_BLOCK, model_dim), lambda i, s, t: (i, 0)),
                pl.BlockSpec((model_dim, TOKEN_BLOCK), lambda i, s, t: (0, i)),
                pl.BlockSpec((model_dim, columns), lambda i, s, t: (0, 0)),
                pl.BlockSpec((8, spread.shape[1]), lambda i, s, t: (0, 0)),
                pl.BlockSpec((8, model_dim), lambda i, s, t: (0, 0)),
            ],
            scratch_shapes=[pltpu.SemaphoreType.DMA((table.shape[0],))],
        ),
        out_shape=(
            sds((length, columns - LANES), bf16),
            sds((length, LANES), f32),
            sds((length, model_dim), bf16),
            sds((model_dim, length), bf16),
            sds((model_dim, columns), bf16),
            sds((8, spread.shape[1]), f32),
            sds((8, model_dim), f32),
        ),
        name="norm_project",
        cost_estimate=cost(9),
    )(starts, table, own, other, spread, low, high)


def token_sum(values):
    total = values[:, :LANES]
    for at in range(LANES, values.shape[1], LANES):
        total = total + values[:, at : at + LANES]
    return jnp.sum(total.T, axis=0, keepdims=True)


def out_grad_kernel(
    starts_ref,
    table_ref,
    own_ref,
    other_ref,
    low_ref,
    high_ref,
    normed_ref,
    mixed_ref,
    gain_ref,
    gate_ref,
    nog_ref,
    turned_ref,
    sums_ref,
    weights_ref,
    sem_ref,
    *,
    own_blocks,
):
    step = pl.program_id(0)
    width = mixed_ref.shape[1]

    @pl.when(step == 0)
    def _():
        place_blocks(table_ref, low_ref, high_ref, weights_ref, sem_ref)

    mine = (step >= starts_ref[0]) & (step < starts_ref[0] + own_blocks)
    tokens = jnp.where(mine, own_ref[...].astype(f32), other_ref[...].astype(f32)).astype(bf16)
    turned_ref[...] = tokens.T
    gate = dot_nn(normed_ref[...], weights_ref[:, :width])
    gate_ref[...] = gate.astype(bf16)
    nog = dot_nn(tokens, weights_ref[:, width:])
    nog_ref[...] = nog.astype(bf16)
    gated = mixed_ref[...].astype(f32) * (gate * sigmoid(gate))
    sums_ref[...] = jnp.concatenate(
        [
            token_sum(gated * gated),
            token_sum(nog * gain_ref[...].astype(f32) * gated),
            jnp.zeros((6, TOKEN_BLOCK), f32),
        ],
        axis=0,
    )


def run_out_grad(starts, table, own, other, low, high, normed, mixed, gain):
    own_rows, model_dim = own.shape
    length, width = mixed.shape
    own_blocks = own_rows // TOKEN_BLOCK
    blocks = length // TOKEN_BLOCK
    sds = jax.ShapeDtypeStruct
    return pl.pallas_call(
        partial(out_grad_kernel, own_blocks=own_blocks),
        grid_spec=pltpu.PrefetchScalarGridSpec(
            num_scalar_prefetch=2,
            grid=(blocks,),
            in_specs=[
                pl.BlockSpec(
                    (TOKEN_BLOCK, model_dim), lambda i, s, t: (own_block(i, s, own_blocks), 0)
                ),
                pl.BlockSpec(
                    (TOKEN_BLOCK, model_dim), lambda i, s, t: (other_block(i, s, own_blocks), 0)
                ),
                pl.BlockSpec(memory_space=pl.ANY),
                pl.BlockSpec(memory_space=pl.ANY),
                pl.BlockSpec((TOKEN_BLOCK, model_dim), lambda i, s, t: (i, 0)),
                pl.BlockSpec((TOKEN_BLOCK, width), lambda i, s, t: (i, 0)),
                pl.BlockSpec((1, width), lambda i, s, t: (0, 0)),
            ],
            out_specs=[
                pl.BlockSpec((TOKEN_BLOCK, width), lambda i, s, t: (i, 0)),
                pl.BlockSpec((TOKEN_BLOCK, width), lambda i, s, t: (i, 0)),
                pl.BlockSpec((model_dim, TOKEN_BLOCK), lambda i, s, t: (0, i)),
                pl.BlockSpec((8, TOKEN_BLOCK), lambda i, s, t: (0, i)),
                pl.BlockSpec((model_dim, 2 * width), lambda i, s, t: (0, 0)),
            ],
            scratch_shapes=[pltpu.SemaphoreType.DMA((table.shape[0],))],
        ),
        out_shape=(
            sds((length, width), bf16),
            sds((length, width), bf16),
            sds((model_dim, length), bf16),
            sds((8, length), f32),
            sds((model_dim, 2 * width), bf16),
        ),
        name="out_grad",
        cost_estimate=cost(9),
    )(starts, table, own, other, low, high, normed, mixed, gain)


def store_blocks(table_ref, source_ref, keep_ref, send_ref):
    count = table_ref.shape[0]
    rows = source_ref.shape[0] // count
    half = count // 2
    for spot in range(half):
        where = pl.multiple_of(table_ref[spot] * rows, rows)
        keep_ref[spot * rows : (spot + 1) * rows, :] = source_ref[pl.ds(where, rows), :]
    for spot in range(half):
        where = pl.multiple_of(table_ref[half + spot] * rows, rows)
        send_ref[spot * rows : (spot + 1) * rows, :] = source_ref[pl.ds(where, rows), :].astype(
            bf16
        )


def gated_kernel(
    table_ref,
    gate_ref,
    nog_ref,
    mixed_ref,
    sums_ref,
    aux_ref,
    gain_ref,
    gturned_ref,
    nturned_ref,
    out_ref,
    dgate_ref,
    grad_ref,
    row_ref,
    keep_ref,
    send_ref,
    total_ref,
    *,
    full_inner,
):
    step = pl.program_id(0)
    width = gate_ref.shape[1]
    inv, mean = token_scales(sums_ref[...], full_inner)
    gain = gain_ref[...].astype(f32)
    gate = gate_ref[...].astype(f32)
    gate_sig = sigmoid(gate)
    gate_silu = gate * gate_sig
    mixed = mixed_ref[...].astype(f32)
    unit = mixed * gate_silu * inv
    nog = nog_ref[...].astype(f32)
    grad = inv * (nog * gain - unit * mean)
    dgate = (grad * mixed * silu_slope(gate, gate_sig)).astype(bf16)
    dgate_ref[...] = dgate
    grad_ref[...] = (grad * gate_silu * aux_ref[:, 7:8]).astype(bf16)
    normed_out = (unit * gain).astype(bf16)
    out_ref[...] = normed_out
    row = jnp.sum((nog * unit).reshape(-1, 8, width), axis=0)
    part_gate = dot_nn(nturned_ref[...], dgate)
    part_out = dot_nn(gturned_ref[...], normed_out)

    @pl.when(step == 0)
    def _():
        total_ref[:, :width] = part_gate
        total_ref[:, width:] = part_out
        row_ref[...] = row

    @pl.when(step > 0)
    def _():
        total_ref[:, :width] += part_gate
        total_ref[:, width:] += part_out
        row_ref[...] += row

    @pl.when(step == pl.num_programs(0) - 1)
    def _():
        store_blocks(table_ref, total_ref, keep_ref, send_ref)


def run_gated(table, gate, nog, mixed, sums, aux, gain, gturned, nturned, full_inner):
    length, width = gate.shape
    model_dim = gturned.shape[0]
    blocks = length // TOKEN_BLOCK
    sds = jax.ShapeDtypeStruct
    tokens = pl.BlockSpec((TOKEN_BLOCK, width), lambda i, t: (i, 0))
    turned = pl.BlockSpec((model_dim, TOKEN_BLOCK), lambda i, t: (0, i))
    halves_spec = pl.BlockSpec((model_dim // 2, 2 * width), lambda i, t: (0, 0))
    return pl.pallas_call(
        partial(gated_kernel, full_inner=float(full_inner)),
        grid_spec=pltpu.PrefetchScalarGridSpec(
            num_scalar_prefetch=1,
            grid=(blocks,),
            in_specs=[
                tokens,
                tokens,
                tokens,
                pl.BlockSpec((8, TOKEN_BLOCK), lambda i, t: (0, i)),
                pl.BlockSpec((TOKEN_BLOCK, aux.shape[1]), lambda i, t: (i, 0)),
                pl.BlockSpec((1, width), lambda i, t: (0, 0)),
                turned,
                turned,
            ],
            out_specs=[
                tokens,
                tokens,
                tokens,
                pl.BlockSpec((8, width), lambda i, t: (0, 0)),
                halves_spec,
                halves_spec,
            ],
            scratch_shapes=[pltpu.VMEM((model_dim, 2 * width), f32)],
        ),
        out_shape=(
            sds((length, width), bf16),
            sds((length, width), bf16),
            sds((length, width), bf16),
            sds((8, width), f32),
            sds((model_dim // 2, 2 * width), f32),
            sds((model_dim // 2, 2 * width), bf16),
        ),
        name="gated_grad",
        cost_estimate=cost(12),
    )(table, gate, nog, mixed, sums, aux, gain, gturned, nturned)


def out_kernel(starts_ref, rows_ref, weights_ref, send_ref, keep_ref):
    step = pl.program_id(0)
    half = pl.num_programs(0) // 2
    rows = dot_nt(rows_ref[...], weights_ref[...]).astype(bf16)

    @pl.when(step < half)
    def _():
        send_ref[...] = rows

    @pl.when(step >= half)
    def _():
        keep_ref[...] = rows


def run_out(starts, rows, weights):
    length, width = rows.shape
    model_dim = weights.shape[0]
    blocks = length // TOKEN_BLOCK
    half = blocks // 2
    sds = jax.ShapeDtypeStruct
    return pl.pallas_call(
        out_kernel,
        grid_spec=pltpu.PrefetchScalarGridSpec(
            num_scalar_prefetch=1,
            grid=(blocks,),
            in_specs=[
                pl.BlockSpec((TOKEN_BLOCK, width), lambda i, s: (lax.rem(i + s[0], blocks), 0)),
                pl.BlockSpec((model_dim, width), lambda i, s: (0, 1)),
            ],
            out_specs=[
                pl.BlockSpec((TOKEN_BLOCK, model_dim), lambda i, s: (jnp.minimum(i, half - 1), 0)),
                pl.BlockSpec((TOKEN_BLOCK, model_dim), lambda i, s: (jnp.maximum(i - half, 0), 0)),
            ],
        ),
        out_shape=(
            sds((length // 2, model_dim), bf16),
            sds((length // 2, model_dim), bf16),
        ),
        name="out_project",
        cost_estimate=cost(4),
    )(starts, rows, weights)


def norm_grad_kernel(
    starts_ref, dgate_ref, dproj_ref, gates_ref, weights_ref, normed_ref, grad_ref, total_ref
):
    grad = dot_nt(dgate_ref[...], gates_ref[...]) + dot_nt(dproj_ref[...], weights_ref[...])
    grad_ref[...] = grad.astype(grad_ref.dtype)
    part = jnp.sum(
        (grad * normed_ref[...].astype(f32)).reshape(-1, 8, grad.shape[1]), axis=0
    )

    @pl.when(pl.program_id(0) == 0)
    def _():
        total_ref[...] = part

    @pl.when(pl.program_id(0) > 0)
    def _():
        total_ref[...] += part


def run_norm_grad(starts, dgate, dproj, gates, weights, normed, kind):
    length, columns = dproj.shape
    width = dgate.shape[1]
    model_dim = weights.shape[0]
    blocks = length // TOKEN_BLOCK // 2
    sds = jax.ShapeDtypeStruct
    return pl.pallas_call(
        norm_grad_kernel,
        grid_spec=pltpu.PrefetchScalarGridSpec(
            num_scalar_prefetch=1,
            grid=(blocks,),
            in_specs=[
                pl.BlockSpec((TOKEN_BLOCK, width), lambda i, s: (i + s[0], 0)),
                pl.BlockSpec((TOKEN_BLOCK, columns), lambda i, s: (i + s[0], 0)),
                pl.BlockSpec((model_dim, width), lambda i, s: (0, 0)),
                pl.BlockSpec((model_dim, columns), lambda i, s: (0, 0)),
                pl.BlockSpec((TOKEN_BLOCK, model_dim), lambda i, s: (i + s[0], 0)),
            ],
            out_specs=[
                pl.BlockSpec((TOKEN_BLOCK, model_dim), lambda i, s: (i, 0)),
                pl.BlockSpec((8, model_dim), lambda i, s: (0, 0)),
            ],
        ),
        out_shape=(sds((length // 2, model_dim), kind), sds((8, model_dim), f32)),
        name="normed_grad",
        cost_estimate=cost(5),
    )(starts, dgate, dproj, gates, weights, normed)


def weight_grad_kernel(table_ref, turned_ref, dproj_ref, keep_ref, send_ref, total_ref):
    total_ref[...] = dot_nn(turned_ref[...], dproj_ref[...])
    store_blocks(table_ref, total_ref, keep_ref, send_ref)


def run_weight_grad(table, turned, dproj):
    model_dim, length = turned.shape
    columns = dproj.shape[1]
    tile = 3 * LANES if columns % (3 * LANES) == 0 else LANES
    sds = jax.ShapeDtypeStruct
    return pl.pallas_call(
        weight_grad_kernel,
        grid_spec=pltpu.PrefetchScalarGridSpec(
            num_scalar_prefetch=1,
            grid=(columns // tile,),
            in_specs=[
                pl.BlockSpec((model_dim, length), lambda i, t: (0, 0)),
                pl.BlockSpec((length, tile), lambda i, t: (0, i)),
            ],
            out_specs=[
                pl.BlockSpec((model_dim // 2, tile), lambda i, t: (0, i)),
                pl.BlockSpec((model_dim // 2, tile), lambda i, t: (0, i)),
            ],
            scratch_shapes=[pltpu.VMEM((model_dim, tile), f32)],
        ),
        out_shape=(
            sds((model_dim // 2, columns), f32),
            sds((model_dim // 2, columns), bf16),
        ),
        name="weight_grad",
        cost_estimate=cost(6),
    )(table, turned, dproj)


def after(value, *others):
    return lax.optimization_barrier((value,) + others)[0]


def cost(microseconds):
    return pl.CostEstimate(flops=int(microseconds * 1.1e9), transcendentals=0, bytes_accessed=0)


def pad_to(values, axis, size):
    pads = [(0, 0)] * values.ndim
    pads[axis] = (0, size - values.shape[axis])
    return jnp.pad(values, pads)


def body(
    hidden_in,
    segment_ids,
    norm_gain,
    proj_inner,
    proj_shared,
    proj_step,
    conv_inner,
    conv_shared,
    step_bias,
    log_decay,
    skip_gain,
    gate_gain,
    proj_out,
    out_grad,
):
    dp_count = lax.axis_size("dp")
    dp_index = lax.axis_index("dp")
    rows = proj_inner.shape[0]
    length = segment_ids.shape[0]
    model_dim = hidden_in.shape[1]
    local_inner = proj_inner.shape[2]
    heads = proj_step.shape[1]
    state_size = proj_shared.shape[2]
    kernel_len = conv_inner.shape[0]
    shared_size = 2 * state_size
    full_inner = local_inner * lax.axis_size("tensor")
    width = -(-local_inner // (2 * LANES)) * 2 * LANES
    tap_block = conv_shared.shape[2]
    tap_count = kernel_len * 2 * tap_block
    stages, core, table = block_plan()
    groups, core_table = core_groups()
    blocks = length // TOKEN_BLOCK
    starts = token_starts(blocks)
    two = lax.axis_size("tensor") == 2

    hidden_own, hidden_other = both_halves(hidden_in)
    tap_rows = conv_shared.transpose(1, 2, 0).reshape(2 * tap_block, kernel_len)
    tap_rows = pad_to(tap_rows, 0, rows)
    packed = jnp.concatenate(
        [
            pad_to(proj_inner[:, 1, :], 1, width),
            proj_shared.reshape(rows, shared_size),
            pad_to(jnp.concatenate([proj_step, norm_gain[:, None], tap_rows], axis=1), 1, LANES),
        ],
        axis=1,
    )
    later = jnp.concatenate(
        [pad_to(proj_inner[:, 0, :], 1, width), pad_to(proj_out.T, 1, width)], axis=1
    )
    at = jnp.arange(model_dim)
    block, inside = at // rows, at % rows
    side, spot = inside // tap_block, inside % tap_block
    spread = jnp.where(side < 2, side * state_size + block * tap_block + spot, -1)
    spread = (spread[:, None] == jnp.arange(shared_size)[None, :]).astype(bf16)
    aux, segr = token_facts(segment_ids)
    heads_block = jnp.stack([step_bias, log_decay, skip_gain])
    heads_block = pad_to(pad_to(heads_block, 1, LANES), 0, 8)
    tapi = pad_to(conv_inner, 1, width)
    gain = pad_to(gate_gain[None], 1, width)

    low = packed
    for number, stage in enumerate(stages):
        got = lax.ppermute(low, "dp", stage)
        if number == 0:
            got, spread, aux, segr, heads_block, tapi, gain, later = lax.optimization_barrier(
                (got, spread, aux, segr, heads_block, tapi, gain, later)
            )
        low = jnp.concatenate([low, got], axis=0)
    low, later = lax.optimization_barrier((low, later))
    high = lax.ppermute(low, "dp", core)
    later_low = exchange(jnp.concatenate([later] * (dp_count // 2), axis=0), groups)
    grad_own, grad_other = both_halves(after(out_grad, hidden_other))

    proj, praw, normed, normed_t, weights, taps, norm_scale = run_project(
        starts, table, hidden_own, hidden_other, spread, low, high, heads
    )
    norm_scale = norm_scale[:1]
    mixed, u, su, entry = run_forward(proj, praw, tapi, taps, heads_block, aux, segr)

    later_low, mixed, grad_other = lax.optimization_barrier((later_low, mixed, grad_other))
    later_high = lax.ppermute(later_low, "dp", core)
    gate, nog, grad_t, sums, later_rows = run_out_grad(
        starts, core_table, grad_own, grad_other, later_low, later_high, normed, mixed, gain
    )
    sums = total_over_tensor(sums)
    normed_out, dgate, mixed_grad, gain_rows, gkeep, gsend = run_gated(
        core_table, gate, nog, mixed, sums, aux, gain, grad_t, normed_t, full_inner
    )
    ggot = lax.ppermute(gsend, "dp", core)
    send_start = starts[1:] if two else jnp.zeros((1,), jnp.int32)
    keep_start = starts[:1] if two else jnp.full((1,), blocks // 2, jnp.int32)
    out_send, out_keep = run_out(send_start, normed_out, later_rows)
    ggot, out_send = lax.optimization_barrier((ggot, out_send))
    gsum = exchange((gkeep + ggot.astype(f32)).astype(bf16), groups)
    out_other = swap(out_send) if two else None

    dproj, wide, dtaps = run_backward(
        proj, praw, u, su, entry, mixed_grad, tapi, taps, heads_block, aux, segr
    )
    dproj, gsum = lax.optimization_barrier((dproj, gsum))
    if two:
        dproj, out_other = lax.optimization_barrier((dproj, out_other))
        out_half = out_keep.astype(f32) + out_other.astype(f32)
    else:
        out_half = add_halves(out_send, out_keep)
    hidden_out = (hidden_in.astype(f32) + out_half).astype(bf16)
    grad_send, norm_sum = run_norm_grad(
        send_start, dgate, dproj, later_rows, weights, normed, bf16
    )
    wkeep, wsend = run_weight_grad(core_table, normed_t, dproj)
    grad_keep, norm_more = run_norm_grad(
        keep_start, dgate, dproj, later_rows, weights, normed, f32
    )
    wgot = lax.ppermute(wsend, "dp", core)
    wgot, grad_keep = lax.optimization_barrier((wgot, grad_keep))
    wsum = exchange((wkeep + wgot.astype(f32)).astype(bf16), groups)
    if two:
        own_grad = grad_keep + swap(grad_send).astype(f32)
    else:
        own_grad = add_halves(grad_send, grad_keep)
    gsum = sum_blocks(gsum, rows)
    out_sum = gsum[:, width : width + local_inner].T
    wsum = sum_blocks(wsum, rows)
    ssum = wsum[:, width:]

    lanes = max(width, model_dim)
    norm_sum = jnp.sum(norm_sum + norm_more, axis=0, keepdims=True) / norm_scale
    small = jnp.concatenate(
        [
            pad_to(wide[:4], 1, lanes),
            pad_to(jnp.sum(gain_rows, axis=0, keepdims=True), 1, lanes),
            pad_to(wide[5:], 1, lanes),
            pad_to(dtaps[:kernel_len], 1, lanes),
            pad_to(norm_sum, 1, lanes),
            jnp.zeros((3, lanes), f32),
        ],
        axis=0,
    )
    small = total_over_dp(small)
    conv_total = small[:kernel_len, :local_inner]
    gain_total = small[4, :local_inner]
    skip_total = jnp.sum(small[5, :width].reshape(-1, HEAD_DIM), axis=1)[:heads]
    bias_total = small[6, :heads]
    decay_total = small[6, LANES : LANES + heads]
    small = total_over_tensor(small[8:16])
    norm_total = lax.dynamic_slice_in_dim(small[4, :model_dim], dp_index * rows, rows)
    taps_total = lax.dynamic_slice_in_dim(
        small[:kernel_len, :shared_size].reshape(kernel_len, 2, state_size),
        dp_index * tap_block,
        tap_block,
        axis=2,
    )
    inner_sum = jnp.stack([gsum[:, :local_inner], wsum[:, :local_inner]], axis=1)
    step_sum = ssum[:, shared_size : shared_size + heads]
    shared_total = total_over_tensor(ssum[:, :shared_size]).reshape(rows, 2, state_size)

    own = hidden_in.astype(f32)
    own_inv = lax.rsqrt(jnp.mean(own * own, axis=-1, keepdims=True) + epsilon)
    own_unit = own * own_inv
    scaled_in = own_grad * norm_scale
    hidden_grad = own_inv * (
        scaled_in - own_unit * jnp.mean(scaled_in * own_unit, axis=-1, keepdims=True)
    ) + out_grad.astype(f32)
    return (
        hidden_out,
        hidden_grad,
        norm_total,
        inner_sum,
        shared_total,
        step_sum,
        conv_total,
        taps_total,
        bias_total,
        decay_total,
        skip_total,
        gain_total,
        out_sum,
    )


def solution(mesh):
    in_specs = (
        P(("dp", "tensor"), None),
        P("dp"),
        P("dp"),
        P("dp", None, "tensor"),
        P("dp", None, None),
        P("dp", "tensor"),
        P(None, "tensor"),
        P(None, None, "dp"),
        P("tensor"),
        P("tensor"),
        P("tensor"),
        P("tensor"),
        P("tensor", "dp"),
        P(("dp", "tensor"), None),
    )
    out_specs = (
        P(("dp", "tensor"), None),
        P(("dp", "tensor"), None),
        P("dp"),
        P("dp", None, "tensor"),
        P("dp", None, None),
        P("dp", "tensor"),
        P(None, "tensor"),
        P(None, None, "dp"),
        P("tensor"),
        P("tensor"),
        P("tensor"),
        P("tensor"),
        P("tensor", "dp"),
    )
    return jax.shard_map(body, mesh=mesh, in_specs=in_specs, out_specs=out_specs, check_vma=False)
```

```python
from functools import partial

import jax
import jax.numpy as jnp
import numpy as np
from jax import lax
from jax.experimental import pallas as pl
from jax.experimental.pallas import tpu as pltpu
from jax.sharding import PartitionSpec as P

HEAD_DIM = 64
CHUNK = 128
LANES = 128
TOKEN_BLOCK = 256
epsilon = 1e-05
f32 = jnp.float32
bf16 = jnp.bfloat16
highest = lax.Precision.HIGHEST


def dot_nn(a, b):
    return lax.dot_general(a, b, (((1,), (0,)), ((), ())), preferred_element_type=f32)


def dot_nt(a, b):
    return lax.dot_general(a, b, (((1,), (1,)), ((), ())), preferred_element_type=f32)


def dot_tn(a, b):
    return lax.dot_general(a, b, (((0,), (0,)), ((), ())), preferred_element_type=f32)


def dot_exact(a, b):
    return lax.dot_general(
        a, b, (((1,), (0,)), ((), ())), preferred_element_type=f32, precision=highest
    )


def dot_split(a, b):
    high = a.astype(bf16)
    rest = (a - high.astype(f32)).astype(bf16)
    return dot_nn(high, b) + dot_nn(rest, b)


def sigmoid(v):
    return 1.0 / (1.0 + jnp.exp(-v))


def softplus(v):
    return jnp.maximum(v, 0.0) + jnp.log1p(jnp.exp(-jnp.abs(v)))


def halves(lane_low, values, head):
    return jnp.where(lane_low, values[:, head : head + 1], values[:, head + 1 : head + 2])


def back_shift(window, offset):
    return pltpu.roll(window, offset, 0)[8:, :]


def ahead_shift(window, offset):
    rows = window.shape[0]
    return pltpu.roll(window, rows - offset, 0)[: rows - 8, :]


def conv_rows(window, taps, aux):
    total = taps[3:4, :] * window[8:, :]
    for offset in range(1, 4):
        total = total + taps[3 - offset : 4 - offset, :] * (
            back_shift(window, offset) * aux[:, offset : offset + 1]
        )
    return total


def forward_kernel(
    proj_ref,
    step_ref,
    tapi_ref,
    taps_ref,
    heads_ref,
    aux_ref,
    segr_ref,
    mixed_ref,
    u_ref,
    su_ref,
    entry_ref,
    state_ref,
    carry_ref,
    scarry_ref,
    xw_ref,
):
    width = mixed_ref.shape[1]
    pairs = width // LANES
    shared_size = su_ref.shape[1]
    state_size = shared_size // 2
    chunk = pl.program_id(0)

    @pl.when(chunk == 0)
    def _():
        for ref in (state_ref, carry_ref, scarry_ref):
            ref[...] = jnp.zeros_like(ref)

    rows = lax.broadcasted_iota(jnp.int32, (CHUNK, CHUNK), 0)
    cols = lax.broadcasted_iota(jnp.int32, (CHUNK, CHUNK), 1)
    lower = rows >= cols
    summing = lower.astype(f32)
    lane_low = lax.broadcasted_iota(jnp.int32, (CHUNK, LANES), 1) < HEAD_DIM
    bias = heads_ref[0:1, :]
    rate = -jnp.exp(heads_ref[1:2, :])
    skips = heads_ref[2:3, :]
    aux = aux_ref[...]
    live = aux[:, 7:8]
    same = lower & (aux[:, 0:1] == segr_ref[pl.ds(chunk, 1), :])
    shared_now = proj_ref[:, width:].astype(f32)
    su = conv_rows(jnp.concatenate([scarry_ref[...], shared_now], axis=0), taps_ref[...], aux)
    scarry_ref[...] = shared_now[CHUNK - 8 :, :]
    su_ref[...] = su
    shared = (su * sigmoid(su)).astype(bf16)
    b_rows = shared[:, :state_size]
    c_rows = shared[:, state_size:]
    scores = jnp.where(same, dot_nt(c_rows, b_rows), 0.0)
    step = softplus(step_ref[...] + bias) * live
    decay = dot_exact(summing, step * rate)
    decay_t = decay.T
    last = decay[CHUNK - 1 :, :]
    entry_scale = jnp.exp(decay) * aux[:, 8:9]
    end_scale = jnp.exp(last - decay) * aux[:, 9:10]
    keep = jnp.exp(last) * aux[:1, 10:11]
    state = state_ref[...]
    state_low = state.astype(bf16)
    entry_ref[...] = state_low[None]
    past = dot_nn(c_rows, state_low)
    for pair in range(pairs):
        lanes = slice(pair * LANES, (pair + 1) * LANES)
        head = 2 * pair
        now = proj_ref[:, lanes].astype(f32)
        window = jnp.concatenate([carry_ref[:, lanes], now], axis=0)
        carry_ref[:, lanes] = now[CHUNK - 8 :, :]
        u = conv_rows(window, tapi_ref[:, lanes].astype(f32), aux)
        u_ref[:, lanes] = u.astype(bf16)
        x = u * sigmoid(u)
        scaled = x * halves(lane_low, step, head)
        mixing = jnp.concatenate(
            [
                (
                    scores
                    * jnp.exp(jnp.minimum(decay[:, h : h + 1] - decay_t[h : h + 1, :], 0.0))
                ).astype(bf16)
                for h in (head, head + 1)
            ],
            axis=1,
        )
        stacked = jnp.concatenate(
            [jnp.where(lane_low, scaled, 0.0), jnp.where(lane_low, 0.0, scaled)], axis=0
        ).astype(bf16)
        inside = dot_nn(mixing, stacked)
        xw_ref[:, lanes] = (scaled * halves(lane_low, end_scale, head)).astype(bf16)
        mixed = (
            inside
            + past[:, lanes] * halves(lane_low, entry_scale, head)
            + halves(lane_low[:1], skips, head) * x
        ) * live
        mixed_ref[:, lanes] = mixed.astype(bf16)
        state_ref[:, lanes] = state[:, lanes] * halves(lane_low[:1], keep, head)
    state_ref[...] += dot_tn(b_rows, xw_ref[...])


def token_scales(sums, full_inner):
    columns = sums.T
    inv = lax.rsqrt(columns[:, 0:1] / full_inner + epsilon)
    return inv, inv * columns[:, 1:2] / full_inner


def silu_slope(v, s):
    return s * (1.0 + v * (1.0 - s))


def backward_kernel(
    proj_ref,
    praw_ref,
    u_ref,
    su_ref,
    entry_ref,
    grad_ref,
    tapi_ref,
    taps_ref,
    heads_ref,
    aux_ref,
    segr_ref,
    gain_ref,
    dproj_ref,
    small_ref,
    wide_ref,
    shared_ref,
    state_ref,
    ahead_ref,
    sahead_ref,
    xw_ref,
    ge_ref,
    row_ref,
    proda_ref,
    prodb_ref,
):
    width = u_ref.shape[1]
    chunks = pl.num_programs(0)
    pairs = width // LANES
    shared_size = su_ref.shape[1]
    state_size = shared_size // 2
    shared_cols = slice(width, width + shared_size)
    step_cols = slice(width + shared_size, width + shared_size + LANES)
    chunk = chunks - 1 - pl.program_id(0)

    @pl.when(pl.program_id(0) == 0)
    def _():
        for ref in (state_ref, ahead_ref, sahead_ref, row_ref, wide_ref, shared_ref):
            ref[...] = jnp.zeros_like(ref)

    rows = lax.broadcasted_iota(jnp.int32, (CHUNK, CHUNK), 0)
    cols = lax.broadcasted_iota(jnp.int32, (CHUNK, CHUNK), 1)
    upper = rows <= cols
    summing = (rows >= cols).astype(f32)
    unsumming = upper.astype(f32)
    last_row = (lax.broadcasted_iota(jnp.int32, (CHUNK, LANES), 0) == CHUNK - 1).astype(f32)
    lane_ids = lax.broadcasted_iota(jnp.int32, (CHUNK, LANES), 1)
    lane_low = lane_ids < HEAD_DIM
    bias = heads_ref[0:1, :]
    rate = -jnp.exp(heads_ref[1:2, :])
    skips = heads_ref[2:3, :]
    place = (
        lax.broadcasted_iota(jnp.int32, (width, LANES), 0) // HEAD_DIM
        == lax.broadcasted_iota(jnp.int32, (width, LANES), 1)
    ).astype(bf16)

    aux = aux_ref[...]
    live = aux[:, 7:8]
    same = upper & (aux[:, 0:1] == segr_ref[pl.ds(chunk, 1), :])
    su = su_ref[...]
    su_sig = sigmoid(su)
    shared = (su * su_sig).astype(bf16)
    b_rows = shared[:, :state_size]
    c_rows = shared[:, state_size:]
    scores = jnp.where(same, dot_nt(b_rows, c_rows), 0.0)
    pre = praw_ref[...] + bias
    step = softplus(pre) * live
    decay = dot_exact(summing, step * rate)
    decay_t = decay.T
    last = decay[CHUNK - 1 :, :]
    entry_scale = jnp.exp(decay) * aux[:, 8:9]
    end_scale = jnp.exp(last - decay) * aux[:, 9:10]
    keep = jnp.exp(last) * aux[:1, 10:11]
    entry = entry_ref[0]
    dstate = state_ref[...]
    dstate_low = dstate.astype(bf16)
    past = dot_nn(c_rows, entry)
    bds = dot_nn(b_rows, dstate_low)
    score_grad = jnp.zeros((CHUNK, CHUNK), f32)
    col_part = jnp.zeros((CHUNK, LANES), f32)
    for pair in range(pairs):
        lanes = slice(pair * LANES, (pair + 1) * LANES)
        head = 2 * pair
        g_low = grad_ref[:, lanes]
        g = g_low.astype(f32)
        u = u_ref[:, lanes].astype(f32)
        u_sig = sigmoid(u)
        x = u * u_sig
        step_c = halves(lane_low, step, head)
        scaled = x * step_c
        stacked = jnp.concatenate(
            [jnp.where(lane_low, scaled, 0.0), jnp.where(lane_low, 0.0, scaled)], axis=0
        ).astype(bf16)
        dmix = dot_nt(stacked, g_low)
        mixing = []
        for k, h in enumerate((head, head + 1)):
            decays = jnp.exp(jnp.minimum(decay_t[h : h + 1, :] - decay[:, h : h + 1], 0.0))
            dmix_h = dmix[k * CHUNK : (k + 1) * CHUNK, :]
            score_grad = score_grad + dmix_h * decays
            mixing_h = scores * decays
            mixing.append(mixing_h.astype(bf16))
            both = mixing_h * dmix_h
            col_part = jnp.where(lane_ids == h, jnp.sum(both, axis=1, keepdims=True), col_part)
            row_ref[h : h + 1, :] = jnp.sum(both, axis=0, keepdims=True)
        g_stacked = jnp.concatenate(
            [jnp.where(lane_low, g, 0.0), jnp.where(lane_low, 0.0, g)], axis=0
        ).astype(bf16)
        end_c = halves(lane_low, end_scale, head)
        entry_c = halves(lane_low, entry_scale, head)
        keep_c = halves(lane_low[:1], keep, head)
        from_state = end_c * bds[:, lanes]
        dscaled = dot_nn(jnp.concatenate(mixing, axis=1), g_stacked) + from_state
        xw_ref[:, lanes] = (scaled * end_c).astype(bf16)
        q = scaled * from_state
        ge = g * entry_c
        ge_ref[:, lanes] = ge.astype(bf16)
        dstate_p = dstate[:, lanes]
        tail = jnp.sum(q, axis=0, keepdims=True) + keep_c * jnp.sum(
            dstate_p * entry[:, lanes].astype(f32), axis=0, keepdims=True
        )
        proda_ref[:, lanes] = x * dscaled
        prodb_ref[:, lanes] = ge * past[:, lanes] - q + last_row * tail
        state_ref[:, lanes] = dstate_p * keep_c
        dx = step_c * dscaled + halves(lane_low[:1], skips, head) * g
        du = dx * silu_slope(u, u_sig)
        window = jnp.concatenate([du, ahead_ref[:, lanes]], axis=0)
        ahead_ref[:, lanes] = du[:8, :]
        cin = proj_ref[:, lanes].astype(f32)
        taps = tapi_ref[:, lanes].astype(f32)
        dcin = taps[3:4, :] * du
        wide_ref[3:4, lanes] += jnp.sum(cin * du, axis=0, keepdims=True)
        for offset in range(1, 4):
            moved = ahead_shift(window, offset) * aux[:, 3 + offset : 4 + offset]
            dcin = dcin + taps[3 - offset : 4 - offset, :] * moved
            wide_ref[3 - offset : 4 - offset, lanes] += jnp.sum(
                cin * moved, axis=0, keepdims=True
            )
        dproj_ref[:, lanes] = dcin.astype(bf16)
        wide_ref[5:6, lanes] += jnp.sum(g * x, axis=0, keepdims=True)
    score_low = jnp.where(same, score_grad, 0.0).astype(bf16)
    ge_all = ge_ref[...]
    db = dot_nn(score_low, c_rows) + dot_nt(xw_ref[...], dstate_low)
    dc = dot_tn(score_low, b_rows) + dot_nt(ge_all, entry)
    state_ref[...] += dot_tn(c_rows, ge_all)
    ds = jnp.concatenate([db, dc], axis=1) * silu_slope(su, su_sig)
    window = jnp.concatenate([ds, sahead_ref[...]], axis=0)
    sahead_ref[...] = ds[:8, :]
    taps = taps_ref[...]
    sin = proj_ref[:, shared_cols].astype(f32)
    dsin = taps[3:4, :] * ds
    shared_ref[3:4, :] += jnp.sum(sin * ds, axis=0, keepdims=True)
    for offset in range(1, 4):
        moved = ahead_shift(window, offset) * aux[:, 3 + offset : 4 + offset]
        dsin = dsin + taps[3 - offset : 4 - offset, :] * moved
        shared_ref[3 - offset : 4 - offset, :] += jnp.sum(sin * moved, axis=0, keepdims=True)
    dproj_ref[:, shared_cols] = dsin.astype(bf16)
    ddecay = row_ref[...].T - col_part + dot_split(prodb_ref[...], place)
    dlog = dot_exact(unsumming, ddecay)
    dstep = (dot_split(proda_ref[...], place) + rate * dlog) * live * sigmoid(pre)
    dproj_ref[:, step_cols] = dstep.astype(bf16)
    wide_ref[6:7, :LANES] += jnp.sum(dstep, axis=0, keepdims=True)
    wide_ref[6:7, LANES : 2 * LANES] += jnp.sum(step * dlog, axis=0, keepdims=True) * rate

    @pl.when(chunk == 0)
    def _():
        small_ref[...] = jnp.zeros_like(small_ref)
        small_ref[:4, :width] = wide_ref[:4, :]
        small_ref[:4, width : width + shared_size] = shared_ref[:4, :]
        skip_row = dot_split(wide_ref[...], place)[5:6, :]
        small_ref[0:1, step_cols] = skip_row
        small_ref[1:2, step_cols] = wide_ref[6:7, :LANES]
        small_ref[2:3, step_cols] = wide_ref[6:7, LANES : 2 * LANES]
        small_ref[4:5, :width] = jnp.sum(gain_ref[...], axis=0, keepdims=True)


def facts_kernel(seg_ref, aux_ref, segr_ref):
    seg = seg_ref[...].astype(f32)
    chunks = seg.shape[0]
    segr_ref[...] = seg
    none = jnp.full((1, CHUNK), -1.0, f32)
    before = jnp.concatenate([none, seg[: chunks - 1]], axis=0) if chunks > 1 else none
    behind = jnp.concatenate([seg[1:], none], axis=0) if chunks > 1 else none
    lane = lax.broadcasted_iota(jnp.int32, seg.shape, 1)
    facts = [seg]
    for offset in range(1, 4):
        earlier = jnp.where(
            lane >= offset, pltpu.roll(seg, offset, 1), pltpu.roll(before, offset, 1)
        )
        facts.append((earlier == seg).astype(f32))
    for offset in range(1, 4):
        later = jnp.where(
            lane < CHUNK - offset,
            pltpu.roll(seg, CHUNK - offset, 1),
            pltpu.roll(behind, CHUNK - offset, 1),
        )
        facts.append((later == seg).astype(f32))
    last = jnp.broadcast_to(seg[:, CHUNK - 1 :], seg.shape)
    prior = jnp.broadcast_to(before[:, CHUNK - 1 :], seg.shape)
    facts.append((seg != 0.0).astype(f32))
    facts.append((seg == prior).astype(f32))
    facts.append((seg == last).astype(f32))
    facts.append((last == prior).astype(f32))
    empty = jnp.zeros((LANES - len(facts), CHUNK), f32)
    for chunk in range(chunks):
        rows = jnp.concatenate([f[chunk : chunk + 1, :] for f in facts] + [empty], axis=0)
        aux_ref[chunk * CHUNK : (chunk + 1) * CHUNK, :] = rows.T[:, : aux_ref.shape[1]]


def token_facts(segments):
    length = segments.shape[0]
    chunks = length // CHUNK
    return pl.pallas_call(
        facts_kernel,
        out_shape=(
            jax.ShapeDtypeStruct((length, 16), f32),
            jax.ShapeDtypeStruct((chunks, CHUNK), f32),
        ),
        name="token_facts",
        cost_estimate=cost(2),
    )(segments.reshape(chunks, CHUNK))


def chunk_spec(columns, last):
    if last is None:
        return pl.BlockSpec((CHUNK, columns), lambda i: (i, 0))
    return pl.BlockSpec((CHUNK, columns), lambda i: (last - i, 0))


def fixed_spec(values):
    zeros = (0,) * values.ndim
    return pl.BlockSpec(values.shape, lambda i: zeros)


def run_forward(proj, praw, tapi, taps, heads, aux, segr):
    length = proj.shape[0]
    width = tapi.shape[1]
    shared_size = taps.shape[1]
    state_size = shared_size // 2
    chunks = length // CHUNK
    sds = jax.ShapeDtypeStruct
    return pl.pallas_call(
        forward_kernel,
        grid=(chunks,),
        in_specs=[
            chunk_spec(proj.shape[1], None),
            chunk_spec(LANES, None),
            fixed_spec(tapi),
            fixed_spec(taps),
            fixed_spec(heads),
            chunk_spec(aux.shape[1], None),
            fixed_spec(segr),
        ],
        out_specs=[
            chunk_spec(width, None),
            chunk_spec(width, None),
            chunk_spec(shared_size, None),
            pl.BlockSpec((1, state_size, width), lambda i: (i, 0, 0)),
        ],
        out_shape=(
            sds((length, width), bf16),
            sds((length, width), bf16),
            sds((length, shared_size), f32),
            sds((chunks, state_size, width), bf16),
        ),
        scratch_shapes=[
            pltpu.VMEM((state_size, width), f32),
            pltpu.VMEM((8, width), f32),
            pltpu.VMEM((8, shared_size), f32),
            pltpu.VMEM((CHUNK, width), bf16),
        ],
        name="scan_forward",
        cost_estimate=cost(18),
    )(proj, praw, tapi, taps, heads, aux, segr)


def run_backward(proj, praw, u, su, entry, grad, tapi, taps, heads, aux, segr, gain_rows):
    length, width = u.shape
    shared_size = su.shape[1]
    state_size = shared_size // 2
    chunks = length // CHUNK
    last = chunks - 1
    columns = width + shared_size + LANES
    sds = jax.ShapeDtypeStruct
    return pl.pallas_call(
        backward_kernel,
        grid=(chunks,),
        in_specs=[
            chunk_spec(proj.shape[1], last),
            chunk_spec(LANES, last),
            chunk_spec(width, last),
            chunk_spec(shared_size, last),
            pl.BlockSpec((1, state_size, width), lambda i: (last - i, 0, 0)),
            chunk_spec(width, last),
            fixed_spec(tapi),
            fixed_spec(taps),
            fixed_spec(heads),
            chunk_spec(aux.shape[1], last),
            fixed_spec(segr),
            fixed_spec(gain_rows),
        ],
        out_specs=[
            chunk_spec(columns, last),
            pl.BlockSpec((8, columns), lambda i: (0, 0)),
        ],
        out_shape=(
            sds((length, columns), bf16),
            sds((8, columns), f32),
        ),
        scratch_shapes=[
            pltpu.VMEM((8, width), f32),
            pltpu.VMEM((8, shared_size), f32),
            pltpu.VMEM((state_size, width), f32),
            pltpu.VMEM((8, width), f32),
            pltpu.VMEM((8, shared_size), f32),
            pltpu.VMEM((CHUNK, width), bf16),
            pltpu.VMEM((CHUNK, width), bf16),
            pltpu.VMEM((LANES, CHUNK), f32),
            pltpu.VMEM((CHUNK, width), f32),
            pltpu.VMEM((CHUNK, width), f32),
        ],
        name="scan_backward",
        cost_estimate=cost(32),
    )(proj, praw, u, su, entry, grad, tapi, taps, heads, aux, segr, gain_rows)


def block_plan():
    count = lax.axis_size("dp")
    bits = []
    bit = count // 2
    while bit > 1:
        bits.append(bit)
        bit //= 2
    mixed = bits[:-2] + bits[-2:][::-1]
    by_core = (bits, mixed)
    stages = []
    for stage in range(len(bits)):
        stages.append([(i, i ^ by_core[i % 2][stage]) for i in range(count)])
    core = [(i, i ^ 1) for i in range(count)]
    device = np.zeros((count, count), np.int32)
    for own in range(count):
        for spot in range(count):
            other = own ^ 1 if spot >= count // 2 else own
            for stage, bit in enumerate(by_core[other % 2]):
                if (spot >> stage) & 1:
                    other ^= bit
            device[own, spot] = other
    table = jnp.asarray(device)[lax.axis_index("dp")]
    return stages, core, table


def core_groups():
    count = lax.axis_size("dp")
    groups = [list(range(side, count, 2)) for side in range(2)]
    return groups, jnp.asarray(
        [groups[0] + groups[1], groups[1] + groups[0]], jnp.int32
    )[lax.axis_index("dp") % 2]


def exchange(blocks, groups):
    return lax.all_to_all(
        blocks, "dp", 0, 0, axis_index_groups=groups, tiled=True
    )


def sum_blocks(blocks, rows):
    return jnp.sum(blocks.reshape(-1, rows, blocks.shape[1]).astype(f32), axis=0)


def swap(values):
    return lax.ppermute(values, "tensor", [(0, 1), (1, 0)])


def total_over_tensor(values):
    if lax.axis_size("tensor") == 2:
        return values + swap(values)
    return lax.psum(values, "tensor")


def both_halves(own):
    if lax.axis_size("tensor") == 2:
        return own, swap(own)
    whole = lax.all_gather(own, "tensor", axis=0, tiled=True)
    return whole, whole


def token_starts(blocks):
    if lax.axis_size("tensor") == 2:
        index = lax.axis_index("tensor")
        return jnp.stack([index * (blocks // 2), (1 - index) * (blocks // 2)]).astype(jnp.int32)
    return jnp.zeros((2,), jnp.int32)


def add_halves(send, keep):
    if lax.axis_size("tensor") == 2:
        return keep.astype(f32) + swap(send).astype(f32)
    whole = jnp.concatenate([send.astype(bf16), keep.astype(bf16)], axis=0)
    return lax.psum_scatter(whole, "tensor", scatter_dimension=0, tiled=True).astype(f32)


def own_block(step, starts, own_blocks):
    return jnp.clip(step - starts[0], 0, own_blocks - 1)


def other_block(step, starts, own_blocks):
    return jnp.clip(step - starts[1], 0, own_blocks - 1)


def place_blocks(table_ref, low_ref, high_ref, whole_ref, sem_ref):
    count = table_ref.shape[0]
    rows = whole_ref.shape[0] // count
    copies = []
    for spot in range(count):
        source = low_ref if spot < count // 2 else high_ref
        where = pl.multiple_of(table_ref[spot] * rows, rows)
        copies.append(
            pltpu.make_async_copy(
                source.at[pl.ds((spot % (count // 2)) * rows, rows), :],
                whole_ref.at[pl.ds(where, rows), :],
                sem_ref.at[spot],
            )
        )
    for copy in copies:
        copy.start()
    for copy in copies:
        copy.wait()


def project_kernel(
    starts_ref,
    table_ref,
    own_ref,
    other_ref,
    spread_ref,
    low_ref,
    high_ref,
    proj_ref,
    step_ref,
    normed_ref,
    turned_ref,
    weights_ref,
    taps_ref,
    scale_ref,
    sem_ref,
    *,
    own_blocks,
    heads,
):
    step = pl.program_id(0)
    model_dim, columns = weights_ref.shape

    @pl.when(step == 0)
    def _():
        place_blocks(table_ref, low_ref, high_ref, weights_ref, sem_ref)
        extra = weights_ref[:, columns - LANES :].astype(f32).T
        scale_ref[...] = jnp.broadcast_to(extra[heads : heads + 1, :], scale_ref.shape)
        taps = extra[heads + 1 : heads + 5, :]
        taps = jnp.concatenate([taps, jnp.zeros_like(taps)], axis=0).astype(bf16)
        taps_ref[...] = dot_nn(taps, spread_ref[...])

    mine = (step >= starts_ref[0]) & (step < starts_ref[0] + own_blocks)
    tokens = jnp.where(mine, own_ref[...].astype(f32), other_ref[...].astype(f32))
    inv = lax.rsqrt(jnp.mean(tokens * tokens, axis=-1, keepdims=True) + epsilon)
    normed = (tokens * inv * scale_ref[:1, :]).astype(bf16)
    normed_ref[...] = normed
    turned_ref[...] = normed.T
    proj = dot_nn(normed, weights_ref[...])
    proj_ref[...] = proj[:, : columns - LANES].astype(bf16)
    step_ref[...] = proj[:, columns - LANES :]


def run_project(starts, table, own, other, spread, low, high, heads):
    own_rows, model_dim = own.shape
    columns = low.shape[1]
    own_blocks = own_rows // TOKEN_BLOCK
    blocks = own_blocks * (2 if lax.axis_size("tensor") == 2 else 1)
    length = blocks * TOKEN_BLOCK
    sds = jax.ShapeDtypeStruct
    return pl.pallas_call(
        partial(project_kernel, own_blocks=own_blocks, heads=heads),
        grid_spec=pltpu.PrefetchScalarGridSpec(
            num_scalar_prefetch=2,
            grid=(blocks,),
            in_specs=[
                pl.BlockSpec(
                    (TOKEN_BLOCK, model_dim), lambda i, s, t: (own_block(i, s, own_blocks), 0)
                ),
                pl.BlockSpec(
                    (TOKEN_BLOCK, model_dim), lambda i, s, t: (other_block(i, s, own_blocks), 0)
                ),
                pl.BlockSpec(spread.shape, lambda i, s, t: (0, 0)),
                pl.BlockSpec(memory_space=pl.ANY),
                pl.BlockSpec(memory_space=pl.ANY),
            ],
            out_specs=[
                pl.BlockSpec((TOKEN_BLOCK, columns - LANES), lambda i, s, t: (i, 0)),
                pl.BlockSpec((TOKEN_BLOCK, LANES), lambda i, s, t: (i, 0)),
                pl.BlockSpec((TOKEN_BLOCK, model_dim), lambda i, s, t: (i, 0)),
                pl.BlockSpec((model_dim, TOKEN_BLOCK), lambda i, s, t: (0, i)),
                pl.BlockSpec((model_dim, columns), lambda i, s, t: (0, 0)),
                pl.BlockSpec((8, spread.shape[1]), lambda i, s, t: (0, 0)),
                pl.BlockSpec((8, model_dim), lambda i, s, t: (0, 0)),
            ],
            scratch_shapes=[pltpu.SemaphoreType.DMA((table.shape[0],))],
        ),
        out_shape=(
            sds((length, columns - LANES), bf16),
            sds((length, LANES), f32),
            sds((length, model_dim), bf16),
            sds((model_dim, length), bf16),
            sds((model_dim, columns), bf16),
            sds((8, spread.shape[1]), f32),
            sds((8, model_dim), f32),
        ),
        name="norm_project",
        cost_estimate=cost(9),
    )(starts, table, own, other, spread, low, high)


def token_sum(values):
    total = values[:, :LANES]
    for at in range(LANES, values.shape[1], LANES):
        total = total + values[:, at : at + LANES]
    return jnp.sum(total.T, axis=0, keepdims=True)


def out_grad_kernel(
    starts_ref,
    table_ref,
    own_ref,
    other_ref,
    low_ref,
    high_ref,
    normed_ref,
    mixed_ref,
    gain_ref,
    gate_ref,
    nog_ref,
    turned_ref,
    sums_ref,
    weights_ref,
    sem_ref,
    *,
    own_blocks,
):
    step = pl.program_id(0)
    width = mixed_ref.shape[1]

    @pl.when(step == 0)
    def _():
        place_blocks(table_ref, low_ref, high_ref, weights_ref, sem_ref)

    mine = (step >= starts_ref[0]) & (step < starts_ref[0] + own_blocks)
    tokens = jnp.where(mine, own_ref[...].astype(f32), other_ref[...].astype(f32)).astype(bf16)
    turned_ref[...] = tokens.T
    gate = dot_nn(normed_ref[...], weights_ref[:, :width])
    gate_ref[...] = gate.astype(bf16)
    nog = dot_nn(tokens, weights_ref[:, width:])
    nog_ref[...] = nog.astype(bf16)
    gated = mixed_ref[...].astype(f32) * (gate * sigmoid(gate))
    sums_ref[...] = jnp.concatenate(
        [
            token_sum(gated * gated),
            token_sum(nog * gain_ref[...].astype(f32) * gated),
            jnp.zeros((6, TOKEN_BLOCK), f32),
        ],
        axis=0,
    )


def run_out_grad(starts, table, own, other, low, high, normed, mixed, gain):
    own_rows, model_dim = own.shape
    length, width = mixed.shape
    own_blocks = own_rows // TOKEN_BLOCK
    blocks = length // TOKEN_BLOCK
    sds = jax.ShapeDtypeStruct
    return pl.pallas_call(
        partial(out_grad_kernel, own_blocks=own_blocks),
        grid_spec=pltpu.PrefetchScalarGridSpec(
            num_scalar_prefetch=2,
            grid=(blocks,),
            in_specs=[
                pl.BlockSpec(
                    (TOKEN_BLOCK, model_dim), lambda i, s, t: (own_block(i, s, own_blocks), 0)
                ),
                pl.BlockSpec(
                    (TOKEN_BLOCK, model_dim), lambda i, s, t: (other_block(i, s, own_blocks), 0)
                ),
                pl.BlockSpec(memory_space=pl.ANY),
                pl.BlockSpec(memory_space=pl.ANY),
                pl.BlockSpec((TOKEN_BLOCK, model_dim), lambda i, s, t: (i, 0)),
                pl.BlockSpec((TOKEN_BLOCK, width), lambda i, s, t: (i, 0)),
                pl.BlockSpec((1, width), lambda i, s, t: (0, 0)),
            ],
            out_specs=[
                pl.BlockSpec((TOKEN_BLOCK, width), lambda i, s, t: (i, 0)),
                pl.BlockSpec((TOKEN_BLOCK, width), lambda i, s, t: (i, 0)),
                pl.BlockSpec((model_dim, TOKEN_BLOCK), lambda i, s, t: (0, i)),
                pl.BlockSpec((8, TOKEN_BLOCK), lambda i, s, t: (0, i)),
                pl.BlockSpec((model_dim, 2 * width), lambda i, s, t: (0, 0)),
            ],
            scratch_shapes=[pltpu.SemaphoreType.DMA((table.shape[0],))],
        ),
        out_shape=(
            sds((length, width), bf16),
            sds((length, width), bf16),
            sds((model_dim, length), bf16),
            sds((8, length), f32),
            sds((model_dim, 2 * width), bf16),
        ),
        name="out_grad",
        cost_estimate=cost(9),
    )(starts, table, own, other, low, high, normed, mixed, gain)


def store_blocks(table_ref, source_ref, keep_ref, send_ref):
    count = table_ref.shape[0]
    rows = source_ref.shape[0] // count
    half = count // 2
    for spot in range(half):
        where = pl.multiple_of(table_ref[spot] * rows, rows)
        keep_ref[spot * rows : (spot + 1) * rows, :] = source_ref[pl.ds(where, rows), :]
    for spot in range(half):
        where = pl.multiple_of(table_ref[half + spot] * rows, rows)
        send_ref[spot * rows : (spot + 1) * rows, :] = source_ref[pl.ds(where, rows), :].astype(
            bf16
        )


def gated_kernel(
    table_ref,
    gate_ref,
    nog_ref,
    mixed_ref,
    sums_ref,
    more_ref,
    aux_ref,
    gain_ref,
    gturned_ref,
    nturned_ref,
    out_ref,
    dgate_ref,
    grad_ref,
    row_ref,
    keep_ref,
    send_ref,
    total_ref,
    *,
    full_inner,
):
    step = pl.program_id(0)
    width = gate_ref.shape[1]
    inv, mean = token_scales(sums_ref[...] + more_ref[...], full_inner)
    gain = gain_ref[...].astype(f32)
    gate = gate_ref[...].astype(f32)
    gate_sig = sigmoid(gate)
    gate_silu = gate * gate_sig
    mixed = mixed_ref[...].astype(f32)
    unit = mixed * gate_silu * inv
    nog = nog_ref[...].astype(f32)
    grad = inv * (nog * gain - unit * mean)
    dgate = (grad * mixed * silu_slope(gate, gate_sig)).astype(bf16)
    dgate_ref[...] = dgate
    grad_ref[...] = (grad * gate_silu * aux_ref[:, 7:8]).astype(bf16)
    normed_out = (unit * gain).astype(bf16)
    out_ref[...] = normed_out
    row = jnp.sum((nog * unit).reshape(-1, 8, width), axis=0)
    part_gate = dot_nn(nturned_ref[...], dgate)
    part_out = dot_nn(gturned_ref[...], normed_out)

    @pl.when(step == 0)
    def _():
        total_ref[:, :width] = part_gate
        total_ref[:, width:] = part_out
        row_ref[...] = row

    @pl.when(step > 0)
    def _():
        total_ref[:, :width] += part_gate
        total_ref[:, width:] += part_out
        row_ref[...] += row

    @pl.when(step == pl.num_programs(0) - 1)
    def _():
        store_blocks(table_ref, total_ref, keep_ref, send_ref)


def run_gated(table, gate, nog, mixed, sums, more, aux, gain, gturned, nturned, full_inner):
    length, width = gate.shape
    model_dim = gturned.shape[0]
    blocks = length // TOKEN_BLOCK
    sds = jax.ShapeDtypeStruct
    tokens = pl.BlockSpec((TOKEN_BLOCK, width), lambda i, t: (i, 0))
    turned = pl.BlockSpec((model_dim, TOKEN_BLOCK), lambda i, t: (0, i))
    halves_spec = pl.BlockSpec((model_dim // 2, 2 * width), lambda i, t: (0, 0))
    return pl.pallas_call(
        partial(gated_kernel, full_inner=float(full_inner)),
        grid_spec=pltpu.PrefetchScalarGridSpec(
            num_scalar_prefetch=1,
            grid=(blocks,),
            in_specs=[
                tokens,
                tokens,
                tokens,
                pl.BlockSpec((8, TOKEN_BLOCK), lambda i, t: (0, i)),
                pl.BlockSpec((8, TOKEN_BLOCK), lambda i, t: (0, i)),
                pl.BlockSpec((TOKEN_BLOCK, aux.shape[1]), lambda i, t: (i, 0)),
                pl.BlockSpec((1, width), lambda i, t: (0, 0)),
                turned,
                turned,
            ],
            out_specs=[
                tokens,
                tokens,
                tokens,
                pl.BlockSpec((8, width), lambda i, t: (0, 0)),
                halves_spec,
                halves_spec,
            ],
            scratch_shapes=[pltpu.VMEM((model_dim, 2 * width), f32)],
        ),
        out_shape=(
            sds((length, width), bf16),
            sds((length, width), bf16),
            sds((length, width), bf16),
            sds((8, width), f32),
            sds((model_dim // 2, 2 * width), f32),
            sds((model_dim // 2, 2 * width), bf16),
        ),
        name="gated_grad",
        cost_estimate=cost(12),
    )(table, gate, nog, mixed, sums, more, aux, gain, gturned, nturned)


def out_kernel(starts_ref, rows_ref, weights_ref, send_ref, keep_ref):
    step = pl.program_id(0)
    half = pl.num_programs(0) // 2
    rows = dot_nt(rows_ref[...], weights_ref[...]).astype(bf16)

    @pl.when(step < half)
    def _():
        send_ref[...] = rows

    @pl.when(step >= half)
    def _():
        keep_ref[...] = rows


def run_out(starts, rows, weights):
    length, width = rows.shape
    model_dim = weights.shape[0]
    blocks = length // TOKEN_BLOCK
    half = blocks // 2
    sds = jax.ShapeDtypeStruct
    return pl.pallas_call(
        out_kernel,
        grid_spec=pltpu.PrefetchScalarGridSpec(
            num_scalar_prefetch=1,
            grid=(blocks,),
            in_specs=[
                pl.BlockSpec((TOKEN_BLOCK, width), lambda i, s: (lax.rem(i + s[0], blocks), 0)),
                pl.BlockSpec((model_dim, width), lambda i, s: (0, 1)),
            ],
            out_specs=[
                pl.BlockSpec((TOKEN_BLOCK, model_dim), lambda i, s: (jnp.minimum(i, half - 1), 0)),
                pl.BlockSpec((TOKEN_BLOCK, model_dim), lambda i, s: (jnp.maximum(i - half, 0), 0)),
            ],
        ),
        out_shape=(
            sds((length // 2, model_dim), bf16),
            sds((length // 2, model_dim), bf16),
        ),
        name="out_project",
        cost_estimate=cost(4),
    )(starts, rows, weights)


def norm_grad_kernel(starts_ref, dgate_ref, dproj_ref, gates_ref, weights_ref, grad_ref):
    grad = dot_nt(dgate_ref[...], gates_ref[...]) + dot_nt(dproj_ref[...], weights_ref[...])
    grad_ref[...] = grad.astype(grad_ref.dtype)


def run_norm_grad(starts, dgate, dproj, gates, weights, kind):
    length, columns = dproj.shape
    width = dgate.shape[1]
    model_dim = weights.shape[0]
    blocks = length // TOKEN_BLOCK // 2
    return pl.pallas_call(
        norm_grad_kernel,
        grid_spec=pltpu.PrefetchScalarGridSpec(
            num_scalar_prefetch=1,
            grid=(blocks,),
            in_specs=[
                pl.BlockSpec((TOKEN_BLOCK, width), lambda i, s: (i + s[0], 0)),
                pl.BlockSpec((TOKEN_BLOCK, columns), lambda i, s: (i + s[0], 0)),
                pl.BlockSpec((model_dim, width), lambda i, s: (0, 0)),
                pl.BlockSpec((model_dim, columns), lambda i, s: (0, 0)),
            ],
            out_specs=pl.BlockSpec((TOKEN_BLOCK, model_dim), lambda i, s: (i, 0)),
        ),
        out_shape=jax.ShapeDtypeStruct((length // 2, model_dim), kind),
        name="normed_grad",
        cost_estimate=cost(5),
    )(starts, dgate, dproj, gates, weights)


def weight_grad_kernel(
    table_ref, turned_ref, dproj_ref, small_ref, keep_ref, send_ref, total_ref
):
    total_ref[...] = dot_nn(turned_ref[...], dproj_ref[...])
    half = keep_ref.shape[0] - 8
    store_blocks(table_ref, total_ref, keep_ref, send_ref)
    keep_ref[half:, :] = small_ref[...]
    send_ref[half:, :] = small_ref[...].astype(bf16)


def run_weight_grad(table, turned, dproj, small):
    model_dim, length = turned.shape
    columns = dproj.shape[1]
    tile = 3 * LANES if columns % (3 * LANES) == 0 else LANES
    held = model_dim // 2 + 8
    sds = jax.ShapeDtypeStruct
    return pl.pallas_call(
        weight_grad_kernel,
        grid_spec=pltpu.PrefetchScalarGridSpec(
            num_scalar_prefetch=1,
            grid=(columns // tile,),
            in_specs=[
                pl.BlockSpec((model_dim, length), lambda i, t: (0, 0)),
                pl.BlockSpec((length, tile), lambda i, t: (0, i)),
                pl.BlockSpec((8, tile), lambda i, t: (0, i)),
            ],
            out_specs=[
                pl.BlockSpec((held, tile), lambda i, t: (0, i)),
                pl.BlockSpec((held, tile), lambda i, t: (0, i)),
            ],
            scratch_shapes=[pltpu.VMEM((model_dim, tile), f32)],
        ),
        out_shape=(sds((held, columns), f32), sds((held, columns), bf16)),
        name="weight_grad",
        cost_estimate=cost(6),
    )(table, turned, dproj, small)


def after(value, *others):
    return lax.optimization_barrier((value,) + others)[0]


def cost(microseconds):
    return pl.CostEstimate(flops=int(microseconds * 1.1e9), transcendentals=0, bytes_accessed=0)


def pad_to(values, axis, size):
    pads = [(0, 0)] * values.ndim
    pads[axis] = (0, size - values.shape[axis])
    return jnp.pad(values, pads)


def body(
    hidden_in,
    segment_ids,
    norm_gain,
    proj_inner,
    proj_shared,
    proj_step,
    conv_inner,
    conv_shared,
    step_bias,
    log_decay,
    skip_gain,
    gate_gain,
    proj_out,
    out_grad,
):
    dp_count = lax.axis_size("dp")
    dp_index = lax.axis_index("dp")
    rows = proj_inner.shape[0]
    length = segment_ids.shape[0]
    model_dim = hidden_in.shape[1]
    local_inner = proj_inner.shape[2]
    heads = proj_step.shape[1]
    state_size = proj_shared.shape[2]
    kernel_len = conv_inner.shape[0]
    shared_size = 2 * state_size
    full_inner = local_inner * lax.axis_size("tensor")
    width = -(-local_inner // (2 * LANES)) * 2 * LANES
    tap_block = conv_shared.shape[2]
    tap_count = kernel_len * 2 * tap_block
    stages, core, table = block_plan()
    groups, core_table = core_groups()
    blocks = length // TOKEN_BLOCK
    starts = token_starts(blocks)
    two = lax.axis_size("tensor") == 2

    chips = dp_count // 2
    hidden_own, hidden_other = both_halves(hidden_in)
    tap_rows = conv_shared.transpose(1, 2, 0).reshape(2 * tap_block, kernel_len)
    tap_rows = pad_to(tap_rows, 0, rows)
    packed = jnp.concatenate(
        [
            pad_to(proj_inner[:, 1, :], 1, width),
            proj_shared.reshape(rows, shared_size),
            pad_to(jnp.concatenate([proj_step, norm_gain[:, None], tap_rows], axis=1), 1, LANES),
        ],
        axis=1,
    )
    later = jnp.concatenate(
        [pad_to(proj_inner[:, 0, :], 1, width), pad_to(proj_out.T, 1, width)], axis=1
    )
    at = jnp.arange(model_dim)
    block, inside = at // rows, at % rows
    side, spot = inside // tap_block, inside % tap_block
    spread = jnp.where(side < 2, side * state_size + block * tap_block + spot, -1)
    spread = (spread[:, None] == jnp.arange(shared_size)[None, :]).astype(bf16)
    aux, segr = token_facts(segment_ids)
    heads_block = jnp.stack([step_bias, log_decay, skip_gain])
    heads_block = pad_to(pad_to(heads_block, 1, LANES), 0, 8)
    tapi = pad_to(conv_inner, 1, width)
    gain = pad_to(gate_gain[None], 1, width)

    low = packed
    for number, stage in enumerate(stages):
        got = lax.ppermute(low, "dp", stage)
        if number == 0:
            got, aux, segr = lax.optimization_barrier((got, aux, segr))
        if number == 1:
            got, heads_block, tapi, spread, table, core_table = lax.optimization_barrier(
                (got, heads_block, tapi, spread, table, core_table)
            )
        if number == len(stages) - 1:
            later_all = jnp.broadcast_to(later[None], (chips,) + later.shape)
            later_all = later_all.reshape(chips * rows, 2 * width)
            got, later_all, gain = lax.optimization_barrier((got, later_all, gain))
        low = jnp.concatenate([low, got], axis=0)
    low, later_all, hidden_other = lax.optimization_barrier((low, later_all, hidden_other))
    high = lax.ppermute(low, "dp", core)
    later_low = exchange(later_all, groups)
    grad_own, grad_other = both_halves(after(out_grad, hidden_other))

    proj, praw, normed, normed_t, weights, taps, norm_scale = run_project(
        starts, table, hidden_own, hidden_other, spread, low, high, heads
    )
    norm_scale = norm_scale[:1]
    mixed, u, su, entry = run_forward(proj, praw, tapi, taps, heads_block, aux, segr)

    later_low, mixed, grad_other = lax.optimization_barrier((later_low, mixed, grad_other))
    later_high = lax.ppermute(later_low, "dp", core)
    gate, nog, grad_t, sums, later_rows = run_out_grad(
        starts, core_table, grad_own, grad_other, later_low, later_high, normed, mixed, gain
    )
    if two:
        more = swap(sums)
    else:
        sums = lax.psum(sums, "tensor")
        more = jnp.zeros_like(sums)
    normed_out, dgate, mixed_grad, gain_rows, gkeep, gsend = run_gated(
        core_table, gate, nog, mixed, sums, more, aux, gain, grad_t, normed_t, full_inner
    )
    ggot = lax.ppermute(gsend, "dp", core)
    send_start = starts[1:] if two else jnp.zeros((1,), jnp.int32)
    keep_start = starts[:1] if two else jnp.full((1,), blocks // 2, jnp.int32)
    out_send, out_keep = run_out(send_start, normed_out, later_rows)
    ggot, out_send = lax.optimization_barrier((ggot, out_send))
    gsum = exchange((gkeep + ggot.astype(f32)).astype(bf16), groups)
    out_other = swap(out_send) if two else None

    dproj, small = run_backward(
        proj, praw, u, su, entry, mixed_grad, tapi, taps, heads_block, aux, segr, gain_rows
    )
    dproj, gsum = lax.optimization_barrier((dproj, gsum))
    wkeep, wsend = run_weight_grad(core_table, normed_t, dproj, small)
    wgot = lax.ppermute(wsend, "dp", core)
    grad_send = run_norm_grad(send_start, dgate, dproj, later_rows, weights, bf16)
    wgot, grad_send = lax.optimization_barrier((wgot, grad_send))
    held = rows * chips
    wtotal = (wkeep + wgot.astype(f32)).astype(bf16)
    wtotal = jnp.concatenate(
        [
            wtotal[:held].reshape(chips, rows, -1),
            jnp.broadcast_to(wtotal[None, held:], (chips, 8, wtotal.shape[1])),
        ],
        axis=1,
    ).reshape(chips * (rows + 8), -1)
    wtotal, dproj, gsum, out_keep = lax.optimization_barrier((wtotal, dproj, gsum, out_keep))
    wsum = exchange(wtotal, groups)
    grad_keep = run_norm_grad(keep_start, dgate, dproj, later_rows, weights, f32)
    if two:
        out_half = out_keep.astype(f32) + out_other.astype(f32)
        own_grad = grad_keep + swap(grad_send).astype(f32)
    else:
        out_half = add_halves(out_send, out_keep)
        own_grad = add_halves(grad_send, grad_keep)
    hidden_out = (hidden_in.astype(f32) + out_half).astype(bf16)
    gsum = sum_blocks(gsum, rows)
    out_sum = gsum[:, width : width + local_inner].T
    gate_sum = gsum[:, :local_inner]

    wsum = sum_blocks(wsum, rows + 8)
    small = wsum[rows:]
    wsum = wsum[:rows]
    conv_total = small[:kernel_len, :local_inner]
    gain_total = small[4, :local_inner]
    skip_total = small[0, width + shared_size : width + shared_size + heads]
    bias_total = small[1, width + shared_size : width + shared_size + heads]
    decay_total = small[2, width + shared_size : width + shared_size + heads]
    norm_row = jnp.sum(gate_sum * proj_inner[:, 0, :].astype(f32), axis=1) + jnp.sum(
        wsum * packed.astype(f32) * (jnp.arange(packed.shape[1]) < width + shared_size + heads),
        axis=1,
    )
    final = jnp.concatenate(
        [
            wsum[:, width : width + shared_size],
            small[:kernel_len, width : width + shared_size],
            pad_to(norm_row[None], 1, shared_size),
        ],
        axis=0,
    )
    final = total_over_tensor(pad_to(final, 0, rows + 8))
    shared_total = final[:rows].reshape(rows, 2, state_size)
    taps_total = lax.dynamic_slice_in_dim(
        final[rows : rows + kernel_len].reshape(kernel_len, 2, state_size),
        dp_index * tap_block,
        tap_block,
        axis=2,
    )
    norm_total = final[rows + kernel_len, :rows] / norm_gain.astype(f32)
    inner_sum = jnp.stack([gate_sum, wsum[:, :local_inner]], axis=1)
    step_sum = wsum[:, width + shared_size : width + shared_size + heads]

    own = hidden_in.astype(f32)
    own_inv = lax.rsqrt(jnp.mean(own * own, axis=-1, keepdims=True) + epsilon)
    own_unit = own * own_inv
    scaled_in = own_grad * norm_scale
    hidden_grad = own_inv * (
        scaled_in - own_unit * jnp.mean(scaled_in * own_unit, axis=-1, keepdims=True)
    ) + out_grad.astype(f32)
    return (
        hidden_out,
        hidden_grad,
        norm_total,
        inner_sum,
        shared_total,
        step_sum,
        conv_total,
        taps_total,
        bias_total,
        decay_total,
        skip_total,
        gain_total,
        out_sum,
    )


def solution(mesh):
    in_specs = (
        P(("dp", "tensor"), None),
        P("dp"),
        P("dp"),
        P("dp", None, "tensor"),
        P("dp", None, None),
        P("dp", "tensor"),
        P(None, "tensor"),
        P(None, None, "dp"),
        P("tensor"),
        P("tensor"),
        P("tensor"),
        P("tensor"),
        P("tensor", "dp"),
        P(("dp", "tensor"), None),
    )
    out_specs = (
        P(("dp", "tensor"), None),
        P(("dp", "tensor"), None),
        P("dp"),
        P("dp", None, "tensor"),
        P("dp", None, None),
        P("dp", "tensor"),
        P(None, "tensor"),
        P(None, None, "dp"),
        P("tensor"),
        P("tensor"),
        P("tensor"),
        P("tensor"),
        P("tensor", "dp"),
    )
    return jax.shard_map(body, mesh=mesh, in_specs=in_specs, out_specs=out_specs, check_vma=False)
```

```python
from functools import partial

import jax
import jax.numpy as jnp
import numpy as np
from jax import lax
from jax.experimental import pallas as pl
from jax.experimental.pallas import tpu as pltpu
from jax.sharding import PartitionSpec as P

HEAD_DIM = 64
CHUNK = 128
LANES = 128
TOKEN_BLOCK = 256
VMEM_BASE = 16
epsilon = 1e-05
f32 = jnp.float32
bf16 = jnp.bfloat16
highest = lax.Precision.HIGHEST


def dot_nn(a, b):
    return lax.dot_general(a, b, (((1,), (0,)), ((), ())), preferred_element_type=f32)


def dot_nt(a, b):
    return lax.dot_general(a, b, (((1,), (1,)), ((), ())), preferred_element_type=f32)


def dot_tn(a, b):
    return lax.dot_general(a, b, (((0,), (0,)), ((), ())), preferred_element_type=f32)


def dot_exact(a, b):
    return lax.dot_general(
        a, b, (((1,), (0,)), ((), ())), preferred_element_type=f32, precision=highest
    )


def dot_split(a, b):
    high = a.astype(bf16)
    rest = (a - high.astype(f32)).astype(bf16)
    return dot_nn(high, b) + dot_nn(rest, b)


def sigmoid(v):
    return 1.0 / (1.0 + jnp.exp(-v))


def softplus(v):
    return jnp.maximum(v, 0.0) + jnp.log1p(jnp.exp(-jnp.abs(v)))


def halves(lane_low, values, head):
    return jnp.where(lane_low, values[:, head : head + 1], values[:, head + 1 : head + 2])


def back_shift(window, offset):
    return pltpu.roll(window, offset, 0)[8:, :]


def ahead_shift(window, offset):
    rows = window.shape[0]
    return pltpu.roll(window, rows - offset, 0)[: rows - 8, :]


def conv_rows(window, taps, aux):
    total = taps[3:4, :] * window[8:, :]
    for offset in range(1, 4):
        total = total + taps[3 - offset : 4 - offset, :] * (
            back_shift(window, offset) * aux[:, offset : offset + 1]
        )
    return total


def forward_kernel(
    proj_ref,
    step_ref,
    tapi_ref,
    taps_ref,
    heads_ref,
    aux_ref,
    segr_ref,
    mixed_ref,
    u_ref,
    su_ref,
    entry_ref,
    state_ref,
    carry_ref,
    scarry_ref,
    xw_ref,
):
    width = mixed_ref.shape[1]
    pairs = width // LANES
    shared_size = su_ref.shape[1]
    state_size = shared_size // 2
    chunk = pl.program_id(0)

    @pl.when(chunk == 0)
    def _():
        for ref in (state_ref, carry_ref, scarry_ref):
            ref[...] = jnp.zeros_like(ref)

    rows = lax.broadcasted_iota(jnp.int32, (CHUNK, CHUNK), 0)
    cols = lax.broadcasted_iota(jnp.int32, (CHUNK, CHUNK), 1)
    lower = rows >= cols
    summing = lower.astype(f32)
    lane_low = lax.broadcasted_iota(jnp.int32, (CHUNK, LANES), 1) < HEAD_DIM
    bias = heads_ref[0:1, :]
    rate = -jnp.exp(heads_ref[1:2, :])
    skips = heads_ref[2:3, :]
    aux = aux_ref[...]
    live = aux[:, 7:8]
    same = lower & (aux[:, 0:1] == segr_ref[pl.ds(chunk, 1), :])
    shared_now = proj_ref[:, width:].astype(f32)
    su = conv_rows(jnp.concatenate([scarry_ref[...], shared_now], axis=0), taps_ref[...], aux)
    scarry_ref[...] = shared_now[CHUNK - 8 :, :]
    su_ref[...] = su
    shared = (su * sigmoid(su)).astype(bf16)
    b_rows = shared[:, :state_size]
    c_rows = shared[:, state_size:]
    scores = jnp.where(same, dot_nt(c_rows, b_rows), 0.0)
    step = softplus(step_ref[...] + bias) * live
    decay = dot_exact(summing, step * rate)
    decay_t = decay.T
    last = decay[CHUNK - 1 :, :]
    entry_scale = jnp.exp(decay) * aux[:, 8:9]
    end_scale = jnp.exp(last - decay) * aux[:, 9:10]
    keep = jnp.exp(last) * aux[:1, 10:11]
    state = state_ref[...]
    state_low = state.astype(bf16)
    entry_ref[...] = state_low[None]
    past = dot_nn(c_rows, state_low)
    for pair in range(pairs):
        lanes = slice(pair * LANES, (pair + 1) * LANES)
        head = 2 * pair
        now = proj_ref[:, lanes].astype(f32)
        window = jnp.concatenate([carry_ref[:, lanes], now], axis=0)
        carry_ref[:, lanes] = now[CHUNK - 8 :, :]
        u = conv_rows(window, tapi_ref[:, lanes].astype(f32), aux)
        u_ref[:, lanes] = u.astype(bf16)
        x = u * sigmoid(u)
        scaled = x * halves(lane_low, step, head)
        mixing = jnp.concatenate(
            [
                (
                    scores
                    * jnp.exp(jnp.minimum(decay[:, h : h + 1] - decay_t[h : h + 1, :], 0.0))
                ).astype(bf16)
                for h in (head, head + 1)
            ],
            axis=1,
        )
        stacked = jnp.concatenate(
            [jnp.where(lane_low, scaled, 0.0), jnp.where(lane_low, 0.0, scaled)], axis=0
        ).astype(bf16)
        inside = dot_nn(mixing, stacked)
        xw_ref[:, lanes] = (scaled * halves(lane_low, end_scale, head)).astype(bf16)
        mixed = (
            inside
            + past[:, lanes] * halves(lane_low, entry_scale, head)
            + halves(lane_low[:1], skips, head) * x
        ) * live
        mixed_ref[:, lanes] = mixed.astype(bf16)
        state_ref[:, lanes] = state[:, lanes] * halves(lane_low[:1], keep, head)
    state_ref[...] += dot_tn(b_rows, xw_ref[...])


def token_scales(sums, full_inner):
    columns = sums.T
    inv = lax.rsqrt(columns[:, 0:1] / full_inner + epsilon)
    return inv, inv * columns[:, 1:2] / full_inner


def silu_slope(v, s):
    return s * (1.0 + v * (1.0 - s))


def backward_kernel(
    table_ref,
    proj_ref,
    praw_ref,
    u_ref,
    su_ref,
    entry_ref,
    grad_ref,
    tapi_ref,
    taps_ref,
    heads_ref,
    aux_ref,
    segr_ref,
    gain_ref,
    turned_ref,
    dproj_ref,
    keep_ref,
    send_ref,
    wide_ref,
    shared_ref,
    small_ref,
    total_ref,
    grads_ref,
    held_ref,
    sem_ref,
    state_ref,
    ahead_ref,
    sahead_ref,
    xw_ref,
    ge_ref,
    row_ref,
    proda_ref,
    prodb_ref,
):
    width = u_ref.shape[1]
    chunks = pl.num_programs(0)
    pairs = width // LANES
    shared_size = su_ref.shape[1]
    state_size = shared_size // 2
    shared_cols = slice(width, width + shared_size)
    step_cols = slice(width + shared_size, width + shared_size + LANES)
    chunk = chunks - 1 - pl.program_id(0)
    copy = pltpu.make_async_copy(turned_ref, held_ref, sem_ref.at[0])

    @pl.when(pl.program_id(0) == 0)
    def _():
        copy.start()
        for ref in (state_ref, ahead_ref, sahead_ref, row_ref, wide_ref, shared_ref):
            ref[...] = jnp.zeros_like(ref)

    rows = lax.broadcasted_iota(jnp.int32, (CHUNK, CHUNK), 0)
    cols = lax.broadcasted_iota(jnp.int32, (CHUNK, CHUNK), 1)
    upper = rows <= cols
    summing = (rows >= cols).astype(f32)
    unsumming = upper.astype(f32)
    last_row = (lax.broadcasted_iota(jnp.int32, (CHUNK, LANES), 0) == CHUNK - 1).astype(f32)
    lane_ids = lax.broadcasted_iota(jnp.int32, (CHUNK, LANES), 1)
    lane_low = lane_ids < HEAD_DIM
    bias = heads_ref[0:1, :]
    rate = -jnp.exp(heads_ref[1:2, :])
    skips = heads_ref[2:3, :]
    place = (
        lax.broadcasted_iota(jnp.int32, (width, LANES), 0) // HEAD_DIM
        == lax.broadcasted_iota(jnp.int32, (width, LANES), 1)
    ).astype(bf16)

    aux = aux_ref[...]
    live = aux[:, 7:8]
    same = upper & (aux[:, 0:1] == segr_ref[pl.ds(chunk, 1), :])
    su = su_ref[...]
    su_sig = sigmoid(su)
    shared = (su * su_sig).astype(bf16)
    b_rows = shared[:, :state_size]
    c_rows = shared[:, state_size:]
    scores = jnp.where(same, dot_nt(b_rows, c_rows), 0.0)
    pre = praw_ref[...] + bias
    step = softplus(pre) * live
    decay = dot_exact(summing, step * rate)
    decay_t = decay.T
    last = decay[CHUNK - 1 :, :]
    entry_scale = jnp.exp(decay) * aux[:, 8:9]
    end_scale = jnp.exp(last - decay) * aux[:, 9:10]
    keep = jnp.exp(last) * aux[:1, 10:11]
    entry = entry_ref[0]
    dstate = state_ref[...]
    dstate_low = dstate.astype(bf16)
    past = dot_nn(c_rows, entry)
    bds = dot_nn(b_rows, dstate_low)
    here = pl.ds(pl.multiple_of(chunk * CHUNK, CHUNK), CHUNK)
    score_grad = jnp.zeros((CHUNK, CHUNK), f32)
    col_part = jnp.zeros((CHUNK, LANES), f32)
    for pair in range(pairs):
        lanes = slice(pair * LANES, (pair + 1) * LANES)
        head = 2 * pair
        g_low = grad_ref[:, lanes]
        g = g_low.astype(f32)
        u = u_ref[:, lanes].astype(f32)
        u_sig = sigmoid(u)
        x = u * u_sig
        step_c = halves(lane_low, step, head)
        scaled = x * step_c
        stacked = jnp.concatenate(
            [jnp.where(lane_low, scaled, 0.0), jnp.where(lane_low, 0.0, scaled)], axis=0
        ).astype(bf16)
        dmix = dot_nt(stacked, g_low)
        mixing = []
        for k, h in enumerate((head, head + 1)):
            decays = jnp.exp(jnp.minimum(decay_t[h : h + 1, :] - decay[:, h : h + 1], 0.0))
            dmix_h = dmix[k * CHUNK : (k + 1) * CHUNK, :]
            score_grad = score_grad + dmix_h * decays
            mixing_h = scores * decays
            mixing.append(mixing_h.astype(bf16))
            both = mixing_h * dmix_h
            col_part = jnp.where(lane_ids == h, jnp.sum(both, axis=1, keepdims=True), col_part)
            row_ref[h : h + 1, :] = jnp.sum(both, axis=0, keepdims=True)
        g_stacked = jnp.concatenate(
            [jnp.where(lane_low, g, 0.0), jnp.where(lane_low, 0.0, g)], axis=0
        ).astype(bf16)
        end_c = halves(lane_low, end_scale, head)
        entry_c = halves(lane_low, entry_scale, head)
        keep_c = halves(lane_low[:1], keep, head)
        from_state = end_c * bds[:, lanes]
        dscaled = dot_nn(jnp.concatenate(mixing, axis=1), g_stacked) + from_state
        xw_ref[:, lanes] = (scaled * end_c).astype(bf16)
        q = scaled * from_state
        ge = g * entry_c
        ge_ref[:, lanes] = ge.astype(bf16)
        dstate_p = dstate[:, lanes]
        tail = jnp.sum(q, axis=0, keepdims=True) + keep_c * jnp.sum(
            dstate_p * entry[:, lanes].astype(f32), axis=0, keepdims=True
        )
        proda_ref[:, lanes] = x * dscaled
        prodb_ref[:, lanes] = ge * past[:, lanes] - q + last_row * tail
        state_ref[:, lanes] = dstate_p * keep_c
        dx = step_c * dscaled + halves(lane_low[:1], skips, head) * g
        du = dx * silu_slope(u, u_sig)
        window = jnp.concatenate([du, ahead_ref[:, lanes]], axis=0)
        ahead_ref[:, lanes] = du[:8, :]
        cin = proj_ref[:, lanes].astype(f32)
        taps = tapi_ref[:, lanes].astype(f32)
        dcin = taps[3:4, :] * du
        wide_ref[3:4, lanes] += jnp.sum(cin * du, axis=0, keepdims=True)
        for offset in range(1, 4):
            moved = ahead_shift(window, offset) * aux[:, 3 + offset : 4 + offset]
            dcin = dcin + taps[3 - offset : 4 - offset, :] * moved
            wide_ref[3 - offset : 4 - offset, lanes] += jnp.sum(
                cin * moved, axis=0, keepdims=True
            )
        dcin = dcin.astype(bf16)
        dproj_ref[:, lanes] = dcin
        grads_ref[here, lanes] = dcin
        wide_ref[5:6, lanes] += jnp.sum(g * x, axis=0, keepdims=True)
    score_low = jnp.where(same, score_grad, 0.0).astype(bf16)
    ge_all = ge_ref[...]
    db = dot_nn(score_low, c_rows) + dot_nt(xw_ref[...], dstate_low)
    dc = dot_tn(score_low, b_rows) + dot_nt(ge_all, entry)
    state_ref[...] += dot_tn(c_rows, ge_all)
    ds = jnp.concatenate([db, dc], axis=1) * silu_slope(su, su_sig)
    window = jnp.concatenate([ds, sahead_ref[...]], axis=0)
    sahead_ref[...] = ds[:8, :]
    taps = taps_ref[...]
    sin = proj_ref[:, shared_cols].astype(f32)
    dsin = taps[3:4, :] * ds
    shared_ref[3:4, :] += jnp.sum(sin * ds, axis=0, keepdims=True)
    for offset in range(1, 4):
        moved = ahead_shift(window, offset) * aux[:, 3 + offset : 4 + offset]
        dsin = dsin + taps[3 - offset : 4 - offset, :] * moved
        shared_ref[3 - offset : 4 - offset, :] += jnp.sum(sin * moved, axis=0, keepdims=True)
    dsin = dsin.astype(bf16)
    dproj_ref[:, shared_cols] = dsin
    grads_ref[here, shared_cols] = dsin
    ddecay = row_ref[...].T - col_part + dot_split(prodb_ref[...], place)
    dlog = dot_exact(unsumming, ddecay)
    dstep = (dot_split(proda_ref[...], place) + rate * dlog) * live * sigmoid(pre)
    dproj_ref[:, step_cols] = dstep.astype(bf16)
    grads_ref[here, step_cols] = dstep.astype(bf16)
    wide_ref[6:7, :LANES] += jnp.sum(dstep, axis=0, keepdims=True)
    wide_ref[6:7, LANES : 2 * LANES] += jnp.sum(step * dlog, axis=0, keepdims=True) * rate

    @pl.when(chunk == 0)
    def _():
        small_ref[...] = jnp.zeros_like(small_ref)
        small_ref[:4, :width] = wide_ref[:4, :]
        small_ref[:4, width : width + shared_size] = shared_ref[:4, :]
        skip_row = dot_split(wide_ref[...], place)[5:6, :]
        small_ref[0:1, step_cols] = skip_row
        small_ref[1:2, step_cols] = wide_ref[6:7, :LANES]
        small_ref[2:3, step_cols] = wide_ref[6:7, LANES : 2 * LANES]
        small_ref[4:5, :width] = jnp.sum(gain_ref[...], axis=0, keepdims=True)
        copy.wait()
        held = keep_ref.shape[0] - 8
        keep_ref[held:, :] = small_ref[...].astype(bf16)
        send_ref[held:, :] = small_ref[...].astype(bf16)
        tile = total_ref.shape[1]
        for at in range(0, width + shared_size + LANES, tile):
            total_ref[...] = dot_nn(held_ref[...], grads_ref[:, at : at + tile])
            store_blocks(table_ref, total_ref, keep_ref, send_ref, slice(at, at + tile))


def facts_kernel(seg_ref, aux_ref, segr_ref):
    seg = seg_ref[...].astype(f32)
    chunks = seg.shape[0]
    segr_ref[...] = seg
    none = jnp.full((1, CHUNK), -1.0, f32)
    before = jnp.concatenate([none, seg[: chunks - 1]], axis=0) if chunks > 1 else none
    behind = jnp.concatenate([seg[1:], none], axis=0) if chunks > 1 else none
    lane = lax.broadcasted_iota(jnp.int32, seg.shape, 1)
    facts = [seg]
    for offset in range(1, 4):
        earlier = jnp.where(
            lane >= offset, pltpu.roll(seg, offset, 1), pltpu.roll(before, offset, 1)
        )
        facts.append((earlier == seg).astype(f32))
    for offset in range(1, 4):
        later = jnp.where(
            lane < CHUNK - offset,
            pltpu.roll(seg, CHUNK - offset, 1),
            pltpu.roll(behind, CHUNK - offset, 1),
        )
        facts.append((later == seg).astype(f32))
    last = jnp.broadcast_to(seg[:, CHUNK - 1 :], seg.shape)
    prior = jnp.broadcast_to(before[:, CHUNK - 1 :], seg.shape)
    facts.append((seg != 0.0).astype(f32))
    facts.append((seg == prior).astype(f32))
    facts.append((seg == last).astype(f32))
    facts.append((last == prior).astype(f32))
    empty = jnp.zeros((LANES - len(facts), CHUNK), f32)
    for chunk in range(chunks):
        rows = jnp.concatenate([f[chunk : chunk + 1, :] for f in facts] + [empty], axis=0)
        aux_ref[chunk * CHUNK : (chunk + 1) * CHUNK, :] = rows.T[:, : aux_ref.shape[1]]


def token_facts(segments):
    length = segments.shape[0]
    chunks = length // CHUNK
    return pl.pallas_call(
        facts_kernel,
        out_shape=(
            jax.ShapeDtypeStruct((length, 16), f32),
            jax.ShapeDtypeStruct((chunks, CHUNK), f32),
        ),
        name="token_facts",
        cost_estimate=cost(2),
        compiler_params=vmem_limit(length),
    )(segments.reshape(chunks, CHUNK))


def chunk_spec(columns, last):
    if last is None:
        return pl.BlockSpec((CHUNK, columns), lambda i: (i, 0))
    return pl.BlockSpec((CHUNK, columns), lambda i: (last - i, 0))


def fixed_spec(values):
    zeros = (0,) * values.ndim
    return pl.BlockSpec(values.shape, lambda i: zeros)


def run_forward(proj, praw, tapi, taps, heads, aux, segr):
    length = proj.shape[0]
    width = tapi.shape[1]
    shared_size = taps.shape[1]
    state_size = shared_size // 2
    chunks = length // CHUNK
    proj, praw = from_store(proj, praw)
    return pl.pallas_call(
        forward_kernel,
        grid=(chunks,),
        in_specs=[
            chunk_spec(proj.shape[1], None),
            chunk_spec(LANES, None),
            fixed_spec(tapi),
            fixed_spec(taps),
            fixed_spec(heads),
            chunk_spec(aux.shape[1], None),
            fixed_spec(segr),
        ],
        out_specs=[
            chunk_spec(width, None),
            chunk_spec(width, None),
            chunk_spec(shared_size, None),
            pl.BlockSpec((1, state_size, width), lambda i: (i, 0, 0)),
        ],
        out_shape=(
            stored((length, width), bf16),
            stored((length, width), bf16),
            stored((length, shared_size), f32),
            stored((chunks, state_size, width), bf16),
        ),
        scratch_shapes=[
            pltpu.VMEM((state_size, width), f32),
            pltpu.VMEM((8, width), f32),
            pltpu.VMEM((8, shared_size), f32),
            pltpu.VMEM((CHUNK, width), bf16),
        ],
        name="scan_forward",
        cost_estimate=cost(18),
        compiler_params=vmem_limit(length),
    )(proj, praw, tapi, taps, heads, aux, segr)


def run_backward(
    table, proj, praw, u, su, entry, grad, tapi, taps, heads, aux, segr, gain_rows, turned
):
    length, width = u.shape
    shared_size = su.shape[1]
    state_size = shared_size // 2
    model_dim = turned.shape[0]
    chunks = length // CHUNK
    last = chunks - 1
    columns = width + shared_size + LANES
    kept = model_dim // 2 + 8
    sds = jax.ShapeDtypeStruct
    proj, praw, u, su, entry, grad, turned = from_store(proj, praw, u, su, entry, grad, turned)

    def back(size):
        return pl.BlockSpec((CHUNK, size), lambda i, t: (last - i, 0))

    def fixed(shape):
        return pl.BlockSpec(shape, lambda i, t: (0, 0))

    return pl.pallas_call(
        backward_kernel,
        grid_spec=pltpu.PrefetchScalarGridSpec(
            num_scalar_prefetch=1,
            grid=(chunks,),
            in_specs=[
                back(proj.shape[1]),
                back(LANES),
                back(width),
                back(shared_size),
                pl.BlockSpec((1, state_size, width), lambda i, t: (last - i, 0, 0)),
                back(width),
                fixed(tapi.shape),
                fixed(taps.shape),
                fixed(heads.shape),
                back(aux.shape[1]),
                fixed(segr.shape),
                fixed(gain_rows.shape),
                pl.BlockSpec(memory_space=pl.ANY),
            ],
            out_specs=[
                back(columns),
                fixed((kept, columns)),
                fixed((kept, columns)),
            ],
            scratch_shapes=[
                pltpu.VMEM((8, width), f32),
                pltpu.VMEM((8, shared_size), f32),
                pltpu.VMEM((8, columns), f32),
                pltpu.VMEM((model_dim, column_tile(columns)), f32),
                pltpu.VMEM((length, columns), bf16),
                pltpu.VMEM((model_dim, length), bf16),
                pltpu.SemaphoreType.DMA((1,)),
                pltpu.VMEM((state_size, width), f32),
                pltpu.VMEM((8, width), f32),
                pltpu.VMEM((8, shared_size), f32),
                pltpu.VMEM((CHUNK, width), bf16),
                pltpu.VMEM((CHUNK, width), bf16),
                pltpu.VMEM((LANES, CHUNK), f32),
                pltpu.VMEM((CHUNK, width), f32),
                pltpu.VMEM((CHUNK, width), f32),
            ],
        ),
        out_shape=(
            stored((length, columns), bf16),
            stored((kept, columns), bf16),
            stored((kept, columns), bf16),
        ),
        name="scan_backward",
        cost_estimate=cost(36),
        compiler_params=vmem_limit(length),
    )(table, proj, praw, u, su, entry, grad, tapi, taps, heads, aux, segr, gain_rows, turned)


def block_plan():
    count = lax.axis_size("dp")
    bits = []
    bit = count // 2
    while bit > 1:
        bits.append(bit)
        bit //= 2
    mixed = bits[:-2] + bits[-2:][::-1]
    by_core = (bits, mixed)
    stages = []
    for stage in range(len(bits)):
        stages.append([(i, i ^ by_core[i % 2][stage]) for i in range(count)])
    core = [(i, i ^ 1) for i in range(count)]
    device = np.zeros((count, count), np.int32)
    for own in range(count):
        for spot in range(count):
            other = own ^ 1 if spot >= count // 2 else own
            for stage, bit in enumerate(by_core[other % 2]):
                if (spot >> stage) & 1:
                    other ^= bit
            device[own, spot] = other
    table = jnp.asarray(device)[lax.axis_index("dp")]
    return stages, core, table


def core_groups():
    count = lax.axis_size("dp")
    groups = [list(range(side, count, 2)) for side in range(2)]
    return groups, jnp.asarray(
        [groups[0] + groups[1], groups[1] + groups[0]], jnp.int32
    )[lax.axis_index("dp") % 2]


def exchange(blocks, groups):
    return lax.all_to_all(
        blocks, "dp", 0, 0, axis_index_groups=groups, tiled=True
    )


def sum_blocks(blocks, rows):
    return jnp.sum(blocks.reshape(-1, rows, blocks.shape[1]).astype(f32), axis=0)


def swap(values):
    return lax.ppermute(values, "tensor", [(0, 1), (1, 0)])


def total_over_tensor(values):
    if lax.axis_size("tensor") == 2:
        return values + swap(values)
    return lax.psum(values, "tensor")


def both_halves(own):
    if lax.axis_size("tensor") == 2:
        return own, swap(own)
    whole = lax.all_gather(own, "tensor", axis=0, tiled=True)
    return whole, whole


def token_starts(blocks):
    if lax.axis_size("tensor") == 2:
        index = lax.axis_index("tensor")
        return jnp.stack([index * (blocks // 2), (1 - index) * (blocks // 2)]).astype(jnp.int32)
    return jnp.zeros((2,), jnp.int32)


def add_halves(send, keep):
    if lax.axis_size("tensor") == 2:
        return keep.astype(f32) + swap(send).astype(f32)
    whole = jnp.concatenate([send.astype(bf16), keep.astype(bf16)], axis=0)
    return lax.psum_scatter(whole, "tensor", scatter_dimension=0, tiled=True).astype(f32)


def own_block(step, starts, own_blocks):
    return jnp.clip(step - starts[0], 0, own_blocks - 1)


def other_block(step, starts, own_blocks):
    return jnp.clip(step - starts[1], 0, own_blocks - 1)


def place_blocks(table_ref, low_ref, high_ref, whole_ref, sem_ref):
    count = table_ref.shape[0]
    rows = whole_ref.shape[0] // count
    copies = []
    for spot in range(count):
        source = low_ref if spot < count // 2 else high_ref
        where = pl.multiple_of(table_ref[spot] * rows, rows)
        copies.append(
            pltpu.make_async_copy(
                source.at[pl.ds((spot % (count // 2)) * rows, rows), :],
                whole_ref.at[pl.ds(where, rows), :],
                sem_ref.at[spot],
            )
        )
    for copy in copies:
        copy.start()
    for copy in copies:
        copy.wait()


def project_kernel(
    starts_ref,
    table_ref,
    own_ref,
    other_ref,
    spread_ref,
    low_ref,
    high_ref,
    proj_ref,
    step_ref,
    normed_ref,
    turned_ref,
    weights_ref,
    taps_ref,
    scale_ref,
    sem_ref,
    *,
    own_blocks,
    heads,
):
    step = pl.program_id(0)
    model_dim, columns = weights_ref.shape

    @pl.when(step == 0)
    def _():
        place_blocks(table_ref, low_ref, high_ref, weights_ref, sem_ref)
        extra = weights_ref[:, columns - LANES :].astype(f32).T
        scale_ref[...] = jnp.broadcast_to(extra[heads : heads + 1, :], scale_ref.shape)
        taps = extra[heads + 1 : heads + 5, :]
        taps = jnp.concatenate([taps, jnp.zeros_like(taps)], axis=0).astype(bf16)
        taps_ref[...] = dot_nn(taps, spread_ref[...])

    mine = (step >= starts_ref[0]) & (step < starts_ref[0] + own_blocks)
    tokens = jnp.where(mine, own_ref[...].astype(f32), other_ref[...].astype(f32))
    inv = lax.rsqrt(jnp.mean(tokens * tokens, axis=-1, keepdims=True) + epsilon)
    normed = (tokens * inv * scale_ref[:1, :]).astype(bf16)
    normed_ref[...] = normed
    turned_ref[...] = normed.T
    proj = dot_nn(normed, weights_ref[...])
    proj_ref[...] = proj[:, : columns - LANES].astype(bf16)
    step_ref[...] = proj[:, columns - LANES :]


def run_project(starts, table, own, other, spread, low, high, heads):
    own_rows, model_dim = own.shape
    columns = low.shape[1]
    own_blocks = own_rows // TOKEN_BLOCK
    blocks = own_blocks * (2 if lax.axis_size("tensor") == 2 else 1)
    length = blocks * TOKEN_BLOCK
    sds = jax.ShapeDtypeStruct
    own, other, low, high = from_store(own, other, low, high)
    return pl.pallas_call(
        partial(project_kernel, own_blocks=own_blocks, heads=heads),
        grid_spec=pltpu.PrefetchScalarGridSpec(
            num_scalar_prefetch=2,
            grid=(blocks,),
            in_specs=[
                pl.BlockSpec(
                    (TOKEN_BLOCK, model_dim), lambda i, s, t: (own_block(i, s, own_blocks), 0)
                ),
                pl.BlockSpec(
                    (TOKEN_BLOCK, model_dim), lambda i, s, t: (other_block(i, s, own_blocks), 0)
                ),
                pl.BlockSpec(spread.shape, lambda i, s, t: (0, 0)),
                pl.BlockSpec(memory_space=pl.ANY),
                pl.BlockSpec(memory_space=pl.ANY),
            ],
            out_specs=[
                pl.BlockSpec((TOKEN_BLOCK, columns - LANES), lambda i, s, t: (i, 0)),
                pl.BlockSpec((TOKEN_BLOCK, LANES), lambda i, s, t: (i, 0)),
                pl.BlockSpec((TOKEN_BLOCK, model_dim), lambda i, s, t: (i, 0)),
                pl.BlockSpec((model_dim, TOKEN_BLOCK), lambda i, s, t: (0, i)),
                pl.BlockSpec((model_dim, columns), lambda i, s, t: (0, 0)),
                pl.BlockSpec((8, spread.shape[1]), lambda i, s, t: (0, 0)),
                pl.BlockSpec((8, model_dim), lambda i, s, t: (0, 0)),
            ],
            scratch_shapes=[pltpu.SemaphoreType.DMA((table.shape[0],))],
        ),
        out_shape=(
            stored((length, columns - LANES), bf16),
            stored((length, LANES), f32),
            stored((length, model_dim), bf16),
            stored((model_dim, length), bf16),
            stored((model_dim, columns), bf16),
            sds((8, spread.shape[1]), f32),
            sds((8, model_dim), f32),
        ),
        name="norm_project",
        cost_estimate=cost(9),
        compiler_params=vmem_limit(length),
    )(starts, table, own, other, spread, low, high)


def token_sum(values):
    total = values[:, :LANES]
    for at in range(LANES, values.shape[1], LANES):
        total = total + values[:, at : at + LANES]
    return jnp.sum(total.T, axis=0, keepdims=True)


def out_grad_kernel(
    starts_ref,
    table_ref,
    own_ref,
    other_ref,
    low_ref,
    high_ref,
    normed_ref,
    mixed_ref,
    gain_ref,
    gate_ref,
    nog_ref,
    turned_ref,
    sums_ref,
    weights_ref,
    sem_ref,
    *,
    own_blocks,
):
    step = pl.program_id(0)
    width = mixed_ref.shape[1]

    @pl.when(step == 0)
    def _():
        place_blocks(table_ref, low_ref, high_ref, weights_ref, sem_ref)

    mine = (step >= starts_ref[0]) & (step < starts_ref[0] + own_blocks)
    tokens = jnp.where(mine, own_ref[...].astype(f32), other_ref[...].astype(f32)).astype(bf16)
    turned_ref[...] = tokens.T
    gate = dot_nn(normed_ref[...], weights_ref[:, :width])
    gate_ref[...] = gate.astype(bf16)
    nog = dot_nn(tokens, weights_ref[:, width:])
    nog_ref[...] = nog.astype(bf16)
    gated = mixed_ref[...].astype(f32) * (gate * sigmoid(gate))
    sums_ref[...] = jnp.concatenate(
        [
            token_sum(gated * gated),
            token_sum(nog * gain_ref[...].astype(f32) * gated),
            jnp.zeros((6, TOKEN_BLOCK), f32),
        ],
        axis=0,
    )


def run_out_grad(starts, table, own, other, low, high, normed, mixed, gain):
    own_rows, model_dim = own.shape
    length, width = mixed.shape
    own_blocks = own_rows // TOKEN_BLOCK
    blocks = length // TOKEN_BLOCK
    sds = jax.ShapeDtypeStruct
    own, other, normed, mixed = from_store(own, other, normed, mixed)
    return pl.pallas_call(
        partial(out_grad_kernel, own_blocks=own_blocks),
        grid_spec=pltpu.PrefetchScalarGridSpec(
            num_scalar_prefetch=2,
            grid=(blocks,),
            in_specs=[
                pl.BlockSpec(
                    (TOKEN_BLOCK, model_dim), lambda i, s, t: (own_block(i, s, own_blocks), 0)
                ),
                pl.BlockSpec(
                    (TOKEN_BLOCK, model_dim), lambda i, s, t: (other_block(i, s, own_blocks), 0)
                ),
                pl.BlockSpec(memory_space=pl.ANY),
                pl.BlockSpec(memory_space=pl.ANY),
                pl.BlockSpec((TOKEN_BLOCK, model_dim), lambda i, s, t: (i, 0)),
                pl.BlockSpec((TOKEN_BLOCK, width), lambda i, s, t: (i, 0)),
                pl.BlockSpec((1, width), lambda i, s, t: (0, 0)),
            ],
            out_specs=[
                pl.BlockSpec((TOKEN_BLOCK, width), lambda i, s, t: (i, 0)),
                pl.BlockSpec((TOKEN_BLOCK, width), lambda i, s, t: (i, 0)),
                pl.BlockSpec((model_dim, TOKEN_BLOCK), lambda i, s, t: (0, i)),
                pl.BlockSpec((8, TOKEN_BLOCK), lambda i, s, t: (0, i)),
                pl.BlockSpec((model_dim, 2 * width), lambda i, s, t: (0, 0)),
            ],
            scratch_shapes=[pltpu.SemaphoreType.DMA((table.shape[0],))],
        ),
        out_shape=(
            sds((length, width), bf16),
            sds((length, width), bf16),
            sds((model_dim, length), bf16),
            sds((8, length), f32),
            stored((model_dim, 2 * width), bf16),
        ),
        name="out_grad",
        cost_estimate=cost(9),
        compiler_params=vmem_limit(length),
    )(starts, table, own, other, low, high, normed, mixed, gain)


def column_tile(columns):
    return 3 * LANES if columns % (3 * LANES) == 0 else LANES


def store_blocks(table_ref, source_ref, keep_ref, send_ref, columns):
    count = table_ref.shape[0]
    rows = source_ref.shape[0] // count
    half = count // 2
    for spot in range(count):
        target = keep_ref if spot < half else send_ref
        at = (spot % half) * rows
        where = pl.multiple_of(table_ref[spot] * rows, rows)
        target[at : at + rows, columns] = source_ref[pl.ds(where, rows), :].astype(bf16)


def gated_kernel(
    table_ref,
    gate_ref,
    nog_ref,
    mixed_ref,
    sums_ref,
    more_ref,
    aux_ref,
    gain_ref,
    gturned_ref,
    nturned_ref,
    out_ref,
    dgate_ref,
    grad_ref,
    row_ref,
    keep_ref,
    send_ref,
    total_ref,
    both_ref,
    gheld_ref,
    nheld_ref,
    sem_ref,
    *,
    full_inner,
):
    step = pl.program_id(0)
    width = gate_ref.shape[1]
    tile = total_ref.shape[1]
    copies = [
        pltpu.make_async_copy(nturned_ref, nheld_ref, sem_ref.at[0]),
        pltpu.make_async_copy(gturned_ref, gheld_ref, sem_ref.at[1]),
    ]

    @pl.when(step == 0)
    def _():
        for copy in copies:
            copy.start()

    inv, mean = token_scales(sums_ref[...] + more_ref[...], full_inner)
    gain = gain_ref[...].astype(f32)
    here = pl.ds(pl.multiple_of(step * TOKEN_BLOCK, TOKEN_BLOCK), TOKEN_BLOCK)
    live = aux_ref[:, 7:8]
    for at in range(0, width, LANES):
        lanes = slice(at, at + LANES)
        gate = gate_ref[:, lanes].astype(f32)
        gate_sig = sigmoid(gate)
        gate_silu = gate * gate_sig
        mixed = mixed_ref[:, lanes].astype(f32)
        unit = mixed * gate_silu * inv
        nog = nog_ref[:, lanes].astype(f32)
        grad = inv * (nog * gain[:, lanes] - unit * mean)
        dgate = (grad * mixed * silu_slope(gate, gate_sig)).astype(bf16)
        dgate_ref[:, lanes] = dgate
        both_ref[here, lanes] = dgate
        grad_ref[:, lanes] = (grad * gate_silu * live).astype(bf16)
        normed_out = (unit * gain[:, lanes]).astype(bf16)
        out_ref[:, lanes] = normed_out
        both_ref[here, slice(width + at, width + at + LANES)] = normed_out
        row_ref[pl.ds(step * 8, 8), lanes] = jnp.sum((nog * unit).reshape(-1, 8, LANES), axis=0)

    @pl.when(step == pl.num_programs(0) - 1)
    def _():
        for copy in copies:
            copy.wait()
        for at in range(0, 2 * width, tile):
            turned = nheld_ref if at < width else gheld_ref
            total_ref[...] = dot_nn(turned[...], both_ref[:, at : at + tile])
            store_blocks(table_ref, total_ref, keep_ref, send_ref, slice(at, at + tile))


def run_gated(table, gate, nog, mixed, sums, more, aux, gain, gturned, nturned, full_inner):
    length, width = gate.shape
    model_dim = gturned.shape[0]
    blocks = length // TOKEN_BLOCK
    tile = column_tile(width)
    sds = jax.ShapeDtypeStruct
    mixed, nturned = from_store(mixed, nturned)
    tokens = pl.BlockSpec((TOKEN_BLOCK, width), lambda i, t: (i, 0))
    halves_spec = pl.BlockSpec((model_dim // 2, 2 * width), lambda i, t: (0, 0))
    return pl.pallas_call(
        partial(gated_kernel, full_inner=float(full_inner)),
        grid_spec=pltpu.PrefetchScalarGridSpec(
            num_scalar_prefetch=1,
            grid=(blocks,),
            in_specs=[
                tokens,
                tokens,
                tokens,
                pl.BlockSpec((8, TOKEN_BLOCK), lambda i, t: (0, i)),
                pl.BlockSpec((8, TOKEN_BLOCK), lambda i, t: (0, i)),
                pl.BlockSpec((TOKEN_BLOCK, aux.shape[1]), lambda i, t: (i, 0)),
                pl.BlockSpec((1, width), lambda i, t: (0, 0)),
                pl.BlockSpec(memory_space=pl.ANY),
                pl.BlockSpec(memory_space=pl.ANY),
            ],
            out_specs=[
                tokens,
                tokens,
                tokens,
                pl.BlockSpec((8 * blocks, width), lambda i, t: (0, 0)),
                halves_spec,
                halves_spec,
            ],
            scratch_shapes=[
                pltpu.VMEM((model_dim, tile), f32),
                pltpu.VMEM((length, 2 * width), bf16),
                pltpu.VMEM((model_dim, length), bf16),
                pltpu.VMEM((model_dim, length), bf16),
                pltpu.SemaphoreType.DMA((2,)),
            ],
        ),
        out_shape=(
            sds((length, width), bf16),
            stored((length, width), bf16),
            stored((length, width), bf16),
            sds((8 * blocks, width), f32),
            sds((model_dim // 2, 2 * width), bf16),
            sds((model_dim // 2, 2 * width), bf16),
        ),
        name="gated_grad",
        cost_estimate=cost(9),
        compiler_params=vmem_limit(length),
    )(table, gate, nog, mixed, sums, more, aux, gain, gturned, nturned)


def out_kernel(starts_ref, rows_ref, weights_ref, send_ref, keep_ref):
    step = pl.program_id(0)
    half = pl.num_programs(0) // 2
    rows = dot_nt(rows_ref[...], weights_ref[...]).astype(bf16)

    @pl.when(step < half)
    def _():
        send_ref[...] = rows

    @pl.when(step >= half)
    def _():
        keep_ref[...] = rows


def run_out(starts, rows, weights):
    length, width = rows.shape
    model_dim = weights.shape[0]
    blocks = length // TOKEN_BLOCK
    half = blocks // 2
    sds = jax.ShapeDtypeStruct
    (weights,) = from_store(weights)
    return pl.pallas_call(
        out_kernel,
        grid_spec=pltpu.PrefetchScalarGridSpec(
            num_scalar_prefetch=1,
            grid=(blocks,),
            in_specs=[
                pl.BlockSpec((TOKEN_BLOCK, width), lambda i, s: (lax.rem(i + s[0], blocks), 0)),
                pl.BlockSpec((model_dim, width), lambda i, s: (0, 1)),
            ],
            out_specs=[
                pl.BlockSpec((TOKEN_BLOCK, model_dim), lambda i, s: (jnp.minimum(i, half - 1), 0)),
                pl.BlockSpec((TOKEN_BLOCK, model_dim), lambda i, s: (jnp.maximum(i - half, 0), 0)),
            ],
        ),
        out_shape=(
            sds((length // 2, model_dim), bf16),
            sds((length // 2, model_dim), bf16),
        ),
        name="out_project",
        cost_estimate=cost(4),
        compiler_params=vmem_limit(length),
    )(starts, rows, weights)


def norm_grad_kernel(starts_ref, dgate_ref, dproj_ref, gates_ref, weights_ref, grad_ref):
    grad = dot_nt(dgate_ref[...], gates_ref[...]) + dot_nt(dproj_ref[...], weights_ref[...])
    grad_ref[...] = grad.astype(grad_ref.dtype)


def run_norm_grad(starts, dgate, dproj, gates, weights, kind):
    length, columns = dproj.shape
    width = dgate.shape[1]
    model_dim = weights.shape[0]
    blocks = length // TOKEN_BLOCK // 2
    dgate, dproj, gates, weights = from_store(dgate, dproj, gates, weights)
    return pl.pallas_call(
        norm_grad_kernel,
        grid_spec=pltpu.PrefetchScalarGridSpec(
            num_scalar_prefetch=1,
            grid=(blocks,),
            in_specs=[
                pl.BlockSpec((TOKEN_BLOCK, width), lambda i, s: (i + s[0], 0)),
                pl.BlockSpec((TOKEN_BLOCK, columns), lambda i, s: (i + s[0], 0)),
                pl.BlockSpec((model_dim, width), lambda i, s: (0, 0)),
                pl.BlockSpec((model_dim, columns), lambda i, s: (0, 0)),
            ],
            out_specs=pl.BlockSpec((TOKEN_BLOCK, model_dim), lambda i, s: (i, 0)),
        ),
        out_shape=jax.ShapeDtypeStruct((length // 2, model_dim), kind),
        name="normed_grad",
        cost_estimate=cost(5),
        compiler_params=vmem_limit(length),
    )(starts, dgate, dproj, gates, weights)


def after(value, *others):
    return lax.optimization_barrier((value,) + others)[0]


def cost(microseconds):
    return pl.CostEstimate(flops=int(microseconds * 1.1e9), transcendentals=0, bytes_accessed=0)


def stored(shape, kind):
    return pltpu.HBM(shape, kind)


def from_store(*values):
    return tuple(pltpu.with_memory_space_constraint(v, pltpu.HBM) for v in values)


def vmem_limit(length):
    return pltpu.CompilerParams(vmem_limit_bytes=min(60, VMEM_BASE + length // 128) << 20)


def pad_to(values, axis, size):
    pads = [(0, 0)] * values.ndim
    pads[axis] = (0, size - values.shape[axis])
    return jnp.pad(values, pads)


def body(
    hidden_in,
    segment_ids,
    norm_gain,
    proj_inner,
    proj_shared,
    proj_step,
    conv_inner,
    conv_shared,
    step_bias,
    log_decay,
    skip_gain,
    gate_gain,
    proj_out,
    out_grad,
):
    dp_count = lax.axis_size("dp")
    dp_index = lax.axis_index("dp")
    rows = proj_inner.shape[0]
    length = segment_ids.shape[0]
    model_dim = hidden_in.shape[1]
    local_inner = proj_inner.shape[2]
    heads = proj_step.shape[1]
    state_size = proj_shared.shape[2]
    kernel_len = conv_inner.shape[0]
    shared_size = 2 * state_size
    full_inner = local_inner * lax.axis_size("tensor")
    width = -(-local_inner // (2 * LANES)) * 2 * LANES
    tap_block = conv_shared.shape[2]
    tap_count = kernel_len * 2 * tap_block
    stages, core, table = block_plan()
    groups, core_table = core_groups()
    blocks = length // TOKEN_BLOCK
    starts = token_starts(blocks)
    two = lax.axis_size("tensor") == 2

    chips = dp_count // 2
    hidden_own, hidden_other = both_halves(hidden_in)
    tap_rows = conv_shared.transpose(1, 2, 0).reshape(2 * tap_block, kernel_len)
    tap_rows = pad_to(tap_rows, 0, rows)
    packed = jnp.concatenate(
        [
            pad_to(proj_inner[:, 1, :], 1, width),
            proj_shared.reshape(rows, shared_size),
            pad_to(jnp.concatenate([proj_step, norm_gain[:, None], tap_rows], axis=1), 1, LANES),
        ],
        axis=1,
    )
    later = jnp.concatenate(
        [pad_to(proj_inner[:, 0, :], 1, width), pad_to(proj_out.T, 1, width)], axis=1
    )
    at = jnp.arange(model_dim)
    block, inside = at // rows, at % rows
    side, spot = inside // tap_block, inside % tap_block
    spread = jnp.where(side < 2, side * state_size + block * tap_block + spot, -1)
    spread = (spread[:, None] == jnp.arange(shared_size)[None, :]).astype(bf16)
    aux, segr = token_facts(segment_ids)
    heads_block = jnp.stack([step_bias, log_decay, skip_gain])
    heads_block = pad_to(pad_to(heads_block, 1, LANES), 0, 8)
    tapi = pad_to(conv_inner, 1, width)
    gain = pad_to(gate_gain[None], 1, width)

    low = packed
    for number, stage in enumerate(stages):
        got = lax.ppermute(low, "dp", stage)
        if number == 0:
            got, aux, segr = lax.optimization_barrier((got, aux, segr))
        if number == 1:
            got, heads_block, tapi, spread, table, core_table = lax.optimization_barrier(
                (got, heads_block, tapi, spread, table, core_table)
            )
        if number == len(stages) - 1:
            later_all = jnp.broadcast_to(later[None], (chips,) + later.shape)
            later_all = later_all.reshape(chips * rows, 2 * width)
            got, later_all, gain = lax.optimization_barrier((got, later_all, gain))
        low = jnp.concatenate([low, got], axis=0)
    low, later_all, hidden_other = lax.optimization_barrier((low, later_all, hidden_other))
    high = lax.ppermute(low, "dp", core)
    later_low = exchange(later_all, groups)
    grad_own, grad_other = both_halves(after(out_grad, hidden_other))

    proj, praw, normed, normed_t, weights, taps, norm_scale = run_project(
        starts, table, hidden_own, hidden_other, spread, low, high, heads
    )
    norm_scale = norm_scale[:1]
    mixed, u, su, entry = run_forward(proj, praw, tapi, taps, heads_block, aux, segr)

    later_low, mixed, grad_other = lax.optimization_barrier((later_low, mixed, grad_other))
    later_high = lax.ppermute(later_low, "dp", core)
    gate, nog, grad_t, sums, later_rows = run_out_grad(
        starts, core_table, grad_own, grad_other, later_low, later_high, normed, mixed, gain
    )
    if two:
        more = swap(sums)
    else:
        sums = lax.psum(sums, "tensor")
        more = jnp.zeros_like(sums)
    normed_out, dgate, mixed_grad, gain_rows, gkeep, gsend = run_gated(
        core_table, gate, nog, mixed, sums, more, aux, gain, grad_t, normed_t, full_inner
    )
    ggot = lax.ppermute(gsend, "dp", core)
    send_start = starts[1:] if two else jnp.zeros((1,), jnp.int32)
    out_send, out_keep = run_out(send_start, normed_out, later_rows)
    ggot, out_send = lax.optimization_barrier((ggot, out_send))
    gsum = exchange((gkeep.astype(f32) + ggot.astype(f32)).astype(bf16), groups)
    out_other = swap(out_send) if two else None

    dproj, wkeep, wsend = run_backward(
        core_table,
        proj,
        praw,
        u,
        su,
        entry,
        mixed_grad,
        tapi,
        taps,
        heads_block,
        aux,
        segr,
        gain_rows,
        normed_t,
    )
    if two:
        wsend, gsum, out_other = lax.optimization_barrier((wsend, gsum, out_other))
    else:
        wsend, gsum = lax.optimization_barrier((wsend, gsum))
    wgot = lax.ppermute(wsend, "dp", core)
    grad_send = run_norm_grad(send_start, dgate, dproj, later_rows, weights, bf16)
    wgot, grad_send = lax.optimization_barrier((wgot, grad_send))
    grad_other = swap(grad_send) if two else None
    held = rows * chips
    wtotal = (wkeep.astype(f32) + wgot.astype(f32)).astype(bf16)
    wtotal = jnp.concatenate(
        [
            wtotal[:held].reshape(chips, rows, -1),
            jnp.broadcast_to(wtotal[None, held:], (chips, 8, wtotal.shape[1])),
        ],
        axis=1,
    ).reshape(chips * (rows + 8), -1)
    wtotal, dproj = lax.optimization_barrier((wtotal, dproj))
    wsum = exchange(wtotal, groups)
    keep_start = starts[:1] if two else jnp.full((1,), blocks // 2, jnp.int32)
    grad_keep = run_norm_grad(keep_start, dgate, dproj, later_rows, weights, f32)
    if two:
        out_half = out_keep.astype(f32) + out_other.astype(f32)
        own_grad = grad_keep + grad_other.astype(f32)
    else:
        out_half = add_halves(out_send, out_keep)
        own_grad = add_halves(grad_send, grad_keep)
    hidden_out = (hidden_in.astype(f32) + out_half).astype(bf16)
    gsum = sum_blocks(gsum, rows)
    out_sum = gsum[:, width : width + local_inner].T
    gate_sum = gsum[:, :local_inner]

    wsum = sum_blocks(wsum, rows + 8)
    small = wsum[rows:]
    wsum = wsum[:rows]
    conv_total = small[:kernel_len, :local_inner]
    gain_total = small[4, :local_inner]
    skip_total = small[0, width + shared_size : width + shared_size + heads]
    bias_total = small[1, width + shared_size : width + shared_size + heads]
    decay_total = small[2, width + shared_size : width + shared_size + heads]
    norm_row = jnp.sum(gate_sum * proj_inner[:, 0, :].astype(f32), axis=1) + jnp.sum(
        wsum * packed.astype(f32) * (jnp.arange(packed.shape[1]) < width + shared_size + heads),
        axis=1,
    )
    final = jnp.concatenate(
        [
            wsum[:, width : width + shared_size],
            small[:kernel_len, width : width + shared_size],
            pad_to(norm_row[None], 1, shared_size),
        ],
        axis=0,
    )
    final = total_over_tensor(pad_to(final, 0, rows + 8))
    shared_total = final[:rows].reshape(rows, 2, state_size)
    taps_total = lax.dynamic_slice_in_dim(
        final[rows : rows + kernel_len].reshape(kernel_len, 2, state_size),
        dp_index * tap_block,
        tap_block,
        axis=2,
    )
    norm_total = final[rows + kernel_len, :rows] / norm_gain.astype(f32)
    inner_sum = jnp.stack([gate_sum, wsum[:, :local_inner]], axis=1)
    step_sum = wsum[:, width + shared_size : width + shared_size + heads]

    own = hidden_in.astype(f32)
    own_inv = lax.rsqrt(jnp.mean(own * own, axis=-1, keepdims=True) + epsilon)
    own_unit = own * own_inv
    scaled_in = own_grad * norm_scale
    hidden_grad = own_inv * (
        scaled_in - own_unit * jnp.mean(scaled_in * own_unit, axis=-1, keepdims=True)
    ) + out_grad.astype(f32)
    return (
        hidden_out,
        hidden_grad,
        norm_total,
        inner_sum,
        shared_total,
        step_sum,
        conv_total,
        taps_total,
        bias_total,
        decay_total,
        skip_total,
        gain_total,
        out_sum,
    )


def solution(mesh):
    in_specs = (
        P(("dp", "tensor"), None),
        P("dp"),
        P("dp"),
        P("dp", None, "tensor"),
        P("dp", None, None),
        P("dp", "tensor"),
        P(None, "tensor"),
        P(None, None, "dp"),
        P("tensor"),
        P("tensor"),
        P("tensor"),
        P("tensor"),
        P("tensor", "dp"),
        P(("dp", "tensor"), None),
    )
    out_specs = (
        P(("dp", "tensor"), None),
        P(("dp", "tensor"), None),
        P("dp"),
        P("dp", None, "tensor"),
        P("dp", None, None),
        P("dp", "tensor"),
        P(None, "tensor"),
        P(None, None, "dp"),
        P("tensor"),
        P("tensor"),
        P("tensor"),
        P("tensor"),
        P("tensor", "dp"),
    )
    return jax.shard_map(body, mesh=mesh, in_specs=in_specs, out_specs=out_specs, check_vma=False)
```

```python
from functools import partial

import jax
import jax.numpy as jnp
import numpy as np
from jax import lax
from jax.experimental import pallas as pl
from jax.experimental.pallas import tpu as pltpu
from jax.sharding import PartitionSpec as P

HEAD_DIM = 64
CHUNK = 128
LANES = 128
TOKEN_BLOCK = 256
VMEM_BASE = 16
ROW_TILE = 64
epsilon = 1e-05
f32 = jnp.float32
bf16 = jnp.bfloat16
highest = lax.Precision.HIGHEST


def dot_nn(a, b):
    return lax.dot_general(a, b, (((1,), (0,)), ((), ())), preferred_element_type=f32)


def dot_nt(a, b):
    return lax.dot_general(a, b, (((1,), (1,)), ((), ())), preferred_element_type=f32)


def dot_tn(a, b):
    return lax.dot_general(a, b, (((0,), (0,)), ((), ())), preferred_element_type=f32)


def dot_exact(a, b):
    return lax.dot_general(
        a, b, (((1,), (0,)), ((), ())), preferred_element_type=f32, precision=highest
    )


def dot_split(a, b):
    high = a.astype(bf16)
    rest = (a - high.astype(f32)).astype(bf16)
    return dot_nn(high, b) + dot_nn(rest, b)


def two_parts(values):
    high = values.astype(bf16)
    rest = (values - high.astype(f32)).astype(bf16)
    return jnp.concatenate([high, rest], axis=1)


def spread_matrix(shape, size):
    rows = lax.rem(lax.broadcasted_iota(jnp.int32, shape, 0), LANES)
    return (rows == lax.broadcasted_iota(jnp.int32, shape, 1) // size).astype(bf16)


def sigmoid(v):
    return 1.0 / (1.0 + jnp.exp(-v))


def softplus(v):
    return jnp.maximum(v, 0.0) + jnp.log1p(jnp.exp(-jnp.abs(v)))


def halves(lane_low, values, head):
    return jnp.where(lane_low, values[:, head : head + 1], values[:, head + 1 : head + 2])


def back_shift(window, offset):
    return pltpu.roll(window, offset, 0)[8:, :]


def ahead_shift(window, offset):
    rows = window.shape[0]
    return pltpu.roll(window, rows - offset, 0)[: rows - 8, :]


def conv_rows(window, taps, aux):
    total = taps[3:4, :] * window[8:, :]
    for offset in range(1, 4):
        total = total + taps[3 - offset : 4 - offset, :] * (
            back_shift(window, offset) * aux[:, offset : offset + 1]
        )
    return total


def forward_kernel(
    proj_ref,
    step_ref,
    tapi_ref,
    taps_ref,
    heads_ref,
    aux_ref,
    segr_ref,
    mixed_ref,
    u_ref,
    su_ref,
    entry_ref,
    state_ref,
    carry_ref,
    scarry_ref,
    xw_ref,
    channels_ref,
    columns_ref,
):
    width = mixed_ref.shape[1]
    pairs = width // LANES
    shared_size = su_ref.shape[1]
    state_size = shared_size // 2
    chunk = pl.program_id(0)

    @pl.when(chunk == 0)
    def _():
        for ref in (state_ref, carry_ref, scarry_ref):
            ref[...] = jnp.zeros_like(ref)
        channels_ref[...] = spread_matrix(channels_ref.shape, HEAD_DIM)
        columns_ref[...] = spread_matrix(columns_ref.shape, CHUNK)

    rows = lax.broadcasted_iota(jnp.int32, (CHUNK, CHUNK), 0)
    cols = lax.broadcasted_iota(jnp.int32, (CHUNK, CHUNK), 1)
    lower = rows >= cols
    summing = lower.astype(f32)
    lane_low = lax.broadcasted_iota(jnp.int32, (CHUNK, LANES), 1) < HEAD_DIM
    bias = heads_ref[0:1, :]
    rate = -jnp.exp(heads_ref[1:2, :])
    skips = heads_ref[2:3, :]
    aux = aux_ref[...]
    live = aux[:, 7:8]
    same = lower & (aux[:, 0:1] == segr_ref[pl.ds(chunk, 1), :])
    shared_now = proj_ref[:, width:].astype(f32)
    su = conv_rows(jnp.concatenate([scarry_ref[...], shared_now], axis=0), taps_ref[...], aux)
    scarry_ref[...] = shared_now[CHUNK - 8 :, :]
    su_ref[...] = su
    shared = (su * sigmoid(su)).astype(bf16)
    b_rows = shared[:, :state_size]
    c_rows = shared[:, state_size:]
    scores = jnp.where(same, dot_nt(c_rows, b_rows), 0.0)
    step = softplus(step_ref[...] + bias) * live
    decay = dot_exact(summing, step * rate)
    decay_parts = two_parts(decay)
    decay = decay_parts[:, :LANES].astype(f32) + decay_parts[:, LANES:].astype(f32)
    decay_wide = dot_nn(decay_parts, columns_ref[...])
    decay_t = decay.T
    last = decay[CHUNK - 1 :, :]
    entry_scale = jnp.exp(decay) * aux[:, 8:9]
    end_scale = jnp.exp(last - decay) * aux[:, 9:10]
    keep = jnp.exp(last) * aux[:1, 10:11]
    step_wide = dot_nn(two_parts(step), channels_ref[...])
    entry_wide = dot_nn(two_parts(entry_scale), channels_ref[...])
    end_wide = dot_nn(two_parts(end_scale), channels_ref[...])
    state = state_ref[...]
    state_low = state.astype(bf16)
    entry_ref[...] = state_low[None]
    past = dot_nn(c_rows, state_low)
    for pair in range(pairs):
        lanes = slice(pair * LANES, (pair + 1) * LANES)
        head = 2 * pair
        now = proj_ref[:, lanes].astype(f32)
        window = jnp.concatenate([carry_ref[:, lanes], now], axis=0)
        carry_ref[:, lanes] = now[CHUNK - 8 :, :]
        u = conv_rows(window, tapi_ref[:, lanes].astype(f32), aux)
        u_ref[:, lanes] = u.astype(bf16)
        x = u * sigmoid(u)
        scaled = x * step_wide[:, lanes]
        mixing = jnp.concatenate(
            [
                (
                    scores
                    * jnp.exp(jnp.minimum(decay_wide[:, h * CHUNK : (h + 1) * CHUNK] - decay_t[h : h + 1, :], 0.0))
                ).astype(bf16)
                for h in (head, head + 1)
            ],
            axis=1,
        )
        stacked = jnp.concatenate(
            [jnp.where(lane_low, scaled, 0.0), jnp.where(lane_low, 0.0, scaled)], axis=0
        ).astype(bf16)
        inside = dot_nn(mixing, stacked)
        xw_ref[:, lanes] = (scaled * end_wide[:, lanes]).astype(bf16)
        mixed = (
            inside
            + past[:, lanes] * entry_wide[:, lanes]
            + halves(lane_low[:1], skips, head) * x
        ) * live
        mixed_ref[:, lanes] = mixed.astype(bf16)
        state_ref[:, lanes] = state[:, lanes] * halves(lane_low[:1], keep, head)
    state_ref[...] += dot_tn(b_rows, xw_ref[...])


def token_scales(sums, full_inner):
    columns = sums.T
    inv = lax.rsqrt(columns[:, 0:1] / full_inner + epsilon)
    return inv, inv * columns[:, 1:2] / full_inner


def silu_slope(v, s):
    return s * (1.0 + v * (1.0 - s))


def backward_kernel(
    table_ref,
    proj_ref,
    praw_ref,
    u_ref,
    su_ref,
    entry_ref,
    grad_ref,
    tapi_ref,
    taps_ref,
    heads_ref,
    aux_ref,
    segr_ref,
    gain_ref,
    turned_ref,
    dproj_ref,
    keep_ref,
    send_ref,
    wide_ref,
    shared_ref,
    small_ref,
    total_ref,
    grads_ref,
    held_ref,
    sem_ref,
    state_ref,
    ahead_ref,
    sahead_ref,
    xw_ref,
    ge_ref,
    row_ref,
    proda_ref,
    prodb_ref,
    channels_ref,
    columns_ref,
):
    width = u_ref.shape[1]
    chunks = pl.num_programs(0)
    pairs = width // LANES
    shared_size = su_ref.shape[1]
    state_size = shared_size // 2
    shared_cols = slice(width, width + shared_size)
    step_cols = slice(width + shared_size, width + shared_size + LANES)
    chunk = chunks - 1 - pl.program_id(0)
    copy = pltpu.make_async_copy(turned_ref, held_ref, sem_ref.at[0])

    @pl.when(pl.program_id(0) == 0)
    def _():
        copy.start()
        channels_ref[...] = spread_matrix(channels_ref.shape, HEAD_DIM)
        columns_ref[...] = spread_matrix(columns_ref.shape, CHUNK)
        for ref in (state_ref, ahead_ref, sahead_ref, row_ref, wide_ref, shared_ref):
            ref[...] = jnp.zeros_like(ref)

    rows = lax.broadcasted_iota(jnp.int32, (CHUNK, CHUNK), 0)
    cols = lax.broadcasted_iota(jnp.int32, (CHUNK, CHUNK), 1)
    upper = rows <= cols
    summing = (rows >= cols).astype(f32)
    unsumming = upper.astype(f32)
    last_row = (lax.broadcasted_iota(jnp.int32, (CHUNK, LANES), 0) == CHUNK - 1).astype(f32)
    lane_ids = lax.broadcasted_iota(jnp.int32, (CHUNK, LANES), 1)
    lane_low = lane_ids < HEAD_DIM
    bias = heads_ref[0:1, :]
    rate = -jnp.exp(heads_ref[1:2, :])
    skips = heads_ref[2:3, :]
    place = (
        lax.broadcasted_iota(jnp.int32, (width, LANES), 0) // HEAD_DIM
        == lax.broadcasted_iota(jnp.int32, (width, LANES), 1)
    ).astype(bf16)

    aux = aux_ref[...]
    live = aux[:, 7:8]
    same = upper & (aux[:, 0:1] == segr_ref[pl.ds(chunk, 1), :])
    su = su_ref[...]
    su_sig = sigmoid(su)
    shared = (su * su_sig).astype(bf16)
    b_rows = shared[:, :state_size]
    c_rows = shared[:, state_size:]
    scores = jnp.where(same, dot_nt(b_rows, c_rows), 0.0)
    pre = praw_ref[...] + bias
    step = softplus(pre) * live
    decay = dot_exact(summing, step * rate)
    decay_parts = two_parts(decay)
    decay = decay_parts[:, :LANES].astype(f32) + decay_parts[:, LANES:].astype(f32)
    decay_wide = dot_nn(decay_parts, columns_ref[...])
    decay_t = decay.T
    last = decay[CHUNK - 1 :, :]
    entry_scale = jnp.exp(decay) * aux[:, 8:9]
    end_scale = jnp.exp(last - decay) * aux[:, 9:10]
    keep = jnp.exp(last) * aux[:1, 10:11]
    step_wide = dot_nn(two_parts(step), channels_ref[...])
    entry_wide = dot_nn(two_parts(entry_scale), channels_ref[...])
    end_wide = dot_nn(two_parts(end_scale), channels_ref[...])
    entry = entry_ref[0]
    dstate = state_ref[...]
    dstate_low = dstate.astype(bf16)
    past = dot_nn(c_rows, entry)
    bds = dot_nn(b_rows, dstate_low)
    here = pl.ds(pl.multiple_of(chunk * CHUNK, CHUNK), CHUNK)
    score_grad = jnp.zeros((CHUNK, CHUNK), f32)
    col_part = jnp.zeros((CHUNK, LANES), f32)
    for pair in range(pairs):
        lanes = slice(pair * LANES, (pair + 1) * LANES)
        head = 2 * pair
        g_low = grad_ref[:, lanes]
        g = g_low.astype(f32)
        u = u_ref[:, lanes].astype(f32)
        u_sig = sigmoid(u)
        x = u * u_sig
        step_c = step_wide[:, lanes]
        scaled = x * step_c
        stacked = jnp.concatenate(
            [jnp.where(lane_low, scaled, 0.0), jnp.where(lane_low, 0.0, scaled)], axis=0
        ).astype(bf16)
        dmix = dot_nt(stacked, g_low)
        mixing = []
        for k, h in enumerate((head, head + 1)):
            decays = jnp.exp(jnp.minimum(decay_t[h : h + 1, :] - decay_wide[:, h * CHUNK : (h + 1) * CHUNK], 0.0))
            dmix_h = dmix[k * CHUNK : (k + 1) * CHUNK, :]
            score_grad = score_grad + dmix_h * decays
            mixing_h = scores * decays
            mixing.append(mixing_h.astype(bf16))
            both = mixing_h * dmix_h
            col_part = jnp.where(lane_ids == h, jnp.sum(both, axis=1, keepdims=True), col_part)
            row_ref[h : h + 1, :] = jnp.sum(both, axis=0, keepdims=True)
        g_stacked = jnp.concatenate(
            [jnp.where(lane_low, g, 0.0), jnp.where(lane_low, 0.0, g)], axis=0
        ).astype(bf16)
        end_c = end_wide[:, lanes]
        entry_c = entry_wide[:, lanes]
        keep_c = halves(lane_low[:1], keep, head)
        from_state = end_c * bds[:, lanes]
        dscaled = dot_nn(jnp.concatenate(mixing, axis=1), g_stacked) + from_state
        xw_ref[:, lanes] = (scaled * end_c).astype(bf16)
        q = scaled * from_state
        ge = g * entry_c
        ge_ref[:, lanes] = ge.astype(bf16)
        dstate_p = dstate[:, lanes]
        tail = jnp.sum(q, axis=0, keepdims=True) + keep_c * jnp.sum(
            dstate_p * entry[:, lanes].astype(f32), axis=0, keepdims=True
        )
        proda_ref[:, lanes] = x * dscaled
        prodb_ref[:, lanes] = ge * past[:, lanes] - q + last_row * tail
        state_ref[:, lanes] = dstate_p * keep_c
        dx = step_c * dscaled + halves(lane_low[:1], skips, head) * g
        du = dx * silu_slope(u, u_sig)
        window = jnp.concatenate([du, ahead_ref[:, lanes]], axis=0)
        ahead_ref[:, lanes] = du[:8, :]
        cin = proj_ref[:, lanes].astype(f32)
        taps = tapi_ref[:, lanes].astype(f32)
        dcin = taps[3:4, :] * du
        wide_ref[3:4, lanes] += jnp.sum(cin * du, axis=0, keepdims=True)
        for offset in range(1, 4):
            moved = ahead_shift(window, offset) * aux[:, 3 + offset : 4 + offset]
            dcin = dcin + taps[3 - offset : 4 - offset, :] * moved
            wide_ref[3 - offset : 4 - offset, lanes] += jnp.sum(
                cin * moved, axis=0, keepdims=True
            )
        dcin = dcin.astype(bf16)
        dproj_ref[:, lanes] = dcin
        grads_ref[here, lanes] = dcin
        wide_ref[5:6, lanes] += jnp.sum(g * x, axis=0, keepdims=True)
    score_low = jnp.where(same, score_grad, 0.0).astype(bf16)
    ge_all = ge_ref[...]
    db = dot_nn(score_low, c_rows) + dot_nt(xw_ref[...], dstate_low)
    dc = dot_tn(score_low, b_rows) + dot_nt(ge_all, entry)
    state_ref[...] += dot_tn(c_rows, ge_all)
    ds = jnp.concatenate([db, dc], axis=1) * silu_slope(su, su_sig)
    window = jnp.concatenate([ds, sahead_ref[...]], axis=0)
    sahead_ref[...] = ds[:8, :]
    taps = taps_ref[...]
    sin = proj_ref[:, shared_cols].astype(f32)
    dsin = taps[3:4, :] * ds
    shared_ref[3:4, :] += jnp.sum(sin * ds, axis=0, keepdims=True)
    for offset in range(1, 4):
        moved = ahead_shift(window, offset) * aux[:, 3 + offset : 4 + offset]
        dsin = dsin + taps[3 - offset : 4 - offset, :] * moved
        shared_ref[3 - offset : 4 - offset, :] += jnp.sum(sin * moved, axis=0, keepdims=True)
    dsin = dsin.astype(bf16)
    dproj_ref[:, shared_cols] = dsin
    grads_ref[here, shared_cols] = dsin
    ddecay = row_ref[...].T - col_part + dot_split(prodb_ref[...], place)
    dlog = dot_exact(unsumming, ddecay)
    dstep = (dot_split(proda_ref[...], place) + rate * dlog) * live * sigmoid(pre)
    dproj_ref[:, step_cols] = dstep.astype(bf16)
    grads_ref[here, step_cols] = dstep.astype(bf16)
    wide_ref[6:7, :LANES] += jnp.sum(dstep, axis=0, keepdims=True)
    wide_ref[6:7, LANES : 2 * LANES] += jnp.sum(step * dlog, axis=0, keepdims=True) * rate

    @pl.when(chunk == 0)
    def _():
        small_ref[...] = jnp.zeros_like(small_ref)
        small_ref[:4, :width] = wide_ref[:4, :]
        small_ref[:4, width : width + shared_size] = shared_ref[:4, :]
        skip_row = dot_split(wide_ref[...], place)[5:6, :]
        small_ref[0:1, step_cols] = skip_row
        small_ref[1:2, step_cols] = wide_ref[6:7, :LANES]
        small_ref[2:3, step_cols] = wide_ref[6:7, LANES : 2 * LANES]
        small_ref[4:5, :width] = jnp.sum(gain_ref[...], axis=0, keepdims=True)
        copy.wait()
        held = keep_ref.shape[0] - 8
        keep_ref[held:, :] = small_ref[...].astype(bf16)
        send_ref[held:, :] = small_ref[...].astype(bf16)
        tile = total_ref.shape[1]
        for at in range(0, width + shared_size + LANES, tile):
            total_ref[...] = dot_nn(held_ref[...], grads_ref[:, at : at + tile])
            store_blocks(table_ref, total_ref, keep_ref, send_ref, slice(at, at + tile))


def facts_kernel(seg_ref, aux_ref, segr_ref):
    seg = seg_ref[...].astype(f32)
    chunks = seg.shape[0]
    segr_ref[...] = seg
    none = jnp.full((1, CHUNK), -1.0, f32)
    before = jnp.concatenate([none, seg[: chunks - 1]], axis=0) if chunks > 1 else none
    behind = jnp.concatenate([seg[1:], none], axis=0) if chunks > 1 else none
    lane = lax.broadcasted_iota(jnp.int32, seg.shape, 1)
    facts = [seg]
    for offset in range(1, 4):
        earlier = jnp.where(
            lane >= offset, pltpu.roll(seg, offset, 1), pltpu.roll(before, offset, 1)
        )
        facts.append((earlier == seg).astype(f32))
    for offset in range(1, 4):
        later = jnp.where(
            lane < CHUNK - offset,
            pltpu.roll(seg, CHUNK - offset, 1),
            pltpu.roll(behind, CHUNK - offset, 1),
        )
        facts.append((later == seg).astype(f32))
    last = jnp.broadcast_to(seg[:, CHUNK - 1 :], seg.shape)
    prior = jnp.broadcast_to(before[:, CHUNK - 1 :], seg.shape)
    facts.append((seg != 0.0).astype(f32))
    facts.append((seg == prior).astype(f32))
    facts.append((seg == last).astype(f32))
    facts.append((last == prior).astype(f32))
    empty = jnp.zeros((LANES - len(facts), CHUNK), f32)
    for chunk in range(chunks):
        rows = jnp.concatenate([f[chunk : chunk + 1, :] for f in facts] + [empty], axis=0)
        aux_ref[chunk * CHUNK : (chunk + 1) * CHUNK, :] = rows.T[:, : aux_ref.shape[1]]


def token_facts(segments):
    length = segments.shape[0]
    chunks = length // CHUNK
    return pl.pallas_call(
        facts_kernel,
        out_shape=(
            jax.ShapeDtypeStruct((length, 16), f32),
            jax.ShapeDtypeStruct((chunks, CHUNK), f32),
        ),
        name="token_facts",
        cost_estimate=cost(2),
        compiler_params=vmem_limit(length),
    )(segments.reshape(chunks, CHUNK))


def chunk_spec(columns, last):
    if last is None:
        return pl.BlockSpec((CHUNK, columns), lambda i: (i, 0))
    return pl.BlockSpec((CHUNK, columns), lambda i: (last - i, 0))


def fixed_spec(values):
    zeros = (0,) * values.ndim
    return pl.BlockSpec(values.shape, lambda i: zeros)


def run_forward(proj, praw, tapi, taps, heads, aux, segr):
    length = proj.shape[0]
    width = tapi.shape[1]
    shared_size = taps.shape[1]
    state_size = shared_size // 2
    chunks = length // CHUNK
    proj, praw = from_store(proj, praw)
    return pl.pallas_call(
        forward_kernel,
        grid=(chunks,),
        in_specs=[
            chunk_spec(proj.shape[1], None),
            chunk_spec(LANES, None),
            fixed_spec(tapi),
            fixed_spec(taps),
            fixed_spec(heads),
            chunk_spec(aux.shape[1], None),
            fixed_spec(segr),
        ],
        out_specs=[
            chunk_spec(width, None),
            chunk_spec(width, None),
            chunk_spec(shared_size, None),
            pl.BlockSpec((1, state_size, width), lambda i: (i, 0, 0)),
        ],
        out_shape=(
            stored((length, width), bf16),
            stored((length, width), bf16),
            stored((length, shared_size), f32),
            stored((chunks, state_size, width), bf16),
        ),
        scratch_shapes=[
            pltpu.VMEM((state_size, width), f32),
            pltpu.VMEM((8, width), f32),
            pltpu.VMEM((8, shared_size), f32),
            pltpu.VMEM((CHUNK, width), bf16),
            pltpu.VMEM((2 * LANES, width), bf16),
            pltpu.VMEM((2 * LANES, width // HEAD_DIM * CHUNK), bf16),
        ],
        name="scan_forward",
        cost_estimate=cost(3),
        compiler_params=vmem_limit(length),
    )(proj, praw, tapi, taps, heads, aux, segr)


def run_backward(
    table, proj, praw, u, su, entry, grad, tapi, taps, heads, aux, segr, gain_rows, turned
):
    length, width = u.shape
    shared_size = su.shape[1]
    state_size = shared_size // 2
    model_dim = turned.shape[0]
    chunks = length // CHUNK
    last = chunks - 1
    columns = width + shared_size + LANES
    kept = model_dim // 2 + 8
    sds = jax.ShapeDtypeStruct
    proj, praw, u, su, entry, grad, turned = from_store(proj, praw, u, su, entry, grad, turned)

    def back(size):
        return pl.BlockSpec((CHUNK, size), lambda i, t: (last - i, 0))

    def fixed(shape):
        return pl.BlockSpec(shape, lambda i, t: (0, 0))

    return pl.pallas_call(
        backward_kernel,
        grid_spec=pltpu.PrefetchScalarGridSpec(
            num_scalar_prefetch=1,
            grid=(chunks,),
            in_specs=[
                back(proj.shape[1]),
                back(LANES),
                back(width),
                back(shared_size),
                pl.BlockSpec((1, state_size, width), lambda i, t: (last - i, 0, 0)),
                back(width),
                fixed(tapi.shape),
                fixed(taps.shape),
                fixed(heads.shape),
                back(aux.shape[1]),
                fixed(segr.shape),
                fixed(gain_rows.shape),
                pl.BlockSpec(memory_space=pl.ANY),
            ],
            out_specs=[
                back(columns),
                fixed((kept, columns)),
                fixed((kept, columns)),
            ],
            scratch_shapes=[
                pltpu.VMEM((8, width), f32),
                pltpu.VMEM((8, shared_size), f32),
                pltpu.VMEM((8, columns), f32),
                pltpu.VMEM((model_dim, column_tile(columns)), f32),
                pltpu.VMEM((length, columns), bf16),
                pltpu.VMEM((model_dim, length), bf16),
                pltpu.SemaphoreType.DMA((1,)),
                pltpu.VMEM((state_size, width), f32),
                pltpu.VMEM((8, width), f32),
                pltpu.VMEM((8, shared_size), f32),
                pltpu.VMEM((CHUNK, width), bf16),
                pltpu.VMEM((CHUNK, width), bf16),
                pltpu.VMEM((LANES, CHUNK), f32),
                pltpu.VMEM((CHUNK, width), f32),
                pltpu.VMEM((CHUNK, width), f32),
                pltpu.VMEM((2 * LANES, width), bf16),
                pltpu.VMEM((2 * LANES, width // HEAD_DIM * CHUNK), bf16),
            ],
        ),
        out_shape=(
            stored((length, columns), bf16),
            stored((kept, columns), bf16),
            stored((kept, columns), bf16),
        ),
        name="scan_backward",
        cost_estimate=cost(36),
        compiler_params=vmem_limit(length),
    )(table, proj, praw, u, su, entry, grad, tapi, taps, heads, aux, segr, gain_rows, turned)


def block_plan():
    count = lax.axis_size("dp")
    bits = []
    bit = count // 2
    while bit > 1:
        bits.append(bit)
        bit //= 2
    mixed = bits[:-2] + bits[-2:][::-1]
    by_core = (bits, mixed)
    stages = []
    for stage in range(len(bits)):
        stages.append([(i, i ^ by_core[i % 2][stage]) for i in range(count)])
    core = [(i, i ^ 1) for i in range(count)]
    device = np.zeros((count, count), np.int32)
    for own in range(count):
        for spot in range(count):
            other = own ^ 1 if spot >= count // 2 else own
            for stage, bit in enumerate(by_core[other % 2]):
                if (spot >> stage) & 1:
                    other ^= bit
            device[own, spot] = other
    table = jnp.asarray(device)[lax.axis_index("dp")]
    return stages, core, table


def core_groups():
    count = lax.axis_size("dp")
    groups = [list(range(side, count, 2)) for side in range(2)]
    return groups, jnp.asarray(
        [groups[0] + groups[1], groups[1] + groups[0]], jnp.int32
    )[lax.axis_index("dp") % 2]


def exchange(blocks, groups):
    return lax.all_to_all(
        blocks, "dp", 0, 0, axis_index_groups=groups, tiled=True
    )


def sum_blocks(blocks, rows):
    return jnp.sum(blocks.reshape(-1, rows, blocks.shape[1]).astype(f32), axis=0)


def swap(values):
    return lax.ppermute(values, "tensor", [(0, 1), (1, 0)])


def total_over_tensor(values):
    if lax.axis_size("tensor") == 2:
        return values + swap(values)
    return lax.psum(values, "tensor")


def both_halves(own):
    if lax.axis_size("tensor") == 2:
        return own, swap(own)
    whole = lax.all_gather(own, "tensor", axis=0, tiled=True)
    return whole, whole


def token_starts(blocks):
    if lax.axis_size("tensor") == 2:
        index = lax.axis_index("tensor")
        return jnp.stack([index * (blocks // 2), (1 - index) * (blocks // 2)]).astype(jnp.int32)
    return jnp.zeros((2,), jnp.int32)


def add_halves(send, keep):
    if lax.axis_size("tensor") == 2:
        return keep.astype(f32) + swap(send).astype(f32)
    whole = jnp.concatenate([send.astype(bf16), keep.astype(bf16)], axis=0)
    return lax.psum_scatter(whole, "tensor", scatter_dimension=0, tiled=True).astype(f32)


def own_block(step, starts, own_blocks):
    return jnp.clip(step - starts[0], 0, own_blocks - 1)


def other_block(step, starts, own_blocks):
    return jnp.clip(step - starts[1], 0, own_blocks - 1)


def place_blocks(table_ref, low_ref, high_ref, whole_ref, sem_ref):
    count = table_ref.shape[0]
    rows = whole_ref.shape[0] // count
    copies = []
    for spot in range(count):
        source = low_ref if spot < count // 2 else high_ref
        where = pl.multiple_of(table_ref[spot] * rows, rows)
        copies.append(
            pltpu.make_async_copy(
                source.at[pl.ds((spot % (count // 2)) * rows, rows), :],
                whole_ref.at[pl.ds(where, rows), :],
                sem_ref.at[spot],
            )
        )
    for copy in copies:
        copy.start()
    for copy in copies:
        copy.wait()


def project_kernel(
    starts_ref,
    table_ref,
    own_ref,
    other_ref,
    spread_ref,
    low_ref,
    high_ref,
    proj_ref,
    step_ref,
    normed_ref,
    turned_ref,
    whole_ref,
    taps_ref,
    scale_ref,
    weights_ref,
    sem_ref,
    *,
    own_blocks,
    heads,
):
    step = pl.program_id(0)
    model_dim, columns = weights_ref.shape
    store = pltpu.make_async_copy(weights_ref, whole_ref, sem_ref.at[table_ref.shape[0]])

    @pl.when(step == pl.num_programs(0) - 1)
    def _():
        store.wait()

    @pl.when(step == 0)
    def _():
        place_blocks(table_ref, low_ref, high_ref, weights_ref, sem_ref)
        store.start()
        extra = weights_ref[:, columns - LANES :].astype(f32).T
        scale_ref[...] = jnp.broadcast_to(extra[heads : heads + 1, :], scale_ref.shape)
        taps = extra[heads + 1 : heads + 5, :]
        taps = jnp.concatenate([taps, jnp.zeros_like(taps)], axis=0).astype(bf16)
        taps_ref[...] = dot_nn(taps, spread_ref[...])

    mine = (step >= starts_ref[0]) & (step < starts_ref[0] + own_blocks)
    tokens = jnp.where(mine, own_ref[...].astype(f32), other_ref[...].astype(f32))
    inv = lax.rsqrt(jnp.mean(tokens * tokens, axis=-1, keepdims=True) + epsilon)
    normed = (tokens * inv * scale_ref[:1, :]).astype(bf16)
    normed_ref[...] = normed
    turned_ref[...] = normed.T
    proj = dot_nn(normed, weights_ref[...])
    proj_ref[...] = proj[:, : columns - LANES].astype(bf16)
    step_ref[...] = proj[:, columns - LANES :]


def run_project(starts, table, own, other, spread, low, high, heads):
    own_rows, model_dim = own.shape
    columns = low.shape[1]
    own_blocks = own_rows // TOKEN_BLOCK
    blocks = own_blocks * (2 if lax.axis_size("tensor") == 2 else 1)
    length = blocks * TOKEN_BLOCK
    sds = jax.ShapeDtypeStruct
    own, other, low, high = from_store(own, other, low, high)
    return pl.pallas_call(
        partial(project_kernel, own_blocks=own_blocks, heads=heads),
        grid_spec=pltpu.PrefetchScalarGridSpec(
            num_scalar_prefetch=2,
            grid=(blocks,),
            in_specs=[
                pl.BlockSpec(
                    (TOKEN_BLOCK, model_dim), lambda i, s, t: (own_block(i, s, own_blocks), 0)
                ),
                pl.BlockSpec(
                    (TOKEN_BLOCK, model_dim), lambda i, s, t: (other_block(i, s, own_blocks), 0)
                ),
                pl.BlockSpec(spread.shape, lambda i, s, t: (0, 0)),
                pl.BlockSpec(memory_space=pl.ANY),
                pl.BlockSpec(memory_space=pl.ANY),
            ],
            out_specs=[
                pl.BlockSpec((TOKEN_BLOCK, columns - LANES), lambda i, s, t: (i, 0)),
                pl.BlockSpec((TOKEN_BLOCK, LANES), lambda i, s, t: (i, 0)),
                pl.BlockSpec((TOKEN_BLOCK, model_dim), lambda i, s, t: (i, 0)),
                pl.BlockSpec((model_dim, TOKEN_BLOCK), lambda i, s, t: (0, i)),
                pl.BlockSpec(memory_space=pl.ANY),
                pl.BlockSpec((8, spread.shape[1]), lambda i, s, t: (0, 0)),
                pl.BlockSpec((8, model_dim), lambda i, s, t: (0, 0)),
            ],
            scratch_shapes=[
                pltpu.VMEM((model_dim, columns), bf16),
                pltpu.SemaphoreType.DMA((table.shape[0] + 1,)),
            ],
        ),
        out_shape=(
            stored((length, columns - LANES), bf16),
            stored((length, LANES), f32),
            stored((length, model_dim), bf16),
            stored((model_dim, length), bf16),
            stored((model_dim, columns), bf16),
            sds((8, spread.shape[1]), f32),
            sds((8, model_dim), f32),
        ),
        name="norm_project",
        cost_estimate=cost(2),
        compiler_params=vmem_limit(length),
    )(starts, table, own, other, spread, low, high)


def token_sum(values):
    total = values[:, :LANES]
    for at in range(LANES, values.shape[1], LANES):
        total = total + values[:, at : at + LANES]
    return jnp.sum(total.T, axis=0, keepdims=True)


def out_grad_kernel(
    starts_ref,
    table_ref,
    own_ref,
    other_ref,
    low_ref,
    high_ref,
    normed_ref,
    mixed_ref,
    gain_ref,
    gate_ref,
    nog_ref,
    turned_ref,
    sums_ref,
    whole_ref,
    weights_ref,
    sem_ref,
    *,
    own_blocks,
):
    step = pl.program_id(0)
    width = mixed_ref.shape[1]
    store = pltpu.make_async_copy(weights_ref, whole_ref, sem_ref.at[table_ref.shape[0]])

    @pl.when(step == 0)
    def _():
        place_blocks(table_ref, low_ref, high_ref, weights_ref, sem_ref)
        store.start()

    @pl.when(step == pl.num_programs(0) - 1)
    def _():
        store.wait()

    mine = (step >= starts_ref[0]) & (step < starts_ref[0] + own_blocks)
    tokens = jnp.where(mine, own_ref[...].astype(f32), other_ref[...].astype(f32)).astype(bf16)
    turned_ref[...] = tokens.T
    gate = dot_nn(normed_ref[...], weights_ref[:, :width])
    gate_ref[...] = gate.astype(bf16)
    nog = dot_nn(tokens, weights_ref[:, width:])
    nog_ref[...] = nog.astype(bf16)
    gated = mixed_ref[...].astype(f32) * (gate * sigmoid(gate))
    sums_ref[...] = jnp.concatenate(
        [
            token_sum(gated * gated),
            token_sum(nog * gain_ref[...].astype(f32) * gated),
            jnp.zeros((6, TOKEN_BLOCK), f32),
        ],
        axis=0,
    )


def run_out_grad(starts, table, own, other, low, high, normed, mixed, gain):
    own_rows, model_dim = own.shape
    length, width = mixed.shape
    own_blocks = own_rows // TOKEN_BLOCK
    blocks = length // TOKEN_BLOCK
    sds = jax.ShapeDtypeStruct
    own, other, normed, mixed = from_store(own, other, normed, mixed)
    return pl.pallas_call(
        partial(out_grad_kernel, own_blocks=own_blocks),
        grid_spec=pltpu.PrefetchScalarGridSpec(
            num_scalar_prefetch=2,
            grid=(blocks,),
            in_specs=[
                pl.BlockSpec(
                    (TOKEN_BLOCK, model_dim), lambda i, s, t: (own_block(i, s, own_blocks), 0)
                ),
                pl.BlockSpec(
                    (TOKEN_BLOCK, model_dim), lambda i, s, t: (other_block(i, s, own_blocks), 0)
                ),
                pl.BlockSpec(memory_space=pl.ANY),
                pl.BlockSpec(memory_space=pl.ANY),
                pl.BlockSpec((TOKEN_BLOCK, model_dim), lambda i, s, t: (i, 0)),
                pl.BlockSpec((TOKEN_BLOCK, width), lambda i, s, t: (i, 0)),
                pl.BlockSpec((1, width), lambda i, s, t: (0, 0)),
            ],
            out_specs=[
                pl.BlockSpec((TOKEN_BLOCK, width), lambda i, s, t: (i, 0)),
                pl.BlockSpec((TOKEN_BLOCK, width), lambda i, s, t: (i, 0)),
                pl.BlockSpec((model_dim, TOKEN_BLOCK), lambda i, s, t: (0, i)),
                pl.BlockSpec((8, TOKEN_BLOCK), lambda i, s, t: (0, i)),
                pl.BlockSpec(memory_space=pl.ANY),
            ],
            scratch_shapes=[
                pltpu.VMEM((model_dim, 2 * width), bf16),
                pltpu.SemaphoreType.DMA((table.shape[0] + 1,)),
            ],
        ),
        out_shape=(
            sds((length, width), bf16),
            sds((length, width), bf16),
            sds((model_dim, length), bf16),
            sds((8, length), f32),
            stored((model_dim, 2 * width), bf16),
        ),
        name="out_grad",
        cost_estimate=cost(9),
        compiler_params=vmem_limit(length),
    )(starts, table, own, other, low, high, normed, mixed, gain)


def column_tile(columns):
    return 3 * LANES if columns % (3 * LANES) == 0 else LANES


def store_blocks(table_ref, source_ref, keep_ref, send_ref, columns):
    count = table_ref.shape[0]
    rows = source_ref.shape[0] // count
    half = count // 2
    for spot in range(count):
        target = keep_ref if spot < half else send_ref
        at = (spot % half) * rows
        where = pl.multiple_of(table_ref[spot] * rows, rows)
        target[at : at + rows, columns] = source_ref[pl.ds(where, rows), :].astype(bf16)


def gated_kernel(
    table_ref,
    gate_ref,
    nog_ref,
    mixed_ref,
    sums_ref,
    more_ref,
    aux_ref,
    gain_ref,
    gturned_ref,
    nturned_ref,
    out_ref,
    dgate_ref,
    grad_ref,
    row_ref,
    keep_ref,
    send_ref,
    total_ref,
    both_ref,
    gheld_ref,
    nheld_ref,
    sem_ref,
    *,
    full_inner,
):
    step = pl.program_id(0)
    width = gate_ref.shape[1]
    tile = total_ref.shape[1]
    copies = [
        pltpu.make_async_copy(nturned_ref, nheld_ref, sem_ref.at[0]),
        pltpu.make_async_copy(gturned_ref, gheld_ref, sem_ref.at[1]),
    ]

    @pl.when(step == 0)
    def _():
        for copy in copies:
            copy.start()

    inv, mean = token_scales(sums_ref[...] + more_ref[...], full_inner)
    gain = gain_ref[...].astype(f32)
    start = pl.multiple_of(step * TOKEN_BLOCK, TOKEN_BLOCK)
    sums = {}
    for top in range(0, TOKEN_BLOCK, ROW_TILE):
        part = slice(top, top + ROW_TILE)
        here = pl.ds(start + top, ROW_TILE)
        live = aux_ref[part, 7:8]
        inv_part = inv[part]
        mean_part = mean[part]
        for at in range(0, width, LANES):
            lanes = slice(at, at + LANES)
            gate = gate_ref[part, lanes].astype(f32)
            gate_sig = sigmoid(gate)
            gate_silu = gate * gate_sig
            mixed = mixed_ref[part, lanes].astype(f32)
            unit = mixed * gate_silu * inv_part
            nog = nog_ref[part, lanes].astype(f32)
            grad = inv_part * (nog * gain[:, lanes] - unit * mean_part)
            dgate = (grad * mixed * silu_slope(gate, gate_sig)).astype(bf16)
            dgate_ref[part, lanes] = dgate
            both_ref[here, lanes] = dgate
            grad_ref[part, lanes] = (grad * gate_silu * live).astype(bf16)
            normed_out = (unit * gain[:, lanes]).astype(bf16)
            out_ref[part, lanes] = normed_out
            both_ref[here, slice(width + at, width + at + LANES)] = normed_out
            row = jnp.sum((nog * unit).reshape(-1, 8, LANES), axis=0)
            sums[at] = row if top == 0 else sums[at] + row
    for at in range(0, width, LANES):
        row_ref[pl.ds(step * 8, 8), slice(at, at + LANES)] = sums[at]

    @pl.when(step == pl.num_programs(0) - 1)
    def _():
        for copy in copies:
            copy.wait()
        for at in range(0, 2 * width, tile):
            turned = nheld_ref if at < width else gheld_ref
            total_ref[...] = dot_nn(turned[...], both_ref[:, at : at + tile])
            store_blocks(table_ref, total_ref, keep_ref, send_ref, slice(at, at + tile))


def run_gated(table, gate, nog, mixed, sums, more, aux, gain, gturned, nturned, full_inner):
    length, width = gate.shape
    model_dim = gturned.shape[0]
    blocks = length // TOKEN_BLOCK
    tile = column_tile(width)
    sds = jax.ShapeDtypeStruct
    mixed, nturned = from_store(mixed, nturned)
    tokens = pl.BlockSpec((TOKEN_BLOCK, width), lambda i, t: (i, 0))
    halves_spec = pl.BlockSpec((model_dim // 2, 2 * width), lambda i, t: (0, 0))
    return pl.pallas_call(
        partial(gated_kernel, full_inner=float(full_inner)),
        grid_spec=pltpu.PrefetchScalarGridSpec(
            num_scalar_prefetch=1,
            grid=(blocks,),
            in_specs=[
                tokens,
                tokens,
                tokens,
                pl.BlockSpec((8, TOKEN_BLOCK), lambda i, t: (0, i)),
                pl.BlockSpec((8, TOKEN_BLOCK), lambda i, t: (0, i)),
                pl.BlockSpec((TOKEN_BLOCK, aux.shape[1]), lambda i, t: (i, 0)),
                pl.BlockSpec((1, width), lambda i, t: (0, 0)),
                pl.BlockSpec(memory_space=pl.ANY),
                pl.BlockSpec(memory_space=pl.ANY),
            ],
            out_specs=[
                tokens,
                tokens,
                tokens,
                pl.BlockSpec((8 * blocks, width), lambda i, t: (0, 0)),
                halves_spec,
                halves_spec,
            ],
            scratch_shapes=[
                pltpu.VMEM((model_dim, tile), f32),
                pltpu.VMEM((length, 2 * width), bf16),
                pltpu.VMEM((model_dim, length), bf16),
                pltpu.VMEM((model_dim, length), bf16),
                pltpu.SemaphoreType.DMA((2,)),
            ],
        ),
        out_shape=(
            sds((length, width), bf16),
            stored((length, width), bf16),
            stored((length, width), bf16),
            sds((8 * blocks, width), f32),
            sds((model_dim // 2, 2 * width), bf16),
            sds((model_dim // 2, 2 * width), bf16),
        ),
        name="gated_grad",
        cost_estimate=cost(9),
        compiler_params=vmem_limit(length),
    )(table, gate, nog, mixed, sums, more, aux, gain, gturned, nturned)


def out_kernel(starts_ref, rows_ref, weights_ref, send_ref, keep_ref):
    step = pl.program_id(0)
    half = pl.num_programs(0) // 2
    rows = dot_nt(rows_ref[...], weights_ref[...]).astype(bf16)

    @pl.when(step < half)
    def _():
        send_ref[...] = rows

    @pl.when(step >= half)
    def _():
        keep_ref[...] = rows


def run_out(starts, rows, weights):
    length, width = rows.shape
    model_dim = weights.shape[0]
    blocks = length // TOKEN_BLOCK
    half = blocks // 2
    sds = jax.ShapeDtypeStruct
    (weights,) = from_store(weights)
    return pl.pallas_call(
        out_kernel,
        grid_spec=pltpu.PrefetchScalarGridSpec(
            num_scalar_prefetch=1,
            grid=(blocks,),
            in_specs=[
                pl.BlockSpec((TOKEN_BLOCK, width), lambda i, s: (lax.rem(i + s[0], blocks), 0)),
                pl.BlockSpec((model_dim, width), lambda i, s: (0, 1)),
            ],
            out_specs=[
                pl.BlockSpec((TOKEN_BLOCK, model_dim), lambda i, s: (jnp.minimum(i, half - 1), 0)),
                pl.BlockSpec((TOKEN_BLOCK, model_dim), lambda i, s: (jnp.maximum(i - half, 0), 0)),
            ],
        ),
        out_shape=(
            sds((length // 2, model_dim), bf16),
            sds((length // 2, model_dim), bf16),
        ),
        name="out_project",
        cost_estimate=cost(4),
        compiler_params=vmem_limit(length),
    )(starts, rows, weights)


def norm_grad_kernel(starts_ref, dgate_ref, dproj_ref, gates_ref, weights_ref, grad_ref):
    grad = dot_nt(dgate_ref[...], gates_ref[...]) + dot_nt(dproj_ref[...], weights_ref[...])
    grad_ref[...] = grad.astype(grad_ref.dtype)


def run_norm_grad(starts, dgate, dproj, gates, weights, kind):
    length, columns = dproj.shape
    width = dgate.shape[1]
    model_dim = weights.shape[0]
    blocks = length // TOKEN_BLOCK // 2
    dgate, dproj, gates, weights = from_store(dgate, dproj, gates, weights)
    return pl.pallas_call(
        norm_grad_kernel,
        grid_spec=pltpu.PrefetchScalarGridSpec(
            num_scalar_prefetch=1,
            grid=(blocks,),
            in_specs=[
                pl.BlockSpec((TOKEN_BLOCK, width), lambda i, s: (i + s[0], 0)),
                pl.BlockSpec((TOKEN_BLOCK, columns), lambda i, s: (i + s[0], 0)),
                pl.BlockSpec((model_dim, width), lambda i, s: (0, 0)),
                pl.BlockSpec((model_dim, columns), lambda i, s: (0, 0)),
            ],
            out_specs=pl.BlockSpec((TOKEN_BLOCK, model_dim), lambda i, s: (i, 0)),
        ),
        out_shape=jax.ShapeDtypeStruct((length // 2, model_dim), kind),
        name="normed_grad",
        cost_estimate=cost(5),
        compiler_params=vmem_limit(length),
    )(starts, dgate, dproj, gates, weights)


def after(value, *others):
    return lax.optimization_barrier((value,) + others)[0]


def cost(microseconds):
    return pl.CostEstimate(flops=int(microseconds * 1.1e9), transcendentals=0, bytes_accessed=0)


def stored(shape, kind):
    return pltpu.HBM(shape, kind)


def from_store(*values):
    return tuple(pltpu.with_memory_space_constraint(v, pltpu.HBM) for v in values)


def vmem_limit(length):
    return pltpu.CompilerParams(vmem_limit_bytes=min(60, VMEM_BASE + length // 128) << 20)


def pad_to(values, axis, size):
    pads = [(0, 0)] * values.ndim
    pads[axis] = (0, size - values.shape[axis])
    return jnp.pad(values, pads)


def body(
    hidden_in,
    segment_ids,
    norm_gain,
    proj_inner,
    proj_shared,
    proj_step,
    conv_inner,
    conv_shared,
    step_bias,
    log_decay,
    skip_gain,
    gate_gain,
    proj_out,
    out_grad,
):
    dp_count = lax.axis_size("dp")
    dp_index = lax.axis_index("dp")
    rows = proj_inner.shape[0]
    length = segment_ids.shape[0]
    model_dim = hidden_in.shape[1]
    local_inner = proj_inner.shape[2]
    heads = proj_step.shape[1]
    state_size = proj_shared.shape[2]
    kernel_len = conv_inner.shape[0]
    shared_size = 2 * state_size
    full_inner = local_inner * lax.axis_size("tensor")
    width = -(-local_inner // (2 * LANES)) * 2 * LANES
    tap_block = conv_shared.shape[2]
    tap_count = kernel_len * 2 * tap_block
    stages, core, table = block_plan()
    groups, core_table = core_groups()
    blocks = length // TOKEN_BLOCK
    starts = token_starts(blocks)
    two = lax.axis_size("tensor") == 2

    chips = dp_count // 2
    hidden_own, hidden_other = both_halves(hidden_in)
    tap_rows = conv_shared.transpose(1, 2, 0).reshape(2 * tap_block, kernel_len)
    tap_rows = pad_to(tap_rows, 0, rows)
    packed = jnp.concatenate(
        [
            pad_to(proj_inner[:, 1, :], 1, width),
            proj_shared.reshape(rows, shared_size),
            pad_to(jnp.concatenate([proj_step, norm_gain[:, None], tap_rows], axis=1), 1, LANES),
        ],
        axis=1,
    )
    later = jnp.concatenate(
        [pad_to(proj_inner[:, 0, :], 1, width), pad_to(proj_out.T, 1, width)], axis=1
    )
    at = jnp.arange(model_dim)
    block, inside = at // rows, at % rows
    side, spot = inside // tap_block, inside % tap_block
    spread = jnp.where(side < 2, side * state_size + block * tap_block + spot, -1)
    spread = (spread[:, None] == jnp.arange(shared_size)[None, :]).astype(bf16)
    aux, segr = token_facts(segment_ids)
    heads_block = jnp.stack([step_bias, log_decay, skip_gain])
    heads_block = pad_to(pad_to(heads_block, 1, LANES), 0, 8)
    tapi = pad_to(conv_inner, 1, width)
    gain = pad_to(gate_gain[None], 1, width)

    later_all = jnp.broadcast_to(later[None], (chips,) + later.shape)
    later_all = later_all.reshape(chips * rows, 2 * width)
    low = packed
    for number, stage in enumerate(stages):
        if number == len(stages) - 1:
            low, later_all = lax.optimization_barrier((low, later_all))
        got = lax.ppermute(low, "dp", stage)
        if number == 0:
            got, aux, segr = lax.optimization_barrier((got, aux, segr))
        if number == 1:
            got, heads_block, tapi, spread, table, core_table = lax.optimization_barrier(
                (got, heads_block, tapi, spread, table, core_table)
            )
        if number == len(stages) - 1:
            got, gain = lax.optimization_barrier((got, gain))
        low = jnp.concatenate([low, got], axis=0)
    later_low = exchange(later_all, groups)
    low, hidden_other = lax.optimization_barrier((low, hidden_other))
    high = lax.ppermute(low, "dp", core)
    grad_own, grad_other = both_halves(after(out_grad, hidden_other))

    proj, praw, normed, normed_t, weights, taps, norm_scale = run_project(
        starts, table, hidden_own, hidden_other, spread, low, high, heads
    )
    norm_scale = norm_scale[:1]
    mixed, u, su, entry = run_forward(proj, praw, tapi, taps, heads_block, aux, segr)

    later_low, mixed, grad_other = lax.optimization_barrier((later_low, mixed, grad_other))
    later_high = lax.ppermute(later_low, "dp", core)
    gate, nog, grad_t, sums, later_rows = run_out_grad(
        starts, core_table, grad_own, grad_other, later_low, later_high, normed, mixed, gain
    )
    if two:
        more = swap(sums)
    else:
        sums = lax.psum(sums, "tensor")
        more = jnp.zeros_like(sums)
    normed_out, dgate, mixed_grad, gain_rows, gkeep, gsend = run_gated(
        core_table, gate, nog, mixed, sums, more, aux, gain, grad_t, normed_t, full_inner
    )
    ggot = lax.ppermute(gsend, "dp", core)
    send_start = starts[1:] if two else jnp.zeros((1,), jnp.int32)
    out_send, out_keep = run_out(send_start, normed_out, later_rows)
    ggot, out_send = lax.optimization_barrier((ggot, out_send))
    gsum = exchange((gkeep.astype(f32) + ggot.astype(f32)).astype(bf16), groups)
    out_other = swap(out_send) if two else None

    dproj, wkeep, wsend = run_backward(
        core_table,
        proj,
        praw,
        u,
        su,
        entry,
        mixed_grad,
        tapi,
        taps,
        heads_block,
        aux,
        segr,
        gain_rows,
        normed_t,
    )
    if two:
        wsend, gsum, out_other = lax.optimization_barrier((wsend, gsum, out_other))
    else:
        wsend, gsum = lax.optimization_barrier((wsend, gsum))
    wgot = lax.ppermute(wsend, "dp", core)
    grad_send = run_norm_grad(send_start, dgate, dproj, later_rows, weights, bf16)
    wgot, grad_send = lax.optimization_barrier((wgot, grad_send))
    grad_other = swap(grad_send) if two else None
    held = rows * chips
    wtotal = (wkeep.astype(f32) + wgot.astype(f32)).astype(bf16)
    wtotal = jnp.concatenate(
        [
            wtotal[:held].reshape(chips, rows, -1),
            jnp.broadcast_to(wtotal[None, held:], (chips, 8, wtotal.shape[1])),
        ],
        axis=1,
    ).reshape(chips * (rows + 8), -1)
    wtotal, dproj = lax.optimization_barrier((wtotal, dproj))
    wsum = exchange(wtotal, groups)
    keep_start = starts[:1] if two else jnp.full((1,), blocks // 2, jnp.int32)
    grad_keep = run_norm_grad(keep_start, dgate, dproj, later_rows, weights, f32)
    if two:
        out_half = out_keep.astype(f32) + out_other.astype(f32)
        own_grad = grad_keep + grad_other.astype(f32)
    else:
        out_half = add_halves(out_send, out_keep)
        own_grad = add_halves(grad_send, grad_keep)
    hidden_out = (hidden_in.astype(f32) + out_half).astype(bf16)
    gsum = sum_blocks(gsum, rows)
    out_sum = gsum[:, width : width + local_inner].T
    gate_sum = gsum[:, :local_inner]

    wsum = sum_blocks(wsum, rows + 8)
    small = wsum[rows:]
    wsum = wsum[:rows]
    conv_total = small[:kernel_len, :local_inner]
    gain_total = small[4, :local_inner]
    skip_total = small[0, width + shared_size : width + shared_size + heads]
    bias_total = small[1, width + shared_size : width + shared_size + heads]
    decay_total = small[2, width + shared_size : width + shared_size + heads]
    norm_row = jnp.sum(gate_sum * proj_inner[:, 0, :].astype(f32), axis=1) + jnp.sum(
        wsum * packed.astype(f32) * (jnp.arange(packed.shape[1]) < width + shared_size + heads),
        axis=1,
    )
    final = jnp.concatenate(
        [
            wsum[:, width : width + shared_size],
            small[:kernel_len, width : width + shared_size],
            pad_to(norm_row[None], 1, shared_size),
        ],
        axis=0,
    )
    final = total_over_tensor(pad_to(final, 0, rows + 8))
    shared_total = final[:rows].reshape(rows, 2, state_size)
    taps_total = lax.dynamic_slice_in_dim(
        final[rows : rows + kernel_len].reshape(kernel_len, 2, state_size),
        dp_index * tap_block,
        tap_block,
        axis=2,
    )
    norm_total = final[rows + kernel_len, :rows] / norm_gain.astype(f32)
    inner_sum = jnp.stack([gate_sum, wsum[:, :local_inner]], axis=1)
    step_sum = wsum[:, width + shared_size : width + shared_size + heads]

    own = hidden_in.astype(f32)
    own_inv = lax.rsqrt(jnp.mean(own * own, axis=-1, keepdims=True) + epsilon)
    own_unit = own * own_inv
    scaled_in = own_grad * norm_scale
    hidden_grad = own_inv * (
        scaled_in - own_unit * jnp.mean(scaled_in * own_unit, axis=-1, keepdims=True)
    ) + out_grad.astype(f32)
    return (
        hidden_out,
        hidden_grad,
        norm_total,
        inner_sum,
        shared_total,
        step_sum,
        conv_total,
        taps_total,
        bias_total,
        decay_total,
        skip_total,
        gain_total,
        out_sum,
    )


def solution(mesh):
    in_specs = (
        P(("dp", "tensor"), None),
        P("dp"),
        P("dp"),
        P("dp", None, "tensor"),
        P("dp", None, None),
        P("dp", "tensor"),
        P(None, "tensor"),
        P(None, None, "dp"),
        P("tensor"),
        P("tensor"),
        P("tensor"),
        P("tensor"),
        P("tensor", "dp"),
        P(("dp", "tensor"), None),
    )
    out_specs = (
        P(("dp", "tensor"), None),
        P(("dp", "tensor"), None),
        P("dp"),
        P("dp", None, "tensor"),
        P("dp", None, None),
        P("dp", "tensor"),
        P(None, "tensor"),
        P(None, None, "dp"),
        P("tensor"),
        P("tensor"),
        P("tensor"),
        P("tensor"),
        P("tensor", "dp"),
    )
    return jax.shard_map(body, mesh=mesh, in_specs=in_specs, out_specs=out_specs, check_vma=False)
```

```python
from functools import partial

import jax
import jax.numpy as jnp
import numpy as np
from jax import lax
from jax.experimental import pallas as pl
from jax.experimental.pallas import tpu as pltpu
from jax.sharding import PartitionSpec as P

HEAD_DIM = 64
CHUNK = 128
LANES = 128
TOKEN_BLOCK = 256
VMEM_BASE = 16
ROW_TILE = 64
epsilon = 1e-05
f32 = jnp.float32
bf16 = jnp.bfloat16
highest = lax.Precision.HIGHEST


def dot_nn(a, b):
    return lax.dot_general(a, b, (((1,), (0,)), ((), ())), preferred_element_type=f32)


def dot_nt(a, b):
    return lax.dot_general(a, b, (((1,), (1,)), ((), ())), preferred_element_type=f32)


def dot_tn(a, b):
    return lax.dot_general(a, b, (((0,), (0,)), ((), ())), preferred_element_type=f32)


def dot_exact(a, b):
    return lax.dot_general(
        a, b, (((1,), (0,)), ((), ())), preferred_element_type=f32, precision=highest
    )


def dot_split(a, b):
    high = a.astype(bf16)
    rest = (a - high.astype(f32)).astype(bf16)
    return dot_nn(high, b) + dot_nn(rest, b)


def two_parts(values):
    high = values.astype(bf16)
    rest = (values - high.astype(f32)).astype(bf16)
    return jnp.concatenate([high, rest], axis=1)


def spread_matrix(shape, size):
    rows = lax.rem(lax.broadcasted_iota(jnp.int32, shape, 0), LANES)
    return (rows == lax.broadcasted_iota(jnp.int32, shape, 1) // size).astype(bf16)


def sigmoid(v):
    return 1.0 / (1.0 + jnp.exp(-v))


def softplus(v):
    return jnp.maximum(v, 0.0) + jnp.log1p(jnp.exp(-jnp.abs(v)))


def halves(lane_low, values, head):
    return jnp.where(lane_low, values[:, head : head + 1], values[:, head + 1 : head + 2])


def head_sides():
    low = (lax.broadcasted_iota(jnp.int32, (CHUNK, LANES), 1) < HEAD_DIM).astype(f32)
    return low.astype(bf16), (1.0 - low).astype(bf16)


def by_head(values, sides):
    return jnp.concatenate([values * sides[0], values * sides[1]], axis=0)


def back_shift(window, offset):
    return pltpu.roll(window, offset, 0)[8:, :]


def ahead_shift(window, offset):
    rows = window.shape[0]
    return pltpu.roll(window, rows - offset, 0)[: rows - 8, :]


def conv_rows(window, taps, aux):
    total = taps[3:4, :] * window[8:, :]
    for offset in range(1, 4):
        total = total + taps[3 - offset : 4 - offset, :] * (
            back_shift(window, offset) * aux[:, offset : offset + 1]
        )
    return total


def forward_kernel(
    proj_ref,
    step_ref,
    tapi_ref,
    taps_ref,
    heads_ref,
    aux_ref,
    segr_ref,
    mixed_ref,
    u_ref,
    su_ref,
    entry_ref,
    state_ref,
    carry_ref,
    scarry_ref,
    xw_ref,
    channels_ref,
    columns_ref,
):
    width = mixed_ref.shape[1]
    pairs = width // LANES
    shared_size = su_ref.shape[1]
    state_size = shared_size // 2
    chunk = pl.program_id(0)

    @pl.when(chunk == 0)
    def _():
        for ref in (state_ref, carry_ref, scarry_ref):
            ref[...] = jnp.zeros_like(ref)
        channels_ref[...] = spread_matrix(channels_ref.shape, HEAD_DIM)
        columns_ref[...] = spread_matrix(columns_ref.shape, CHUNK)

    rows = lax.broadcasted_iota(jnp.int32, (CHUNK, CHUNK), 0)
    cols = lax.broadcasted_iota(jnp.int32, (CHUNK, CHUNK), 1)
    lower = rows >= cols
    summing = lower.astype(f32)
    lane_low = lax.broadcasted_iota(jnp.int32, (CHUNK, LANES), 1) < HEAD_DIM
    sides = head_sides()
    bias = heads_ref[0:1, :]
    rate = -jnp.exp(heads_ref[1:2, :])
    skips = heads_ref[2:3, :]
    aux = aux_ref[...]
    live = aux[:, 7:8]
    same = lower & (aux[:, 0:1] == segr_ref[pl.ds(chunk, 1), :])
    shared_now = proj_ref[:, width:].astype(f32)
    su = conv_rows(jnp.concatenate([scarry_ref[...], shared_now], axis=0), taps_ref[...], aux)
    scarry_ref[...] = shared_now[CHUNK - 8 :, :]
    su_ref[...] = su
    shared = (su * sigmoid(su)).astype(bf16)
    b_rows = shared[:, :state_size]
    c_rows = shared[:, state_size:]
    scores = jnp.where(same, dot_nt(c_rows, b_rows), 0.0)
    step = softplus(step_ref[...] + bias) * live
    decay = dot_exact(summing, step * rate)
    decay_parts = two_parts(decay)
    decay = decay_parts[:, :LANES].astype(f32) + decay_parts[:, LANES:].astype(f32)
    decay_wide = dot_nn(decay_parts, columns_ref[...])
    decay_t = decay.T
    last = decay[CHUNK - 1 :, :]
    entry_scale = jnp.exp(decay) * aux[:, 8:9]
    end_scale = jnp.exp(last - decay) * aux[:, 9:10]
    keep = jnp.exp(last) * aux[:1, 10:11]
    step_wide = dot_nn(two_parts(step), channels_ref[...])
    entry_wide = dot_nn(two_parts(entry_scale), channels_ref[...])
    end_wide = dot_nn(two_parts(end_scale), channels_ref[...])
    state = state_ref[...]
    state_low = state.astype(bf16)
    entry_ref[...] = state_low[None]
    past = dot_nn(c_rows, state_low)
    for pair in range(pairs):
        lanes = slice(pair * LANES, (pair + 1) * LANES)
        head = 2 * pair
        now = proj_ref[:, lanes].astype(f32)
        window = jnp.concatenate([carry_ref[:, lanes], now], axis=0)
        carry_ref[:, lanes] = now[CHUNK - 8 :, :]
        u = conv_rows(window, tapi_ref[:, lanes].astype(f32), aux)
        u_ref[:, lanes] = u.astype(bf16)
        x = u * sigmoid(u)
        scaled = x * step_wide[:, lanes]
        mixing = jnp.concatenate(
            [
                (
                    scores
                    * jnp.exp(jnp.minimum(decay_wide[:, h * CHUNK : (h + 1) * CHUNK] - decay_t[h : h + 1, :], 0.0))
                ).astype(bf16)
                for h in (head, head + 1)
            ],
            axis=1,
        )
        stacked = by_head(scaled.astype(bf16), sides)
        inside = dot_nn(mixing, stacked)
        xw_ref[:, lanes] = (scaled * end_wide[:, lanes]).astype(bf16)
        mixed = (
            inside
            + past[:, lanes] * entry_wide[:, lanes]
            + halves(lane_low[:1], skips, head) * x
        ) * live
        mixed_ref[:, lanes] = mixed.astype(bf16)
        state_ref[:, lanes] = state[:, lanes] * halves(lane_low[:1], keep, head)
    state_ref[...] += dot_tn(b_rows, xw_ref[...])


def token_scales(sums, full_inner):
    columns = sums.T
    inv = lax.rsqrt(columns[:, 0:1] / full_inner + epsilon)
    return inv, inv * columns[:, 1:2] / full_inner


def silu_slope(v, s):
    return s * (1.0 + v * (1.0 - s))


def backward_kernel(
    table_ref,
    proj_ref,
    praw_ref,
    u_ref,
    su_ref,
    entry_ref,
    grad_ref,
    tapi_ref,
    taps_ref,
    heads_ref,
    aux_ref,
    segr_ref,
    gain_ref,
    turned_ref,
    dproj_ref,
    keep_ref,
    send_ref,
    wide_ref,
    shared_ref,
    small_ref,
    total_ref,
    grads_ref,
    held_ref,
    sem_ref,
    state_ref,
    ahead_ref,
    sahead_ref,
    xw_ref,
    ge_ref,
    row_ref,
    proda_ref,
    prodb_ref,
    channels_ref,
    columns_ref,
):
    width = u_ref.shape[1]
    chunks = pl.num_programs(0)
    pairs = width // LANES
    shared_size = su_ref.shape[1]
    state_size = shared_size // 2
    shared_cols = slice(width, width + shared_size)
    step_cols = slice(width + shared_size, width + shared_size + LANES)
    chunk = chunks - 1 - pl.program_id(0)
    copy = pltpu.make_async_copy(turned_ref, held_ref, sem_ref.at[0])

    @pl.when(pl.program_id(0) == 0)
    def _():
        copy.start()
        channels_ref[...] = spread_matrix(channels_ref.shape, HEAD_DIM)
        columns_ref[...] = spread_matrix(columns_ref.shape, CHUNK)
        for ref in (state_ref, ahead_ref, sahead_ref, row_ref, wide_ref, shared_ref):
            ref[...] = jnp.zeros_like(ref)

    rows = lax.broadcasted_iota(jnp.int32, (CHUNK, CHUNK), 0)
    cols = lax.broadcasted_iota(jnp.int32, (CHUNK, CHUNK), 1)
    upper = rows <= cols
    summing = (rows >= cols).astype(f32)
    unsumming = upper.astype(f32)
    last_row = (lax.broadcasted_iota(jnp.int32, (CHUNK, LANES), 0) == CHUNK - 1).astype(f32)
    lane_ids = lax.broadcasted_iota(jnp.int32, (CHUNK, LANES), 1)
    lane_low = lane_ids < HEAD_DIM
    sides = head_sides()
    bias = heads_ref[0:1, :]
    rate = -jnp.exp(heads_ref[1:2, :])
    skips = heads_ref[2:3, :]
    place = (
        lax.broadcasted_iota(jnp.int32, (width, LANES), 0) // HEAD_DIM
        == lax.broadcasted_iota(jnp.int32, (width, LANES), 1)
    ).astype(bf16)

    aux = aux_ref[...]
    live = aux[:, 7:8]
    same = upper & (aux[:, 0:1] == segr_ref[pl.ds(chunk, 1), :])
    su = su_ref[...]
    su_sig = sigmoid(su)
    shared = (su * su_sig).astype(bf16)
    b_rows = shared[:, :state_size]
    c_rows = shared[:, state_size:]
    scores = jnp.where(same, dot_nt(b_rows, c_rows), 0.0)
    pre = praw_ref[...] + bias
    step = softplus(pre) * live
    decay = dot_exact(summing, step * rate)
    decay_parts = two_parts(decay)
    decay = decay_parts[:, :LANES].astype(f32) + decay_parts[:, LANES:].astype(f32)
    decay_wide = dot_nn(decay_parts, columns_ref[...])
    decay_t = decay.T
    last = decay[CHUNK - 1 :, :]
    entry_scale = jnp.exp(decay) * aux[:, 8:9]
    end_scale = jnp.exp(last - decay) * aux[:, 9:10]
    keep = jnp.exp(last) * aux[:1, 10:11]
    step_wide = dot_nn(two_parts(step), channels_ref[...])
    entry_wide = dot_nn(two_parts(entry_scale), channels_ref[...])
    end_wide = dot_nn(two_parts(end_scale), channels_ref[...])
    entry = entry_ref[0]
    dstate = state_ref[...]
    dstate_low = dstate.astype(bf16)
    past = dot_nn(c_rows, entry)
    bds = dot_nn(b_rows, dstate_low)
    here = pl.ds(pl.multiple_of(chunk * CHUNK, CHUNK), CHUNK)
    score_grad = jnp.zeros((CHUNK, CHUNK), f32)
    col_part = jnp.zeros((CHUNK, LANES), f32)
    for pair in range(pairs):
        lanes = slice(pair * LANES, (pair + 1) * LANES)
        head = 2 * pair
        g_low = grad_ref[:, lanes]
        g = g_low.astype(f32)
        u = u_ref[:, lanes].astype(f32)
        u_sig = sigmoid(u)
        x = u * u_sig
        step_c = step_wide[:, lanes]
        scaled = x * step_c
        stacked = by_head(scaled.astype(bf16), sides)
        dmix = dot_nt(stacked, g_low)
        mixing = []
        for k, h in enumerate((head, head + 1)):
            decays = jnp.exp(jnp.minimum(decay_t[h : h + 1, :] - decay_wide[:, h * CHUNK : (h + 1) * CHUNK], 0.0))
            dmix_h = dmix[k * CHUNK : (k + 1) * CHUNK, :]
            score_grad = score_grad + dmix_h * decays
            mixing_h = scores * decays
            mixing.append(mixing_h.astype(bf16))
            both = mixing_h * dmix_h
            col_part = jnp.where(lane_ids == h, jnp.sum(both, axis=1, keepdims=True), col_part)
            row_ref[h : h + 1, :] = jnp.sum(both, axis=0, keepdims=True)
        g_stacked = by_head(g_low, sides)
        end_c = end_wide[:, lanes]
        entry_c = entry_wide[:, lanes]
        keep_c = halves(lane_low[:1], keep, head)
        from_state = end_c * bds[:, lanes]
        dscaled = dot_nn(jnp.concatenate(mixing, axis=1), g_stacked) + from_state
        xw_ref[:, lanes] = (scaled * end_c).astype(bf16)
        q = scaled * from_state
        ge = g * entry_c
        ge_ref[:, lanes] = ge.astype(bf16)
        dstate_p = dstate[:, lanes]
        tail = jnp.sum(q, axis=0, keepdims=True) + keep_c * jnp.sum(
            dstate_p * entry[:, lanes].astype(f32), axis=0, keepdims=True
        )
        proda_ref[:, lanes] = (x * dscaled).astype(bf16)
        prodb_ref[:, lanes] = ge * past[:, lanes] - q + last_row * tail
        state_ref[:, lanes] = dstate_p * keep_c
        dx = step_c * dscaled + halves(lane_low[:1], skips, head) * g
        du = dx * silu_slope(u, u_sig)
        window = jnp.concatenate([du, ahead_ref[:, lanes]], axis=0)
        ahead_ref[:, lanes] = du[:8, :]
        cin = proj_ref[:, lanes].astype(f32)
        taps = tapi_ref[:, lanes].astype(f32)
        dcin = taps[3:4, :] * du
        wide_ref[3:4, lanes] += jnp.sum(cin * du, axis=0, keepdims=True)
        for offset in range(1, 4):
            moved = ahead_shift(window, offset) * aux[:, 3 + offset : 4 + offset]
            dcin = dcin + taps[3 - offset : 4 - offset, :] * moved
            wide_ref[3 - offset : 4 - offset, lanes] += jnp.sum(
                cin * moved, axis=0, keepdims=True
            )
        dcin = dcin.astype(bf16)
        dproj_ref[:, lanes] = dcin
        grads_ref[here, lanes] = dcin
        wide_ref[5:6, lanes] += jnp.sum(g * x, axis=0, keepdims=True)
    score_low = jnp.where(same, score_grad, 0.0).astype(bf16)
    ge_all = ge_ref[...]
    db = dot_nn(score_low, c_rows) + dot_nt(xw_ref[...], dstate_low)
    dc = dot_tn(score_low, b_rows) + dot_nt(ge_all, entry)
    state_ref[...] += dot_tn(c_rows, ge_all)
    ds = jnp.concatenate([db, dc], axis=1) * silu_slope(su, su_sig)
    window = jnp.concatenate([ds, sahead_ref[...]], axis=0)
    sahead_ref[...] = ds[:8, :]
    taps = taps_ref[...]
    sin = proj_ref[:, shared_cols].astype(f32)
    dsin = taps[3:4, :] * ds
    shared_ref[3:4, :] += jnp.sum(sin * ds, axis=0, keepdims=True)
    for offset in range(1, 4):
        moved = ahead_shift(window, offset) * aux[:, 3 + offset : 4 + offset]
        dsin = dsin + taps[3 - offset : 4 - offset, :] * moved
        shared_ref[3 - offset : 4 - offset, :] += jnp.sum(sin * moved, axis=0, keepdims=True)
    dsin = dsin.astype(bf16)
    dproj_ref[:, shared_cols] = dsin
    grads_ref[here, shared_cols] = dsin
    ddecay = row_ref[...].T - col_part + dot_split(prodb_ref[...], place)
    dlog = dot_exact(unsumming, ddecay)
    dstep = (dot_nn(proda_ref[...], place) + rate * dlog) * live * sigmoid(pre)
    dproj_ref[:, step_cols] = dstep.astype(bf16)
    grads_ref[here, step_cols] = dstep.astype(bf16)
    wide_ref[6:7, :LANES] += jnp.sum(dstep, axis=0, keepdims=True)
    wide_ref[6:7, LANES : 2 * LANES] += jnp.sum(step * dlog, axis=0, keepdims=True) * rate

    @pl.when(chunk == 0)
    def _():
        small_ref[...] = jnp.zeros_like(small_ref)
        small_ref[:4, :width] = wide_ref[:4, :]
        small_ref[:4, width : width + shared_size] = shared_ref[:4, :]
        skip_row = dot_split(wide_ref[...], place)[5:6, :]
        small_ref[0:1, step_cols] = skip_row
        small_ref[1:2, step_cols] = wide_ref[6:7, :LANES]
        small_ref[2:3, step_cols] = wide_ref[6:7, LANES : 2 * LANES]
        small_ref[4:5, :width] = jnp.sum(gain_ref[...], axis=0, keepdims=True)
        copy.wait()
        held = keep_ref.shape[0] - 8
        keep_ref[held:, :] = small_ref[...].astype(bf16)
        send_ref[held:, :] = small_ref[...].astype(bf16)
        tile = total_ref.shape[1]
        for at in range(0, width + shared_size + LANES, tile):
            total_ref[...] = dot_nn(held_ref[...], grads_ref[:, at : at + tile])
            store_blocks(table_ref, total_ref, keep_ref, send_ref, slice(at, at + tile))


def facts_kernel(seg_ref, aux_ref, segr_ref):
    seg = seg_ref[...].astype(f32)
    chunks = seg.shape[0]
    segr_ref[...] = seg
    none = jnp.full((1, CHUNK), -1.0, f32)
    before = jnp.concatenate([none, seg[: chunks - 1]], axis=0) if chunks > 1 else none
    behind = jnp.concatenate([seg[1:], none], axis=0) if chunks > 1 else none
    lane = lax.broadcasted_iota(jnp.int32, seg.shape, 1)
    facts = [seg]
    for offset in range(1, 4):
        earlier = jnp.where(
            lane >= offset, pltpu.roll(seg, offset, 1), pltpu.roll(before, offset, 1)
        )
        facts.append((earlier == seg).astype(f32))
    for offset in range(1, 4):
        later = jnp.where(
            lane < CHUNK - offset,
            pltpu.roll(seg, CHUNK - offset, 1),
            pltpu.roll(behind, CHUNK - offset, 1),
        )
        facts.append((later == seg).astype(f32))
    last = jnp.broadcast_to(seg[:, CHUNK - 1 :], seg.shape)
    prior = jnp.broadcast_to(before[:, CHUNK - 1 :], seg.shape)
    facts.append((seg != 0.0).astype(f32))
    facts.append((seg == prior).astype(f32))
    facts.append((seg == last).astype(f32))
    facts.append((last == prior).astype(f32))
    empty = jnp.zeros((LANES - len(facts), CHUNK), f32)
    for chunk in range(chunks):
        rows = jnp.concatenate([f[chunk : chunk + 1, :] for f in facts] + [empty], axis=0)
        aux_ref[chunk * CHUNK : (chunk + 1) * CHUNK, :] = rows.T[:, : aux_ref.shape[1]]


def token_facts(segments):
    length = segments.shape[0]
    chunks = length // CHUNK
    return pl.pallas_call(
        facts_kernel,
        out_shape=(
            jax.ShapeDtypeStruct((length, 16), f32),
            jax.ShapeDtypeStruct((chunks, CHUNK), f32),
        ),
        name="token_facts",
        cost_estimate=cost(2),
        compiler_params=vmem_limit(length),
    )(segments.reshape(chunks, CHUNK))


def chunk_spec(columns, last):
    if last is None:
        return pl.BlockSpec((CHUNK, columns), lambda i: (i, 0))
    return pl.BlockSpec((CHUNK, columns), lambda i: (last - i, 0))


def fixed_spec(values):
    zeros = (0,) * values.ndim
    return pl.BlockSpec(values.shape, lambda i: zeros)


def run_forward(proj, praw, tapi, taps, heads, aux, segr):
    length = proj.shape[0]
    width = tapi.shape[1]
    shared_size = taps.shape[1]
    state_size = shared_size // 2
    chunks = length // CHUNK
    proj, praw = from_store(proj, praw)
    return pl.pallas_call(
        forward_kernel,
        grid=(chunks,),
        in_specs=[
            chunk_spec(proj.shape[1], None),
            chunk_spec(LANES, None),
            fixed_spec(tapi),
            fixed_spec(taps),
            fixed_spec(heads),
            chunk_spec(aux.shape[1], None),
            fixed_spec(segr),
        ],
        out_specs=[
            chunk_spec(width, None),
            chunk_spec(width, None),
            chunk_spec(shared_size, None),
            pl.BlockSpec((1, state_size, width), lambda i: (i, 0, 0)),
        ],
        out_shape=(
            stored((length, width), bf16),
            stored((length, width), bf16),
            stored((length, shared_size), f32),
            stored((chunks, state_size, width), bf16),
        ),
        scratch_shapes=[
            pltpu.VMEM((state_size, width), f32),
            pltpu.VMEM((8, width), f32),
            pltpu.VMEM((8, shared_size), f32),
            pltpu.VMEM((CHUNK, width), bf16),
            pltpu.VMEM((2 * LANES, width), bf16),
            pltpu.VMEM((2 * LANES, width // HEAD_DIM * CHUNK), bf16),
        ],
        name="scan_forward",
        cost_estimate=cost(3),
        compiler_params=vmem_limit(length),
    )(proj, praw, tapi, taps, heads, aux, segr)


def run_backward(
    table, proj, praw, u, su, entry, grad, tapi, taps, heads, aux, segr, gain_rows, turned
):
    length, width = u.shape
    shared_size = su.shape[1]
    state_size = shared_size // 2
    model_dim = turned.shape[0]
    chunks = length // CHUNK
    last = chunks - 1
    columns = width + shared_size + LANES
    kept = model_dim // 2 + 8
    sds = jax.ShapeDtypeStruct
    proj, praw, u, su, entry, grad, turned = from_store(proj, praw, u, su, entry, grad, turned)

    def back(size):
        return pl.BlockSpec((CHUNK, size), lambda i, t: (last - i, 0))

    def fixed(shape):
        return pl.BlockSpec(shape, lambda i, t: (0, 0))

    return pl.pallas_call(
        backward_kernel,
        grid_spec=pltpu.PrefetchScalarGridSpec(
            num_scalar_prefetch=1,
            grid=(chunks,),
            in_specs=[
                back(proj.shape[1]),
                back(LANES),
                back(width),
                back(shared_size),
                pl.BlockSpec((1, state_size, width), lambda i, t: (last - i, 0, 0)),
                back(width),
                fixed(tapi.shape),
                fixed(taps.shape),
                fixed(heads.shape),
                back(aux.shape[1]),
                fixed(segr.shape),
                fixed(gain_rows.shape),
                pl.BlockSpec(memory_space=pl.ANY),
            ],
            out_specs=[
                back(columns),
                fixed((kept, columns)),
                fixed((kept, columns)),
            ],
            scratch_shapes=[
                pltpu.VMEM((8, width), f32),
                pltpu.VMEM((8, shared_size), f32),
                pltpu.VMEM((8, columns), f32),
                pltpu.VMEM((model_dim, column_tile(columns)), f32),
                pltpu.VMEM((length, columns), bf16),
                pltpu.VMEM((model_dim, length), bf16),
                pltpu.SemaphoreType.DMA((1,)),
                pltpu.VMEM((state_size, width), f32),
                pltpu.VMEM((8, width), f32),
                pltpu.VMEM((8, shared_size), f32),
                pltpu.VMEM((CHUNK, width), bf16),
                pltpu.VMEM((CHUNK, width), bf16),
                pltpu.VMEM((LANES, CHUNK), f32),
                pltpu.VMEM((CHUNK, width), bf16),
                pltpu.VMEM((CHUNK, width), f32),
                pltpu.VMEM((2 * LANES, width), bf16),
                pltpu.VMEM((2 * LANES, width // HEAD_DIM * CHUNK), bf16),
            ],
        ),
        out_shape=(
            stored((length, columns), bf16),
            stored((kept, columns), bf16),
            stored((kept, columns), bf16),
        ),
        name="scan_backward",
        cost_estimate=cost(36),
        compiler_params=vmem_limit(length),
    )(table, proj, praw, u, su, entry, grad, tapi, taps, heads, aux, segr, gain_rows, turned)


def block_plan():
    count = lax.axis_size("dp")
    bits = []
    bit = count // 2
    while bit > 1:
        bits.append(bit)
        bit //= 2
    mixed = bits[:-2] + bits[-2:][::-1]
    by_core = (bits, mixed)
    stages = []
    for stage in range(len(bits)):
        stages.append([(i, i ^ by_core[i % 2][stage]) for i in range(count)])
    core = [(i, i ^ 1) for i in range(count)]
    device = np.zeros((count, count), np.int32)
    for own in range(count):
        for spot in range(count):
            other = own ^ 1 if spot >= count // 2 else own
            for stage, bit in enumerate(by_core[other % 2]):
                if (spot >> stage) & 1:
                    other ^= bit
            device[own, spot] = other
    table = jnp.asarray(device)[lax.axis_index("dp")]
    return stages, core, table


def core_groups():
    count = lax.axis_size("dp")
    groups = [list(range(side, count, 2)) for side in range(2)]
    return groups, jnp.asarray(
        [groups[0] + groups[1], groups[1] + groups[0]], jnp.int32
    )[lax.axis_index("dp") % 2]


def exchange(blocks, groups):
    return lax.all_to_all(
        blocks, "dp", 0, 0, axis_index_groups=groups, tiled=True
    )


def sum_blocks(blocks, rows):
    return jnp.sum(blocks.reshape(-1, rows, blocks.shape[1]).astype(f32), axis=0)


def swap(values):
    return lax.ppermute(values, "tensor", [(0, 1), (1, 0)])


def total_over_tensor(values):
    if lax.axis_size("tensor") == 2:
        return values + swap(values)
    return lax.psum(values, "tensor")


def both_halves(own):
    if lax.axis_size("tensor") == 2:
        return own, swap(own)
    whole = lax.all_gather(own, "tensor", axis=0, tiled=True)
    return whole, whole


def token_starts(blocks):
    if lax.axis_size("tensor") == 2:
        index = lax.axis_index("tensor")
        return jnp.stack([index * (blocks // 2), (1 - index) * (blocks // 2)]).astype(jnp.int32)
    return jnp.zeros((2,), jnp.int32)


def add_halves(send, keep):
    if lax.axis_size("tensor") == 2:
        return keep.astype(f32) + swap(send).astype(f32)
    whole = jnp.concatenate([send.astype(bf16), keep.astype(bf16)], axis=0)
    return lax.psum_scatter(whole, "tensor", scatter_dimension=0, tiled=True).astype(f32)


def own_block(step, starts, own_blocks):
    return jnp.clip(step - starts[0], 0, own_blocks - 1)


def other_block(step, starts, own_blocks):
    return jnp.clip(step - starts[1], 0, own_blocks - 1)


def place_blocks(table_ref, low_ref, high_ref, whole_ref, sem_ref):
    count = table_ref.shape[0]
    rows = whole_ref.shape[0] // count
    copies = []
    for spot in range(count):
        source = low_ref if spot < count // 2 else high_ref
        where = pl.multiple_of(table_ref[spot] * rows, rows)
        copies.append(
            pltpu.make_async_copy(
                source.at[pl.ds((spot % (count // 2)) * rows, rows), :],
                whole_ref.at[pl.ds(where, rows), :],
                sem_ref.at[spot],
            )
        )
    for copy in copies:
        copy.start()
    for copy in copies:
        copy.wait()


def project_kernel(
    starts_ref,
    table_ref,
    own_ref,
    other_ref,
    spread_ref,
    low_ref,
    high_ref,
    proj_ref,
    step_ref,
    normed_ref,
    turned_ref,
    whole_ref,
    taps_ref,
    scale_ref,
    weights_ref,
    sem_ref,
    *,
    own_blocks,
    heads,
):
    step = pl.program_id(0)
    model_dim, columns = weights_ref.shape
    store = pltpu.make_async_copy(weights_ref, whole_ref, sem_ref.at[table_ref.shape[0]])

    @pl.when(step == pl.num_programs(0) - 1)
    def _():
        store.wait()

    @pl.when(step == 0)
    def _():
        place_blocks(table_ref, low_ref, high_ref, weights_ref, sem_ref)
        store.start()
        extra = weights_ref[:, columns - LANES :].astype(f32).T
        scale_ref[...] = jnp.broadcast_to(extra[heads : heads + 1, :], scale_ref.shape)
        taps = extra[heads + 1 : heads + 5, :]
        taps = jnp.concatenate([taps, jnp.zeros_like(taps)], axis=0).astype(bf16)
        taps_ref[...] = dot_nn(taps, spread_ref[...])

    mine = (step >= starts_ref[0]) & (step < starts_ref[0] + own_blocks)
    tokens = jnp.where(mine, own_ref[...].astype(f32), other_ref[...].astype(f32))
    inv = lax.rsqrt(jnp.mean(tokens * tokens, axis=-1, keepdims=True) + epsilon)
    normed = (tokens * inv * scale_ref[:1, :]).astype(bf16)
    normed_ref[...] = normed
    turned_ref[...] = normed.T
    proj = dot_nn(normed, weights_ref[...])
    proj_ref[...] = proj[:, : columns - LANES].astype(bf16)
    step_ref[...] = proj[:, columns - LANES :]


def run_project(starts, table, own, other, spread, low, high, heads):
    own_rows, model_dim = own.shape
    columns = low.shape[1]
    own_blocks = own_rows // TOKEN_BLOCK
    blocks = own_blocks * (2 if lax.axis_size("tensor") == 2 else 1)
    length = blocks * TOKEN_BLOCK
    sds = jax.ShapeDtypeStruct
    own, other, low, high = from_store(own, other, low, high)
    return pl.pallas_call(
        partial(project_kernel, own_blocks=own_blocks, heads=heads),
        grid_spec=pltpu.PrefetchScalarGridSpec(
            num_scalar_prefetch=2,
            grid=(blocks,),
            in_specs=[
                pl.BlockSpec(
                    (TOKEN_BLOCK, model_dim), lambda i, s, t: (own_block(i, s, own_blocks), 0)
                ),
                pl.BlockSpec(
                    (TOKEN_BLOCK, model_dim), lambda i, s, t: (other_block(i, s, own_blocks), 0)
                ),
                pl.BlockSpec(spread.shape, lambda i, s, t: (0, 0)),
                pl.BlockSpec(memory_space=pl.ANY),
                pl.BlockSpec(memory_space=pl.ANY),
            ],
            out_specs=[
                pl.BlockSpec((TOKEN_BLOCK, columns - LANES), lambda i, s, t: (i, 0)),
                pl.BlockSpec((TOKEN_BLOCK, LANES), lambda i, s, t: (i, 0)),
                pl.BlockSpec((TOKEN_BLOCK, model_dim), lambda i, s, t: (i, 0)),
                pl.BlockSpec((model_dim, TOKEN_BLOCK), lambda i, s, t: (0, i)),
                pl.BlockSpec(memory_space=pl.ANY),
                pl.BlockSpec((8, spread.shape[1]), lambda i, s, t: (0, 0)),
                pl.BlockSpec((8, model_dim), lambda i, s, t: (0, 0)),
            ],
            scratch_shapes=[
                pltpu.VMEM((model_dim, columns), bf16),
                pltpu.SemaphoreType.DMA((table.shape[0] + 1,)),
            ],
        ),
        out_shape=(
            stored((length, columns - LANES), bf16),
            stored((length, LANES), f32),
            stored((length, model_dim), bf16),
            stored((model_dim, length), bf16),
            stored((model_dim, columns), bf16),
            sds((8, spread.shape[1]), f32),
            sds((8, model_dim), f32),
        ),
        name="norm_project",
        cost_estimate=cost(2),
        compiler_params=vmem_limit(length),
    )(starts, table, own, other, spread, low, high)


def token_sum(values):
    total = values[:, :LANES]
    for at in range(LANES, values.shape[1], LANES):
        total = total + values[:, at : at + LANES]
    return jnp.sum(total.T, axis=0, keepdims=True)


def out_grad_kernel(
    starts_ref,
    table_ref,
    own_ref,
    other_ref,
    low_ref,
    high_ref,
    normed_ref,
    mixed_ref,
    gain_ref,
    gate_ref,
    nog_ref,
    turned_ref,
    sums_ref,
    whole_ref,
    weights_ref,
    sem_ref,
    *,
    own_blocks,
):
    step = pl.program_id(0)
    width = mixed_ref.shape[1]
    store = pltpu.make_async_copy(weights_ref, whole_ref, sem_ref.at[table_ref.shape[0]])

    @pl.when(step == 0)
    def _():
        place_blocks(table_ref, low_ref, high_ref, weights_ref, sem_ref)
        store.start()

    @pl.when(step == pl.num_programs(0) - 1)
    def _():
        store.wait()

    mine = (step >= starts_ref[0]) & (step < starts_ref[0] + own_blocks)
    tokens = jnp.where(mine, own_ref[...].astype(f32), other_ref[...].astype(f32)).astype(bf16)
    turned_ref[...] = tokens.T
    gate = dot_nn(normed_ref[...], weights_ref[:, :width])
    gate_ref[...] = gate.astype(bf16)
    nog = dot_nn(tokens, weights_ref[:, width:])
    nog_ref[...] = nog.astype(bf16)
    gated = mixed_ref[...].astype(f32) * (gate * sigmoid(gate))
    sums_ref[...] = jnp.concatenate(
        [
            token_sum(gated * gated),
            token_sum(nog * gain_ref[...].astype(f32) * gated),
            jnp.zeros((6, TOKEN_BLOCK), f32),
        ],
        axis=0,
    )


def run_out_grad(starts, table, own, other, low, high, normed, mixed, gain):
    own_rows, model_dim = own.shape
    length, width = mixed.shape
    own_blocks = own_rows // TOKEN_BLOCK
    blocks = length // TOKEN_BLOCK
    sds = jax.ShapeDtypeStruct
    own, other, normed, mixed, low, high = from_store(own, other, normed, mixed, low, high)
    return pl.pallas_call(
        partial(out_grad_kernel, own_blocks=own_blocks),
        grid_spec=pltpu.PrefetchScalarGridSpec(
            num_scalar_prefetch=2,
            grid=(blocks,),
            in_specs=[
                pl.BlockSpec(
                    (TOKEN_BLOCK, model_dim), lambda i, s, t: (own_block(i, s, own_blocks), 0)
                ),
                pl.BlockSpec(
                    (TOKEN_BLOCK, model_dim), lambda i, s, t: (other_block(i, s, own_blocks), 0)
                ),
                pl.BlockSpec(memory_space=pl.ANY),
                pl.BlockSpec(memory_space=pl.ANY),
                pl.BlockSpec((TOKEN_BLOCK, model_dim), lambda i, s, t: (i, 0)),
                pl.BlockSpec((TOKEN_BLOCK, width), lambda i, s, t: (i, 0)),
                pl.BlockSpec((1, width), lambda i, s, t: (0, 0)),
            ],
            out_specs=[
                pl.BlockSpec((TOKEN_BLOCK, width), lambda i, s, t: (i, 0)),
                pl.BlockSpec((TOKEN_BLOCK, width), lambda i, s, t: (i, 0)),
                pl.BlockSpec((model_dim, TOKEN_BLOCK), lambda i, s, t: (0, i)),
                pl.BlockSpec((8, TOKEN_BLOCK), lambda i, s, t: (0, i)),
                pl.BlockSpec(memory_space=pl.ANY),
            ],
            scratch_shapes=[
                pltpu.VMEM((model_dim, 2 * width), bf16),
                pltpu.SemaphoreType.DMA((table.shape[0] + 1,)),
            ],
        ),
        out_shape=(
            sds((length, width), bf16),
            sds((length, width), bf16),
            sds((model_dim, length), bf16),
            sds((8, length), f32),
            stored((model_dim, 2 * width), bf16),
        ),
        name="out_grad",
        cost_estimate=cost(9),
        compiler_params=vmem_limit(length),
    )(starts, table, own, other, low, high, normed, mixed, gain)


def column_tile(columns):
    return 3 * LANES if columns % (3 * LANES) == 0 else LANES


def store_blocks(table_ref, source_ref, keep_ref, send_ref, columns):
    count = table_ref.shape[0]
    rows = source_ref.shape[0] // count
    half = count // 2
    for spot in range(count):
        target = keep_ref if spot < half else send_ref
        at = (spot % half) * rows
        where = pl.multiple_of(table_ref[spot] * rows, rows)
        target[at : at + rows, columns] = source_ref[pl.ds(where, rows), :].astype(bf16)


def gated_kernel(
    table_ref,
    gate_ref,
    nog_ref,
    mixed_ref,
    sums_ref,
    more_ref,
    aux_ref,
    gain_ref,
    gturned_ref,
    nturned_ref,
    out_ref,
    dgate_ref,
    grad_ref,
    row_ref,
    keep_ref,
    send_ref,
    total_ref,
    both_ref,
    gheld_ref,
    nheld_ref,
    sem_ref,
    *,
    full_inner,
):
    step = pl.program_id(0)
    width = gate_ref.shape[1]
    tile = total_ref.shape[1]
    copies = [
        pltpu.make_async_copy(nturned_ref, nheld_ref, sem_ref.at[0]),
        pltpu.make_async_copy(gturned_ref, gheld_ref, sem_ref.at[1]),
    ]

    @pl.when(step == 0)
    def _():
        for copy in copies:
            copy.start()

    inv, mean = token_scales(sums_ref[...] + more_ref[...], full_inner)
    gain = gain_ref[...].astype(f32)
    start = pl.multiple_of(step * TOKEN_BLOCK, TOKEN_BLOCK)
    sums = {}
    for top in range(0, TOKEN_BLOCK, ROW_TILE):
        part = slice(top, top + ROW_TILE)
        here = pl.ds(start + top, ROW_TILE)
        live = aux_ref[part, 7:8]
        inv_part = inv[part]
        mean_part = mean[part]
        for at in range(0, width, LANES):
            lanes = slice(at, at + LANES)
            gate = gate_ref[part, lanes].astype(f32)
            gate_sig = sigmoid(gate)
            gate_silu = gate * gate_sig
            mixed = mixed_ref[part, lanes].astype(f32)
            unit = mixed * gate_silu * inv_part
            nog = nog_ref[part, lanes].astype(f32)
            grad = inv_part * (nog * gain[:, lanes] - unit * mean_part)
            dgate = (grad * mixed * silu_slope(gate, gate_sig)).astype(bf16)
            dgate_ref[part, lanes] = dgate
            both_ref[here, lanes] = dgate
            grad_ref[part, lanes] = (grad * gate_silu * live).astype(bf16)
            normed_out = (unit * gain[:, lanes]).astype(bf16)
            out_ref[part, lanes] = normed_out
            both_ref[here, slice(width + at, width + at + LANES)] = normed_out
            row = jnp.sum((nog * unit).reshape(-1, 8, LANES), axis=0)
            sums[at] = row if top == 0 else sums[at] + row
    for at in range(0, width, LANES):
        row_ref[pl.ds(step * 8, 8), slice(at, at + LANES)] = sums[at]

    @pl.when(step == pl.num_programs(0) - 1)
    def _():
        for copy in copies:
            copy.wait()
        for at in range(0, 2 * width, tile):
            turned = nheld_ref if at < width else gheld_ref
            total_ref[...] = dot_nn(turned[...], both_ref[:, at : at + tile])
            store_blocks(table_ref, total_ref, keep_ref, send_ref, slice(at, at + tile))


def run_gated(table, gate, nog, mixed, sums, more, aux, gain, gturned, nturned, full_inner):
    length, width = gate.shape
    model_dim = gturned.shape[0]
    blocks = length // TOKEN_BLOCK
    tile = column_tile(width)
    sds = jax.ShapeDtypeStruct
    mixed, nturned = from_store(mixed, nturned)
    tokens = pl.BlockSpec((TOKEN_BLOCK, width), lambda i, t: (i, 0))
    halves_spec = pl.BlockSpec((model_dim // 2, 2 * width), lambda i, t: (0, 0))
    return pl.pallas_call(
        partial(gated_kernel, full_inner=float(full_inner)),
        grid_spec=pltpu.PrefetchScalarGridSpec(
            num_scalar_prefetch=1,
            grid=(blocks,),
            in_specs=[
                tokens,
                tokens,
                tokens,
                pl.BlockSpec((8, TOKEN_BLOCK), lambda i, t: (0, i)),
                pl.BlockSpec((8, TOKEN_BLOCK), lambda i, t: (0, i)),
                pl.BlockSpec((TOKEN_BLOCK, aux.shape[1]), lambda i, t: (i, 0)),
                pl.BlockSpec((1, width), lambda i, t: (0, 0)),
                pl.BlockSpec(memory_space=pl.ANY),
                pl.BlockSpec(memory_space=pl.ANY),
            ],
            out_specs=[
                tokens,
                tokens,
                tokens,
                pl.BlockSpec((8 * blocks, width), lambda i, t: (0, 0)),
                halves_spec,
                halves_spec,
            ],
            scratch_shapes=[
                pltpu.VMEM((model_dim, tile), f32),
                pltpu.VMEM((length, 2 * width), bf16),
                pltpu.VMEM((model_dim, length), bf16),
                pltpu.VMEM((model_dim, length), bf16),
                pltpu.SemaphoreType.DMA((2,)),
            ],
        ),
        out_shape=(
            sds((length, width), bf16),
            stored((length, width), bf16),
            stored((length, width), bf16),
            sds((8 * blocks, width), f32),
            sds((model_dim // 2, 2 * width), bf16),
            sds((model_dim // 2, 2 * width), bf16),
        ),
        name="gated_grad",
        cost_estimate=cost(9),
        compiler_params=vmem_limit(length),
    )(table, gate, nog, mixed, sums, more, aux, gain, gturned, nturned)


def out_kernel(starts_ref, rows_ref, weights_ref, send_ref, keep_ref):
    step = pl.program_id(0)
    half = pl.num_programs(0) // 2
    rows = dot_nt(rows_ref[...], weights_ref[...]).astype(bf16)

    @pl.when(step < half)
    def _():
        send_ref[...] = rows

    @pl.when(step >= half)
    def _():
        keep_ref[...] = rows


def run_out(starts, rows, weights):
    length, width = rows.shape
    model_dim = weights.shape[0]
    blocks = length // TOKEN_BLOCK
    half = blocks // 2
    sds = jax.ShapeDtypeStruct
    (weights,) = from_store(weights)
    return pl.pallas_call(
        out_kernel,
        grid_spec=pltpu.PrefetchScalarGridSpec(
            num_scalar_prefetch=1,
            grid=(blocks,),
            in_specs=[
                pl.BlockSpec((TOKEN_BLOCK, width), lambda i, s: (lax.rem(i + s[0], blocks), 0)),
                pl.BlockSpec((model_dim, width), lambda i, s: (0, 1)),
            ],
            out_specs=[
                pl.BlockSpec((TOKEN_BLOCK, model_dim), lambda i, s: (jnp.minimum(i, half - 1), 0)),
                pl.BlockSpec((TOKEN_BLOCK, model_dim), lambda i, s: (jnp.maximum(i - half, 0), 0)),
            ],
        ),
        out_shape=(
            sds((length // 2, model_dim), bf16),
            sds((length // 2, model_dim), bf16),
        ),
        name="out_project",
        cost_estimate=cost(4),
        compiler_params=vmem_limit(length),
    )(starts, rows, weights)


def norm_grad_kernel(starts_ref, dgate_ref, dproj_ref, gates_ref, weights_ref, grad_ref):
    grad = dot_nt(dgate_ref[...], gates_ref[...]) + dot_nt(dproj_ref[...], weights_ref[...])
    grad_ref[...] = grad.astype(grad_ref.dtype)


def run_norm_grad(starts, dgate, dproj, gates, weights, kind):
    length, columns = dproj.shape
    width = dgate.shape[1]
    model_dim = weights.shape[0]
    blocks = length // TOKEN_BLOCK // 2
    dgate, dproj, gates, weights = from_store(dgate, dproj, gates, weights)
    return pl.pallas_call(
        norm_grad_kernel,
        grid_spec=pltpu.PrefetchScalarGridSpec(
            num_scalar_prefetch=1,
            grid=(blocks,),
            in_specs=[
                pl.BlockSpec((TOKEN_BLOCK, width), lambda i, s: (i + s[0], 0)),
                pl.BlockSpec((TOKEN_BLOCK, columns), lambda i, s: (i + s[0], 0)),
                pl.BlockSpec((model_dim, width), lambda i, s: (0, 0)),
                pl.BlockSpec((model_dim, columns), lambda i, s: (0, 0)),
            ],
            out_specs=pl.BlockSpec((TOKEN_BLOCK, model_dim), lambda i, s: (i, 0)),
        ),
        out_shape=jax.ShapeDtypeStruct((length // 2, model_dim), kind),
        name="normed_grad",
        cost_estimate=cost(5),
        compiler_params=vmem_limit(length),
    )(starts, dgate, dproj, gates, weights)


def finish_kernel(
    got_ref, gate_ref, later_ref, packed_ref, inner_ref, step_ref, small_ref, final_ref, *, heads
):
    rows, width = gate_ref.shape
    columns = packed_ref.shape[1]
    shared_cols = slice(width, columns - LANES)
    group = rows + 8
    total = got_ref[:group, :].astype(f32)
    for chip in range(1, got_ref.shape[0] // group):
        total = total + got_ref[chip * group : (chip + 1) * group, :].astype(f32)
    weights = total[:rows]
    small = total[rows:]
    gate = gate_ref[...]
    inner_ref[:, 0, :] = gate
    inner_ref[:, 1, :] = weights[:, :width]
    step_ref[...] = weights[:, columns - LANES :]
    small_ref[...] = small
    real = lax.broadcasted_iota(jnp.int32, (rows, columns), 1) < columns - LANES + heads
    scaled = jnp.where(real, weights * packed_ref[...].astype(f32), 0.0)
    norm = jnp.sum(scaled, axis=1, keepdims=True) + jnp.sum(
        gate * later_ref[...].astype(f32), axis=1, keepdims=True
    )
    final_ref[...] = jnp.zeros_like(final_ref)
    shared_size = columns - LANES - width
    final_ref[:rows, :shared_size] = weights[:, shared_cols]
    final_ref[rows:, :shared_size] = small[:, shared_cols]
    final_ref[:rows, shared_size:] = jnp.broadcast_to(norm, (rows, LANES))


def run_finish(got, gate, later, packed, heads):
    rows, width = gate.shape
    columns = packed.shape[1]
    sds = jax.ShapeDtypeStruct
    return pl.pallas_call(
        partial(finish_kernel, heads=heads),
        grid=(1,),
        in_specs=[
            fixed_spec(got),
            fixed_spec(gate),
            pl.BlockSpec((rows, width), lambda i: (0, 0)),
            fixed_spec(packed),
        ],
        out_specs=[
            pl.BlockSpec((rows, 2, width), lambda i: (0, 0, 0)),
            pl.BlockSpec((rows, LANES), lambda i: (0, 0)),
            pl.BlockSpec((8, columns), lambda i: (0, 0)),
            pl.BlockSpec((rows + 8, columns - width), lambda i: (0, 0)),
        ],
        out_shape=(
            sds((rows, 2, width), f32),
            sds((rows, LANES), f32),
            sds((8, columns), f32),
            sds((rows + 8, columns - width), f32),
        ),
        name="finish",
        cost_estimate=cost(2),
        compiler_params=vmem_limit(1024),
    )(got, gate, later, packed)


def after(value, *others):
    return lax.optimization_barrier((value,) + others)[0]


def cost(microseconds):
    return pl.CostEstimate(flops=int(microseconds * 1.1e9), transcendentals=0, bytes_accessed=0)


def stored(shape, kind):
    return pltpu.HBM(shape, kind)


def from_store(*values):
    return tuple(pltpu.with_memory_space_constraint(v, pltpu.HBM) for v in values)


def vmem_limit(length):
    return pltpu.CompilerParams(vmem_limit_bytes=min(60, VMEM_BASE + length // 128) << 20)


def pad_to(values, axis, size):
    pads = [(0, 0)] * values.ndim
    pads[axis] = (0, size - values.shape[axis])
    return jnp.pad(values, pads)


def body(
    hidden_in,
    segment_ids,
    norm_gain,
    proj_inner,
    proj_shared,
    proj_step,
    conv_inner,
    conv_shared,
    step_bias,
    log_decay,
    skip_gain,
    gate_gain,
    proj_out,
    out_grad,
):
    dp_count = lax.axis_size("dp")
    dp_index = lax.axis_index("dp")
    rows = proj_inner.shape[0]
    length = segment_ids.shape[0]
    model_dim = hidden_in.shape[1]
    local_inner = proj_inner.shape[2]
    heads = proj_step.shape[1]
    state_size = proj_shared.shape[2]
    kernel_len = conv_inner.shape[0]
    shared_size = 2 * state_size
    full_inner = local_inner * lax.axis_size("tensor")
    width = -(-local_inner // (2 * LANES)) * 2 * LANES
    tap_block = conv_shared.shape[2]
    tap_count = kernel_len * 2 * tap_block
    stages, core, table = block_plan()
    groups, core_table = core_groups()
    blocks = length // TOKEN_BLOCK
    starts = token_starts(blocks)
    two = lax.axis_size("tensor") == 2

    chips = dp_count // 2
    hidden_own, hidden_other = both_halves(hidden_in)
    tap_rows = conv_shared.transpose(1, 2, 0).reshape(2 * tap_block, kernel_len)
    tap_rows = pad_to(tap_rows, 0, rows)
    packed = jnp.concatenate(
        [
            pad_to(proj_inner[:, 1, :], 1, width),
            proj_shared.reshape(rows, shared_size),
            pad_to(jnp.concatenate([proj_step, norm_gain[:, None], tap_rows], axis=1), 1, LANES),
        ],
        axis=1,
    )
    later = jnp.concatenate(
        [pad_to(proj_inner[:, 0, :], 1, width), pad_to(proj_out.T, 1, width)], axis=1
    )
    at = jnp.arange(model_dim)
    block, inside = at // rows, at % rows
    side, spot = inside // tap_block, inside % tap_block
    spread = jnp.where(side < 2, side * state_size + block * tap_block + spot, -1)
    spread = (spread[:, None] == jnp.arange(shared_size)[None, :]).astype(bf16)
    aux, segr = token_facts(segment_ids)
    heads_block = jnp.stack([step_bias, log_decay, skip_gain])
    heads_block = pad_to(pad_to(heads_block, 1, LANES), 0, 8)
    tapi = pad_to(conv_inner, 1, width)
    gain = pad_to(gate_gain[None], 1, width)

    later_all = jnp.broadcast_to(later[None], (chips,) + later.shape)
    later_all = later_all.reshape(chips * rows, 2 * width)
    low = packed
    for number, stage in enumerate(stages):
        if number == len(stages) - 1:
            low, later_all = lax.optimization_barrier((low, later_all))
        got = lax.ppermute(low, "dp", stage)
        if number == 0:
            got, aux, segr = lax.optimization_barrier((got, aux, segr))
        if number == 1:
            got, heads_block, tapi, spread, table, core_table = lax.optimization_barrier(
                (got, heads_block, tapi, spread, table, core_table)
            )
        if number == len(stages) - 1:
            got, gain = lax.optimization_barrier((got, gain))
        low = jnp.concatenate([low, got], axis=0)
    later_low = exchange(later_all, groups)
    low, hidden_other = lax.optimization_barrier((low, hidden_other))
    high = lax.ppermute(low, "dp", core)
    grad_own, grad_other = both_halves(after(out_grad, hidden_other))

    proj, praw, normed, normed_t, weights, taps, norm_scale = run_project(
        starts, table, hidden_own, hidden_other, spread, low, high, heads
    )
    norm_scale = norm_scale[:1]
    mixed, u, su, entry = run_forward(proj, praw, tapi, taps, heads_block, aux, segr)

    later_low, mixed, grad_other = lax.optimization_barrier((later_low, mixed, grad_other))
    later_high = lax.ppermute(later_low, "dp", core)
    gate, nog, grad_t, sums, later_rows = run_out_grad(
        starts, core_table, grad_own, grad_other, later_low, later_high, normed, mixed, gain
    )
    if two:
        more = swap(sums)
    else:
        sums = lax.psum(sums, "tensor")
        more = jnp.zeros_like(sums)
    normed_out, dgate, mixed_grad, gain_rows, gkeep, gsend = run_gated(
        core_table, gate, nog, mixed, sums, more, aux, gain, grad_t, normed_t, full_inner
    )
    ggot = lax.ppermute(gsend, "dp", core)
    send_start = starts[1:] if two else jnp.zeros((1,), jnp.int32)
    out_send, out_keep = run_out(send_start, normed_out, later_rows)
    ggot, out_send = lax.optimization_barrier((ggot, out_send))
    gsum = exchange((gkeep.astype(f32) + ggot.astype(f32)).astype(bf16), groups)
    out_other = swap(out_send) if two else None

    dproj, wkeep, wsend = run_backward(
        core_table,
        proj,
        praw,
        u,
        su,
        entry,
        mixed_grad,
        tapi,
        taps,
        heads_block,
        aux,
        segr,
        gain_rows,
        normed_t,
    )
    if two:
        wsend, gsum, out_other = lax.optimization_barrier((wsend, gsum, out_other))
    else:
        wsend, gsum = lax.optimization_barrier((wsend, gsum))
    wgot = lax.ppermute(wsend, "dp", core)
    grad_send = run_norm_grad(send_start, dgate, dproj, later_rows, weights, bf16)
    wgot, grad_send = lax.optimization_barrier((wgot, grad_send))
    grad_other = swap(grad_send) if two else None
    held = rows * chips
    wtotal = (wkeep.astype(f32) + wgot.astype(f32)).astype(bf16)
    wtotal = jnp.concatenate(
        [
            wtotal[:held].reshape(chips, rows, -1),
            jnp.broadcast_to(wtotal[None, held:], (chips, 8, wtotal.shape[1])),
        ],
        axis=1,
    ).reshape(chips * (rows + 8), -1)
    wtotal, dproj = lax.optimization_barrier((wtotal, dproj))
    wsum = exchange(wtotal, groups)
    keep_start = starts[:1] if two else jnp.full((1,), blocks // 2, jnp.int32)
    grad_keep = run_norm_grad(keep_start, dgate, dproj, later_rows, weights, f32)
    if two:
        out_half = out_keep.astype(f32) + out_other.astype(f32)
        own_grad = grad_keep + grad_other.astype(f32)
    else:
        out_half = add_halves(out_send, out_keep)
        own_grad = add_halves(grad_send, grad_keep)
    hidden_out = (hidden_in.astype(f32) + out_half).astype(bf16)
    gsum = sum_blocks(gsum, rows)
    out_sum = gsum[:, width : width + local_inner].T
    inner_sum, step_sum, small, final = run_finish(wsum, gsum[:, :width], later, packed, heads)
    conv_total = small[:kernel_len, :local_inner]
    gain_total = small[4, :local_inner]
    skip_total = small[0, width + shared_size : width + shared_size + heads]
    bias_total = small[1, width + shared_size : width + shared_size + heads]
    decay_total = small[2, width + shared_size : width + shared_size + heads]
    final = total_over_tensor(final)
    shared_total = final[:rows, :shared_size].reshape(rows, 2, state_size)
    taps_total = lax.dynamic_slice_in_dim(
        final[rows : rows + kernel_len, :shared_size].reshape(kernel_len, 2, state_size),
        dp_index * tap_block,
        tap_block,
        axis=2,
    )
    norm_total = final[:rows, shared_size] / norm_gain.astype(f32)
    inner_sum = inner_sum[:, :, :local_inner]
    step_sum = step_sum[:, :heads]

    own = hidden_in.astype(f32)
    own_inv = lax.rsqrt(jnp.mean(own * own, axis=-1, keepdims=True) + epsilon)
    own_unit = own * own_inv
    scaled_in = own_grad * norm_scale
    hidden_grad = own_inv * (
        scaled_in - own_unit * jnp.mean(scaled_in * own_unit, axis=-1, keepdims=True)
    ) + out_grad.astype(f32)
    return (
        hidden_out,
        hidden_grad,
        norm_total,
        inner_sum,
        shared_total,
        step_sum,
        conv_total,
        taps_total,
        bias_total,
        decay_total,
        skip_total,
        gain_total,
        out_sum,
    )


def solution(mesh):
    in_specs = (
        P(("dp", "tensor"), None),
        P("dp"),
        P("dp"),
        P("dp", None, "tensor"),
        P("dp", None, None),
        P("dp", "tensor"),
        P(None, "tensor"),
        P(None, None, "dp"),
        P("tensor"),
        P("tensor"),
        P("tensor"),
        P("tensor"),
        P("tensor", "dp"),
        P(("dp", "tensor"), None),
    )
    out_specs = (
        P(("dp", "tensor"), None),
        P(("dp", "tensor"), None),
        P("dp"),
        P("dp", None, "tensor"),
        P("dp", None, None),
        P("dp", "tensor"),
        P(None, "tensor"),
        P(None, None, "dp"),
        P("tensor"),
        P("tensor"),
        P("tensor"),
        P("tensor"),
        P("tensor", "dp"),
    )
    return jax.shard_map(body, mesh=mesh, in_specs=in_specs, out_specs=out_specs, check_vma=False)
```

```python
from functools import partial

import jax
import jax.numpy as jnp
import numpy as np
from jax import lax
from jax.experimental import pallas as pl
from jax.experimental.pallas import tpu as pltpu
from jax.sharding import PartitionSpec as P

HEAD_DIM = 64
CHUNK = 128
LANES = 128
TOKEN_BLOCK = 256
VMEM_BASE = 16
ROW_TILE = 64
epsilon = 1e-05
f32 = jnp.float32
bf16 = jnp.bfloat16
highest = lax.Precision.HIGHEST


def dot_nn(a, b):
    return lax.dot_general(a, b, (((1,), (0,)), ((), ())), preferred_element_type=f32)


def dot_nt(a, b):
    return lax.dot_general(a, b, (((1,), (1,)), ((), ())), preferred_element_type=f32)


def dot_tn(a, b):
    return lax.dot_general(a, b, (((0,), (0,)), ((), ())), preferred_element_type=f32)


def dot_exact(a, b):
    return lax.dot_general(
        a, b, (((1,), (0,)), ((), ())), preferred_element_type=f32, precision=highest
    )


def dot_split(a, b):
    high = a.astype(bf16)
    rest = (a - high.astype(f32)).astype(bf16)
    return dot_nn(high, b) + dot_nn(rest, b)


def two_parts(values):
    high = values.astype(bf16)
    rest = (values - high.astype(f32)).astype(bf16)
    return jnp.concatenate([high, rest], axis=1)


def spread_matrix(shape, size):
    rows = lax.rem(lax.broadcasted_iota(jnp.int32, shape, 0), LANES)
    return (rows == lax.broadcasted_iota(jnp.int32, shape, 1) // size).astype(bf16)


def sigmoid(v):
    return 1.0 / (1.0 + jnp.exp(-v))


def softplus(v):
    return jnp.maximum(v, 0.0) + jnp.log1p(jnp.exp(-jnp.abs(v)))


def halves(lane_low, values, head):
    return jnp.where(lane_low, values[:, head : head + 1], values[:, head + 1 : head + 2])


def head_sides():
    low = (lax.broadcasted_iota(jnp.int32, (CHUNK, LANES), 1) < HEAD_DIM).astype(f32)
    return low.astype(bf16), (1.0 - low).astype(bf16)


def by_head(values, sides):
    return jnp.concatenate([values * sides[0], values * sides[1]], axis=0)


def back_shift(window, offset):
    return pltpu.roll(window, offset, 0)[8:, :]


def ahead_shift(window, offset):
    rows = window.shape[0]
    return pltpu.roll(window, rows - offset, 0)[: rows - 8, :]


def conv_rows(window, taps, aux):
    total = taps[3:4, :] * window[8:, :]
    for offset in range(1, 4):
        total = total + taps[3 - offset : 4 - offset, :] * (
            back_shift(window, offset) * aux[:, offset : offset + 1]
        )
    return total


def forward_kernel(
    proj_ref,
    step_ref,
    tapi_ref,
    taps_ref,
    heads_ref,
    aux_ref,
    segr_ref,
    mixed_ref,
    u_ref,
    su_ref,
    entry_ref,
    state_ref,
    carry_ref,
    scarry_ref,
    xw_ref,
    channels_ref,
    columns_ref,
):
    width = mixed_ref.shape[1]
    pairs = width // LANES
    shared_size = su_ref.shape[1]
    state_size = shared_size // 2
    chunk = pl.program_id(0)

    @pl.when(chunk == 0)
    def _():
        for ref in (state_ref, carry_ref, scarry_ref):
            ref[...] = jnp.zeros_like(ref)
        channels_ref[...] = spread_matrix(channels_ref.shape, HEAD_DIM)
        columns_ref[...] = spread_matrix(columns_ref.shape, CHUNK)

    rows = lax.broadcasted_iota(jnp.int32, (CHUNK, CHUNK), 0)
    cols = lax.broadcasted_iota(jnp.int32, (CHUNK, CHUNK), 1)
    lower = rows >= cols
    summing = lower.astype(f32)
    lane_low = lax.broadcasted_iota(jnp.int32, (CHUNK, LANES), 1) < HEAD_DIM
    sides = head_sides()
    bias = heads_ref[0:1, :]
    rate = -jnp.exp(heads_ref[1:2, :])
    skips = heads_ref[2:3, :]
    aux = aux_ref[...]
    live = aux[:, 7:8]
    same = lower & (aux[:, 0:1] == segr_ref[pl.ds(chunk, 1), :])
    shared_now = proj_ref[:, width:].astype(f32)
    su = conv_rows(jnp.concatenate([scarry_ref[...], shared_now], axis=0), taps_ref[...], aux)
    scarry_ref[...] = shared_now[CHUNK - 8 :, :]
    su_ref[...] = su
    shared = (su * sigmoid(su)).astype(bf16)
    b_rows = shared[:, :state_size]
    c_rows = shared[:, state_size:]
    scores = jnp.where(same, dot_nt(c_rows, b_rows), 0.0)
    step = softplus(step_ref[...] + bias) * live
    decay = dot_exact(summing, step * rate)
    decay_parts = two_parts(decay)
    decay = decay_parts[:, :LANES].astype(f32) + decay_parts[:, LANES:].astype(f32)
    decay_wide = dot_nn(decay_parts, columns_ref[...])
    decay_t = decay.T
    last = decay[CHUNK - 1 :, :]
    entry_scale = jnp.exp(decay) * aux[:, 8:9]
    end_scale = jnp.exp(last - decay) * aux[:, 9:10]
    keep = jnp.exp(last) * aux[:1, 10:11]
    step_wide = dot_nn(two_parts(step), channels_ref[...])
    entry_wide = dot_nn(two_parts(entry_scale), channels_ref[...])
    end_wide = dot_nn(two_parts(end_scale), channels_ref[...])
    state = state_ref[...]
    state_low = state.astype(bf16)
    entry_ref[...] = state_low[None]
    past = dot_nn(c_rows, state_low)
    for pair in range(pairs):
        lanes = slice(pair * LANES, (pair + 1) * LANES)
        head = 2 * pair
        now = proj_ref[:, lanes].astype(f32)
        window = jnp.concatenate([carry_ref[:, lanes], now], axis=0)
        carry_ref[:, lanes] = now[CHUNK - 8 :, :]
        u = conv_rows(window, tapi_ref[:, lanes].astype(f32), aux)
        u_ref[:, lanes] = u.astype(bf16)
        x = u * sigmoid(u)
        scaled = x * step_wide[:, lanes]
        mixing = jnp.concatenate(
            [
                (
                    scores
                    * jnp.exp(jnp.minimum(decay_wide[:, h * CHUNK : (h + 1) * CHUNK] - decay_t[h : h + 1, :], 0.0))
                ).astype(bf16)
                for h in (head, head + 1)
            ],
            axis=1,
        )
        stacked = by_head(scaled.astype(bf16), sides)
        inside = dot_nn(mixing, stacked)
        xw_ref[:, lanes] = (scaled * end_wide[:, lanes]).astype(bf16)
        mixed = (
            inside
            + past[:, lanes] * entry_wide[:, lanes]
            + halves(lane_low[:1], skips, head) * x
        ) * live
        mixed_ref[:, lanes] = mixed.astype(bf16)
        state_ref[:, lanes] = state[:, lanes] * halves(lane_low[:1], keep, head)
    state_ref[...] += dot_tn(b_rows, xw_ref[...])


def token_scales(sums, full_inner):
    columns = sums.T
    inv = lax.rsqrt(columns[:, 0:1] / full_inner + epsilon)
    return inv, inv * columns[:, 1:2] / full_inner


def silu_slope(v, s):
    return s * (1.0 + v * (1.0 - s))


def backward_kernel(
    table_ref,
    proj_ref,
    praw_ref,
    u_ref,
    su_ref,
    entry_ref,
    grad_ref,
    tapi_ref,
    taps_ref,
    heads_ref,
    aux_ref,
    segr_ref,
    gain_ref,
    turned_ref,
    dproj_ref,
    keep_ref,
    send_ref,
    wide_ref,
    shared_ref,
    small_ref,
    total_ref,
    grads_ref,
    held_ref,
    sem_ref,
    state_ref,
    ahead_ref,
    sahead_ref,
    xw_ref,
    ge_ref,
    row_ref,
    proda_ref,
    prodb_ref,
    channels_ref,
    columns_ref,
):
    width = u_ref.shape[1]
    chunks = pl.num_programs(0)
    pairs = width // LANES
    shared_size = su_ref.shape[1]
    state_size = shared_size // 2
    shared_cols = slice(width, width + shared_size)
    step_cols = slice(width + shared_size, width + shared_size + LANES)
    chunk = chunks - 1 - pl.program_id(0)
    copy = pltpu.make_async_copy(turned_ref, held_ref, sem_ref.at[0])

    @pl.when(pl.program_id(0) == 0)
    def _():
        copy.start()
        channels_ref[...] = spread_matrix(channels_ref.shape, HEAD_DIM)
        columns_ref[...] = spread_matrix(columns_ref.shape, CHUNK)
        for ref in (state_ref, ahead_ref, sahead_ref, row_ref, wide_ref, shared_ref):
            ref[...] = jnp.zeros_like(ref)

    rows = lax.broadcasted_iota(jnp.int32, (CHUNK, CHUNK), 0)
    cols = lax.broadcasted_iota(jnp.int32, (CHUNK, CHUNK), 1)
    upper = rows <= cols
    summing = (rows >= cols).astype(f32)
    unsumming = upper.astype(f32)
    last_row = (lax.broadcasted_iota(jnp.int32, (CHUNK, LANES), 0) == CHUNK - 1).astype(f32)
    lane_ids = lax.broadcasted_iota(jnp.int32, (CHUNK, LANES), 1)
    lane_low = lane_ids < HEAD_DIM
    sides = head_sides()
    bias = heads_ref[0:1, :]
    rate = -jnp.exp(heads_ref[1:2, :])
    skips = heads_ref[2:3, :]
    place = (
        lax.broadcasted_iota(jnp.int32, (width, LANES), 0) // HEAD_DIM
        == lax.broadcasted_iota(jnp.int32, (width, LANES), 1)
    ).astype(bf16)

    aux = aux_ref[...]
    live = aux[:, 7:8]
    same = upper & (aux[:, 0:1] == segr_ref[pl.ds(chunk, 1), :])
    su = su_ref[...]
    su_sig = sigmoid(su)
    shared = (su * su_sig).astype(bf16)
    b_rows = shared[:, :state_size]
    c_rows = shared[:, state_size:]
    scores = jnp.where(same, dot_nt(b_rows, c_rows), 0.0)
    pre = praw_ref[...] + bias
    step = softplus(pre) * live
    decay = dot_exact(summing, step * rate)
    decay_parts = two_parts(decay)
    decay = decay_parts[:, :LANES].astype(f32) + decay_parts[:, LANES:].astype(f32)
    decay_wide = dot_nn(decay_parts, columns_ref[...])
    decay_t = decay.T
    last = decay[CHUNK - 1 :, :]
    entry_scale = jnp.exp(decay) * aux[:, 8:9]
    end_scale = jnp.exp(last - decay) * aux[:, 9:10]
    keep = jnp.exp(last) * aux[:1, 10:11]
    step_wide = dot_nn(two_parts(step), channels_ref[...])
    entry_wide = dot_nn(two_parts(entry_scale), channels_ref[...])
    end_wide = dot_nn(two_parts(end_scale), channels_ref[...])
    entry = entry_ref[0]
    dstate = state_ref[...]
    dstate_low = dstate.astype(bf16)
    past = dot_nn(c_rows, entry)
    bds = dot_nn(b_rows, dstate_low)
    here = pl.ds(pl.multiple_of(chunk * CHUNK, CHUNK), CHUNK)
    score_grad = jnp.zeros((CHUNK, CHUNK), f32)
    col_part = jnp.zeros((CHUNK, LANES), f32)
    for pair in range(pairs):
        lanes = slice(pair * LANES, (pair + 1) * LANES)
        head = 2 * pair
        g_low = grad_ref[:, lanes]
        g = g_low.astype(f32)
        u = u_ref[:, lanes].astype(f32)
        u_sig = sigmoid(u)
        x = u * u_sig
        step_c = step_wide[:, lanes]
        scaled = x * step_c
        stacked = by_head(scaled.astype(bf16), sides)
        dmix = dot_nt(stacked, g_low)
        mixing = []
        for k, h in enumerate((head, head + 1)):
            decays = jnp.exp(jnp.minimum(decay_t[h : h + 1, :] - decay_wide[:, h * CHUNK : (h + 1) * CHUNK], 0.0))
            dmix_h = dmix[k * CHUNK : (k + 1) * CHUNK, :]
            score_grad = score_grad + dmix_h * decays
            mixing_h = scores * decays
            mixing.append(mixing_h.astype(bf16))
            both = mixing_h * dmix_h
            col_part = jnp.where(lane_ids == h, jnp.sum(both, axis=1, keepdims=True), col_part)
            row_ref[h : h + 1, :] = jnp.sum(both, axis=0, keepdims=True)
        g_stacked = by_head(g_low, sides)
        end_c = end_wide[:, lanes]
        entry_c = entry_wide[:, lanes]
        keep_c = halves(lane_low[:1], keep, head)
        from_state = end_c * bds[:, lanes]
        dscaled = dot_nn(jnp.concatenate(mixing, axis=1), g_stacked) + from_state
        xw_ref[:, lanes] = (scaled * end_c).astype(bf16)
        q = scaled * from_state
        ge = g * entry_c
        ge_ref[:, lanes] = ge.astype(bf16)
        dstate_p = dstate[:, lanes]
        tail = jnp.sum(q, axis=0, keepdims=True) + keep_c * jnp.sum(
            dstate_p * entry[:, lanes].astype(f32), axis=0, keepdims=True
        )
        proda_ref[:, lanes] = (x * dscaled).astype(bf16)
        prodb_ref[:, lanes] = ge * past[:, lanes] - q + last_row * tail
        state_ref[:, lanes] = dstate_p * keep_c
        dx = step_c * dscaled + halves(lane_low[:1], skips, head) * g
        du = dx * silu_slope(u, u_sig)
        window = jnp.concatenate([du, ahead_ref[:, lanes]], axis=0)
        ahead_ref[:, lanes] = du[:8, :]
        cin = proj_ref[:, lanes].astype(f32)
        taps = tapi_ref[:, lanes].astype(f32)
        dcin = taps[3:4, :] * du
        wide_ref[3:4, lanes] += jnp.sum(cin * du, axis=0, keepdims=True)
        for offset in range(1, 4):
            moved = ahead_shift(window, offset) * aux[:, 3 + offset : 4 + offset]
            dcin = dcin + taps[3 - offset : 4 - offset, :] * moved
            wide_ref[3 - offset : 4 - offset, lanes] += jnp.sum(
                cin * moved, axis=0, keepdims=True
            )
        dcin = dcin.astype(bf16)
        dproj_ref[:, lanes] = dcin
        grads_ref[here, lanes] = dcin
        wide_ref[5:6, lanes] += jnp.sum(g * x, axis=0, keepdims=True)
    score_low = jnp.where(same, score_grad, 0.0).astype(bf16)
    ge_all = ge_ref[...]
    db = dot_nn(score_low, c_rows) + dot_nt(xw_ref[...], dstate_low)
    dc = dot_tn(score_low, b_rows) + dot_nt(ge_all, entry)
    state_ref[...] += dot_tn(c_rows, ge_all)
    ds = jnp.concatenate([db, dc], axis=1) * silu_slope(su, su_sig)
    window = jnp.concatenate([ds, sahead_ref[...]], axis=0)
    sahead_ref[...] = ds[:8, :]
    taps = taps_ref[...]
    sin = proj_ref[:, shared_cols].astype(f32)
    dsin = taps[3:4, :] * ds
    shared_ref[3:4, :] += jnp.sum(sin * ds, axis=0, keepdims=True)
    for offset in range(1, 4):
        moved = ahead_shift(window, offset) * aux[:, 3 + offset : 4 + offset]
        dsin = dsin + taps[3 - offset : 4 - offset, :] * moved
        shared_ref[3 - offset : 4 - offset, :] += jnp.sum(sin * moved, axis=0, keepdims=True)
    dsin = dsin.astype(bf16)
    dproj_ref[:, shared_cols] = dsin
    grads_ref[here, shared_cols] = dsin
    ddecay = row_ref[...].T - col_part + dot_split(prodb_ref[...], place)
    dlog = dot_exact(unsumming, ddecay)
    dstep = (dot_nn(proda_ref[...], place) + rate * dlog) * live * sigmoid(pre)
    dproj_ref[:, step_cols] = dstep.astype(bf16)
    grads_ref[here, step_cols] = dstep.astype(bf16)
    wide_ref[6:7, :LANES] += jnp.sum(dstep, axis=0, keepdims=True)
    wide_ref[6:7, LANES : 2 * LANES] += jnp.sum(step * dlog, axis=0, keepdims=True) * rate

    @pl.when(chunk == 0)
    def _():
        small_ref[...] = jnp.zeros_like(small_ref)
        small_ref[:4, :width] = wide_ref[:4, :]
        small_ref[:4, width : width + shared_size] = shared_ref[:4, :]
        skip_row = dot_split(wide_ref[...], place)[5:6, :]
        small_ref[0:1, step_cols] = skip_row
        small_ref[1:2, step_cols] = wide_ref[6:7, :LANES]
        small_ref[2:3, step_cols] = wide_ref[6:7, LANES : 2 * LANES]
        small_ref[4:5, :width] = jnp.sum(gain_ref[...], axis=0, keepdims=True)
        copy.wait()
        held = keep_ref.shape[0] - 8
        keep_ref[held:, :] = small_ref[...].astype(bf16)
        send_ref[held:, :] = small_ref[...].astype(bf16)
        tile = total_ref.shape[1]
        for at in range(0, width + shared_size + LANES, tile):
            total_ref[...] = dot_nn(held_ref[...], grads_ref[:, at : at + tile])
            store_blocks(table_ref, total_ref, keep_ref, send_ref, slice(at, at + tile))


def facts_kernel(seg_ref, aux_ref, segr_ref):
    seg = seg_ref[...].astype(f32)
    chunks = seg.shape[0]
    segr_ref[...] = seg
    none = jnp.full((1, CHUNK), -1.0, f32)
    before = jnp.concatenate([none, seg[: chunks - 1]], axis=0) if chunks > 1 else none
    behind = jnp.concatenate([seg[1:], none], axis=0) if chunks > 1 else none
    lane = lax.broadcasted_iota(jnp.int32, seg.shape, 1)
    facts = [seg]
    for offset in range(1, 4):
        earlier = jnp.where(
            lane >= offset, pltpu.roll(seg, offset, 1), pltpu.roll(before, offset, 1)
        )
        facts.append((earlier == seg).astype(f32))
    for offset in range(1, 4):
        later = jnp.where(
            lane < CHUNK - offset,
            pltpu.roll(seg, CHUNK - offset, 1),
            pltpu.roll(behind, CHUNK - offset, 1),
        )
        facts.append((later == seg).astype(f32))
    last = jnp.broadcast_to(seg[:, CHUNK - 1 :], seg.shape)
    prior = jnp.broadcast_to(before[:, CHUNK - 1 :], seg.shape)
    facts.append((seg != 0.0).astype(f32))
    facts.append((seg == prior).astype(f32))
    facts.append((seg == last).astype(f32))
    facts.append((last == prior).astype(f32))
    empty = jnp.zeros((LANES - len(facts), CHUNK), f32)
    for chunk in range(chunks):
        rows = jnp.concatenate([f[chunk : chunk + 1, :] for f in facts] + [empty], axis=0)
        aux_ref[chunk * CHUNK : (chunk + 1) * CHUNK, :] = rows.T[:, : aux_ref.shape[1]]


def token_facts(segments):
    length = segments.shape[0]
    chunks = length // CHUNK
    return pl.pallas_call(
        facts_kernel,
        out_shape=(
            jax.ShapeDtypeStruct((length, 16), f32),
            jax.ShapeDtypeStruct((chunks, CHUNK), f32),
        ),
        name="token_facts",
        cost_estimate=cost(2),
        compiler_params=vmem_limit(length),
    )(segments.reshape(chunks, CHUNK))


def chunk_spec(columns, last):
    if last is None:
        return pl.BlockSpec((CHUNK, columns), lambda i: (i, 0))
    return pl.BlockSpec((CHUNK, columns), lambda i: (last - i, 0))


def fixed_spec(values):
    zeros = (0,) * values.ndim
    return pl.BlockSpec(values.shape, lambda i: zeros)


def run_forward(proj, praw, tapi, taps, heads, aux, segr):
    length = proj.shape[0]
    width = tapi.shape[1]
    shared_size = taps.shape[1]
    state_size = shared_size // 2
    chunks = length // CHUNK
    proj, praw = from_store(proj, praw)
    return pl.pallas_call(
        forward_kernel,
        grid=(chunks,),
        in_specs=[
            chunk_spec(proj.shape[1], None),
            chunk_spec(LANES, None),
            fixed_spec(tapi),
            fixed_spec(taps),
            fixed_spec(heads),
            chunk_spec(aux.shape[1], None),
            fixed_spec(segr),
        ],
        out_specs=[
            chunk_spec(width, None),
            chunk_spec(width, None),
            chunk_spec(shared_size, None),
            pl.BlockSpec((1, state_size, width), lambda i: (i, 0, 0)),
        ],
        out_shape=(
            stored((length, width), bf16),
            stored((length, width), bf16),
            stored((length, shared_size), f32),
            stored((chunks, state_size, width), bf16),
        ),
        scratch_shapes=[
            pltpu.VMEM((state_size, width), f32),
            pltpu.VMEM((8, width), f32),
            pltpu.VMEM((8, shared_size), f32),
            pltpu.VMEM((CHUNK, width), bf16),
            pltpu.VMEM((2 * LANES, width), bf16),
            pltpu.VMEM((2 * LANES, width // HEAD_DIM * CHUNK), bf16),
        ],
        name="scan_forward",
        cost_estimate=cost(3),
        compiler_params=vmem_limit(length),
    )(proj, praw, tapi, taps, heads, aux, segr)


def run_backward(
    table, proj, praw, u, su, entry, grad, tapi, taps, heads, aux, segr, gain_rows, turned
):
    length, width = u.shape
    shared_size = su.shape[1]
    state_size = shared_size // 2
    model_dim = turned.shape[0]
    chunks = length // CHUNK
    last = chunks - 1
    columns = width + shared_size + LANES
    kept = model_dim // 2 + 8
    sds = jax.ShapeDtypeStruct
    proj, praw, u, su, entry, grad, turned = from_store(proj, praw, u, su, entry, grad, turned)

    def back(size):
        return pl.BlockSpec((CHUNK, size), lambda i, t: (last - i, 0))

    def fixed(shape):
        return pl.BlockSpec(shape, lambda i, t: (0, 0))

    return pl.pallas_call(
        backward_kernel,
        grid_spec=pltpu.PrefetchScalarGridSpec(
            num_scalar_prefetch=1,
            grid=(chunks,),
            in_specs=[
                back(proj.shape[1]),
                back(LANES),
                back(width),
                back(shared_size),
                pl.BlockSpec((1, state_size, width), lambda i, t: (last - i, 0, 0)),
                back(width),
                fixed(tapi.shape),
                fixed(taps.shape),
                fixed(heads.shape),
                back(aux.shape[1]),
                fixed(segr.shape),
                fixed(gain_rows.shape),
                pl.BlockSpec(memory_space=pl.ANY),
            ],
            out_specs=[
                back(columns),
                fixed((kept, columns)),
                fixed((kept, columns)),
            ],
            scratch_shapes=[
                pltpu.VMEM((8, width), f32),
                pltpu.VMEM((8, shared_size), f32),
                pltpu.VMEM((8, columns), f32),
                pltpu.VMEM((model_dim, column_tile(columns)), f32),
                pltpu.VMEM((length, columns), bf16),
                pltpu.VMEM((model_dim, length), bf16),
                pltpu.SemaphoreType.DMA((1,)),
                pltpu.VMEM((state_size, width), f32),
                pltpu.VMEM((8, width), f32),
                pltpu.VMEM((8, shared_size), f32),
                pltpu.VMEM((CHUNK, width), bf16),
                pltpu.VMEM((CHUNK, width), bf16),
                pltpu.VMEM((LANES, CHUNK), f32),
                pltpu.VMEM((CHUNK, width), bf16),
                pltpu.VMEM((CHUNK, width), f32),
                pltpu.VMEM((2 * LANES, width), bf16),
                pltpu.VMEM((2 * LANES, width // HEAD_DIM * CHUNK), bf16),
            ],
        ),
        out_shape=(
            stored((length, columns), bf16),
            stored((kept, columns), bf16),
            stored((kept, columns), bf16),
        ),
        name="scan_backward",
        cost_estimate=cost(36),
        compiler_params=vmem_limit(length),
    )(table, proj, praw, u, su, entry, grad, tapi, taps, heads, aux, segr, gain_rows, turned)


def block_plan():
    count = lax.axis_size("dp")
    bits = []
    bit = count // 2
    while bit > 1:
        bits.append(bit)
        bit //= 2
    mixed = bits[:-2] + bits[-2:][::-1]
    by_core = (bits, mixed)
    stages = []
    for stage in range(len(bits)):
        stages.append([(i, i ^ by_core[i % 2][stage]) for i in range(count)])
    core = [(i, i ^ 1) for i in range(count)]
    device = np.zeros((count, count), np.int32)
    for own in range(count):
        for spot in range(count):
            other = own ^ 1 if spot >= count // 2 else own
            for stage, bit in enumerate(by_core[other % 2]):
                if (spot >> stage) & 1:
                    other ^= bit
            device[own, spot] = other
    table = jnp.asarray(device)[lax.axis_index("dp")]
    return stages, core, table


def core_groups():
    count = lax.axis_size("dp")
    groups = [list(range(side, count, 2)) for side in range(2)]
    return groups, jnp.asarray(
        [groups[0] + groups[1], groups[1] + groups[0]], jnp.int32
    )[lax.axis_index("dp") % 2]


def exchange(blocks, groups):
    return lax.all_to_all(
        blocks, "dp", 0, 0, axis_index_groups=groups, tiled=True
    )


def sum_blocks(blocks, rows):
    return jnp.sum(blocks.reshape(-1, rows, blocks.shape[1]).astype(f32), axis=0)


def swap(values):
    return lax.ppermute(values, "tensor", [(0, 1), (1, 0)])


def total_over_tensor(values):
    if lax.axis_size("tensor") == 2:
        return values + swap(values)
    return lax.psum(values, "tensor")


def both_halves(own):
    if lax.axis_size("tensor") == 2:
        return own, swap(own)
    whole = lax.all_gather(own, "tensor", axis=0, tiled=True)
    return whole, whole


def token_starts(blocks):
    if lax.axis_size("tensor") == 2:
        index = lax.axis_index("tensor")
        return jnp.stack([index * (blocks // 2), (1 - index) * (blocks // 2)]).astype(jnp.int32)
    return jnp.zeros((2,), jnp.int32)


def add_halves(send, keep):
    if lax.axis_size("tensor") == 2:
        return keep.astype(f32) + swap(send).astype(f32)
    whole = jnp.concatenate([send.astype(bf16), keep.astype(bf16)], axis=0)
    return lax.psum_scatter(whole, "tensor", scatter_dimension=0, tiled=True).astype(f32)


def own_block(step, starts, own_blocks):
    return jnp.clip(step - starts[0], 0, own_blocks - 1)


def other_block(step, starts, own_blocks):
    return jnp.clip(step - starts[1], 0, own_blocks - 1)


def place_blocks(table_ref, low_ref, high_ref, whole_ref, sem_ref):
    count = table_ref.shape[0]
    rows = whole_ref.shape[0] // count
    copies = []
    for spot in range(count):
        source = low_ref if spot < count // 2 else high_ref
        where = pl.multiple_of(table_ref[spot] * rows, rows)
        copies.append(
            pltpu.make_async_copy(
                source.at[pl.ds((spot % (count // 2)) * rows, rows), :],
                whole_ref.at[pl.ds(where, rows), :],
                sem_ref.at[spot],
            )
        )
    for copy in copies:
        copy.start()
    for copy in copies:
        copy.wait()


def project_kernel(
    starts_ref,
    table_ref,
    own_ref,
    other_ref,
    spread_ref,
    low_ref,
    high_ref,
    proj_ref,
    step_ref,
    normed_ref,
    turned_ref,
    whole_ref,
    taps_ref,
    scale_ref,
    weights_ref,
    sem_ref,
    *,
    own_blocks,
    heads,
):
    step = pl.program_id(0)
    model_dim, columns = weights_ref.shape
    store = pltpu.make_async_copy(weights_ref, whole_ref, sem_ref.at[table_ref.shape[0]])

    @pl.when(step == pl.num_programs(0) - 1)
    def _():
        store.wait()

    @pl.when(step == 0)
    def _():
        place_blocks(table_ref, low_ref, high_ref, weights_ref, sem_ref)
        store.start()
        extra = weights_ref[:, columns - LANES :].astype(f32).T
        scale_ref[...] = jnp.broadcast_to(extra[heads : heads + 1, :], scale_ref.shape)
        taps = extra[heads + 1 : heads + 5, :]
        taps = jnp.concatenate([taps, jnp.zeros_like(taps)], axis=0).astype(bf16)
        taps_ref[...] = dot_nn(taps, spread_ref[...])

    mine = (step >= starts_ref[0]) & (step < starts_ref[0] + own_blocks)
    tokens = jnp.where(mine, own_ref[...].astype(f32), other_ref[...].astype(f32))
    inv = lax.rsqrt(jnp.mean(tokens * tokens, axis=-1, keepdims=True) + epsilon)
    normed = (tokens * inv * scale_ref[:1, :]).astype(bf16)
    normed_ref[...] = normed
    turned_ref[...] = normed.T
    proj = dot_nn(normed, weights_ref[...])
    proj_ref[...] = proj[:, : columns - LANES].astype(bf16)
    step_ref[...] = proj[:, columns - LANES :]


def run_project(starts, table, own, other, spread, low, high, heads):
    own_rows, model_dim = own.shape
    columns = low.shape[1]
    own_blocks = own_rows // TOKEN_BLOCK
    blocks = own_blocks * (2 if lax.axis_size("tensor") == 2 else 1)
    length = blocks * TOKEN_BLOCK
    sds = jax.ShapeDtypeStruct
    own, other, low, high = from_store(own, other, low, high)
    return pl.pallas_call(
        partial(project_kernel, own_blocks=own_blocks, heads=heads),
        grid_spec=pltpu.PrefetchScalarGridSpec(
            num_scalar_prefetch=2,
            grid=(blocks,),
            in_specs=[
                pl.BlockSpec(
                    (TOKEN_BLOCK, model_dim), lambda i, s, t: (own_block(i, s, own_blocks), 0)
                ),
                pl.BlockSpec(
                    (TOKEN_BLOCK, model_dim), lambda i, s, t: (other_block(i, s, own_blocks), 0)
                ),
                pl.BlockSpec(spread.shape, lambda i, s, t: (0, 0)),
                pl.BlockSpec(memory_space=pl.ANY),
                pl.BlockSpec(memory_space=pl.ANY),
            ],
            out_specs=[
                pl.BlockSpec((TOKEN_BLOCK, columns - LANES), lambda i, s, t: (i, 0)),
                pl.BlockSpec((TOKEN_BLOCK, LANES), lambda i, s, t: (i, 0)),
                pl.BlockSpec((TOKEN_BLOCK, model_dim), lambda i, s, t: (i, 0)),
                pl.BlockSpec((model_dim, TOKEN_BLOCK), lambda i, s, t: (0, i)),
                pl.BlockSpec(memory_space=pl.ANY),
                pl.BlockSpec((8, spread.shape[1]), lambda i, s, t: (0, 0)),
                pl.BlockSpec((8, model_dim), lambda i, s, t: (0, 0)),
            ],
            scratch_shapes=[
                pltpu.VMEM((model_dim, columns), bf16),
                pltpu.SemaphoreType.DMA((table.shape[0] + 1,)),
            ],
        ),
        out_shape=(
            stored((length, columns - LANES), bf16),
            stored((length, LANES), f32),
            stored((length, model_dim), bf16),
            stored((model_dim, length), bf16),
            stored((model_dim, columns), bf16),
            sds((8, spread.shape[1]), f32),
            sds((8, model_dim), f32),
        ),
        name="norm_project",
        cost_estimate=cost(2),
        compiler_params=vmem_limit(length),
    )(starts, table, own, other, spread, low, high)


def token_sum(values):
    total = values[:, :LANES]
    for at in range(LANES, values.shape[1], LANES):
        total = total + values[:, at : at + LANES]
    return jnp.sum(total.T, axis=0, keepdims=True)


def out_grad_kernel(
    starts_ref,
    table_ref,
    own_ref,
    other_ref,
    low_ref,
    high_ref,
    normed_ref,
    mixed_ref,
    gain_ref,
    gate_ref,
    nog_ref,
    turned_ref,
    sums_ref,
    whole_ref,
    weights_ref,
    sem_ref,
    *,
    own_blocks,
):
    step = pl.program_id(0)
    width = mixed_ref.shape[1]
    store = pltpu.make_async_copy(weights_ref, whole_ref, sem_ref.at[table_ref.shape[0]])

    @pl.when(step == 0)
    def _():
        place_blocks(table_ref, low_ref, high_ref, weights_ref, sem_ref)
        store.start()

    @pl.when(step == pl.num_programs(0) - 1)
    def _():
        store.wait()

    mine = (step >= starts_ref[0]) & (step < starts_ref[0] + own_blocks)
    tokens = jnp.where(mine, own_ref[...].astype(f32), other_ref[...].astype(f32)).astype(bf16)
    turned_ref[...] = tokens.T
    gate = dot_nn(normed_ref[...], weights_ref[:, :width])
    gate_ref[...] = gate.astype(bf16)
    nog = dot_nn(tokens, weights_ref[:, width:])
    nog_ref[...] = nog.astype(bf16)
    gated = mixed_ref[...].astype(f32) * (gate * sigmoid(gate))
    sums_ref[...] = jnp.concatenate(
        [
            token_sum(gated * gated),
            token_sum(nog * gain_ref[...].astype(f32) * gated),
            jnp.zeros((6, TOKEN_BLOCK), f32),
        ],
        axis=0,
    )


def run_out_grad(starts, table, own, other, low, high, normed, mixed, gain):
    own_rows, model_dim = own.shape
    length, width = mixed.shape
    own_blocks = own_rows // TOKEN_BLOCK
    blocks = length // TOKEN_BLOCK
    sds = jax.ShapeDtypeStruct
    own, other, normed, mixed, low, high = from_store(own, other, normed, mixed, low) + (high,)
    return pl.pallas_call(
        partial(out_grad_kernel, own_blocks=own_blocks),
        grid_spec=pltpu.PrefetchScalarGridSpec(
            num_scalar_prefetch=2,
            grid=(blocks,),
            in_specs=[
                pl.BlockSpec(
                    (TOKEN_BLOCK, model_dim), lambda i, s, t: (own_block(i, s, own_blocks), 0)
                ),
                pl.BlockSpec(
                    (TOKEN_BLOCK, model_dim), lambda i, s, t: (other_block(i, s, own_blocks), 0)
                ),
                pl.BlockSpec(memory_space=pl.ANY),
                pl.BlockSpec(memory_space=pl.ANY),
                pl.BlockSpec((TOKEN_BLOCK, model_dim), lambda i, s, t: (i, 0)),
                pl.BlockSpec((TOKEN_BLOCK, width), lambda i, s, t: (i, 0)),
                pl.BlockSpec((1, width), lambda i, s, t: (0, 0)),
            ],
            out_specs=[
                pl.BlockSpec((TOKEN_BLOCK, width), lambda i, s, t: (i, 0)),
                pl.BlockSpec((TOKEN_BLOCK, width), lambda i, s, t: (i, 0)),
                pl.BlockSpec((model_dim, TOKEN_BLOCK), lambda i, s, t: (0, i)),
                pl.BlockSpec((8, TOKEN_BLOCK), lambda i, s, t: (0, i)),
                pl.BlockSpec(memory_space=pl.ANY),
            ],
            scratch_shapes=[
                pltpu.VMEM((model_dim, 2 * width), bf16),
                pltpu.SemaphoreType.DMA((table.shape[0] + 1,)),
            ],
        ),
        out_shape=(
            sds((length, width), bf16),
            sds((length, width), bf16),
            sds((model_dim, length), bf16),
            sds((8, length), f32),
            stored((model_dim, 2 * width), bf16),
        ),
        name="out_grad",
        cost_estimate=cost(9),
        compiler_params=vmem_limit(length),
    )(starts, table, own, other, low, high, normed, mixed, gain)


def column_tile(columns):
    return 3 * LANES if columns % (3 * LANES) == 0 else LANES


def store_blocks(table_ref, source_ref, keep_ref, send_ref, columns):
    count = table_ref.shape[0]
    rows = source_ref.shape[0] // count
    half = count // 2
    for spot in range(count):
        target = keep_ref if spot < half else send_ref
        at = (spot % half) * rows
        where = pl.multiple_of(table_ref[spot] * rows, rows)
        target[at : at + rows, columns] = source_ref[pl.ds(where, rows), :].astype(bf16)


def gated_kernel(
    table_ref,
    gate_ref,
    nog_ref,
    mixed_ref,
    sums_ref,
    more_ref,
    aux_ref,
    gain_ref,
    gturned_ref,
    nturned_ref,
    out_ref,
    dgate_ref,
    grad_ref,
    row_ref,
    keep_ref,
    send_ref,
    total_ref,
    both_ref,
    gheld_ref,
    nheld_ref,
    sem_ref,
    *,
    full_inner,
):
    step = pl.program_id(0)
    width = gate_ref.shape[1]
    tile = total_ref.shape[1]
    copies = [
        pltpu.make_async_copy(nturned_ref, nheld_ref, sem_ref.at[0]),
        pltpu.make_async_copy(gturned_ref, gheld_ref, sem_ref.at[1]),
    ]

    @pl.when(step == 0)
    def _():
        for copy in copies:
            copy.start()

    inv, mean = token_scales(sums_ref[...] + more_ref[...], full_inner)
    gain = gain_ref[...].astype(f32)
    start = pl.multiple_of(step * TOKEN_BLOCK, TOKEN_BLOCK)
    sums = {}
    for top in range(0, TOKEN_BLOCK, ROW_TILE):
        part = slice(top, top + ROW_TILE)
        here = pl.ds(start + top, ROW_TILE)
        live = aux_ref[part, 7:8]
        inv_part = inv[part]
        mean_part = mean[part]
        for at in range(0, width, LANES):
            lanes = slice(at, at + LANES)
            gate = gate_ref[part, lanes].astype(f32)
            gate_sig = sigmoid(gate)
            gate_silu = gate * gate_sig
            mixed = mixed_ref[part, lanes].astype(f32)
            unit = mixed * gate_silu * inv_part
            nog = nog_ref[part, lanes].astype(f32)
            grad = inv_part * (nog * gain[:, lanes] - unit * mean_part)
            dgate = (grad * mixed * silu_slope(gate, gate_sig)).astype(bf16)
            dgate_ref[part, lanes] = dgate
            both_ref[here, lanes] = dgate
            grad_ref[part, lanes] = (grad * gate_silu * live).astype(bf16)
            normed_out = (unit * gain[:, lanes]).astype(bf16)
            out_ref[part, lanes] = normed_out
            both_ref[here, slice(width + at, width + at + LANES)] = normed_out
            row = jnp.sum((nog * unit).reshape(-1, 8, LANES), axis=0)
            sums[at] = row if top == 0 else sums[at] + row
    for at in range(0, width, LANES):
        row_ref[pl.ds(step * 8, 8), slice(at, at + LANES)] = sums[at]

    @pl.when(step == pl.num_programs(0) - 1)
    def _():
        for copy in copies:
            copy.wait()
        for at in range(0, 2 * width, tile):
            turned = nheld_ref if at < width else gheld_ref
            total_ref[...] = dot_nn(turned[...], both_ref[:, at : at + tile])
            store_blocks(table_ref, total_ref, keep_ref, send_ref, slice(at, at + tile))


def run_gated(table, gate, nog, mixed, sums, more, aux, gain, gturned, nturned, full_inner):
    length, width = gate.shape
    model_dim = gturned.shape[0]
    blocks = length // TOKEN_BLOCK
    tile = column_tile(width)
    sds = jax.ShapeDtypeStruct
    mixed, nturned = from_store(mixed, nturned)
    tokens = pl.BlockSpec((TOKEN_BLOCK, width), lambda i, t: (i, 0))
    halves_spec = pl.BlockSpec((model_dim // 2, 2 * width), lambda i, t: (0, 0))
    return pl.pallas_call(
        partial(gated_kernel, full_inner=float(full_inner)),
        grid_spec=pltpu.PrefetchScalarGridSpec(
            num_scalar_prefetch=1,
            grid=(blocks,),
            in_specs=[
                tokens,
                tokens,
                tokens,
                pl.BlockSpec((8, TOKEN_BLOCK), lambda i, t: (0, i)),
                pl.BlockSpec((8, TOKEN_BLOCK), lambda i, t: (0, i)),
                pl.BlockSpec((TOKEN_BLOCK, aux.shape[1]), lambda i, t: (i, 0)),
                pl.BlockSpec((1, width), lambda i, t: (0, 0)),
                pl.BlockSpec(memory_space=pl.ANY),
                pl.BlockSpec(memory_space=pl.ANY),
            ],
            out_specs=[
                tokens,
                tokens,
                tokens,
                pl.BlockSpec((8 * blocks, width), lambda i, t: (0, 0)),
                halves_spec,
                halves_spec,
            ],
            scratch_shapes=[
                pltpu.VMEM((model_dim, tile), f32),
                pltpu.VMEM((length, 2 * width), bf16),
                pltpu.VMEM((model_dim, length), bf16),
                pltpu.VMEM((model_dim, length), bf16),
                pltpu.SemaphoreType.DMA((2,)),
            ],
        ),
        out_shape=(
            sds((length, width), bf16),
            stored((length, width), bf16),
            stored((length, width), bf16),
            sds((8 * blocks, width), f32),
            sds((model_dim // 2, 2 * width), bf16),
            sds((model_dim // 2, 2 * width), bf16),
        ),
        name="gated_grad",
        cost_estimate=cost(9),
        compiler_params=vmem_limit(length),
    )(table, gate, nog, mixed, sums, more, aux, gain, gturned, nturned)


def out_kernel(starts_ref, rows_ref, weights_ref, send_ref, keep_ref):
    step = pl.program_id(0)
    half = pl.num_programs(0) // 2
    rows = dot_nt(rows_ref[...], weights_ref[...]).astype(bf16)

    @pl.when(step < half)
    def _():
        send_ref[...] = rows

    @pl.when(step >= half)
    def _():
        keep_ref[...] = rows


def run_out(starts, rows, weights):
    length, width = rows.shape
    model_dim = weights.shape[0]
    blocks = length // TOKEN_BLOCK
    half = blocks // 2
    sds = jax.ShapeDtypeStruct
    (weights,) = from_store(weights)
    return pl.pallas_call(
        out_kernel,
        grid_spec=pltpu.PrefetchScalarGridSpec(
            num_scalar_prefetch=1,
            grid=(blocks,),
            in_specs=[
                pl.BlockSpec((TOKEN_BLOCK, width), lambda i, s: (lax.rem(i + s[0], blocks), 0)),
                pl.BlockSpec((model_dim, width), lambda i, s: (0, 1)),
            ],
            out_specs=[
                pl.BlockSpec((TOKEN_BLOCK, model_dim), lambda i, s: (jnp.minimum(i, half - 1), 0)),
                pl.BlockSpec((TOKEN_BLOCK, model_dim), lambda i, s: (jnp.maximum(i - half, 0), 0)),
            ],
        ),
        out_shape=(
            sds((length // 2, model_dim), bf16),
            sds((length // 2, model_dim), bf16),
        ),
        name="out_project",
        cost_estimate=cost(4),
        compiler_params=vmem_limit(length),
    )(starts, rows, weights)


def norm_grad_kernel(starts_ref, dgate_ref, dproj_ref, gates_ref, weights_ref, grad_ref):
    grad = dot_nt(dgate_ref[...], gates_ref[...]) + dot_nt(dproj_ref[...], weights_ref[...])
    grad_ref[...] = grad.astype(grad_ref.dtype)


def run_norm_grad(starts, dgate, dproj, gates, weights, kind):
    length, columns = dproj.shape
    width = dgate.shape[1]
    model_dim = weights.shape[0]
    blocks = length // TOKEN_BLOCK // 2
    dgate, dproj, gates, weights = from_store(dgate, dproj, gates, weights)
    return pl.pallas_call(
        norm_grad_kernel,
        grid_spec=pltpu.PrefetchScalarGridSpec(
            num_scalar_prefetch=1,
            grid=(blocks,),
            in_specs=[
                pl.BlockSpec((TOKEN_BLOCK, width), lambda i, s: (i + s[0], 0)),
                pl.BlockSpec((TOKEN_BLOCK, columns), lambda i, s: (i + s[0], 0)),
                pl.BlockSpec((model_dim, width), lambda i, s: (0, 0)),
                pl.BlockSpec((model_dim, columns), lambda i, s: (0, 0)),
            ],
            out_specs=pl.BlockSpec((TOKEN_BLOCK, model_dim), lambda i, s: (i, 0)),
        ),
        out_shape=jax.ShapeDtypeStruct((length // 2, model_dim), kind),
        name="normed_grad",
        cost_estimate=cost(5),
        compiler_params=vmem_limit(length),
    )(starts, dgate, dproj, gates, weights)


def finish_kernel(
    got_ref, gate_ref, later_ref, packed_ref, inner_ref, step_ref, small_ref, final_ref, *, heads
):
    rows, width = gate_ref.shape
    columns = packed_ref.shape[1]
    shared_cols = slice(width, columns - LANES)
    group = rows + 8
    total = got_ref[:group, :].astype(f32)
    for chip in range(1, got_ref.shape[0] // group):
        total = total + got_ref[chip * group : (chip + 1) * group, :].astype(f32)
    weights = total[:rows]
    small = total[rows:]
    gate = gate_ref[...]
    inner_ref[:, 0, :] = gate
    inner_ref[:, 1, :] = weights[:, :width]
    step_ref[...] = weights[:, columns - LANES :]
    small_ref[...] = small
    real = lax.broadcasted_iota(jnp.int32, (rows, columns), 1) < columns - LANES + heads
    scaled = jnp.where(real, weights * packed_ref[...].astype(f32), 0.0)
    norm = jnp.sum(scaled, axis=1, keepdims=True) + jnp.sum(
        gate * later_ref[...].astype(f32), axis=1, keepdims=True
    )
    final_ref[...] = jnp.zeros_like(final_ref)
    shared_size = columns - LANES - width
    final_ref[:rows, :shared_size] = weights[:, shared_cols]
    final_ref[rows:, :shared_size] = small[:, shared_cols]
    final_ref[:rows, shared_size:] = jnp.broadcast_to(norm, (rows, LANES))


def run_finish(got, gate, later, packed, heads):
    rows, width = gate.shape
    columns = packed.shape[1]
    sds = jax.ShapeDtypeStruct
    return pl.pallas_call(
        partial(finish_kernel, heads=heads),
        grid=(1,),
        in_specs=[
            fixed_spec(got),
            fixed_spec(gate),
            pl.BlockSpec((rows, width), lambda i: (0, 0)),
            fixed_spec(packed),
        ],
        out_specs=[
            pl.BlockSpec((rows, 2, width), lambda i: (0, 0, 0)),
            pl.BlockSpec((rows, LANES), lambda i: (0, 0)),
            pl.BlockSpec((8, columns), lambda i: (0, 0)),
            pl.BlockSpec((rows + 8, columns - width), lambda i: (0, 0)),
        ],
        out_shape=(
            sds((rows, 2, width), f32),
            sds((rows, LANES), f32),
            sds((8, columns), f32),
            sds((rows + 8, columns - width), f32),
        ),
        name="finish",
        cost_estimate=cost(2),
        compiler_params=vmem_limit(1024),
    )(got, gate, later, packed)


def after(value, *others):
    return lax.optimization_barrier((value,) + others)[0]


def cost(microseconds):
    return pl.CostEstimate(flops=int(microseconds * 1.1e9), transcendentals=0, bytes_accessed=0)


def stored(shape, kind):
    return pltpu.HBM(shape, kind)


def from_store(*values):
    return tuple(pltpu.with_memory_space_constraint(v, pltpu.HBM) for v in values)


def vmem_limit(length):
    return pltpu.CompilerParams(vmem_limit_bytes=min(60, VMEM_BASE + length // 128) << 20)


def pad_to(values, axis, size):
    pads = [(0, 0)] * values.ndim
    pads[axis] = (0, size - values.shape[axis])
    return jnp.pad(values, pads)


def body(
    hidden_in,
    segment_ids,
    norm_gain,
    proj_inner,
    proj_shared,
    proj_step,
    conv_inner,
    conv_shared,
    step_bias,
    log_decay,
    skip_gain,
    gate_gain,
    proj_out,
    out_grad,
):
    dp_count = lax.axis_size("dp")
    dp_index = lax.axis_index("dp")
    rows = proj_inner.shape[0]
    length = segment_ids.shape[0]
    model_dim = hidden_in.shape[1]
    local_inner = proj_inner.shape[2]
    heads = proj_step.shape[1]
    state_size = proj_shared.shape[2]
    kernel_len = conv_inner.shape[0]
    shared_size = 2 * state_size
    full_inner = local_inner * lax.axis_size("tensor")
    width = -(-local_inner // (2 * LANES)) * 2 * LANES
    tap_block = conv_shared.shape[2]
    tap_count = kernel_len * 2 * tap_block
    stages, core, table = block_plan()
    groups, core_table = core_groups()
    blocks = length // TOKEN_BLOCK
    starts = token_starts(blocks)
    two = lax.axis_size("tensor") == 2

    chips = dp_count // 2
    hidden_own, hidden_other = both_halves(hidden_in)
    tap_rows = conv_shared.transpose(1, 2, 0).reshape(2 * tap_block, kernel_len)
    tap_rows = pad_to(tap_rows, 0, rows)
    packed = jnp.concatenate(
        [
            pad_to(proj_inner[:, 1, :], 1, width),
            proj_shared.reshape(rows, shared_size),
            pad_to(jnp.concatenate([proj_step, norm_gain[:, None], tap_rows], axis=1), 1, LANES),
        ],
        axis=1,
    )
    later = jnp.concatenate(
        [pad_to(proj_inner[:, 0, :], 1, width), pad_to(proj_out.T, 1, width)], axis=1
    )
    at = jnp.arange(model_dim)
    block, inside = at // rows, at % rows
    side, spot = inside // tap_block, inside % tap_block
    spread = jnp.where(side < 2, side * state_size + block * tap_block + spot, -1)
    spread = (spread[:, None] == jnp.arange(shared_size)[None, :]).astype(bf16)
    aux, segr = token_facts(segment_ids)
    heads_block = jnp.stack([step_bias, log_decay, skip_gain])
    heads_block = pad_to(pad_to(heads_block, 1, LANES), 0, 8)
    tapi = pad_to(conv_inner, 1, width)
    gain = pad_to(gate_gain[None], 1, width)

    later_all = jnp.broadcast_to(later[None], (chips,) + later.shape)
    later_all = later_all.reshape(chips * rows, 2 * width)
    low = packed
    for number, stage in enumerate(stages):
        if number == len(stages) - 1:
            low, later_all = lax.optimization_barrier((low, later_all))
        got = lax.ppermute(low, "dp", stage)
        if number == 0:
            got, aux, segr = lax.optimization_barrier((got, aux, segr))
        if number == 1:
            got, heads_block, tapi, spread, table, core_table = lax.optimization_barrier(
                (got, heads_block, tapi, spread, table, core_table)
            )
        if number == len(stages) - 1:
            got, gain = lax.optimization_barrier((got, gain))
        low = jnp.concatenate([low, got], axis=0)
    later_low = exchange(later_all, groups)
    low, hidden_other = lax.optimization_barrier((low, hidden_other))
    high = lax.ppermute(low, "dp", core)
    grad_own, grad_other = both_halves(after(out_grad, hidden_other))

    proj, praw, normed, normed_t, weights, taps, norm_scale = run_project(
        starts, table, hidden_own, hidden_other, spread, low, high, heads
    )
    norm_scale = norm_scale[:1]
    mixed, u, su, entry = run_forward(proj, praw, tapi, taps, heads_block, aux, segr)

    later_low, mixed, grad_other = lax.optimization_barrier((later_low, mixed, grad_other))
    later_high = lax.ppermute(later_low, "dp", core)
    gate, nog, grad_t, sums, later_rows = run_out_grad(
        starts, core_table, grad_own, grad_other, later_low, later_high, normed, mixed, gain
    )
    if two:
        more = swap(sums)
    else:
        sums = lax.psum(sums, "tensor")
        more = jnp.zeros_like(sums)
    normed_out, dgate, mixed_grad, gain_rows, gkeep, gsend = run_gated(
        core_table, gate, nog, mixed, sums, more, aux, gain, grad_t, normed_t, full_inner
    )
    ggot = lax.ppermute(gsend, "dp", core)
    send_start = starts[1:] if two else jnp.zeros((1,), jnp.int32)
    out_send, out_keep = run_out(send_start, normed_out, later_rows)
    ggot, out_send = lax.optimization_barrier((ggot, out_send))
    gsum = exchange((gkeep.astype(f32) + ggot.astype(f32)).astype(bf16), groups)
    out_other = swap(out_send) if two else None

    dproj, wkeep, wsend = run_backward(
        core_table,
        proj,
        praw,
        u,
        su,
        entry,
        mixed_grad,
        tapi,
        taps,
        heads_block,
        aux,
        segr,
        gain_rows,
        normed_t,
    )
    if two:
        wsend, gsum, out_other = lax.optimization_barrier((wsend, gsum, out_other))
    else:
        wsend, gsum = lax.optimization_barrier((wsend, gsum))
    wgot = lax.ppermute(wsend, "dp", core)
    grad_send = run_norm_grad(send_start, dgate, dproj, later_rows, weights, bf16)
    wgot, grad_send = lax.optimization_barrier((wgot, grad_send))
    grad_other = swap(grad_send) if two else None
    held = rows * chips
    wtotal = (wkeep.astype(f32) + wgot.astype(f32)).astype(bf16)
    wtotal = jnp.concatenate(
        [
            wtotal[:held].reshape(chips, rows, -1),
            jnp.broadcast_to(wtotal[None, held:], (chips, 8, wtotal.shape[1])),
        ],
        axis=1,
    ).reshape(chips * (rows + 8), -1)
    wtotal, dproj = lax.optimization_barrier((wtotal, dproj))
    wsum = exchange(wtotal, groups)
    keep_start = starts[:1] if two else jnp.full((1,), blocks // 2, jnp.int32)
    grad_keep = run_norm_grad(keep_start, dgate, dproj, later_rows, weights, f32)
    if two:
        out_half = out_keep.astype(f32) + out_other.astype(f32)
        own_grad = grad_keep + grad_other.astype(f32)
    else:
        out_half = add_halves(out_send, out_keep)
        own_grad = add_halves(grad_send, grad_keep)
    hidden_out = (hidden_in.astype(f32) + out_half).astype(bf16)
    gsum = sum_blocks(gsum, rows)
    out_sum = gsum[:, width : width + local_inner].T
    inner_sum, step_sum, small, final = run_finish(wsum, gsum[:, :width], later, packed, heads)
    conv_total = small[:kernel_len, :local_inner]
    gain_total = small[4, :local_inner]
    skip_total = small[0, width + shared_size : width + shared_size + heads]
    bias_total = small[1, width + shared_size : width + shared_size + heads]
    decay_total = small[2, width + shared_size : width + shared_size + heads]
    final = total_over_tensor(final)
    shared_total = final[:rows, :shared_size].reshape(rows, 2, state_size)
    taps_total = lax.dynamic_slice_in_dim(
        final[rows : rows + kernel_len, :shared_size].reshape(kernel_len, 2, state_size),
        dp_index * tap_block,
        tap_block,
        axis=2,
    )
    norm_total = final[:rows, shared_size] / norm_gain.astype(f32)
    inner_sum = inner_sum[:, :, :local_inner]
    step_sum = step_sum[:, :heads]

    own = hidden_in.astype(f32)
    own_inv = lax.rsqrt(jnp.mean(own * own, axis=-1, keepdims=True) + epsilon)
    own_unit = own * own_inv
    scaled_in = own_grad * norm_scale
    hidden_grad = own_inv * (
        scaled_in - own_unit * jnp.mean(scaled_in * own_unit, axis=-1, keepdims=True)
    ) + out_grad.astype(f32)
    return (
        hidden_out,
        hidden_grad,
        norm_total,
        inner_sum,
        shared_total,
        step_sum,
        conv_total,
        taps_total,
        bias_total,
        decay_total,
        skip_total,
        gain_total,
        out_sum,
    )


def solution(mesh):
    in_specs = (
        P(("dp", "tensor"), None),
        P("dp"),
        P("dp"),
        P("dp", None, "tensor"),
        P("dp", None, None),
        P("dp", "tensor"),
        P(None, "tensor"),
        P(None, None, "dp"),
        P("tensor"),
        P("tensor"),
        P("tensor"),
        P("tensor"),
        P("tensor", "dp"),
        P(("dp", "tensor"), None),
    )
    out_specs = (
        P(("dp", "tensor"), None),
        P(("dp", "tensor"), None),
        P("dp"),
        P("dp", None, "tensor"),
        P("dp", None, None),
        P("dp", "tensor"),
        P(None, "tensor"),
        P(None, None, "dp"),
        P("tensor"),
        P("tensor"),
        P("tensor"),
        P("tensor"),
        P("tensor", "dp"),
    )
    return jax.shard_map(body, mesh=mesh, in_specs=in_specs, out_specs=out_specs, check_vma=False)
```

```python
from functools import partial

import jax
import jax.numpy as jnp
import numpy as np
from jax import lax
from jax.experimental import pallas as pl
from jax.experimental.pallas import tpu as pltpu
from jax.sharding import PartitionSpec as P

HEAD_DIM = 64
CHUNK = 128
LANES = 128
TOKEN_BLOCK = 256
VMEM_BASE = 16
ROW_TILE = 64
epsilon = 1e-05
f32 = jnp.float32
bf16 = jnp.bfloat16
highest = lax.Precision.HIGHEST


def dot_nn(a, b):
    return lax.dot_general(a, b, (((1,), (0,)), ((), ())), preferred_element_type=f32)


def dot_nt(a, b):
    return lax.dot_general(a, b, (((1,), (1,)), ((), ())), preferred_element_type=f32)


def dot_tn(a, b):
    return lax.dot_general(a, b, (((0,), (0,)), ((), ())), preferred_element_type=f32)


def dot_exact(a, b):
    return lax.dot_general(
        a, b, (((1,), (0,)), ((), ())), preferred_element_type=f32, precision=highest
    )


def dot_split(a, b):
    high = a.astype(bf16)
    rest = (a - high.astype(f32)).astype(bf16)
    return dot_nn(high, b) + dot_nn(rest, b)


def two_parts(values):
    high = values.astype(bf16)
    rest = (values - high.astype(f32)).astype(bf16)
    return jnp.concatenate([high, rest], axis=1)


def spread_matrix(shape, size):
    rows = lax.rem(lax.broadcasted_iota(jnp.int32, shape, 0), LANES)
    return (rows == lax.broadcasted_iota(jnp.int32, shape, 1) // size).astype(bf16)


def sigmoid(v):
    return 1.0 / (1.0 + jnp.exp(-v))


def softplus(v):
    return jnp.maximum(v, 0.0) + jnp.log1p(jnp.exp(-jnp.abs(v)))


def halves(lane_low, values, head):
    return jnp.where(lane_low, values[:, head : head + 1], values[:, head + 1 : head + 2])


def head_sides():
    low = (lax.broadcasted_iota(jnp.int32, (CHUNK, LANES), 1) < HEAD_DIM).astype(f32)
    return low.astype(bf16), (1.0 - low).astype(bf16)


def by_head(values, sides):
    return jnp.concatenate([values * sides[0], values * sides[1]], axis=0)


def back_shift(window, offset):
    return pltpu.roll(window, offset, 0)[8:, :]


def ahead_shift(window, offset):
    rows = window.shape[0]
    return pltpu.roll(window, rows - offset, 0)[: rows - 8, :]


def conv_rows(window, taps, aux):
    total = taps[3:4, :] * window[8:, :]
    for offset in range(1, 4):
        total = total + taps[3 - offset : 4 - offset, :] * (
            back_shift(window, offset) * aux[:, offset : offset + 1]
        )
    return total


def forward_kernel(
    proj_ref,
    step_ref,
    tapi_ref,
    taps_ref,
    heads_ref,
    aux_ref,
    segr_ref,
    mixed_ref,
    u_ref,
    su_ref,
    entry_ref,
    state_ref,
    carry_ref,
    scarry_ref,
    xw_ref,
    channels_ref,
    columns_ref,
):
    width = mixed_ref.shape[1]
    pairs = width // LANES
    shared_size = su_ref.shape[1]
    state_size = shared_size // 2
    chunk = pl.program_id(0)

    @pl.when(chunk == 0)
    def _():
        for ref in (state_ref, carry_ref, scarry_ref):
            ref[...] = jnp.zeros_like(ref)
        channels_ref[...] = spread_matrix(channels_ref.shape, HEAD_DIM)
        columns_ref[...] = spread_matrix(columns_ref.shape, CHUNK)

    rows = lax.broadcasted_iota(jnp.int32, (CHUNK, CHUNK), 0)
    cols = lax.broadcasted_iota(jnp.int32, (CHUNK, CHUNK), 1)
    lower = rows >= cols
    summing = lower.astype(f32)
    lane_low = lax.broadcasted_iota(jnp.int32, (CHUNK, LANES), 1) < HEAD_DIM
    sides = head_sides()
    bias = heads_ref[0:1, :]
    rate = -jnp.exp(heads_ref[1:2, :])
    skips = heads_ref[2:3, :]
    aux = aux_ref[...]
    live = aux[:, 7:8]
    same = lower & (aux[:, 0:1] == segr_ref[pl.ds(chunk, 1), :])
    shared_now = proj_ref[:, width:].astype(f32)
    su = conv_rows(jnp.concatenate([scarry_ref[...], shared_now], axis=0), taps_ref[...], aux)
    scarry_ref[...] = shared_now[CHUNK - 8 :, :]
    su_ref[...] = su
    shared = (su * sigmoid(su)).astype(bf16)
    b_rows = shared[:, :state_size]
    c_rows = shared[:, state_size:]
    scores = jnp.where(same, dot_nt(c_rows, b_rows), 0.0)
    step = softplus(step_ref[...] + bias) * live
    decay = dot_exact(summing, step * rate)
    decay_parts = two_parts(decay)
    decay = decay_parts[:, :LANES].astype(f32) + decay_parts[:, LANES:].astype(f32)
    decay_wide = dot_nn(decay_parts, columns_ref[...])
    decay_t = decay.T
    last = decay[CHUNK - 1 :, :]
    entry_scale = jnp.exp(decay) * aux[:, 8:9]
    end_scale = jnp.exp(last - decay) * aux[:, 9:10]
    keep = jnp.exp(last) * aux[:1, 10:11]
    step_wide = dot_nn(two_parts(step), channels_ref[...])
    entry_wide = dot_nn(two_parts(entry_scale), channels_ref[...])
    end_wide = dot_nn(two_parts(end_scale), channels_ref[...])
    state = state_ref[...]
    state_low = state.astype(bf16)
    entry_ref[...] = state_low[None]
    past = dot_nn(c_rows, state_low)
    for pair in range(pairs):
        lanes = slice(pair * LANES, (pair + 1) * LANES)
        head = 2 * pair
        now = proj_ref[:, lanes].astype(f32)
        window = jnp.concatenate([carry_ref[:, lanes], now], axis=0)
        carry_ref[:, lanes] = now[CHUNK - 8 :, :]
        u = conv_rows(window, tapi_ref[:, lanes].astype(f32), aux)
        u_ref[:, lanes] = u.astype(bf16)
        x = u * sigmoid(u)
        scaled = x * step_wide[:, lanes]
        mixing = jnp.concatenate(
            [
                (
                    scores
                    * jnp.exp(jnp.minimum(decay_wide[:, h * CHUNK : (h + 1) * CHUNK] - decay_t[h : h + 1, :], 0.0))
                ).astype(bf16)
                for h in (head, head + 1)
            ],
            axis=1,
        )
        stacked = by_head(scaled.astype(bf16), sides)
        inside = dot_nn(mixing, stacked)
        xw_ref[:, lanes] = (scaled * end_wide[:, lanes]).astype(bf16)
        mixed = (
            inside
            + past[:, lanes] * entry_wide[:, lanes]
            + halves(lane_low[:1], skips, head) * x
        ) * live
        mixed_ref[:, lanes] = mixed.astype(bf16)
        state_ref[:, lanes] = state[:, lanes] * halves(lane_low[:1], keep, head)
    state_ref[...] += dot_tn(b_rows, xw_ref[...])


def token_scales(sums, full_inner):
    columns = sums.T
    inv = lax.rsqrt(columns[:, 0:1] / full_inner + epsilon)
    return inv, inv * columns[:, 1:2] / full_inner


def silu_slope(v, s):
    return s * (1.0 + v * (1.0 - s))


def backward_kernel(
    table_ref,
    proj_ref,
    praw_ref,
    u_ref,
    su_ref,
    entry_ref,
    grad_ref,
    tapi_ref,
    taps_ref,
    heads_ref,
    aux_ref,
    segr_ref,
    gain_ref,
    turned_ref,
    dproj_ref,
    keep_ref,
    send_ref,
    wide_ref,
    shared_ref,
    small_ref,
    total_ref,
    grads_ref,
    held_ref,
    sem_ref,
    state_ref,
    ahead_ref,
    sahead_ref,
    xw_ref,
    ge_ref,
    row_ref,
    proda_ref,
    prodb_ref,
    channels_ref,
    columns_ref,
):
    width = u_ref.shape[1]
    chunks = pl.num_programs(0)
    pairs = width // LANES
    shared_size = su_ref.shape[1]
    state_size = shared_size // 2
    shared_cols = slice(width, width + shared_size)
    step_cols = slice(width + shared_size, width + shared_size + LANES)
    chunk = chunks - 1 - pl.program_id(0)
    copy = pltpu.make_async_copy(turned_ref, held_ref, sem_ref.at[0])

    @pl.when(pl.program_id(0) == 0)
    def _():
        copy.start()
        channels_ref[...] = spread_matrix(channels_ref.shape, HEAD_DIM)
        columns_ref[...] = spread_matrix(columns_ref.shape, CHUNK)
        for ref in (state_ref, ahead_ref, sahead_ref, row_ref, wide_ref, shared_ref):
            ref[...] = jnp.zeros_like(ref)

    rows = lax.broadcasted_iota(jnp.int32, (CHUNK, CHUNK), 0)
    cols = lax.broadcasted_iota(jnp.int32, (CHUNK, CHUNK), 1)
    upper = rows <= cols
    summing = (rows >= cols).astype(f32)
    unsumming = upper.astype(f32)
    last_row = (lax.broadcasted_iota(jnp.int32, (CHUNK, LANES), 0) == CHUNK - 1).astype(f32)
    lane_ids = lax.broadcasted_iota(jnp.int32, (CHUNK, LANES), 1)
    lane_low = lane_ids < HEAD_DIM
    sides = head_sides()
    bias = heads_ref[0:1, :]
    rate = -jnp.exp(heads_ref[1:2, :])
    skips = heads_ref[2:3, :]
    place = (
        lax.broadcasted_iota(jnp.int32, (width, LANES), 0) // HEAD_DIM
        == lax.broadcasted_iota(jnp.int32, (width, LANES), 1)
    ).astype(bf16)

    aux = aux_ref[...]
    live = aux[:, 7:8]
    same = upper & (aux[:, 0:1] == segr_ref[pl.ds(chunk, 1), :])
    su = su_ref[...]
    su_sig = sigmoid(su)
    shared = (su * su_sig).astype(bf16)
    b_rows = shared[:, :state_size]
    c_rows = shared[:, state_size:]
    scores = jnp.where(same, dot_nt(b_rows, c_rows), 0.0)
    pre = praw_ref[...] + bias
    step = softplus(pre) * live
    decay = dot_exact(summing, step * rate)
    decay_parts = two_parts(decay)
    decay = decay_parts[:, :LANES].astype(f32) + decay_parts[:, LANES:].astype(f32)
    decay_wide = dot_nn(decay_parts, columns_ref[...])
    decay_t = decay.T
    last = decay[CHUNK - 1 :, :]
    entry_scale = jnp.exp(decay) * aux[:, 8:9]
    end_scale = jnp.exp(last - decay) * aux[:, 9:10]
    keep = jnp.exp(last) * aux[:1, 10:11]
    step_wide = dot_nn(two_parts(step), channels_ref[...])
    entry_wide = dot_nn(two_parts(entry_scale), channels_ref[...])
    end_wide = dot_nn(two_parts(end_scale), channels_ref[...])
    entry = entry_ref[0]
    dstate = state_ref[...]
    dstate_low = dstate.astype(bf16)
    past = dot_nn(c_rows, entry)
    bds = dot_nn(b_rows, dstate_low)
    here = pl.ds(pl.multiple_of(chunk * CHUNK, CHUNK), CHUNK)
    score_grad = jnp.zeros((CHUNK, CHUNK), f32)
    col_part = jnp.zeros((CHUNK, LANES), f32)
    for pair in range(pairs):
        lanes = slice(pair * LANES, (pair + 1) * LANES)
        head = 2 * pair
        g_low = grad_ref[:, lanes]
        g = g_low.astype(f32)
        u = u_ref[:, lanes].astype(f32)
        u_sig = sigmoid(u)
        x = u * u_sig
        step_c = step_wide[:, lanes]
        scaled = x * step_c
        stacked = by_head(scaled.astype(bf16), sides)
        dmix = dot_nt(stacked, g_low)
        mixing = []
        for k, h in enumerate((head, head + 1)):
            decays = jnp.exp(jnp.minimum(decay_t[h : h + 1, :] - decay_wide[:, h * CHUNK : (h + 1) * CHUNK], 0.0))
            dmix_h = dmix[k * CHUNK : (k + 1) * CHUNK, :]
            score_grad = score_grad + dmix_h * decays
            mixing_h = scores * decays
            mixing.append(mixing_h.astype(bf16))
            both = mixing_h * dmix_h
            col_part = jnp.where(lane_ids == h, jnp.sum(both, axis=1, keepdims=True), col_part)
            row_ref[h : h + 1, :] = jnp.sum(both, axis=0, keepdims=True)
        g_stacked = by_head(g_low, sides)
        end_c = end_wide[:, lanes]
        entry_c = entry_wide[:, lanes]
        keep_c = halves(lane_low[:1], keep, head)
        from_state = end_c * bds[:, lanes]
        dscaled = dot_nn(jnp.concatenate(mixing, axis=1), g_stacked) + from_state
        xw_ref[:, lanes] = (scaled * end_c).astype(bf16)
        q = scaled * from_state
        ge = g * entry_c
        ge_ref[:, lanes] = ge.astype(bf16)
        dstate_p = dstate[:, lanes]
        tail = jnp.sum(q, axis=0, keepdims=True) + keep_c * jnp.sum(
            dstate_p * entry[:, lanes].astype(f32), axis=0, keepdims=True
        )
        proda_ref[:, lanes] = (x * dscaled).astype(bf16)
        prodb_ref[:, lanes] = ge * past[:, lanes] - q + last_row * tail
        state_ref[:, lanes] = dstate_p * keep_c
        dx = step_c * dscaled + halves(lane_low[:1], skips, head) * g
        du = dx * silu_slope(u, u_sig)
        window = jnp.concatenate([du, ahead_ref[:, lanes]], axis=0)
        ahead_ref[:, lanes] = du[:8, :]
        cin = proj_ref[:, lanes].astype(f32)
        taps = tapi_ref[:, lanes].astype(f32)
        dcin = taps[3:4, :] * du
        wide_ref[3:4, lanes] += jnp.sum(cin * du, axis=0, keepdims=True)
        for offset in range(1, 4):
            moved = ahead_shift(window, offset) * aux[:, 3 + offset : 4 + offset]
            dcin = dcin + taps[3 - offset : 4 - offset, :] * moved
            wide_ref[3 - offset : 4 - offset, lanes] += jnp.sum(
                cin * moved, axis=0, keepdims=True
            )
        dcin = dcin.astype(bf16)
        dproj_ref[:, lanes] = dcin
        grads_ref[here, lanes] = dcin
        wide_ref[5:6, lanes] += jnp.sum(g * x, axis=0, keepdims=True)
    score_low = jnp.where(same, score_grad, 0.0).astype(bf16)
    ge_all = ge_ref[...]
    db = dot_nn(score_low, c_rows) + dot_nt(xw_ref[...], dstate_low)
    dc = dot_tn(score_low, b_rows) + dot_nt(ge_all, entry)
    state_ref[...] += dot_tn(c_rows, ge_all)
    ds = jnp.concatenate([db, dc], axis=1) * silu_slope(su, su_sig)
    window = jnp.concatenate([ds, sahead_ref[...]], axis=0)
    sahead_ref[...] = ds[:8, :]
    taps = taps_ref[...]
    sin = proj_ref[:, shared_cols].astype(f32)
    dsin = taps[3:4, :] * ds
    shared_ref[3:4, :] += jnp.sum(sin * ds, axis=0, keepdims=True)
    for offset in range(1, 4):
        moved = ahead_shift(window, offset) * aux[:, 3 + offset : 4 + offset]
        dsin = dsin + taps[3 - offset : 4 - offset, :] * moved
        shared_ref[3 - offset : 4 - offset, :] += jnp.sum(sin * moved, axis=0, keepdims=True)
    dsin = dsin.astype(bf16)
    dproj_ref[:, shared_cols] = dsin
    grads_ref[here, shared_cols] = dsin
    ddecay = row_ref[...].T - col_part + dot_split(prodb_ref[...], place)
    dlog = dot_exact(unsumming, ddecay)
    dstep = (dot_nn(proda_ref[...], place) + rate * dlog) * live * sigmoid(pre)
    dproj_ref[:, step_cols] = dstep.astype(bf16)
    grads_ref[here, step_cols] = dstep.astype(bf16)
    wide_ref[6:7, :LANES] += jnp.sum(dstep, axis=0, keepdims=True)
    wide_ref[6:7, LANES : 2 * LANES] += jnp.sum(step * dlog, axis=0, keepdims=True) * rate

    @pl.when(chunk == 0)
    def _():
        small_ref[...] = jnp.zeros_like(small_ref)
        small_ref[:4, :width] = wide_ref[:4, :]
        small_ref[:4, width : width + shared_size] = shared_ref[:4, :]
        skip_row = dot_split(wide_ref[...], place)[5:6, :]
        small_ref[0:1, step_cols] = skip_row
        small_ref[1:2, step_cols] = wide_ref[6:7, :LANES]
        small_ref[2:3, step_cols] = wide_ref[6:7, LANES : 2 * LANES]
        small_ref[4:5, :width] = jnp.sum(gain_ref[...], axis=0, keepdims=True)
        copy.wait()
        held = keep_ref.shape[0] - 8
        keep_ref[held:, :] = small_ref[...].astype(bf16)
        send_ref[held:, :] = small_ref[...].astype(bf16)
        tile = total_ref.shape[1]
        for at in range(0, width + shared_size + LANES, tile):
            total_ref[...] = dot_nn(held_ref[...], grads_ref[:, at : at + tile])
            store_blocks(table_ref, total_ref, keep_ref, send_ref, slice(at, at + tile))


def facts_kernel(seg_ref, aux_ref, segr_ref):
    seg = seg_ref[...].astype(f32)
    chunks = seg.shape[0]
    segr_ref[...] = seg
    none = jnp.full((1, CHUNK), -1.0, f32)
    before = jnp.concatenate([none, seg[: chunks - 1]], axis=0) if chunks > 1 else none
    behind = jnp.concatenate([seg[1:], none], axis=0) if chunks > 1 else none
    lane = lax.broadcasted_iota(jnp.int32, seg.shape, 1)
    facts = [seg]
    for offset in range(1, 4):
        earlier = jnp.where(
            lane >= offset, pltpu.roll(seg, offset, 1), pltpu.roll(before, offset, 1)
        )
        facts.append((earlier == seg).astype(f32))
    for offset in range(1, 4):
        later = jnp.where(
            lane < CHUNK - offset,
            pltpu.roll(seg, CHUNK - offset, 1),
            pltpu.roll(behind, CHUNK - offset, 1),
        )
        facts.append((later == seg).astype(f32))
    last = jnp.broadcast_to(seg[:, CHUNK - 1 :], seg.shape)
    prior = jnp.broadcast_to(before[:, CHUNK - 1 :], seg.shape)
    facts.append((seg != 0.0).astype(f32))
    facts.append((seg == prior).astype(f32))
    facts.append((seg == last).astype(f32))
    facts.append((last == prior).astype(f32))
    empty = jnp.zeros((LANES - len(facts), CHUNK), f32)
    for chunk in range(chunks):
        rows = jnp.concatenate([f[chunk : chunk + 1, :] for f in facts] + [empty], axis=0)
        aux_ref[chunk * CHUNK : (chunk + 1) * CHUNK, :] = rows.T[:, : aux_ref.shape[1]]


def token_facts(segments):
    length = segments.shape[0]
    chunks = length // CHUNK
    return pl.pallas_call(
        facts_kernel,
        out_shape=(
            jax.ShapeDtypeStruct((length, 16), f32),
            jax.ShapeDtypeStruct((chunks, CHUNK), f32),
        ),
        name="token_facts",
        cost_estimate=cost(2),
        compiler_params=vmem_limit(length),
    )(segments.reshape(chunks, CHUNK))


def chunk_spec(columns, last):
    if last is None:
        return pl.BlockSpec((CHUNK, columns), lambda i: (i, 0))
    return pl.BlockSpec((CHUNK, columns), lambda i: (last - i, 0))


def fixed_spec(values):
    zeros = (0,) * values.ndim
    return pl.BlockSpec(values.shape, lambda i: zeros)


def run_forward(proj, praw, tapi, taps, heads, aux, segr):
    length = proj.shape[0]
    width = tapi.shape[1]
    shared_size = taps.shape[1]
    state_size = shared_size // 2
    chunks = length // CHUNK
    proj, praw = from_store(proj, praw)
    return pl.pallas_call(
        forward_kernel,
        grid=(chunks,),
        in_specs=[
            chunk_spec(proj.shape[1], None),
            chunk_spec(LANES, None),
            fixed_spec(tapi),
            fixed_spec(taps),
            fixed_spec(heads),
            chunk_spec(aux.shape[1], None),
            fixed_spec(segr),
        ],
        out_specs=[
            chunk_spec(width, None),
            chunk_spec(width, None),
            chunk_spec(shared_size, None),
            pl.BlockSpec((1, state_size, width), lambda i: (i, 0, 0)),
        ],
        out_shape=(
            stored((length, width), bf16),
            stored((length, width), bf16),
            stored((length, shared_size), f32),
            stored((chunks, state_size, width), bf16),
        ),
        scratch_shapes=[
            pltpu.VMEM((state_size, width), f32),
            pltpu.VMEM((8, width), f32),
            pltpu.VMEM((8, shared_size), f32),
            pltpu.VMEM((CHUNK, width), bf16),
            pltpu.VMEM((2 * LANES, width), bf16),
            pltpu.VMEM((2 * LANES, width // HEAD_DIM * CHUNK), bf16),
        ],
        name="scan_forward",
        cost_estimate=cost(3),
        compiler_params=vmem_limit(length),
    )(proj, praw, tapi, taps, heads, aux, segr)


def run_backward(
    table, proj, praw, u, su, entry, grad, tapi, taps, heads, aux, segr, gain_rows, turned
):
    length, width = u.shape
    shared_size = su.shape[1]
    state_size = shared_size // 2
    model_dim = turned.shape[0]
    chunks = length // CHUNK
    last = chunks - 1
    columns = width + shared_size + LANES
    kept = model_dim // 2 + 8
    sds = jax.ShapeDtypeStruct
    proj, praw, u, su, entry, grad, turned = from_store(proj, praw, u, su, entry, grad, turned)

    def back(size):
        return pl.BlockSpec((CHUNK, size), lambda i, t: (last - i, 0))

    def fixed(shape):
        return pl.BlockSpec(shape, lambda i, t: (0, 0))

    return pl.pallas_call(
        backward_kernel,
        grid_spec=pltpu.PrefetchScalarGridSpec(
            num_scalar_prefetch=1,
            grid=(chunks,),
            in_specs=[
                back(proj.shape[1]),
                back(LANES),
                back(width),
                back(shared_size),
                pl.BlockSpec((1, state_size, width), lambda i, t: (last - i, 0, 0)),
                back(width),
                fixed(tapi.shape),
                fixed(taps.shape),
                fixed(heads.shape),
                back(aux.shape[1]),
                fixed(segr.shape),
                fixed(gain_rows.shape),
                pl.BlockSpec(memory_space=pl.ANY),
            ],
            out_specs=[
                back(columns),
                fixed((kept, columns)),
                fixed((kept, columns)),
            ],
            scratch_shapes=[
                pltpu.VMEM((8, width), f32),
                pltpu.VMEM((8, shared_size), f32),
                pltpu.VMEM((8, columns), f32),
                pltpu.VMEM((model_dim, column_tile(columns)), f32),
                pltpu.VMEM((length, columns), bf16),
                pltpu.VMEM((model_dim, length), bf16),
                pltpu.SemaphoreType.DMA((1,)),
                pltpu.VMEM((state_size, width), f32),
                pltpu.VMEM((8, width), f32),
                pltpu.VMEM((8, shared_size), f32),
                pltpu.VMEM((CHUNK, width), bf16),
                pltpu.VMEM((CHUNK, width), bf16),
                pltpu.VMEM((LANES, CHUNK), f32),
                pltpu.VMEM((CHUNK, width), bf16),
                pltpu.VMEM((CHUNK, width), f32),
                pltpu.VMEM((2 * LANES, width), bf16),
                pltpu.VMEM((2 * LANES, width // HEAD_DIM * CHUNK), bf16),
            ],
        ),
        out_shape=(
            stored((length, columns), bf16),
            stored((kept, columns), bf16),
            stored((kept, columns), bf16),
        ),
        name="scan_backward",
        cost_estimate=cost(36),
        compiler_params=vmem_limit(length),
    )(table, proj, praw, u, su, entry, grad, tapi, taps, heads, aux, segr, gain_rows, turned)


def block_plan():
    count = lax.axis_size("dp")
    bits = []
    bit = count // 2
    while bit > 1:
        bits.append(bit)
        bit //= 2
    mixed = bits[:-2] + bits[-2:][::-1]
    by_core = (bits, mixed)
    stages = []
    for stage in range(len(bits)):
        stages.append([(i, i ^ by_core[i % 2][stage]) for i in range(count)])
    core = [(i, i ^ 1) for i in range(count)]
    device = np.zeros((count, count), np.int32)
    for own in range(count):
        for spot in range(count):
            other = own ^ 1 if spot >= count // 2 else own
            for stage, bit in enumerate(by_core[other % 2]):
                if (spot >> stage) & 1:
                    other ^= bit
            device[own, spot] = other
    table = jnp.asarray(device)[lax.axis_index("dp")]
    return stages, core, table


def core_groups():
    count = lax.axis_size("dp")
    groups = [list(range(side, count, 2)) for side in range(2)]
    return groups, jnp.asarray(
        [groups[0] + groups[1], groups[1] + groups[0]], jnp.int32
    )[lax.axis_index("dp") % 2]


def exchange(blocks, groups):
    return lax.all_to_all(
        blocks, "dp", 0, 0, axis_index_groups=groups, tiled=True
    )


def sum_blocks(blocks, rows):
    return jnp.sum(blocks.reshape(-1, rows, blocks.shape[1]).astype(f32), axis=0)


def swap(values):
    return lax.ppermute(values, "tensor", [(0, 1), (1, 0)])


def total_over_tensor(values):
    if lax.axis_size("tensor") == 2:
        return values + swap(values)
    return lax.psum(values, "tensor")


def both_halves(own):
    if lax.axis_size("tensor") == 2:
        return own, swap(own)
    whole = lax.all_gather(own, "tensor", axis=0, tiled=True)
    return whole, whole


def token_starts(blocks):
    if lax.axis_size("tensor") == 2:
        index = lax.axis_index("tensor")
        return jnp.stack([index * (blocks // 2), (1 - index) * (blocks // 2)]).astype(jnp.int32)
    return jnp.zeros((2,), jnp.int32)


def add_halves(send, keep):
    if lax.axis_size("tensor") == 2:
        return keep.astype(f32) + swap(send).astype(f32)
    whole = jnp.concatenate([send.astype(bf16), keep.astype(bf16)], axis=0)
    return lax.psum_scatter(whole, "tensor", scatter_dimension=0, tiled=True).astype(f32)


def own_block(step, starts, own_blocks):
    return jnp.clip(step - starts[0], 0, own_blocks - 1)


def other_block(step, starts, own_blocks):
    return jnp.clip(step - starts[1], 0, own_blocks - 1)


def place_blocks(table_ref, low_ref, high_ref, whole_ref, sem_ref):
    count = table_ref.shape[0]
    rows = whole_ref.shape[0] // count
    copies = []
    for spot in range(count):
        source = low_ref if spot < count // 2 else high_ref
        where = pl.multiple_of(table_ref[spot] * rows, rows)
        copies.append(
            pltpu.make_async_copy(
                source.at[pl.ds((spot % (count // 2)) * rows, rows), :],
                whole_ref.at[pl.ds(where, rows), :],
                sem_ref.at[spot],
            )
        )
    for copy in copies:
        copy.start()
    for copy in copies:
        copy.wait()


def project_kernel(
    starts_ref,
    table_ref,
    own_ref,
    other_ref,
    spread_ref,
    low_ref,
    high_ref,
    proj_ref,
    step_ref,
    normed_ref,
    turned_ref,
    whole_ref,
    taps_ref,
    scale_ref,
    weights_ref,
    sem_ref,
    *,
    own_blocks,
    heads,
):
    step = pl.program_id(0)
    model_dim, columns = weights_ref.shape
    store = pltpu.make_async_copy(weights_ref, whole_ref, sem_ref.at[table_ref.shape[0]])

    @pl.when(step == pl.num_programs(0) - 1)
    def _():
        store.wait()

    @pl.when(step == 0)
    def _():
        place_blocks(table_ref, low_ref, high_ref, weights_ref, sem_ref)
        store.start()
        extra = weights_ref[:, columns - LANES :].astype(f32).T
        scale_ref[...] = jnp.broadcast_to(extra[heads : heads + 1, :], scale_ref.shape)
        taps = extra[heads + 1 : heads + 5, :]
        taps = jnp.concatenate([taps, jnp.zeros_like(taps)], axis=0).astype(bf16)
        taps_ref[...] = dot_nn(taps, spread_ref[...])

    mine = (step >= starts_ref[0]) & (step < starts_ref[0] + own_blocks)
    tokens = jnp.where(mine, own_ref[...].astype(f32), other_ref[...].astype(f32))
    inv = lax.rsqrt(jnp.mean(tokens * tokens, axis=-1, keepdims=True) + epsilon)
    normed = (tokens * inv * scale_ref[:1, :]).astype(bf16)
    normed_ref[...] = normed
    turned_ref[...] = normed.T
    proj = dot_nn(normed, weights_ref[...])
    proj_ref[...] = proj[:, : columns - LANES].astype(bf16)
    step_ref[...] = proj[:, columns - LANES :]


def run_project(starts, table, own, other, spread, low, high, heads):
    own_rows, model_dim = own.shape
    columns = low.shape[1]
    own_blocks = own_rows // TOKEN_BLOCK
    blocks = own_blocks * (2 if lax.axis_size("tensor") == 2 else 1)
    length = blocks * TOKEN_BLOCK
    sds = jax.ShapeDtypeStruct
    own, other, low = from_store(own, other, low)
    return pl.pallas_call(
        partial(project_kernel, own_blocks=own_blocks, heads=heads),
        grid_spec=pltpu.PrefetchScalarGridSpec(
            num_scalar_prefetch=2,
            grid=(blocks,),
            in_specs=[
                pl.BlockSpec(
                    (TOKEN_BLOCK, model_dim), lambda i, s, t: (own_block(i, s, own_blocks), 0)
                ),
                pl.BlockSpec(
                    (TOKEN_BLOCK, model_dim), lambda i, s, t: (other_block(i, s, own_blocks), 0)
                ),
                pl.BlockSpec(spread.shape, lambda i, s, t: (0, 0)),
                pl.BlockSpec(memory_space=pl.ANY),
                pl.BlockSpec(memory_space=pl.ANY),
            ],
            out_specs=[
                pl.BlockSpec((TOKEN_BLOCK, columns - LANES), lambda i, s, t: (i, 0)),
                pl.BlockSpec((TOKEN_BLOCK, LANES), lambda i, s, t: (i, 0)),
                pl.BlockSpec((TOKEN_BLOCK, model_dim), lambda i, s, t: (i, 0)),
                pl.BlockSpec((model_dim, TOKEN_BLOCK), lambda i, s, t: (0, i)),
                pl.BlockSpec(memory_space=pl.ANY),
                pl.BlockSpec((8, spread.shape[1]), lambda i, s, t: (0, 0)),
                pl.BlockSpec((8, model_dim), lambda i, s, t: (0, 0)),
            ],
            scratch_shapes=[
                pltpu.VMEM((model_dim, columns), bf16),
                pltpu.SemaphoreType.DMA((table.shape[0] + 1,)),
            ],
        ),
        out_shape=(
            stored((length, columns - LANES), bf16),
            stored((length, LANES), f32),
            stored((length, model_dim), bf16),
            stored((model_dim, length), bf16),
            stored((model_dim, columns), bf16),
            sds((8, spread.shape[1]), f32),
            sds((8, model_dim), f32),
        ),
        name="norm_project",
        cost_estimate=cost(2),
        compiler_params=vmem_limit(length),
    )(starts, table, own, other, spread, low, high)


def token_sum(values):
    total = values[:, :LANES]
    for at in range(LANES, values.shape[1], LANES):
        total = total + values[:, at : at + LANES]
    return jnp.sum(total.T, axis=0, keepdims=True)


def out_grad_kernel(
    starts_ref,
    table_ref,
    own_ref,
    other_ref,
    low_ref,
    high_ref,
    normed_ref,
    mixed_ref,
    gain_ref,
    gate_ref,
    nog_ref,
    turned_ref,
    sums_ref,
    whole_ref,
    weights_ref,
    sem_ref,
    *,
    own_blocks,
):
    step = pl.program_id(0)
    width = mixed_ref.shape[1]
    store = pltpu.make_async_copy(weights_ref, whole_ref, sem_ref.at[table_ref.shape[0]])

    @pl.when(step == 0)
    def _():
        place_blocks(table_ref, low_ref, high_ref, weights_ref, sem_ref)
        store.start()

    @pl.when(step == pl.num_programs(0) - 1)
    def _():
        store.wait()

    mine = (step >= starts_ref[0]) & (step < starts_ref[0] + own_blocks)
    tokens = jnp.where(mine, own_ref[...].astype(f32), other_ref[...].astype(f32)).astype(bf16)
    turned_ref[...] = tokens.T
    gate = dot_nn(normed_ref[...], weights_ref[:, :width])
    gate_ref[...] = gate.astype(bf16)
    nog = dot_nn(tokens, weights_ref[:, width:])
    nog_ref[...] = nog.astype(bf16)
    gated = mixed_ref[...].astype(f32) * (gate * sigmoid(gate))
    sums_ref[...] = jnp.concatenate(
        [
            token_sum(gated * gated),
            token_sum(nog * gain_ref[...].astype(f32) * gated),
            jnp.zeros((6, TOKEN_BLOCK), f32),
        ],
        axis=0,
    )


def run_out_grad(starts, table, own, other, low, high, normed, mixed, gain):
    own_rows, model_dim = own.shape
    length, width = mixed.shape
    own_blocks = own_rows // TOKEN_BLOCK
    blocks = length // TOKEN_BLOCK
    sds = jax.ShapeDtypeStruct
    own, other, normed, mixed, low, high = from_store(own, other, normed, mixed, low) + (high,)
    return pl.pallas_call(
        partial(out_grad_kernel, own_blocks=own_blocks),
        grid_spec=pltpu.PrefetchScalarGridSpec(
            num_scalar_prefetch=2,
            grid=(blocks,),
            in_specs=[
                pl.BlockSpec(
                    (TOKEN_BLOCK, model_dim), lambda i, s, t: (own_block(i, s, own_blocks), 0)
                ),
                pl.BlockSpec(
                    (TOKEN_BLOCK, model_dim), lambda i, s, t: (other_block(i, s, own_blocks), 0)
                ),
                pl.BlockSpec(memory_space=pl.ANY),
                pl.BlockSpec(memory_space=pl.ANY),
                pl.BlockSpec((TOKEN_BLOCK, model_dim), lambda i, s, t: (i, 0)),
                pl.BlockSpec((TOKEN_BLOCK, width), lambda i, s, t: (i, 0)),
                pl.BlockSpec((1, width), lambda i, s, t: (0, 0)),
            ],
            out_specs=[
                pl.BlockSpec((TOKEN_BLOCK, width), lambda i, s, t: (i, 0)),
                pl.BlockSpec((TOKEN_BLOCK, width), lambda i, s, t: (i, 0)),
                pl.BlockSpec((model_dim, TOKEN_BLOCK), lambda i, s, t: (0, i)),
                pl.BlockSpec((8, TOKEN_BLOCK), lambda i, s, t: (0, i)),
                pl.BlockSpec(memory_space=pl.ANY),
            ],
            scratch_shapes=[
                pltpu.VMEM((model_dim, 2 * width), bf16),
                pltpu.SemaphoreType.DMA((table.shape[0] + 1,)),
            ],
        ),
        out_shape=(
            sds((length, width), bf16),
            sds((length, width), bf16),
            sds((model_dim, length), bf16),
            sds((8, length), f32),
            stored((model_dim, 2 * width), bf16),
        ),
        name="out_grad",
        cost_estimate=cost(9),
        compiler_params=vmem_limit(length),
    )(starts, table, own, other, low, high, normed, mixed, gain)


def column_tile(columns):
    return 3 * LANES if columns % (3 * LANES) == 0 else LANES


def store_blocks(table_ref, source_ref, keep_ref, send_ref, columns):
    count = table_ref.shape[0]
    rows = source_ref.shape[0] // count
    half = count // 2
    for spot in range(count):
        target = keep_ref if spot < half else send_ref
        at = (spot % half) * rows
        where = pl.multiple_of(table_ref[spot] * rows, rows)
        target[at : at + rows, columns] = source_ref[pl.ds(where, rows), :].astype(bf16)


def gated_kernel(
    table_ref,
    gate_ref,
    nog_ref,
    mixed_ref,
    sums_ref,
    more_ref,
    aux_ref,
    gain_ref,
    gturned_ref,
    nturned_ref,
    out_ref,
    dgate_ref,
    grad_ref,
    row_ref,
    keep_ref,
    send_ref,
    total_ref,
    both_ref,
    gheld_ref,
    nheld_ref,
    sem_ref,
    *,
    full_inner,
):
    step = pl.program_id(0)
    width = gate_ref.shape[1]
    tile = total_ref.shape[1]
    copies = [
        pltpu.make_async_copy(nturned_ref, nheld_ref, sem_ref.at[0]),
        pltpu.make_async_copy(gturned_ref, gheld_ref, sem_ref.at[1]),
    ]

    @pl.when(step == 0)
    def _():
        for copy in copies:
            copy.start()

    inv, mean = token_scales(sums_ref[...] + more_ref[...], full_inner)
    gain = gain_ref[...].astype(f32)
    start = pl.multiple_of(step * TOKEN_BLOCK, TOKEN_BLOCK)
    sums = {}
    for top in range(0, TOKEN_BLOCK, ROW_TILE):
        part = slice(top, top + ROW_TILE)
        here = pl.ds(start + top, ROW_TILE)
        live = aux_ref[part, 7:8]
        inv_part = inv[part]
        mean_part = mean[part]
        for at in range(0, width, LANES):
            lanes = slice(at, at + LANES)
            gate = gate_ref[part, lanes].astype(f32)
            gate_sig = sigmoid(gate)
            gate_silu = gate * gate_sig
            mixed = mixed_ref[part, lanes].astype(f32)
            unit = mixed * gate_silu * inv_part
            nog = nog_ref[part, lanes].astype(f32)
            grad = inv_part * (nog * gain[:, lanes] - unit * mean_part)
            dgate = (grad * mixed * silu_slope(gate, gate_sig)).astype(bf16)
            dgate_ref[part, lanes] = dgate
            both_ref[here, lanes] = dgate
            grad_ref[part, lanes] = (grad * gate_silu * live).astype(bf16)
            normed_out = (unit * gain[:, lanes]).astype(bf16)
            out_ref[part, lanes] = normed_out
            both_ref[here, slice(width + at, width + at + LANES)] = normed_out
            row = jnp.sum((nog * unit).reshape(-1, 8, LANES), axis=0)
            sums[at] = row if top == 0 else sums[at] + row
    for at in range(0, width, LANES):
        row_ref[pl.ds(step * 8, 8), slice(at, at + LANES)] = sums[at]

    @pl.when(step == pl.num_programs(0) - 1)
    def _():
        for copy in copies:
            copy.wait()
        for at in range(0, 2 * width, tile):
            turned = nheld_ref if at < width else gheld_ref
            total_ref[...] = dot_nn(turned[...], both_ref[:, at : at + tile])
            store_blocks(table_ref, total_ref, keep_ref, send_ref, slice(at, at + tile))


def run_gated(table, gate, nog, mixed, sums, more, aux, gain, gturned, nturned, full_inner):
    length, width = gate.shape
    model_dim = gturned.shape[0]
    blocks = length // TOKEN_BLOCK
    tile = column_tile(width)
    sds = jax.ShapeDtypeStruct
    mixed, nturned = from_store(mixed, nturned)
    tokens = pl.BlockSpec((TOKEN_BLOCK, width), lambda i, t: (i, 0))
    halves_spec = pl.BlockSpec((model_dim // 2, 2 * width), lambda i, t: (0, 0))
    return pl.pallas_call(
        partial(gated_kernel, full_inner=float(full_inner)),
        grid_spec=pltpu.PrefetchScalarGridSpec(
            num_scalar_prefetch=1,
            grid=(blocks,),
            in_specs=[
                tokens,
                tokens,
                tokens,
                pl.BlockSpec((8, TOKEN_BLOCK), lambda i, t: (0, i)),
                pl.BlockSpec((8, TOKEN_BLOCK), lambda i, t: (0, i)),
                pl.BlockSpec((TOKEN_BLOCK, aux.shape[1]), lambda i, t: (i, 0)),
                pl.BlockSpec((1, width), lambda i, t: (0, 0)),
                pl.BlockSpec(memory_space=pl.ANY),
                pl.BlockSpec(memory_space=pl.ANY),
            ],
            out_specs=[
                tokens,
                tokens,
                tokens,
                pl.BlockSpec((8 * blocks, width), lambda i, t: (0, 0)),
                halves_spec,
                halves_spec,
            ],
            scratch_shapes=[
                pltpu.VMEM((model_dim, tile), f32),
                pltpu.VMEM((length, 2 * width), bf16),
                pltpu.VMEM((model_dim, length), bf16),
                pltpu.VMEM((model_dim, length), bf16),
                pltpu.SemaphoreType.DMA((2,)),
            ],
        ),
        out_shape=(
            sds((length, width), bf16),
            stored((length, width), bf16),
            stored((length, width), bf16),
            sds((8 * blocks, width), f32),
            sds((model_dim // 2, 2 * width), bf16),
            sds((model_dim // 2, 2 * width), bf16),
        ),
        name="gated_grad",
        cost_estimate=cost(9),
        compiler_params=vmem_limit(length),
    )(table, gate, nog, mixed, sums, more, aux, gain, gturned, nturned)


def out_kernel(starts_ref, rows_ref, weights_ref, send_ref, keep_ref):
    step = pl.program_id(0)
    half = pl.num_programs(0) // 2
    rows = dot_nt(rows_ref[...], weights_ref[...]).astype(bf16)

    @pl.when(step < half)
    def _():
        send_ref[...] = rows

    @pl.when(step >= half)
    def _():
        keep_ref[...] = rows


def run_out(starts, rows, weights):
    length, width = rows.shape
    model_dim = weights.shape[0]
    blocks = length // TOKEN_BLOCK
    half = blocks // 2
    sds = jax.ShapeDtypeStruct
    (weights,) = from_store(weights)
    return pl.pallas_call(
        out_kernel,
        grid_spec=pltpu.PrefetchScalarGridSpec(
            num_scalar_prefetch=1,
            grid=(blocks,),
            in_specs=[
                pl.BlockSpec((TOKEN_BLOCK, width), lambda i, s: (lax.rem(i + s[0], blocks), 0)),
                pl.BlockSpec((model_dim, width), lambda i, s: (0, 1)),
            ],
            out_specs=[
                pl.BlockSpec((TOKEN_BLOCK, model_dim), lambda i, s: (jnp.minimum(i, half - 1), 0)),
                pl.BlockSpec((TOKEN_BLOCK, model_dim), lambda i, s: (jnp.maximum(i - half, 0), 0)),
            ],
        ),
        out_shape=(
            sds((length // 2, model_dim), bf16),
            sds((length // 2, model_dim), bf16),
        ),
        name="out_project",
        cost_estimate=cost(4),
        compiler_params=vmem_limit(length),
    )(starts, rows, weights)


def norm_grad_kernel(starts_ref, dgate_ref, dproj_ref, gates_ref, weights_ref, grad_ref):
    grad = dot_nt(dgate_ref[...], gates_ref[...]) + dot_nt(dproj_ref[...], weights_ref[...])
    grad_ref[...] = grad.astype(grad_ref.dtype)


def run_norm_grad(starts, dgate, dproj, gates, weights, kind):
    length, columns = dproj.shape
    width = dgate.shape[1]
    model_dim = weights.shape[0]
    blocks = length // TOKEN_BLOCK // 2
    dgate, dproj, gates, weights = from_store(dgate, dproj, gates, weights)
    return pl.pallas_call(
        norm_grad_kernel,
        grid_spec=pltpu.PrefetchScalarGridSpec(
            num_scalar_prefetch=1,
            grid=(blocks,),
            in_specs=[
                pl.BlockSpec((TOKEN_BLOCK, width), lambda i, s: (i + s[0], 0)),
                pl.BlockSpec((TOKEN_BLOCK, columns), lambda i, s: (i + s[0], 0)),
                pl.BlockSpec((model_dim, width), lambda i, s: (0, 0)),
                pl.BlockSpec((model_dim, columns), lambda i, s: (0, 0)),
            ],
            out_specs=pl.BlockSpec((TOKEN_BLOCK, model_dim), lambda i, s: (i, 0)),
        ),
        out_shape=jax.ShapeDtypeStruct((length // 2, model_dim), kind),
        name="normed_grad",
        cost_estimate=cost(5),
        compiler_params=vmem_limit(length),
    )(starts, dgate, dproj, gates, weights)


def finish_kernel(
    got_ref, gate_ref, later_ref, packed_ref, inner_ref, step_ref, small_ref, final_ref, *, heads
):
    rows, width = gate_ref.shape
    columns = packed_ref.shape[1]
    shared_cols = slice(width, columns - LANES)
    group = rows + 8
    total = got_ref[:group, :].astype(f32)
    for chip in range(1, got_ref.shape[0] // group):
        total = total + got_ref[chip * group : (chip + 1) * group, :].astype(f32)
    weights = total[:rows]
    small = total[rows:]
    gate = gate_ref[...]
    inner_ref[:, 0, :] = gate
    inner_ref[:, 1, :] = weights[:, :width]
    step_ref[...] = weights[:, columns - LANES :]
    small_ref[...] = small
    real = lax.broadcasted_iota(jnp.int32, (rows, columns), 1) < columns - LANES + heads
    scaled = jnp.where(real, weights * packed_ref[...].astype(f32), 0.0)
    norm = jnp.sum(scaled, axis=1, keepdims=True) + jnp.sum(
        gate * later_ref[...].astype(f32), axis=1, keepdims=True
    )
    final_ref[...] = jnp.zeros_like(final_ref)
    shared_size = columns - LANES - width
    final_ref[:rows, :shared_size] = weights[:, shared_cols]
    final_ref[rows:, :shared_size] = small[:, shared_cols]
    final_ref[:rows, shared_size:] = jnp.broadcast_to(norm, (rows, LANES))


def run_finish(got, gate, later, packed, heads):
    rows, width = gate.shape
    columns = packed.shape[1]
    sds = jax.ShapeDtypeStruct
    return pl.pallas_call(
        partial(finish_kernel, heads=heads),
        grid=(1,),
        in_specs=[
            fixed_spec(got),
            fixed_spec(gate),
            pl.BlockSpec((rows, width), lambda i: (0, 0)),
            fixed_spec(packed),
        ],
        out_specs=[
            pl.BlockSpec((rows, 2, width), lambda i: (0, 0, 0)),
            pl.BlockSpec((rows, LANES), lambda i: (0, 0)),
            pl.BlockSpec((8, columns), lambda i: (0, 0)),
            pl.BlockSpec((rows + 8, columns - width), lambda i: (0, 0)),
        ],
        out_shape=(
            sds((rows, 2, width), f32),
            sds((rows, LANES), f32),
            sds((8, columns), f32),
            sds((rows + 8, columns - width), f32),
        ),
        name="finish",
        cost_estimate=cost(2),
        compiler_params=vmem_limit(1024),
    )(got, gate, later, packed)


def after(value, *others):
    return lax.optimization_barrier((value,) + others)[0]


def cost(microseconds):
    return pl.CostEstimate(flops=int(microseconds * 1.1e9), transcendentals=0, bytes_accessed=0)


def stored(shape, kind):
    return pltpu.HBM(shape, kind)


def from_store(*values):
    return tuple(pltpu.with_memory_space_constraint(v, pltpu.HBM) for v in values)


def vmem_limit(length):
    return pltpu.CompilerParams(vmem_limit_bytes=min(60, VMEM_BASE + length // 128) << 20)


def pad_to(values, axis, size):
    pads = [(0, 0)] * values.ndim
    pads[axis] = (0, size - values.shape[axis])
    return jnp.pad(values, pads)


def body(
    hidden_in,
    segment_ids,
    norm_gain,
    proj_inner,
    proj_shared,
    proj_step,
    conv_inner,
    conv_shared,
    step_bias,
    log_decay,
    skip_gain,
    gate_gain,
    proj_out,
    out_grad,
):
    dp_count = lax.axis_size("dp")
    dp_index = lax.axis_index("dp")
    rows = proj_inner.shape[0]
    length = segment_ids.shape[0]
    model_dim = hidden_in.shape[1]
    local_inner = proj_inner.shape[2]
    heads = proj_step.shape[1]
    state_size = proj_shared.shape[2]
    kernel_len = conv_inner.shape[0]
    shared_size = 2 * state_size
    full_inner = local_inner * lax.axis_size("tensor")
    width = -(-local_inner // (2 * LANES)) * 2 * LANES
    tap_block = conv_shared.shape[2]
    tap_count = kernel_len * 2 * tap_block
    stages, core, table = block_plan()
    groups, core_table = core_groups()
    blocks = length // TOKEN_BLOCK
    starts = token_starts(blocks)
    two = lax.axis_size("tensor") == 2

    chips = dp_count // 2
    hidden_own, hidden_other = both_halves(hidden_in)
    tap_rows = conv_shared.transpose(1, 2, 0).reshape(2 * tap_block, kernel_len)
    tap_rows = pad_to(tap_rows, 0, rows)
    packed = jnp.concatenate(
        [
            pad_to(proj_inner[:, 1, :], 1, width),
            proj_shared.reshape(rows, shared_size),
            pad_to(jnp.concatenate([proj_step, norm_gain[:, None], tap_rows], axis=1), 1, LANES),
        ],
        axis=1,
    )
    later = jnp.concatenate(
        [pad_to(proj_inner[:, 0, :], 1, width), pad_to(proj_out.T, 1, width)], axis=1
    )
    at = jnp.arange(model_dim)
    block, inside = at // rows, at % rows
    side, spot = inside // tap_block, inside % tap_block
    spread = jnp.where(side < 2, side * state_size + block * tap_block + spot, -1)
    spread = (spread[:, None] == jnp.arange(shared_size)[None, :]).astype(bf16)
    aux, segr = token_facts(segment_ids)
    heads_block = jnp.stack([step_bias, log_decay, skip_gain])
    heads_block = pad_to(pad_to(heads_block, 1, LANES), 0, 8)
    tapi = pad_to(conv_inner, 1, width)
    gain = pad_to(gate_gain[None], 1, width)

    later_all = jnp.broadcast_to(later[None], (chips,) + later.shape)
    later_all = later_all.reshape(chips * rows, 2 * width)
    low = packed
    for number, stage in enumerate(stages):
        if number == len(stages) - 1:
            low, later_all = lax.optimization_barrier((low, later_all))
        got = lax.ppermute(low, "dp", stage)
        if number == 0:
            got, aux, segr = lax.optimization_barrier((got, aux, segr))
        if number == 1:
            got, heads_block, tapi, spread, table, core_table = lax.optimization_barrier(
                (got, heads_block, tapi, spread, table, core_table)
            )
        if number == len(stages) - 1:
            got, gain = lax.optimization_barrier((got, gain))
        low = jnp.concatenate([low, got], axis=0)
    later_low = exchange(later_all, groups)
    low, hidden_other = lax.optimization_barrier((low, hidden_other))
    high = lax.ppermute(low, "dp", core)
    grad_own, grad_other = both_halves(after(out_grad, hidden_other))

    proj, praw, normed, normed_t, weights, taps, norm_scale = run_project(
        starts, table, hidden_own, hidden_other, spread, low, high, heads
    )
    norm_scale = norm_scale[:1]
    mixed, u, su, entry = run_forward(proj, praw, tapi, taps, heads_block, aux, segr)

    later_low, mixed, grad_other = lax.optimization_barrier((later_low, mixed, grad_other))
    later_high = lax.ppermute(later_low, "dp", core)
    gate, nog, grad_t, sums, later_rows = run_out_grad(
        starts, core_table, grad_own, grad_other, later_low, later_high, normed, mixed, gain
    )
    if two:
        more = swap(sums)
    else:
        sums = lax.psum(sums, "tensor")
        more = jnp.zeros_like(sums)
    normed_out, dgate, mixed_grad, gain_rows, gkeep, gsend = run_gated(
        core_table, gate, nog, mixed, sums, more, aux, gain, grad_t, normed_t, full_inner
    )
    ggot = lax.ppermute(gsend, "dp", core)
    send_start = starts[1:] if two else jnp.zeros((1,), jnp.int32)
    out_send, out_keep = run_out(send_start, normed_out, later_rows)
    ggot, out_send = lax.optimization_barrier((ggot, out_send))
    gsum = exchange((gkeep.astype(f32) + ggot.astype(f32)).astype(bf16), groups)
    out_other = swap(out_send) if two else None

    dproj, wkeep, wsend = run_backward(
        core_table,
        proj,
        praw,
        u,
        su,
        entry,
        mixed_grad,
        tapi,
        taps,
        heads_block,
        aux,
        segr,
        gain_rows,
        normed_t,
    )
    if two:
        wsend, gsum, out_other = lax.optimization_barrier((wsend, gsum, out_other))
    else:
        wsend, gsum = lax.optimization_barrier((wsend, gsum))
    wgot = lax.ppermute(wsend, "dp", core)
    grad_send = run_norm_grad(send_start, dgate, dproj, later_rows, weights, bf16)
    wgot, grad_send = lax.optimization_barrier((wgot, grad_send))
    grad_other = swap(grad_send) if two else None
    held = rows * chips
    wtotal = (wkeep.astype(f32) + wgot.astype(f32)).astype(bf16)
    wtotal = jnp.concatenate(
        [
            wtotal[:held].reshape(chips, rows, -1),
            jnp.broadcast_to(wtotal[None, held:], (chips, 8, wtotal.shape[1])),
        ],
        axis=1,
    ).reshape(chips * (rows + 8), -1)
    wtotal, dproj = lax.optimization_barrier((wtotal, dproj))
    wsum = exchange(wtotal, groups)
    keep_start = starts[:1] if two else jnp.full((1,), blocks // 2, jnp.int32)
    grad_keep = run_norm_grad(keep_start, dgate, dproj, later_rows, weights, f32)
    if two:
        out_half = out_keep.astype(f32) + out_other.astype(f32)
        own_grad = grad_keep + grad_other.astype(f32)
    else:
        out_half = add_halves(out_send, out_keep)
        own_grad = add_halves(grad_send, grad_keep)
    hidden_out = (hidden_in.astype(f32) + out_half).astype(bf16)
    gsum = sum_blocks(gsum, rows)
    out_sum = gsum[:, width : width + local_inner].T
    inner_sum, step_sum, small, final = run_finish(wsum, gsum[:, :width], later, packed, heads)
    conv_total = small[:kernel_len, :local_inner]
    gain_total = small[4, :local_inner]
    skip_total = small[0, width + shared_size : width + shared_size + heads]
    bias_total = small[1, width + shared_size : width + shared_size + heads]
    decay_total = small[2, width + shared_size : width + shared_size + heads]
    final = total_over_tensor(final)
    shared_total = final[:rows, :shared_size].reshape(rows, 2, state_size)
    taps_total = lax.dynamic_slice_in_dim(
        final[rows : rows + kernel_len, :shared_size].reshape(kernel_len, 2, state_size),
        dp_index * tap_block,
        tap_block,
        axis=2,
    )
    norm_total = final[:rows, shared_size] / norm_gain.astype(f32)
    inner_sum = inner_sum[:, :, :local_inner]
    step_sum = step_sum[:, :heads]

    own = hidden_in.astype(f32)
    own_inv = lax.rsqrt(jnp.mean(own * own, axis=-1, keepdims=True) + epsilon)
    own_unit = own * own_inv
    scaled_in = own_grad * norm_scale
    hidden_grad = own_inv * (
        scaled_in - own_unit * jnp.mean(scaled_in * own_unit, axis=-1, keepdims=True)
    ) + out_grad.astype(f32)
    return (
        hidden_out,
        hidden_grad,
        norm_total,
        inner_sum,
        shared_total,
        step_sum,
        conv_total,
        taps_total,
        bias_total,
        decay_total,
        skip_total,
        gain_total,
        out_sum,
    )


def solution(mesh):
    in_specs = (
        P(("dp", "tensor"), None),
        P("dp"),
        P("dp"),
        P("dp", None, "tensor"),
        P("dp", None, None),
        P("dp", "tensor"),
        P(None, "tensor"),
        P(None, None, "dp"),
        P("tensor"),
        P("tensor"),
        P("tensor"),
        P("tensor"),
        P("tensor", "dp"),
        P(("dp", "tensor"), None),
    )
    out_specs = (
        P(("dp", "tensor"), None),
        P(("dp", "tensor"), None),
        P("dp"),
        P("dp", None, "tensor"),
        P("dp", None, None),
        P("dp", "tensor"),
        P(None, "tensor"),
        P(None, None, "dp"),
        P("tensor"),
        P("tensor"),
        P("tensor"),
        P("tensor"),
        P("tensor", "dp"),
    )
    return jax.shard_map(body, mesh=mesh, in_specs=in_specs, out_specs=out_specs, check_vma=False)
```
